32 devices in a mesh: dp: 4 (over y, core), wide: 4 (over z), narrow: 2 (over x).
Axes of the slice: x: 2, y: 2, z: 4, core: 2. Of those that a mesh axis runs over, the one named last changes fastest.
Arguments:
- patches: bfloat16 [2, 38535168], P('narrow', ('dp', 'wide')), may hold values from -6 to 6
- visible: int32 [512, 49], P(('dp', 'wide')), may hold values from 0 to 195, as said below
- w_qkv: bfloat16 [768, 3, 768], P('narrow', None, 'wide'), may hold values from -0.3125 to 0.3125
- b_qv: bfloat16 [2, 768], P(None, 'wide'), may hold values from -3 to 3
- w_out: bfloat16 [768, 768], P('wide', 'narrow'), may hold values from -0.875 to 0.875
- b_out: bfloat16 [768], P('narrow'), may hold values from -2 to 2
- w_up: bfloat16 [768, 3072], P('narrow', 'wide'), may hold values from -0.21875 to 0.21875
- b_up: bfloat16 [3072], P('wide'), may hold values from -3 to 3
- w_down: bfloat16 [768, 3072], P('narrow', 'wide'), may hold values from -0.15625 to 0.15625
- b_down: bfloat16 [768], P('narrow'), may hold values from -2 to 2
- gain_one: bfloat16 [768], P('narrow'), may hold values from 0.099609375 to 1.8984375
- shift_one: bfloat16 [768], P('narrow'), may hold values from -2 to 2
- gain_two: bfloat16 [768], P('narrow'), may hold values from 0.099609375 to 1.8984375
- shift_two: bfloat16 [768], P('narrow'), may hold values from -2 to 2
- cotangent: bfloat16 [2, 9633792], P('narrow', ('dp', 'wide')), may hold values from -6 to 6
Outputs:
- block_output: bfloat16 [2, 9633792], P('narrow', ('dp', 'wide'))
- grad_patches: float32 [2, 38535168], P('narrow', ('dp', 'wide'))
- grad_wqkv: float32 [768, 3, 768], P('narrow', None, 'wide')
- grad_bqv: float32 [2, 768], P(None, 'wide')
- grad_wout: float32 [768, 768], P('wide', 'narrow')
- grad_bout: float32 [768], P('narrow')
- grad_wup: float32 [768, 3072], P('narrow', 'wide')
- grad_bup: float32 [3072], P('wide')
- grad_wdown: float32 [768, 3072], P('narrow', 'wide')
- grad_bdown: float32 [768], P('narrow')
- grad_gain1: float32 [768], P('narrow')
- grad_shift1: float32 [768], P('narrow')
- grad_gain2: float32 [768], P('narrow')
- grad_shift2: float32 [768], P('narrow')
The draws below stay inside these ranges and needn't reach their ends.
Inputs may be any that keep to these rules, and one draw needn't show every extreme that they name: `visible`: each image's 49 indices are distinct and increasing.
All inputs are finite; a program needn't handle non-finite values.
Results may differ from the reference program's by a relative error of at most 0.012.
The reference program's roundings to bfloat16 on the way count: a program that leaves them out, or rounds other values in their place, can miss the bound.
Values may be sent and summed in bfloat16 or wider, within the bound.
No kernel may reach another device: no remote copies, remote signals or barrier semaphores. Data moves between devices by JAX's collectives and lax.ppermute only.
A program may use at most 256 MiB of HBM per device.

```python
import math
import jax
import jax.numpy as jnp
from jax import lax

D = 768
HEADS = 12
HEAD_DIM = 64
FF = 3072
PATCHES = 196
VISIBLE = 49
IMAGES = 512
TOKENS = 25088
FEAT_BLOCK = 384
N_NARROW = 2


def draw_visible(key, part):
    subkeys = jax.random.split(key, IMAGES)

    def pick_one(one_key):
        return jnp.sort(jax.random.permutation(one_key, PATCHES)[:VISIBLE])
    return jax.vmap(pick_one)(subkeys).astype(jnp.int32)


def shard_levels(key, shape, cuts, low, largest):
    def one(axis_at, blocks):
        draws = jax.random.uniform(jax.random.fold_in(jax.random.fold_in(key, 6), axis_at), (blocks,), jnp.float32, low / len(cuts), largest / len(cuts))
        return jnp.repeat(jnp.exp(draws), shape[axis_at] // blocks).reshape((-1,) + (1,) * (len(shape) - axis_at - 1))

    loudness = one(*cuts[0])
    for cut in cuts[1:]:
        loudness = loudness * one(*cut)
    return loudness


def normal_values(stream_key, extent, width, bound, pieces=(), held_as=jnp.bfloat16):
    level = shard_levels(stream_key, extent, pieces, -0.22, 0.18) if pieces else 1.0
    array = jax.random.normal(stream_key, extent, jnp.float32) * width * level
    return jnp.minimum(jnp.maximum(array, -bound), bound).astype(held_as)


def setup_inputs(seed: int = 0) -> dict:
    splits = jax.random.split(jax.random.key(seed), 16)
    patches = normal_values(splits[0], (N_NARROW, IMAGES * PATCHES * FEAT_BLOCK), 1.0, 6.0, ((0, 2), (1, 16)))
    visible = draw_visible(jax.random.fold_in(splits[15], 71), 0)
    w_qkv = normal_values(splits[2], (D, 3, D), (D // 2) ** -0.5, 0.3125, ((0, 2), (2, 4)))
    b_qv = normal_values(splits[3], (2, D), 0.5, 3.0, ((1, 4),))
    w_out = normal_values(splits[4], (D, D), (D // 16) ** -0.5, 0.875, ((0, 4), (1, 2)))
    b_out = normal_values(splits[5], (D,), 0.3, 2.0, ((0, 2),))
    w_up = normal_values(splits[6], (D, FF), D ** -0.5, 0.21875, ((0, 2), (1, 4)))
    b_up = normal_values(splits[7], (FF,), 0.5, 3.0, ((0, 4),))
    w_down = normal_values(splits[8], (D, FF), (FF // 2) ** -0.5, 0.15625, ((0, 2), (1, 4)))
    b_down = normal_values(splits[9], (D,), 0.3, 2.0, ((0, 2),))
    gain_one = jnp.clip(1.0 + 0.18 * jax.random.normal(splits[10], (D,), jnp.float32), 0.099609375, 1.8984375).astype(jnp.bfloat16)
    shift_one = normal_values(splits[11], (D,), 0.3, 2.0, ((0, 2),))
    gain_two = jnp.clip(1.0 + 0.18 * jax.random.normal(splits[12], (D,), jnp.float32), 0.099609375, 1.8984375).astype(jnp.bfloat16)
    shift_two = normal_values(splits[13], (D,), 0.3, 2.0, ((0, 2),))
    cotangent = normal_values(splits[14], (N_NARROW, TOKENS * FEAT_BLOCK), 1.0, 6.0, ((0, 2), (1, 16)))
    return {"patches": patches, "visible": visible, "w_qkv": w_qkv, "b_qv": b_qv, "w_out": w_out, "b_out": b_out, "w_up": w_up, "b_up": b_up, "w_down": w_down, "b_down": b_down, "gain_one": gain_one, "shift_one": shift_one, "gain_two": gain_two, "shift_two": shift_two, "cotangent": cotangent}


@jax.custom_vjp
def low(v):
    return lax.optimization_barrier(v.astype(jnp.bfloat16)).astype(jnp.float32)

@jax.custom_vjp
def low_back(v):
    return v

def low_keep(v):
    return (low(v), None)

def low_pass(kept, grad):
    return (grad,)

def back_keep(v):
    return (v, None)

def back_low(kept, grad):
    return (low(grad),)
low.defvjp(low_keep, low_pass)
low_back.defvjp(back_keep, back_low)

def product(left, right):
    return jnp.dot(left, right, precision=lax.Precision.HIGHEST, preferred_element_type=jnp.float32)

def layer_norm(values, gain, shift):
    row_mean = lax.optimization_barrier(jnp.mean(values, -1, keepdims=True))
    row_var = lax.optimization_barrier(jnp.mean(jnp.square(values - row_mean), -1, keepdims=True))
    return (values - row_mean) * lax.rsqrt(row_var + 1e-06) * gain + shift

def from_blocks(flat, count, rows):
    block = D // N_NARROW
    return flat.reshape(N_NARROW, count, rows, block).transpose(1, 2, 0, 3).reshape(count, rows, D)

def to_blocks(whole):
    block = D // N_NARROW
    count, rows = (whole.shape[0], whole.shape[1])
    return whole.reshape(count, rows, N_NARROW, block).transpose(2, 0, 1, 3).reshape(N_NARROW, count * rows * block)

def forward(patches, visible, w_qkv, b_qv, w_out, b_out, w_up, b_up, w_down, b_down, gain_one, shift_one, gain_two, shift_two):
    images = patches.shape[0]
    vis_rows = jnp.take_along_axis(patches, visible[:, :, None], axis=1).reshape(images * VISIBLE, D)
    hidden_one = low(layer_norm(vis_rows, gain_one, shift_one))
    bias_rows = jnp.stack([b_qv[0], jnp.zeros((D,), jnp.float32), b_qv[1]])
    triple = product(hidden_one, w_qkv.reshape(D, 3 * D)).reshape(-1, 3, D) + bias_rows
    triple = low_back(low(triple)).reshape(images, VISIBLE, 3, HEADS, HEAD_DIM)
    queries = triple[:, :, 0]
    keys_all = triple[:, :, 1]
    values_all = triple[:, :, 2]
    scores = jnp.einsum('nqhd,nkhd->nhqk', queries, keys_all, precision=lax.Precision.HIGHEST) * HEAD_DIM ** (-0.5)
    scores = low_back(scores)
    prob_low = low(jax.nn.softmax(scores, axis=-1))
    mixed = jnp.einsum('nhqk,nkhd->nqhd', prob_low, values_all, precision=lax.Precision.HIGHEST).reshape(-1, D)
    mixed = low_back(low(mixed))
    middle = vis_rows + low_back(product(mixed, w_out) + b_out)
    hidden_two = low(layer_norm(middle, gain_two, shift_two))
    inner = low_back(product(hidden_two, w_up) + b_up)
    active = low(jax.nn.gelu(inner, approximate=False))
    result = middle + low_back(product(active, w_down.T) + b_down)
    return result.reshape(images, VISIBLE, D)

def reference(patches, visible, w_qkv, b_qv, w_out, b_out, w_up, b_up, w_down, b_down, gain_one, shift_one, gain_two, shift_two, cotangent):
    floats = tuple((item.astype(jnp.float32) for item in (w_qkv, b_qv, w_out, b_out, w_up, b_up, w_down, b_down, gain_one, shift_one, gain_two, shift_two)))
    whole_patches = from_blocks(patches, IMAGES, PATCHES)
    whole_cot = from_blocks(cotangent, IMAGES, VISIBLE)
    group = math.gcd(IMAGES, 64)
    blocks = IMAGES // group

    def step(carry, item):
        part_patches, part_visible, part_cot = item

        def run(patch_block, *weight_list):
            return forward(patch_block, part_visible, *weight_list)
        output, pull = jax.vjp(run, part_patches.astype(jnp.float32), *floats)
        grads = pull(part_cot.astype(jnp.float32))
        carry = tuple((total + grad for total, grad in zip(carry, grads[1:])))
        return (carry, (output.astype(jnp.bfloat16), grads[0]))
    start = tuple((jnp.zeros(item.shape, jnp.float32) for item in floats))
    inputs = (whole_patches.reshape(blocks, group, PATCHES, D), visible.reshape(blocks, group, VISIBLE), whole_cot.reshape(blocks, group, VISIBLE, D))
    totals, (outputs, patch_grads) = lax.scan(step, start, inputs)
    block_output = to_blocks(outputs.reshape(IMAGES, VISIBLE, D))
    grad_patches = to_blocks(patch_grads.reshape(IMAGES, PATCHES, D))
    return (block_output, grad_patches, totals[0], totals[1], totals[2], totals[3], totals[4], totals[5], totals[6], totals[7], totals[8], totals[9], totals[10], totals[11])
```

```python
from functools import partial

import jax
import jax.numpy as jnp
from jax import lax
from jax.experimental import pallas as pl
from jax.experimental.pallas import tpu as pltpu
from jax.sharding import PartitionSpec as P

D = 768
HEAD_DIM = 64
HEADS = 12
PATCHES = 196
VISIBLE = 49
PAIR = 2 * VISIBLE
ROWS = 112
TILE = 256
EPS = 1e-06
BF = jnp.bfloat16
F32 = jnp.float32
MB = 1024 * 1024


def dot(a, b, ca, cb):
    return lax.dot_general(a, b, (((ca,), (cb,)), ((), ())), preferred_element_type=F32)


def call(body, grid, ins, outs, shapes, scratch=(), prefetch=0, flops=0, nbytes=0, vmem=48):
    return pl.pallas_call(
        body,
        out_shape=shapes,
        grid_spec=pltpu.PrefetchScalarGridSpec(
            num_scalar_prefetch=prefetch,
            grid=grid,
            in_specs=ins,
            out_specs=outs,
            scratch_shapes=scratch,
        ),
        compiler_params=pltpu.CompilerParams(
            dimension_semantics=("arbitrary",) * len(grid), vmem_limit_bytes=vmem * MB
        ),
        cost_estimate=pl.CostEstimate(flops=flops, bytes_accessed=nbytes, transcendentals=0),
    )


def spec(shape, index):
    return pl.BlockSpec(shape, index)


def struct(shape, dtype):
    return jax.ShapeDtypeStruct(shape, dtype)


def pick_body(cols, patch_ref, cot_ref, index_ref, rows_ref, cot_rows_ref, wide_ref, cot_scr):
    lanes = cols // 128
    wide_ref[...] = patch_ref[...].astype(F32).reshape(wide_ref.shape)
    parts = [wide_ref[pl.ds(k, 2 * PATCHES, stride=lanes), :] for k in range(lanes)]
    both = jnp.concatenate(parts, axis=1).astype(BF)
    hit = index_ref[0] == lax.broadcasted_iota(jnp.int32, (ROWS, 2 * PATCHES), 1)
    rows_ref[...] = dot(hit.astype(BF), both, 1, 0).astype(BF)
    cot_scr[...] = cot_ref[...].astype(F32).reshape(cot_scr.shape)
    parts = [cot_scr[pl.ds(k, PAIR, stride=lanes), :] for k in range(lanes)]
    cot = jnp.concatenate(parts, axis=1)
    cot_rows_ref[...] = jnp.concatenate(
        [cot, jnp.zeros((ROWS - PAIR, cols), F32)], axis=0
    ).astype(BF)


def pick_rows(patches, cotangent, index, cols):
    pairs = index.shape[0]
    width = 2 * PATCHES * cols
    cot_width = PAIR * cols
    return call(
        partial(pick_body, cols),
        (pairs,),
        [
            spec((1, width), lambda i: (0, i)),
            spec((1, cot_width), lambda i: (0, i)),
            spec((1, ROWS, 1), lambda i: (i, 0, 0)),
        ],
        [spec((ROWS, cols), lambda i: (i, 0)), spec((ROWS, cols), lambda i: (i, 0))],
        [struct((pairs * ROWS, cols), BF), struct((pairs * ROWS, cols), BF)],
        [pltpu.VMEM((width // 128, 128), F32), pltpu.VMEM((cot_width // 128, 128), F32)],
        flops=2 * pairs * ROWS * 2 * PATCHES * cols,
        nbytes=pairs * (width + cot_width) * 4,
    )(patches, cotangent, index)


def put_body(cols, rows_ref, index_ref, out_ref):
    lanes = cols // 128
    hit = index_ref[0] == lax.broadcasted_iota(jnp.int32, (ROWS, 2 * PATCHES), 1)
    hit = hit.astype(BF)
    rest = rows_ref[...]
    total = None
    for _ in range(3):
        part = rest.astype(BF)
        rest = rest - part.astype(F32)
        term = dot(hit, part, 0, 0)
        total = term if total is None else total + term
    for k in range(lanes):
        out_ref[pl.ds(k, 2 * PATCHES, stride=lanes), :] = total[:, k * 128 : (k + 1) * 128]


def put_rows(rows, index, cols):
    pairs = index.shape[0]
    tall = 2 * PATCHES * cols // 128
    return call(
        partial(put_body, cols),
        (pairs,),
        [spec((ROWS, cols), lambda i: (i, 0)), spec((1, ROWS, 1), lambda i: (i, 0, 0))],
        spec((tall, 128), lambda i: (i, 0)),
        struct((pairs * tall, 128), F32),
        flops=6 * pairs * ROWS * 2 * PATCHES * cols,
        nbytes=pairs * (tall * 512 + ROWS * cols * 4),
    )(rows, index)


def flat_body(cols, rows_ref, out_ref, scr):
    lanes = cols // 128
    rows = rows_ref[...].astype(F32)
    for k in range(lanes):
        scr[pl.ds(k, PAIR, stride=lanes), :] = rows[:PAIR, k * 128 : (k + 1) * 128]
    out_ref[...] = scr[...].reshape(out_ref.shape).astype(BF)


def flat_rows(rows, cols):
    pairs = rows.shape[0] // ROWS
    width = PAIR * cols
    return call(
        partial(flat_body, cols),
        (pairs,),
        [spec((ROWS, cols), lambda i: (i, 0))],
        spec((1, width), lambda i: (0, i)),
        struct((1, pairs * width), BF),
        [pltpu.VMEM((width // 128, 128), F32)],
        nbytes=pairs * width * 6,
    )(rows)


def stats(rows):
    mean = jnp.mean(rows, 1, keepdims=True)
    off = rows - mean
    inv = lax.rsqrt(jnp.mean(off * off, 1, keepdims=True) + EPS)
    return off * inv, inv


def norm_body(rows_ref, gain_ref, shift_ref, out_ref):
    normed, _ = stats(rows_ref[...].astype(F32))
    out_ref[...] = (normed * gain_ref[...] + shift_ref[...]).astype(BF)


def norm(rows, gain, shift):
    r = rows.shape[0]
    return call(
        norm_body,
        (r // ROWS,),
        [
            spec((ROWS, D), lambda i: (i, 0)),
            spec((1, D), lambda i: (0, 0)),
            spec((1, D), lambda i: (0, 0)),
        ],
        spec((ROWS, D), lambda i: (i, 0)),
        struct((r, D), BF),
        nbytes=r * D * 4,
    )(rows, gain, shift)


def qkv_body(hidden_ref, w_ref, bias_ref, out_ref):
    out_ref[...] = (dot(hidden_ref[...], w_ref[...], 1, 1) + bias_ref[...]).astype(BF)


def qkv(hidden, w, bias):
    r = hidden.shape[0]
    return call(
        qkv_body,
        (3 * D // TILE,),
        [
            spec((r, D), lambda j: (0, 0)),
            spec((TILE, D), lambda j: (j, 0)),
            spec((1, TILE), lambda j: (0, j)),
        ],
        spec((r, TILE), lambda j: (0, j)),
        struct((r, 3 * D), BF),
        flops=2 * r * D * 3 * D,
        nbytes=r * D * 8 + 3 * D * D * 2,
    )(hidden, w, bias)


def same_image():
    at_row = lax.broadcasted_iota(jnp.int32, (ROWS, ROWS), 0)
    at_col = lax.broadcasted_iota(jnp.int32, (ROWS, ROWS), 1)

    def image(at):
        return (at >= VISIBLE).astype(jnp.int32) + (at >= PAIR).astype(jnp.int32)

    return image(at_row) == image(at_col)


def attend_body(triple_ref, mixed_ref, prob_ref):
    keep = same_image()
    left = lax.broadcasted_iota(jnp.int32, (ROWS, 128), 1) < HEAD_DIM
    for pair in range(HEADS // 2):
        q = triple_ref[:, pair * 128 : (pair + 1) * 128]
        k = triple_ref[:, D + pair * 128 : D + (pair + 1) * 128]
        v = triple_ref[:, 2 * D + pair * 128 : 2 * D + (pair + 1) * 128]
        halves = []
        for side in range(2):
            mine = left if side == 0 else jnp.logical_not(left)
            scores = dot(jnp.where(mine, q, jnp.zeros_like(q)), k, 1, 1) * HEAD_DIM**-0.5
            scores = jnp.where(keep, scores, -1e30)
            expo = jnp.exp(scores - jnp.max(scores, 1, keepdims=True))
            prob = expo / jnp.sum(expo, 1, keepdims=True)
            prob_ref[0, 2 * pair + side] = prob
            halves.append(dot(prob.astype(BF), v, 1, 0))
        mixed_ref[:, pair * 128 : (pair + 1) * 128] = jnp.where(left, halves[0], halves[1]).astype(
            BF
        )


def attend(triple):
    groups = triple.shape[0] // ROWS
    return call(
        attend_body,
        (groups,),
        [spec((ROWS, 3 * D), lambda g: (g, 0))],
        [spec((ROWS, D), lambda g: (g, 0)), spec((1, HEADS, ROWS, ROWS), lambda g: (g, 0, 0, 0))],
        [struct((groups * ROWS, D), BF), struct((groups, HEADS, ROWS, ROWS), F32)],
        flops=groups * HEADS * 4 * ROWS * ROWS * 128,
        nbytes=groups * ROWS * (8 * D + HEADS * 512),
    )(triple)


def mix_body(mixed_ref, w_ref, bias_ref, rows_ref, gain_ref, shift_ref, middle_ref, hidden_ref):
    middle = rows_ref[...].astype(F32) + (dot(mixed_ref[...], w_ref[...], 1, 0) + bias_ref[...])
    middle_ref[...] = middle
    normed, _ = stats(middle)
    hidden_ref[...] = (normed * gain_ref[...] + shift_ref[...]).astype(BF)


def row_tile(r):
    return r // 2


def mix(mixed, w, bias, rows, gain, shift):
    r = rows.shape[0]
    m = row_tile(r)
    vec = spec((1, D), lambda i: (0, 0))
    row = spec((m, D), lambda i: (i, 0))
    return call(
        mix_body,
        (r // m,),
        [row, spec((D, D), lambda i: (0, 0)), vec, row, vec, vec],
        [row, row],
        [struct((r, D), F32), struct((r, D), BF)],
        flops=2 * r * D * D,
        nbytes=r * D * 10 + D * D * 2,
    )(mixed, w, bias, rows, gain, shift)


def up_body(hidden_ref, w_ref, bias_ref, active_ref, slope_ref):
    inner = dot(hidden_ref[...], w_ref[...], 1, 0) + bias_ref[...]
    phi = 0.5 * (1.0 + lax.erf(inner * (0.5**0.5)))
    active_ref[...] = (inner * phi).astype(BF)
    slope_ref[...] = phi + inner * (jnp.exp(-0.5 * inner * inner) * 0.3989422804014327)


def up(hidden, w, bias):
    r = hidden.shape[0]
    units = w.shape[1]
    tile = spec((r, TILE), lambda j: (0, j))
    return call(
        up_body,
        (units // TILE,),
        [
            spec((r, D), lambda j: (0, 0)),
            spec((D, TILE), lambda j: (0, j)),
            spec((1, TILE), lambda j: (0, j)),
        ],
        [tile, tile],
        [struct((r, units), BF), struct((r, units), F32)],
        flops=2 * r * D * units,
        nbytes=r * D * 2 + D * units * 2 + r * units * 6,
    )(hidden, w, bias)


def down_body(active_ref, w_ref, bias_ref, middle_ref, out_ref):
    out = middle_ref[...] + (dot(active_ref[...], w_ref[...], 1, 1) + bias_ref[...])
    out_ref[...] = out.astype(BF)


def down(active, w, bias, middle):
    r, units = active.shape
    m = row_tile(r)
    return call(
        down_body,
        (r // m,),
        [
            spec((m, units), lambda i: (i, 0)),
            spec((D, units), lambda i: (0, 0)),
            spec((1, D), lambda i: (0, 0)),
            spec((m, D), lambda i: (i, 0)),
        ],
        spec((m, D), lambda i: (i, 0)),
        struct((r, D), BF),
        flops=2 * r * D * units,
        nbytes=r * units * 2 + D * units * 2 + r * D * 6,
    )(active, w, bias, middle)


def outer_body(left_ref, right_ref, out_ref, sum_ref, turned):
    @pl.when(pl.program_id(0) == 0)
    def _():
        turned[...] = left_ref[...].T

    right = right_ref[...]
    out_ref[...] = dot(turned[...], right, 1, 0).astype(BF)
    sum_ref[...] = jnp.sum(right.astype(F32), 0, keepdims=True)


def outer(left, right):
    r, width = right.shape
    rows = left.shape[1]
    return call(
        outer_body,
        (width // TILE,),
        [spec((r, rows), lambda j: (0, 0)), spec((r, TILE), lambda j: (0, j))],
        [spec((rows, TILE), lambda j: (0, j)), spec((1, TILE), lambda j: (0, j))],
        [struct((rows, width), BF), struct((1, width), F32)],
        [pltpu.VMEM((rows, r), BF)],
        flops=2 * r * rows * width,
        nbytes=r * rows * 2 + r * width * 2 + rows * width * 2,
    )(left, right)


def inner_back_body(cot_ref, w_ref, slope_ref, hidden_ref, grad_ref, gw_ref, gb_ref, turned):
    @pl.when(pl.program_id(0) == 0)
    def _():
        turned[...] = hidden_ref[...].T

    grad = (dot(cot_ref[...], w_ref[...], 1, 0) * slope_ref[...]).astype(BF)
    grad_ref[...] = grad
    gw_ref[...] = dot(turned[...], grad, 1, 0).astype(BF)
    gb_ref[...] = jnp.sum(grad.astype(F32), 0, keepdims=True)


def inner_back(cot, w, slope, hidden):
    r, units = slope.shape
    full = spec((r, D), lambda j: (0, 0))
    col = spec((D, TILE), lambda j: (0, j))
    tile = spec((r, TILE), lambda j: (0, j))
    return call(
        inner_back_body,
        (units // TILE,),
        [full, col, tile, full],
        [tile, col, spec((1, TILE), lambda j: (0, j))],
        [struct((r, units), BF), struct((D, units), BF), struct((1, units), F32)],
        [pltpu.VMEM((D, r), BF)],
        flops=4 * r * D * units,
        nbytes=r * D * 4 + D * units * 4 + r * units * 6,
    )(cot, w, slope, hidden)


def norm_pull(grad, normed, inv, gain):
    scaled = grad * gain
    return inv * (
        scaled
        - jnp.mean(scaled, 1, keepdims=True)
        - normed * jnp.mean(scaled * normed, 1, keepdims=True)
    )


def middle_back_body(
    grad_ref, w_ref, middle_ref, cot_ref, gain_ref, out_ref, branch_ref, gain_sum, shift_sum, out_sum
):
    grad = dot(grad_ref[...], w_ref[...], 1, 1)
    normed, inv = stats(middle_ref[...])
    total = cot_ref[...].astype(F32) + norm_pull(grad, normed, inv, gain_ref[...])
    out_ref[...] = total
    branch = total.astype(BF)
    branch_ref[...] = branch
    sums = (
        (gain_sum, jnp.sum(grad * normed, 0, keepdims=True)),
        (shift_sum, jnp.sum(grad, 0, keepdims=True)),
        (out_sum, jnp.sum(branch.astype(F32), 0, keepdims=True)),
    )
    for ref, value in sums:
        add_up(ref, value)


def add_up(ref, value):
    @pl.when(pl.program_id(0) == 0)
    def _():
        ref[...] = value

    @pl.when(pl.program_id(0) != 0)
    def _():
        ref[...] += value


def middle_back(grad, w, middle, cot, gain):
    r, units = grad.shape
    m = row_tile(r)
    vec = spec((1, D), lambda i: (0, 0))
    row = spec((m, D), lambda i: (i, 0))
    vec_out = struct((1, D), F32)
    return call(
        middle_back_body,
        (r // m,),
        [spec((m, units), lambda i: (i, 0)), spec((D, units), lambda i: (0, 0)), row, row, vec],
        [row, row, vec, vec, vec],
        [struct((r, D), F32), struct((r, D), BF), vec_out, vec_out, vec_out],
        flops=2 * r * D * units,
        nbytes=r * units * 2 + D * units * 2 + r * D * 12,
    )(grad, w, middle, cot, gain)


def mixed_back_body(branch_ref, tile_ref, w_ref, mixed_ref, grad_ref, gw_ref, turned):
    @pl.when(pl.program_id(0) == 0)
    def _():
        turned[...] = mixed_ref[...].T

    grad_ref[...] = dot(branch_ref[...], w_ref[...], 1, 1).astype(BF)
    gw_ref[...] = dot(turned[...], tile_ref[...], 1, 0).astype(BF)


def mixed_back(branch, w, mixed):
    r = branch.shape[0]
    full = spec((r, D), lambda j: (0, 0))
    tile = spec((r, TILE), lambda j: (0, j))
    return call(
        mixed_back_body,
        (D // TILE,),
        [full, tile, spec((TILE, D), lambda j: (j, 0)), full],
        [tile, spec((D, TILE), lambda j: (0, j))],
        [struct((r, D), BF), struct((D, D), BF)],
        [pltpu.VMEM((D, r), BF)],
        flops=4 * r * D * D,
        nbytes=r * D * 8 + D * D * 4,
    )(branch, branch, w, mixed)


def attend_back_body(triple_ref, prob_ref, grad_ref, out_ref):
    left = lax.broadcasted_iota(jnp.int32, (ROWS, 128), 1) < HEAD_DIM
    scale = HEAD_DIM**-0.5
    for pair in range(HEADS // 2):
        q = triple_ref[:, pair * 128 : (pair + 1) * 128]
        k = triple_ref[:, D + pair * 128 : D + (pair + 1) * 128]
        v = triple_ref[:, 2 * D + pair * 128 : 2 * D + (pair + 1) * 128]
        grad = grad_ref[:, pair * 128 : (pair + 1) * 128]
        gq, gk, gv = [], [], []
        for side in range(2):
            mine = left if side == 0 else jnp.logical_not(left)
            prob = prob_ref[0, 2 * pair + side]
            gv.append(dot(prob.astype(BF), grad, 0, 0))
            grad_prob = dot(jnp.where(mine, grad, jnp.zeros_like(grad)), v, 1, 1)
            inside = jnp.sum(grad_prob * prob, 1, keepdims=True)
            grad_scores = (prob * (grad_prob - inside)).astype(BF)
            gq.append(dot(grad_scores, k, 1, 0))
            gk.append(dot(grad_scores, q, 0, 0))
        for at, pieces, factor in ((0, gq, scale), (1, gk, scale), (2, gv, None)):
            both = jnp.where(left, pieces[0], pieces[1])
            if factor is not None:
                both = both * factor
            out_ref[:, at * D + pair * 128 : at * D + (pair + 1) * 128] = both.astype(BF)


def attend_back(triple, prob, grad):
    groups = triple.shape[0] // ROWS
    wide = spec((ROWS, 3 * D), lambda g: (g, 0))
    return call(
        attend_back_body,
        (groups,),
        [
            wide,
            spec((1, HEADS, ROWS, ROWS), lambda g: (g, 0, 0, 0)),
            spec((ROWS, D), lambda g: (g, 0)),
        ],
        wide,
        struct((groups * ROWS, 3 * D), BF),
        flops=groups * HEADS * 8 * ROWS * ROWS * 128,
        nbytes=groups * ROWS * (14 * D + HEADS * 512),
    )(triple, prob, grad)


def qkv_grad_body(grad_ref, hidden_ref, gw_ref, gb_ref):
    grad = grad_ref[...]
    gw_ref[...] = dot(grad.T, hidden_ref[...], 1, 0).astype(BF)
    gb_ref[...] = jnp.sum(grad.astype(F32), 0, keepdims=True)


def qkv_grad(grad, hidden):
    r, width = grad.shape
    return call(
        qkv_grad_body,
        (width // TILE,),
        [spec((r, TILE), lambda j: (0, j)), spec((r, D), lambda j: (0, 0))],
        [spec((TILE, D), lambda j: (j, 0)), spec((1, TILE), lambda j: (0, j))],
        [struct((width, D), BF), struct((1, width), F32)],
        flops=2 * r * D * width,
        nbytes=r * width * 2 + r * D * 2 + width * D * 2,
    )(grad, hidden)


def first_back_body(grad_ref, w_ref, rows_ref, middle_ref, gain_ref, out_ref, gain_sum, shift_sum):
    grad = dot(grad_ref[...], w_ref[...], 1, 0)
    normed, inv = stats(rows_ref[...].astype(F32))
    out_ref[...] = middle_ref[...] + norm_pull(grad, normed, inv, gain_ref[...])
    add_up(gain_sum, jnp.sum(grad * normed, 0, keepdims=True))
    add_up(shift_sum, jnp.sum(grad, 0, keepdims=True))


def first_back(grad, w, rows, grad_middle, gain):
    r, width = grad.shape
    m = row_tile(r)
    vec = spec((1, D), lambda i: (0, 0))
    row = spec((m, D), lambda i: (i, 0))
    vec_out = struct((1, D), F32)
    return call(
        first_back_body,
        (r // m,),
        [spec((m, width), lambda i: (i, 0)), spec((width, D), lambda i: (0, 0)), row, row, vec],
        [row, vec, vec],
        [struct((r, D), F32), vec_out, vec_out],
        flops=2 * r * D * width,
        nbytes=r * width * 2 + D * width * 2 + r * D * 10,
    )(grad, w, rows, grad_middle, gain)


def to_rows(blocks, narrow):
    got = lax.all_to_all(blocks, "narrow", 0, 0, tiled=True)
    return jnp.concatenate([got[n] for n in range(narrow)], axis=1)


def from_rows(rows, narrow):
    cols = rows.shape[1] // narrow
    blocks = jnp.stack([rows[:, n * cols : (n + 1) * cols] for n in range(narrow)])
    got = lax.all_to_all(blocks, "narrow", 0, 0, tiled=True)
    return got.reshape(-1, cols)


def gather_weight(shard, wide, narrow):
    got = lax.all_gather(shard.reshape(-1, 128), ("wide", "narrow"), axis=0, tiled=True)
    return got.reshape((wide, narrow) + shard.shape)


def scatter_grad(blocks):
    shape = blocks.shape[2:]
    got = lax.psum_scatter(
        blocks.reshape(-1, 128), ("wide", "narrow"), scatter_dimension=0, tiled=True
    )
    return lax.psum(got.astype(F32), "dp").reshape(shape)


def on_device(
    wide,
    narrow,
    patches,
    visible,
    w_qkv,
    b_qv,
    w_out,
    b_out,
    w_up,
    b_up,
    w_down,
    b_down,
    gain_one,
    shift_one,
    gain_two,
    shift_two,
    cotangent,
):
    images = visible.shape[0]
    pairs = images // 2
    cols = w_qkv.shape[0]
    heads_cols = w_qkv.shape[2]
    units = w_up.shape[1]

    index = (visible.reshape(pairs, 2, VISIBLE) + jnp.array([0, PATCHES])[None, :, None]).reshape(
        pairs, PAIR
    )
    index = jnp.pad(index, ((0, 0), (0, ROWS - PAIR)), constant_values=-1)[:, :, None]

    if cols % 128 == 0:
        rows_mine, cot_mine = pick_rows(patches, cotangent, index, cols)
    else:
        table = patches.reshape(images, PATCHES, cols)
        rows_mine = jnp.take_along_axis(table, visible[:, :, None], axis=1)
        rows_mine = jnp.pad(
            rows_mine.reshape(pairs, PAIR, cols), ((0, 0), (0, ROWS - PAIR), (0, 0))
        )
        cot_mine = jnp.pad(
            cotangent.reshape(pairs, PAIR, cols), ((0, 0), (0, ROWS - PAIR), (0, 0))
        )
    rows = to_rows(rows_mine.reshape(narrow, -1, cols), narrow)
    cot = to_rows(cot_mine.reshape(narrow, -1, cols), narrow)

    vec = jnp.concatenate(
        [gain_one, shift_one, gain_two, shift_two, b_out, b_down, b_qv.reshape(-1), b_up]
    )
    vec = lax.all_gather(vec, ("wide", "narrow"), axis=0, tiled=False).astype(F32)
    vec = vec.reshape(wide, narrow, -1)
    by_narrow = vec[0, :, : 6 * cols].reshape(narrow, 6, cols).transpose(1, 0, 2).reshape(6, 1, D)
    gain_a, shift_a, gain_b, shift_b, bias_out, bias_down = (by_narrow[i] for i in range(6))
    by_wide = vec[:, 0, 6 * cols :]
    bias_q = by_wide[:, :heads_cols].reshape(1, D)
    bias_v = by_wide[:, heads_cols : 2 * heads_cols].reshape(1, D)
    bias_qkv = jnp.concatenate([bias_q, jnp.zeros((1, D), F32), bias_v], axis=1)
    bias_up = by_wide[:, 2 * heads_cols :].reshape(1, -1)

    qkv_t = gather_weight(w_qkv.transpose(1, 2, 0), wide, narrow)
    qkv_t = qkv_t.transpose(2, 0, 3, 1, 4).reshape(3 * D, D)
    out_w = gather_weight(w_out, wide, narrow).transpose(0, 2, 1, 3).reshape(D, D)
    up_w = gather_weight(w_up, wide, narrow).transpose(1, 2, 0, 3).reshape(D, -1)
    down_w = gather_weight(w_down, wide, narrow).transpose(1, 2, 0, 3).reshape(D, -1)

    hidden_one = norm(rows, gain_a, shift_a)
    triple = qkv(hidden_one, qkv_t, bias_qkv)
    mixed, prob = attend(triple)
    middle, hidden_two = mix(mixed, out_w, bias_out, rows, gain_b, shift_b)
    active, slope = up(hidden_two, up_w, bias_up)
    result = down(active, down_w, bias_down, middle)

    gw_down, _ = outer(cot, active)
    gb_down = jnp.sum(cot, 0, dtype=F32)
    grad_inner, gw_up, gb_up = inner_back(cot, down_w, slope, hidden_two)
    grad_middle, branch, gg_two, gs_two, gb_out = middle_back(grad_inner, up_w, middle, cot, gain_b)
    grad_mixed, gw_out = mixed_back(branch, out_w, mixed)
    grad_triple = attend_back(triple, prob, grad_mixed)
    gw_qkv, gb_qkv = qkv_grad(grad_triple, hidden_one)
    grad_rows, gg_one, gs_one = first_back(grad_triple, qkv_t, rows, grad_middle, gain_a)

    result = from_rows(result, narrow)
    grad_rows = from_rows(grad_rows, narrow)
    if cols % 128 == 0:
        block_output = flat_rows(result, cols)
        grad_patches = put_rows(grad_rows, index, cols).reshape(1, -1)
    else:
        block_output = result.reshape(pairs, ROWS, cols)[:, :PAIR].reshape(1, -1)
        grad_rows = grad_rows.reshape(pairs, ROWS, cols)[:, :PAIR].reshape(images, VISIBLE, cols)
        grad_patches = (
            jnp.zeros((images, PATCHES, cols), F32)
            .at[jnp.arange(images)[:, None], visible]
            .set(grad_rows)
            .reshape(1, -1)
        )

    g_down = scatter_grad(gw_down.reshape(narrow, cols, wide, units).transpose(2, 0, 1, 3))
    g_up = scatter_grad(gw_up.reshape(narrow, cols, wide, units).transpose(2, 0, 1, 3))
    g_out = scatter_grad(gw_out.reshape(wide, heads_cols, narrow, cols).transpose(0, 2, 1, 3))
    g_qkv = scatter_grad(
        gw_qkv.reshape(3, wide, heads_cols, narrow, cols).transpose(1, 3, 0, 2, 4)
    )
    g_qkv = g_qkv.transpose(2, 0, 1)

    sums = jnp.concatenate(
        [
            gg_one[0],
            gs_one[0],
            gg_two[0],
            gs_two[0],
            gb_out[0],
            gb_down,
            gb_qkv[0, :D],
            gb_qkv[0, 2 * D :],
            gb_up[0],
        ]
    )
    sums = lax.psum(sums, ("dp", "wide", "narrow"))
    at_narrow = lax.axis_index("narrow") * cols
    at_wide = lax.axis_index("wide")

    def narrow_part(i):
        return lax.dynamic_slice_in_dim(sums, i * D + at_narrow, cols)

    g_bqv = jnp.stack(
        [
            lax.dynamic_slice_in_dim(sums, (6 + i) * D + at_wide * heads_cols, heads_cols)
            for i in range(2)
        ]
    )
    g_bup = lax.dynamic_slice_in_dim(sums, 8 * D + at_wide * units, units)
    return (
        block_output,
        grad_patches,
        g_qkv,
        g_bqv,
        g_out,
        narrow_part(4),
        g_up,
        g_bup,
        g_down,
        narrow_part(5),
        narrow_part(0),
        narrow_part(1),
        narrow_part(2),
        narrow_part(3),
    )


def solution(mesh):
    in_specs = (
        P("narrow", ("dp", "wide")),
        P(("dp", "wide"), None),
        P("narrow", None, "wide"),
        P(None, "wide"),
        P("wide", "narrow"),
        P("narrow"),
        P("narrow", "wide"),
        P("wide"),
        P("narrow", "wide"),
        P("narrow"),
        P("narrow"),
        P("narrow"),
        P("narrow"),
        P("narrow"),
        P("narrow", ("dp", "wide")),
    )
    out_specs = (
        P("narrow", ("dp", "wide")),
        P("narrow", ("dp", "wide")),
        P("narrow", None, "wide"),
        P(None, "wide"),
        P("wide", "narrow"),
        P("narrow"),
        P("narrow", "wide"),
        P("wide"),
        P("narrow", "wide"),
        P("narrow"),
        P("narrow"),
        P("narrow"),
        P("narrow"),
        P("narrow"),
    )
    body = partial(on_device, mesh.shape["wide"], mesh.shape["narrow"])
    return jax.shard_map(body, mesh=mesh, in_specs=in_specs, out_specs=out_specs, check_vma=False)
```

```python
from functools import partial

import jax
import jax.numpy as jnp
from jax import lax
from jax.experimental import pallas as pl
from jax.experimental.pallas import tpu as pltpu
from jax.sharding import PartitionSpec as P

D = 768
HEAD_DIM = 64
HEADS = 12
PATCHES = 196
VISIBLE = 49
PAIR = 2 * VISIBLE
ROWS = 112
TILE = 256
EPS = 1e-06
BF = jnp.bfloat16
F32 = jnp.float32
MB = 1024 * 1024


def dot(a, b, ca, cb):
    return lax.dot_general(a, b, (((ca,), (cb,)), ((), ())), preferred_element_type=F32)


def call(body, grid, ins, outs, shapes, scratch=(), prefetch=0, flops=0, nbytes=0, vmem=48):
    return pl.pallas_call(
        body,
        out_shape=shapes,
        grid_spec=pltpu.PrefetchScalarGridSpec(
            num_scalar_prefetch=prefetch,
            grid=grid,
            in_specs=ins,
            out_specs=outs,
            scratch_shapes=scratch,
        ),
        compiler_params=pltpu.CompilerParams(
            dimension_semantics=("arbitrary",) * len(grid), vmem_limit_bytes=vmem * MB
        ),
        cost_estimate=pl.CostEstimate(flops=flops, bytes_accessed=nbytes, transcendentals=0),
    )


def spec(shape, index):
    return pl.BlockSpec(shape, index)


def struct(shape, dtype):
    return jax.ShapeDtypeStruct(shape, dtype)


def pick_body(
    cols, at_ref, patch_ref, cot_ref, index_ref, rows_ref, cot_rows_ref, wide_ref, cot_scr
):
    lanes = cols // 128
    wide_ref[...] = patch_ref[...].astype(F32).reshape(wide_ref.shape)
    parts = [wide_ref[pl.ds(k, 2 * PATCHES, stride=lanes), :] for k in range(lanes)]
    both = jnp.concatenate(parts, axis=1).astype(BF)
    hit = index_ref[0] == lax.broadcasted_iota(jnp.int32, (ROWS, 2 * PATCHES), 1)
    rows_ref[...] = dot(hit.astype(BF), both, 1, 0).astype(BF)
    cot_scr[...] = cot_ref[...].astype(F32).reshape(cot_scr.shape)
    parts = [cot_scr[pl.ds(k, PAIR, stride=lanes), :] for k in range(lanes)]
    cot = jnp.concatenate(parts, axis=1)
    cot_rows_ref[...] = jnp.concatenate(
        [cot, jnp.zeros((ROWS - PAIR, cols), F32)], axis=0
    ).astype(BF)


def pick_rows(at, patches, cotangent, index, cols):
    pairs = index.shape[0]
    own = pairs // 2
    width = 2 * PATCHES * cols
    cot_width = PAIR * cols

    def source(i, at):
        return (i // own ^ 1 ^ at[1]) * own + i % own

    return call(
        partial(pick_body, cols),
        (pairs,),
        [
            spec((1, width), lambda i, at: (0, source(i, at))),
            spec((1, cot_width), lambda i, at: (0, source(i, at))),
            spec((1, ROWS, 1), lambda i, at: (source(i, at), 0, 0)),
        ],
        [spec((ROWS, cols), lambda i, at: (i, 0)), spec((ROWS, cols), lambda i, at: (i, 0))],
        [struct((pairs * ROWS, cols), BF), struct((pairs * ROWS, cols), BF)],
        [pltpu.VMEM((width // 128, 128), F32), pltpu.VMEM((cot_width // 128, 128), F32)],
        prefetch=1,
        flops=2 * pairs * ROWS * 2 * PATCHES * cols,
        nbytes=pairs * (width + cot_width) * 4,
    )(at, patches, cotangent, index)


def own_block(at_ref, keep_ref, got_ref):
    own = pl.num_programs(0) // 2
    mine = pl.program_id(0) // own == at_ref[1]
    return jnp.where(mine, keep_ref[...].astype(F32), got_ref[...].astype(F32))


def put_body(cols, at_ref, keep_ref, got_ref, index_ref, out_ref):
    lanes = cols // 128
    hit = index_ref[0] == lax.broadcasted_iota(jnp.int32, (ROWS, 2 * PATCHES), 1)
    hit = hit.astype(BF)
    rest = own_block(at_ref, keep_ref, got_ref)
    total = None
    for _ in range(3):
        part = rest.astype(BF)
        rest = rest - part.astype(F32)
        term = dot(hit, part, 0, 0)
        total = term if total is None else total + term
    for k in range(lanes):
        out_ref[pl.ds(k, 2 * PATCHES, stride=lanes), :] = total[:, k * 128 : (k + 1) * 128]


def put_rows(at, keep, got, index, cols):
    pairs = index.shape[0]
    own = pairs // 2
    tall = 2 * PATCHES * cols // 128
    rows = spec((ROWS, cols), lambda i, at: (i % own, 0))
    return call(
        partial(put_body, cols),
        (pairs,),
        [rows, rows, spec((1, ROWS, 1), lambda i, at: (i, 0, 0))],
        spec((tall, 128), lambda i, at: (i, 0)),
        struct((pairs * tall, 128), F32),
        prefetch=1,
        flops=6 * pairs * ROWS * 2 * PATCHES * cols,
        nbytes=pairs * (tall * 512 + ROWS * cols * 4),
    )(at, keep, got, index)


def flat_body(cols, at_ref, keep_ref, got_ref, out_ref, scr):
    lanes = cols // 128
    rows = own_block(at_ref, keep_ref, got_ref)
    for k in range(lanes):
        scr[pl.ds(k, PAIR, stride=lanes), :] = rows[:PAIR, k * 128 : (k + 1) * 128]
    out_ref[...] = scr[...].reshape(out_ref.shape).astype(BF)


def flat_rows(at, keep, got, cols):
    own = keep.shape[0] // ROWS
    pairs = 2 * own
    width = PAIR * cols
    rows = spec((ROWS, cols), lambda i, at: (i % own, 0))
    return call(
        partial(flat_body, cols),
        (pairs,),
        [rows, rows],
        spec((1, width), lambda i, at: (0, i)),
        struct((1, pairs * width), BF),
        [pltpu.VMEM((width // 128, 128), F32)],
        prefetch=1,
        nbytes=pairs * width * 6,
    )(at, keep, got)


def stats(rows):
    mean = jnp.mean(rows, 1, keepdims=True)
    off = rows - mean
    inv = lax.rsqrt(jnp.mean(off * off, 1, keepdims=True) + EPS)
    return off * inv, inv


def norm_body(rows_ref, gain_ref, shift_ref, out_ref):
    normed, _ = stats(rows_ref[...].astype(F32))
    out_ref[...] = (normed * gain_ref[...] + shift_ref[...]).astype(BF)


def norm(rows, gain, shift):
    r = rows.shape[0]
    return call(
        norm_body,
        (r // ROWS,),
        [
            spec((ROWS, D), lambda i: (i, 0)),
            spec((1, D), lambda i: (0, 0)),
            spec((1, D), lambda i: (0, 0)),
        ],
        spec((ROWS, D), lambda i: (i, 0)),
        struct((r, D), BF),
        nbytes=r * D * 4,
    )(rows, gain, shift)


def qkv_body(hidden_ref, w_ref, bias_ref, out_ref):
    out_ref[...] = (dot(hidden_ref[...], w_ref[...], 1, 1) + bias_ref[...]).astype(BF)


def qkv(hidden, w, bias):
    r = hidden.shape[0]
    return call(
        qkv_body,
        (3 * D // TILE,),
        [
            spec((r, D), lambda j: (0, 0)),
            spec((TILE, D), lambda j: (j, 0)),
            spec((1, TILE), lambda j: (0, j)),
        ],
        spec((r, TILE), lambda j: (0, j)),
        struct((r, 3 * D), BF),
        flops=2 * r * D * 3 * D,
        nbytes=r * D * 8 + 3 * D * D * 2,
    )(hidden, w, bias)


def same_image():
    at_row = lax.broadcasted_iota(jnp.int32, (ROWS, ROWS), 0)
    at_col = lax.broadcasted_iota(jnp.int32, (ROWS, ROWS), 1)

    def image(at):
        return (at >= VISIBLE).astype(jnp.int32) + (at >= PAIR).astype(jnp.int32)

    return image(at_row) == image(at_col)


def attend_body(triple_ref, mixed_ref, prob_ref):
    keep = same_image()
    left = lax.broadcasted_iota(jnp.int32, (ROWS, 128), 1) < HEAD_DIM
    for pair in range(HEADS // 2):
        q = triple_ref[:, pair * 128 : (pair + 1) * 128]
        k = triple_ref[:, D + pair * 128 : D + (pair + 1) * 128]
        v = triple_ref[:, 2 * D + pair * 128 : 2 * D + (pair + 1) * 128]
        halves = []
        for side in range(2):
            mine = left if side == 0 else jnp.logical_not(left)
            scores = dot(jnp.where(mine, q, jnp.zeros_like(q)), k, 1, 1) * HEAD_DIM**-0.5
            scores = jnp.where(keep, scores, -1e30)
            expo = jnp.exp(scores - jnp.max(scores, 1, keepdims=True))
            prob = expo / jnp.sum(expo, 1, keepdims=True)
            prob_ref[0, 2 * pair + side] = prob
            halves.append(dot(prob.astype(BF), v, 1, 0))
        mixed_ref[:, pair * 128 : (pair + 1) * 128] = jnp.where(left, halves[0], halves[1]).astype(
            BF
        )


def attend(triple):
    groups = triple.shape[0] // ROWS
    return call(
        attend_body,
        (groups,),
        [spec((ROWS, 3 * D), lambda g: (g, 0))],
        [spec((ROWS, D), lambda g: (g, 0)), spec((1, HEADS, ROWS, ROWS), lambda g: (g, 0, 0, 0))],
        [struct((groups * ROWS, D), BF), struct((groups, HEADS, ROWS, ROWS), F32)],
        flops=groups * HEADS * 4 * ROWS * ROWS * 128,
        nbytes=groups * ROWS * (8 * D + HEADS * 512),
    )(triple)


def mix_body(mixed_ref, w_ref, bias_ref, rows_ref, gain_ref, shift_ref, middle_ref, hidden_ref):
    middle = rows_ref[...].astype(F32) + (dot(mixed_ref[...], w_ref[...], 1, 0) + bias_ref[...])
    middle_ref[...] = middle
    normed, _ = stats(middle)
    hidden_ref[...] = (normed * gain_ref[...] + shift_ref[...]).astype(BF)


def row_tile(r):
    return r // 2


def mix(mixed, w, bias, rows, gain, shift):
    r = rows.shape[0]
    m = row_tile(r)
    vec = spec((1, D), lambda i: (0, 0))
    row = spec((m, D), lambda i: (i, 0))
    return call(
        mix_body,
        (r // m,),
        [row, spec((D, D), lambda i: (0, 0)), vec, row, vec, vec],
        [row, row],
        [struct((r, D), F32), struct((r, D), BF)],
        flops=2 * r * D * D,
        nbytes=r * D * 10 + D * D * 2,
    )(mixed, w, bias, rows, gain, shift)


def up_body(hidden_ref, w_ref, bias_ref, active_ref, slope_ref):
    inner = dot(hidden_ref[...], w_ref[...], 1, 0) + bias_ref[...]
    phi = 0.5 * (1.0 + lax.erf(inner * (0.5**0.5)))
    active_ref[...] = (inner * phi).astype(BF)
    slope_ref[...] = phi + inner * (jnp.exp(-0.5 * inner * inner) * 0.3989422804014327)


def up(hidden, w, bias):
    r = hidden.shape[0]
    units = w.shape[1]
    tile = spec((r, TILE), lambda j: (0, j))
    return call(
        up_body,
        (units // TILE,),
        [
            spec((r, D), lambda j: (0, 0)),
            spec((D, TILE), lambda j: (0, j)),
            spec((1, TILE), lambda j: (0, j)),
        ],
        [tile, tile],
        [struct((r, units), BF), struct((r, units), F32)],
        flops=2 * r * D * units,
        nbytes=r * D * 2 + D * units * 2 + r * units * 6,
    )(hidden, w, bias)


def down_body(active_ref, w_ref, bias_ref, middle_ref, out_ref):
    out = middle_ref[...] + (dot(active_ref[...], w_ref[...], 1, 1) + bias_ref[...])
    out_ref[...] = out.astype(BF)


def down(active, w, bias, middle):
    r, units = active.shape
    m = row_tile(r)
    return call(
        down_body,
        (r // m,),
        [
            spec((m, units), lambda i: (i, 0)),
            spec((D, units), lambda i: (0, 0)),
            spec((1, D), lambda i: (0, 0)),
            spec((m, D), lambda i: (i, 0)),
        ],
        spec((m, D), lambda i: (i, 0)),
        struct((r, D), BF),
        flops=2 * r * D * units,
        nbytes=r * units * 2 + D * units * 2 + r * D * 6,
    )(active, w, bias, middle)


def outer_body(left_ref, right_ref, out_ref, sum_ref, turned):
    @pl.when(pl.program_id(0) == 0)
    def _():
        turned[...] = left_ref[...].T

    right = right_ref[...]
    out_ref[...] = dot(turned[...], right, 1, 0).astype(BF)
    sum_ref[...] = jnp.sum(right.astype(F32), 0, keepdims=True)


def outer(left, right):
    r, width = right.shape
    rows = left.shape[1]
    return call(
        outer_body,
        (width // TILE,),
        [spec((r, rows), lambda j: (0, 0)), spec((r, TILE), lambda j: (0, j))],
        [spec((rows, TILE), lambda j: (0, j)), spec((1, TILE), lambda j: (0, j))],
        [struct((rows, width), BF), struct((1, width), F32)],
        [pltpu.VMEM((rows, r), BF)],
        flops=2 * r * rows * width,
        nbytes=r * rows * 2 + r * width * 2 + rows * width * 2,
    )(left, right)


def inner_back_body(cot_ref, w_ref, slope_ref, hidden_ref, grad_ref, gw_ref, gb_ref, turned):
    @pl.when(pl.program_id(0) == 0)
    def _():
        turned[...] = hidden_ref[...].T

    grad = (dot(cot_ref[...], w_ref[...], 1, 0) * slope_ref[...]).astype(BF)
    grad_ref[...] = grad
    gw_ref[...] = dot(turned[...], grad, 1, 0).astype(BF)
    gb_ref[...] = jnp.sum(grad.astype(F32), 0, keepdims=True)


def inner_back(cot, w, slope, hidden):
    r, units = slope.shape
    full = spec((r, D), lambda j: (0, 0))
    col = spec((D, TILE), lambda j: (0, j))
    tile = spec((r, TILE), lambda j: (0, j))
    return call(
        inner_back_body,
        (units // TILE,),
        [full, col, tile, full],
        [tile, col, spec((1, TILE), lambda j: (0, j))],
        [struct((r, units), BF), struct((D, units), BF), struct((1, units), F32)],
        [pltpu.VMEM((D, r), BF)],
        flops=4 * r * D * units,
        nbytes=r * D * 4 + D * units * 4 + r * units * 6,
    )(cot, w, slope, hidden)


def norm_pull(grad, normed, inv, gain):
    scaled = grad * gain
    return inv * (
        scaled
        - jnp.mean(scaled, 1, keepdims=True)
        - normed * jnp.mean(scaled * normed, 1, keepdims=True)
    )


def middle_back_body(
    grad_ref, w_ref, middle_ref, cot_ref, gain_ref, out_ref, branch_ref, gain_sum, shift_sum, out_sum
):
    grad = dot(grad_ref[...], w_ref[...], 1, 1)
    normed, inv = stats(middle_ref[...])
    total = cot_ref[...].astype(F32) + norm_pull(grad, normed, inv, gain_ref[...])
    out_ref[...] = total
    branch = total.astype(BF)
    branch_ref[...] = branch
    sums = (
        (gain_sum, jnp.sum(grad * normed, 0, keepdims=True)),
        (shift_sum, jnp.sum(grad, 0, keepdims=True)),
        (out_sum, jnp.sum(branch.astype(F32), 0, keepdims=True)),
    )
    for ref, value in sums:
        add_up(ref, value)


def add_up(ref, value):
    @pl.when(pl.program_id(0) == 0)
    def _():
        ref[...] = value

    @pl.when(pl.program_id(0) != 0)
    def _():
        ref[...] += value


def middle_back(grad, w, middle, cot, gain):
    r, units = grad.shape
    m = row_tile(r)
    vec = spec((1, D), lambda i: (0, 0))
    row = spec((m, D), lambda i: (i, 0))
    vec_out = struct((1, D), F32)
    return call(
        middle_back_body,
        (r // m,),
        [spec((m, units), lambda i: (i, 0)), spec((D, units), lambda i: (0, 0)), row, row, vec],
        [row, row, vec, vec, vec],
        [struct((r, D), F32), struct((r, D), BF), vec_out, vec_out, vec_out],
        flops=2 * r * D * units,
        nbytes=r * units * 2 + D * units * 2 + r * D * 12,
    )(grad, w, middle, cot, gain)


def mixed_back_body(branch_ref, tile_ref, w_ref, mixed_ref, grad_ref, gw_ref, turned):
    @pl.when(pl.program_id(0) == 0)
    def _():
        turned[...] = mixed_ref[...].T

    grad_ref[...] = dot(branch_ref[...], w_ref[...], 1, 1).astype(BF)
    gw_ref[...] = dot(turned[...], tile_ref[...], 1, 0).astype(BF)


def mixed_back(branch, w, mixed):
    r = branch.shape[0]
    full = spec((r, D), lambda j: (0, 0))
    tile = spec((r, TILE), lambda j: (0, j))
    return call(
        mixed_back_body,
        (D // TILE,),
        [full, tile, spec((TILE, D), lambda j: (j, 0)), full],
        [tile, spec((D, TILE), lambda j: (0, j))],
        [struct((r, D), BF), struct((D, D), BF)],
        [pltpu.VMEM((D, r), BF)],
        flops=4 * r * D * D,
        nbytes=r * D * 8 + D * D * 4,
    )(branch, branch, w, mixed)


def attend_back_body(triple_ref, prob_ref, grad_ref, out_ref):
    left = lax.broadcasted_iota(jnp.int32, (ROWS, 128), 1) < HEAD_DIM
    scale = HEAD_DIM**-0.5
    for pair in range(HEADS // 2):
        q = triple_ref[:, pair * 128 : (pair + 1) * 128]
        k = triple_ref[:, D + pair * 128 : D + (pair + 1) * 128]
        v = triple_ref[:, 2 * D + pair * 128 : 2 * D + (pair + 1) * 128]
        grad = grad_ref[:, pair * 128 : (pair + 1) * 128]
        gq, gk, gv = [], [], []
        for side in range(2):
            mine = left if side == 0 else jnp.logical_not(left)
            prob = prob_ref[0, 2 * pair + side]
            gv.append(dot(prob.astype(BF), grad, 0, 0))
            grad_prob = dot(jnp.where(mine, grad, jnp.zeros_like(grad)), v, 1, 1)
            inside = jnp.sum(grad_prob * prob, 1, keepdims=True)
            grad_scores = (prob * (grad_prob - inside)).astype(BF)
            gq.append(dot(grad_scores, k, 1, 0))
            gk.append(dot(grad_scores, q, 0, 0))
        for at, pieces, factor in ((0, gq, scale), (1, gk, scale), (2, gv, None)):
            both = jnp.where(left, pieces[0], pieces[1])
            if factor is not None:
                both = both * factor
            out_ref[:, at * D + pair * 128 : at * D + (pair + 1) * 128] = both.astype(BF)


def attend_back(triple, prob, grad):
    groups = triple.shape[0] // ROWS
    wide = spec((ROWS, 3 * D), lambda g: (g, 0))
    return call(
        attend_back_body,
        (groups,),
        [
            wide,
            spec((1, HEADS, ROWS, ROWS), lambda g: (g, 0, 0, 0)),
            spec((ROWS, D), lambda g: (g, 0)),
        ],
        wide,
        struct((groups * ROWS, 3 * D), BF),
        flops=groups * HEADS * 8 * ROWS * ROWS * 128,
        nbytes=groups * ROWS * (14 * D + HEADS * 512),
    )(triple, prob, grad)


def qkv_grad_body(grad_ref, hidden_ref, gw_ref, gb_ref):
    grad = grad_ref[...]
    gw_ref[...] = dot(grad.T, hidden_ref[...], 1, 0).astype(BF)
    gb_ref[...] = jnp.sum(grad.astype(F32), 0, keepdims=True)


def qkv_grad(grad, hidden):
    r, width = grad.shape
    return call(
        qkv_grad_body,
        (width // TILE,),
        [spec((r, TILE), lambda j: (0, j)), spec((r, D), lambda j: (0, 0))],
        [spec((TILE, D), lambda j: (j, 0)), spec((1, TILE), lambda j: (0, j))],
        [struct((width, D), BF), struct((1, width), F32)],
        flops=2 * r * D * width,
        nbytes=r * width * 2 + r * D * 2 + width * D * 2,
    )(grad, hidden)


def first_back_body(grad_ref, w_ref, rows_ref, middle_ref, gain_ref, out_ref, gain_sum, shift_sum):
    grad = dot(grad_ref[...], w_ref[...], 1, 0)
    normed, inv = stats(rows_ref[...].astype(F32))
    out_ref[...] = middle_ref[...] + norm_pull(grad, normed, inv, gain_ref[...])
    add_up(gain_sum, jnp.sum(grad * normed, 0, keepdims=True))
    add_up(shift_sum, jnp.sum(grad, 0, keepdims=True))


def first_back(grad, w, rows, grad_middle, gain):
    r, width = grad.shape
    m = row_tile(r)
    vec = spec((1, D), lambda i: (0, 0))
    row = spec((m, D), lambda i: (i, 0))
    vec_out = struct((1, D), F32)
    return call(
        first_back_body,
        (r // m,),
        [spec((m, width), lambda i: (i, 0)), spec((width, D), lambda i: (0, 0)), row, row, vec],
        [row, vec, vec],
        [struct((r, D), F32), vec_out, vec_out],
        flops=2 * r * D * width,
        nbytes=r * width * 2 + D * width * 2 + r * D * 10,
    )(grad, w, rows, grad_middle, gain)


WIDE, NARROW, DP = "wide", "narrow", "dp"


def swap(value, axis, bit):
    size = lax.axis_size(axis)
    return lax.ppermute(value, axis, [(i, i ^ bit) for i in range(size)])


def gather_pieces(piece, steps):
    stack, tags = piece[None], [(0, 0, 0)]
    for axis, bit in steps:
        got = swap(stack, axis, bit)
        move = (bit if axis == WIDE else 0, bit if axis == NARROW else 0, 0)
        stack = jnp.concatenate([stack, got])
        tags = tags + [tuple(a ^ b for a, b in zip(tag, move)) for tag in tags]
    other = swap(stack, DP, 1)
    return [(stack, tags), (other, [(a, b, 1) for a, b, _ in tags])]


def qkv_plan(cols, heads_cols):
    half = heads_cols // 2

    def plan(w, n, h):
        return [
            (0, (pl.ds(p * half, half), slice(None)), (p * D + w * heads_cols + h * half, n * cols))
            for p in range(3)
        ]

    return plan


def flat_plan(cols, units):
    half = cols // 2

    def plan(w, n, h):
        return [(0, (pl.ds(0, half), slice(None)), (n * cols + h * half, w * units))]

    return plan


def up_out_plan(cols, units, heads_cols):
    half = cols // 2
    part = heads_cols // 4

    def plan(w, n, h):
        moves = flat_plan(cols, units)(w, n, h)
        for s in range(2):
            at = (pl.ds(half, part), pl.ds(s * cols, cols))
            moves.append((1, at, (w * heads_cols + h * 2 * part + s * part, n * cols)))
        return moves

    return plan


def build_body(plan, tag_lists, n_out, inverse, at_ref, *refs):
    arrays, outs, sem = refs[: len(tag_lists)], refs[len(tag_lists) : -1], refs[-1]
    if inverse:
        outs, arrays = refs[:n_out], refs[n_out:-1]
    copies = []
    for array, tags in zip(arrays, tag_lists):
        for k, (dw, dn, dc) in enumerate(tags):
            w, n, h = at_ref[0] ^ dw, at_ref[1] ^ dn, at_ref[2] ^ dc
            for which, src, (row, lane) in plan(w, n, h):
                piece = array.at[(k,) + src]
                shape = piece.shape
                whole = outs[which].at[
                    pl.ds(pl.multiple_of(row, 16), shape[-2]),
                    pl.ds(pl.multiple_of(lane, 128), shape[-1]),
                ]
                ends = (whole, piece) if inverse else (piece, whole)
                copies.append(pltpu.make_async_copy(*ends, sem.at[len(copies)]))
    for copy in copies:
        copy.start()
    for copy in copies:
        copy.wait()


ANY = pl.BlockSpec(memory_space=pl.ANY)


def build_weights(at, pieces, plan, shapes):
    arrays = [stack for stack, _ in pieces]
    tags = [t for _, t in pieces]
    moves = sum(len(t) for t in tags) * len(plan(0, 0, 0))
    return pl.pallas_call(
        partial(build_body, plan, tags, len(shapes), False),
        out_shape=[struct(shape, BF) for shape in shapes],
        grid_spec=pltpu.PrefetchScalarGridSpec(
            num_scalar_prefetch=1,
            grid=(1,),
            in_specs=[ANY] * len(arrays),
            out_specs=[ANY] * len(shapes),
            scratch_shapes=[pltpu.SemaphoreType.DMA((moves,))],
        ),
        compiler_params=pltpu.CompilerParams(vmem_limit_bytes=4 * MB),
        cost_estimate=pl.CostEstimate(
            flops=0, bytes_accessed=2 * sum(a.size * 2 for a in arrays), transcendentals=0
        ),
    )(at, *arrays)


def cut_grads(at, grads, plan, tags, shape):
    tag_lists = [[(w, n, dc) for w, n in tags] for dc in range(2)]
    moves = 2 * len(tags) * len(plan(0, 0, 0))
    return pl.pallas_call(
        partial(build_body, plan, tag_lists, len(grads), True),
        out_shape=[struct((len(tags),) + shape, BF)] * 2,
        grid_spec=pltpu.PrefetchScalarGridSpec(
            num_scalar_prefetch=1,
            grid=(1,),
            in_specs=[ANY] * len(grads),
            out_specs=[ANY] * 2,
            scratch_shapes=[pltpu.SemaphoreType.DMA((moves,))],
        ),
        compiler_params=pltpu.CompilerParams(vmem_limit_bytes=4 * MB),
        cost_estimate=pl.CostEstimate(
            flops=0, bytes_accessed=sum(g.size * 4 for g in grads), transcendentals=0
        ),
    )(at, *grads)


def reduce_pieces(kept, sent, steps):
    kept = kept.astype(F32) + swap(sent, DP, 1).astype(F32)
    for axis, bit in steps:
        half = kept.shape[0] // 2
        got = swap(kept[half:].astype(BF), axis, bit)
        kept = kept[:half] + got.astype(F32)
    kept = kept[0]
    bit = 2
    while bit < lax.axis_size(DP):
        kept = kept + swap(kept.astype(BF), DP, bit).astype(F32)
        bit *= 2
    return kept


def both_halves(at, mine):
    other = swap(mine, DP, 1)
    return jnp.where(at[2] == 0, jnp.stack([mine, other]), jnp.stack([other, mine]))


def half_of(at, shard):
    half = shard.shape[-2] // 2
    return lax.dynamic_slice_in_dim(shard, at[2] * half, half, axis=shard.ndim - 2)


def total_over_all(value, axes):
    for axis in axes:
        bit = 1
        while bit < lax.axis_size(axis):
            value = value + swap(value, axis, bit)
            bit *= 2
    return value


def to_rows(blocks, narrow):
    got = lax.all_to_all(blocks, "narrow", 0, 0, tiled=True)
    return jnp.concatenate([got[n] for n in range(narrow)], axis=1)


def from_rows(rows, narrow):
    cols = rows.shape[1] // narrow
    blocks = jnp.stack([rows[:, n * cols : (n + 1) * cols] for n in range(narrow)])
    got = lax.all_to_all(blocks, "narrow", 0, 0, tiled=True)
    return got.reshape(-1, cols)


def gather_weight(shard, wide, narrow):
    got = lax.all_gather(shard.reshape(-1, 128), ("wide", "narrow"), axis=0, tiled=True)
    return got.reshape((wide, narrow) + shard.shape)


def scatter_grad(blocks):
    shape = blocks.shape[2:]
    got = lax.psum_scatter(
        blocks.reshape(-1, 128), ("wide", "narrow"), scatter_dimension=0, tiled=True
    )
    return lax.psum(got.astype(F32), "dp").reshape(shape)


def on_device(
    wide,
    narrow,
    patches,
    visible,
    w_qkv,
    b_qv,
    w_out,
    b_out,
    w_up,
    b_up,
    w_down,
    b_down,
    gain_one,
    shift_one,
    gain_two,
    shift_two,
    cotangent,
):
    images = visible.shape[0]
    pairs = images // 2
    cols = w_qkv.shape[0]
    heads_cols = w_qkv.shape[2]
    units = w_up.shape[1]
    swaps = cols % 128 == 0 and narrow == 2 and wide == 4 and pairs % 2 == 0

    at = jnp.stack(
        [lax.axis_index("wide"), lax.axis_index("narrow"), lax.axis_index("dp") % 2]
    ).astype(jnp.int32)

    index = (visible.reshape(pairs, 2, VISIBLE) + jnp.array([0, PATCHES])[None, :, None]).reshape(
        pairs, PAIR
    )
    index = jnp.pad(index, ((0, 0), (0, ROWS - PAIR)), constant_values=-1)[:, :, None]

    w_qkv_t = w_qkv.transpose(1, 2, 0)
    vec = jnp.concatenate(
        [gain_one, shift_one, gain_two, shift_two, b_out, b_down, b_qv.reshape(-1), b_up]
    )
    if swaps:
        vec_rows = vec.size // cols
        vec_rows_pad = -(-vec_rows // 16) * 16
        first = jnp.concatenate(
            [
                half_of(at, w_qkv_t).reshape(-1, cols),
                jnp.pad(vec.reshape(vec_rows, cols), ((0, vec_rows_pad - vec_rows), (0, 0))),
            ]
        )
        first = gather_pieces(first, [(NARROW, 1), (WIDE, 2), (WIDE, 1)])
        (qkv_t,) = build_weights(at, first, qkv_plan(cols, heads_cols), [(3 * D, D)])
        vecs = first[0][0][:, -vec_rows_pad:]
        order = [(w, n) for w, n, _ in first[0][1]]
        rel = [order.index((w, n)) for w in range(wide) for n in range(narrow)]
        vecs = vecs[:, :vec_rows].reshape(wide * narrow, -1)
        slot = jnp.array(rel)[
            (jnp.arange(wide)[:, None] ^ at[0]) * narrow + (jnp.arange(narrow)[None, :] ^ at[1])
        ]
        hot = (slot.reshape(-1)[:, None] == jnp.arange(wide * narrow)[None, :]).astype(BF)
        vec = jnp.dot(hot, vecs, preferred_element_type=F32)

        rows_out, cot_out = pick_rows(at, patches, cotangent, index, cols)
        own = rows_out.shape[0] // 2

        def join(keep, got):
            return jnp.where(
                at[1] == 0,
                jnp.concatenate([keep, got], axis=1),
                jnp.concatenate([got, keep], axis=1),
            )

        rows = join(rows_out[own:], swap(rows_out[:own], NARROW, 1))
        cot = join(cot_out[own:], swap(cot_out[:own], NARROW, 1))

        out_half = half_of(at, w_out)
        part = out_half.shape[0] // 2
        second = jnp.concatenate(
            [half_of(at, w_up), jnp.concatenate([out_half[:part], out_half[part:]], axis=1)]
        )
        second = gather_pieces(second, [(WIDE, 2), (WIDE, 1), (NARROW, 1)])
        up_w, out_w = build_weights(
            at, second, up_out_plan(cols, units, heads_cols), [(D, wide * units), (D, D)]
        )
        third = gather_pieces(half_of(at, w_down), [(WIDE, 2), (WIDE, 1), (NARROW, 1)])
        (down_w,) = build_weights(at, third, flat_plan(cols, units), [(D, wide * units)])
    else:
        table = patches.reshape(images, PATCHES, cols)
        rows_mine = jnp.take_along_axis(table, visible[:, :, None], axis=1)
        rows_mine = jnp.pad(
            rows_mine.reshape(pairs, PAIR, cols), ((0, 0), (0, ROWS - PAIR), (0, 0))
        )
        cot_mine = jnp.pad(
            cotangent.reshape(pairs, PAIR, cols), ((0, 0), (0, ROWS - PAIR), (0, 0))
        )
        rows = to_rows(rows_mine.reshape(narrow, -1, cols), narrow)
        cot = to_rows(cot_mine.reshape(narrow, -1, cols), narrow)
        vec = lax.all_gather(vec, ("wide", "narrow"), axis=0, tiled=False).astype(F32)
        qkv_t = gather_weight(w_qkv_t, wide, narrow)
        qkv_t = qkv_t.transpose(2, 0, 3, 1, 4).reshape(3 * D, D)
        out_w = gather_weight(w_out, wide, narrow).transpose(0, 2, 1, 3).reshape(D, D)
        up_w = gather_weight(w_up, wide, narrow).transpose(1, 2, 0, 3).reshape(D, -1)
        down_w = gather_weight(w_down, wide, narrow).transpose(1, 2, 0, 3).reshape(D, -1)

    vec = vec.reshape(wide, narrow, -1)
    by_narrow = vec[0, :, : 6 * cols].reshape(narrow, 6, cols).transpose(1, 0, 2).reshape(6, 1, D)
    gain_a, shift_a, gain_b, shift_b, bias_out, bias_down = (by_narrow[i] for i in range(6))
    by_wide = vec[:, 0, 6 * cols :]
    bias_q = by_wide[:, :heads_cols].reshape(1, D)
    bias_v = by_wide[:, heads_cols : 2 * heads_cols].reshape(1, D)
    bias_qkv = jnp.concatenate([bias_q, jnp.zeros((1, D), F32), bias_v], axis=1)
    bias_up = by_wide[:, 2 * heads_cols :].reshape(1, -1)

    hidden_one = norm(rows, gain_a, shift_a)
    triple = qkv(hidden_one, qkv_t, bias_qkv)
    mixed, prob = attend(triple)
    middle, hidden_two = mix(mixed, out_w, bias_out, rows, gain_b, shift_b)
    active, slope = up(hidden_two, up_w, bias_up)
    result = down(active, down_w, bias_down, middle)

    gw_down, _ = outer(cot, active)
    gb_down = jnp.sum(cot, 0, dtype=F32)
    grad_inner, gw_up, gb_up = inner_back(cot, down_w, slope, hidden_two)
    grad_middle, branch, gg_two, gs_two, gb_out = middle_back(grad_inner, up_w, middle, cot, gain_b)
    grad_mixed, gw_out = mixed_back(branch, out_w, mixed)
    grad_triple = attend_back(triple, prob, grad_mixed)
    gw_qkv, gb_qkv = qkv_grad(grad_triple, hidden_one)
    grad_rows, gg_one, gs_one = first_back(grad_triple, qkv_t, rows, grad_middle, gain_a)
    sums = jnp.concatenate(
        [
            gg_one[0],
            gs_one[0],
            gg_two[0],
            gs_two[0],
            gb_out[0],
            gb_down,
            gb_qkv[0, :D],
            gb_qkv[0, 2 * D :],
            gb_up[0],
        ]
    )

    if swaps:

        def part_of(whole, side):
            return lax.dynamic_slice_in_dim(whole, side * cols, cols, axis=1)

        mine, theirs = at[1], 1 - at[1]
        block_output = flat_rows(
            at, part_of(result, mine), swap(part_of(result, theirs), NARROW, 1), cols
        )
        grad_patches = put_rows(
            at,
            part_of(grad_rows, mine),
            swap(part_of(grad_rows, theirs).astype(BF), NARROW, 1),
            index,
            cols,
        ).reshape(1, -1)

        def reduced(grads, plan, shape):
            tags = [(w, n) for n in range(2) for w in (0, 2, 1, 3)]
            kept, sent = cut_grads(at, grads, plan, tags, shape)
            got = reduce_pieces(kept, sent, [(NARROW, 1), (WIDE, 1), (WIDE, 2)])
            return both_halves(at, got)

        g_down = reduced([gw_down], flat_plan(cols, units), (cols // 2, units)).reshape(cols, units)
        g_up = reduced([gw_up], flat_plan(cols, units), (cols // 2, units)).reshape(cols, units)

        def out_plan(w, n, h):
            half = heads_cols // 2
            return [(0, (slice(None), slice(None)), (w * heads_cols + h * half, n * cols))]

        g_out = reduced([gw_out], out_plan, (heads_cols // 2, cols)).reshape(heads_cols, cols)
        g_qkv = reduced([gw_qkv], qkv_plan(cols, heads_cols), (3 * heads_cols // 2, cols))
        g_qkv = g_qkv.reshape(2, 3, heads_cols // 2, cols).transpose(3, 1, 0, 2)
        g_qkv = g_qkv.reshape(cols, 3, heads_cols)
        sums = total_over_all(sums.reshape(-1, 128), ("dp", "narrow", "wide")).reshape(-1)
    else:
        result = from_rows(result, narrow)
        grad_rows = from_rows(grad_rows, narrow)
        block_output = result.reshape(pairs, ROWS, cols)[:, :PAIR].reshape(1, -1)
        grad_rows = grad_rows.reshape(pairs, ROWS, cols)[:, :PAIR].reshape(images, VISIBLE, cols)
        grad_patches = (
            jnp.zeros((images, PATCHES, cols), F32)
            .at[jnp.arange(images)[:, None], visible]
            .set(grad_rows)
            .reshape(1, -1)
        )
        g_down = scatter_grad(gw_down.reshape(narrow, cols, wide, units).transpose(2, 0, 1, 3))
        g_up = scatter_grad(gw_up.reshape(narrow, cols, wide, units).transpose(2, 0, 1, 3))
        g_out = scatter_grad(gw_out.reshape(wide, heads_cols, narrow, cols).transpose(0, 2, 1, 3))
        g_qkv = scatter_grad(
            gw_qkv.reshape(3, wide, heads_cols, narrow, cols).transpose(1, 3, 0, 2, 4)
        )
        g_qkv = g_qkv.transpose(2, 0, 1)
        sums = lax.psum(sums, ("dp", "wide", "narrow"))

    at_narrow = at[1] * cols
    at_wide = at[0]

    def narrow_part(i):
        return lax.dynamic_slice_in_dim(sums, i * D + at_narrow, cols)

    g_bqv = jnp.stack(
        [
            lax.dynamic_slice_in_dim(sums, (6 + i) * D + at_wide * heads_cols, heads_cols)
            for i in range(2)
        ]
    )
    g_bup = lax.dynamic_slice_in_dim(sums, 8 * D + at_wide * units, units)
    return (
        block_output,
        grad_patches,
        g_qkv,
        g_bqv,
        g_out,
        narrow_part(4),
        g_up,
        g_bup,
        g_down,
        narrow_part(5),
        narrow_part(0),
        narrow_part(1),
        narrow_part(2),
        narrow_part(3),
    )


def solution(mesh):
    in_specs = (
        P("narrow", ("dp", "wide")),
        P(("dp", "wide"), None),
        P("narrow", None, "wide"),
        P(None, "wide"),
        P("wide", "narrow"),
        P("narrow"),
        P("narrow", "wide"),
        P("wide"),
        P("narrow", "wide"),
        P("narrow"),
        P("narrow"),
        P("narrow"),
        P("narrow"),
        P("narrow"),
        P("narrow", ("dp", "wide")),
    )
    out_specs = (
        P("narrow", ("dp", "wide")),
        P("narrow", ("dp", "wide")),
        P("narrow", None, "wide"),
        P(None, "wide"),
        P("wide", "narrow"),
        P("narrow"),
        P("narrow", "wide"),
        P("wide"),
        P("narrow", "wide"),
        P("narrow"),
        P("narrow"),
        P("narrow"),
        P("narrow"),
        P("narrow"),
    )
    body = partial(on_device, mesh.shape["wide"], mesh.shape["narrow"])
    return jax.shard_map(body, mesh=mesh, in_specs=in_specs, out_specs=out_specs, check_vma=False)
```

```python
from functools import partial

import jax
import jax.numpy as jnp
from jax import lax
from jax.experimental import pallas as pl
from jax.experimental.pallas import tpu as pltpu
from jax.sharding import PartitionSpec as P

D = 768
HEAD_DIM = 64
HEADS = 12
PATCHES = 196
VISIBLE = 49
PAIR = 2 * VISIBLE
ROWS = 112
TILE = 256
EPS = 1e-06
BF = jnp.bfloat16
F32 = jnp.float32
MB = 1024 * 1024


def dot(a, b, ca, cb):
    return lax.dot_general(a, b, (((ca,), (cb,)), ((), ())), preferred_element_type=F32)


FLOPS_PER_US = 540000000


def call(body, grid, ins, outs, shapes, scratch=(), prefetch=0, us=1.0, nbytes=0, vmem=24):
    return pl.pallas_call(
        body,
        out_shape=shapes,
        grid_spec=pltpu.PrefetchScalarGridSpec(
            num_scalar_prefetch=prefetch,
            grid=grid,
            in_specs=ins,
            out_specs=outs,
            scratch_shapes=scratch,
        ),
        compiler_params=pltpu.CompilerParams(
            dimension_semantics=("arbitrary",) * len(grid), vmem_limit_bytes=vmem * MB
        ),
        cost_estimate=pl.CostEstimate(
            flops=int(us * FLOPS_PER_US), bytes_accessed=1024, transcendentals=0
        ),
    )


def in_hbm(value):
    return pltpu.with_memory_space_constraint(value, pltpu.HBM)


def spec(shape, index):
    return pl.BlockSpec(shape, index)


def struct(shape, dtype):
    return jax.ShapeDtypeStruct(shape, dtype)


def pick_body(cols, at_ref, patch_ref, index_ref, rows_ref, wide_ref):
    lanes = cols // 128
    wide_ref[...] = patch_ref[...].astype(F32).reshape(wide_ref.shape)
    parts = [wide_ref[pl.ds(k, 2 * PATCHES, stride=lanes), :] for k in range(lanes)]
    both = jnp.concatenate(parts, axis=1).astype(BF)
    hit = index_ref[0] == lax.broadcasted_iota(jnp.int32, (ROWS, 2 * PATCHES), 1)
    rows_ref[...] = dot(hit.astype(BF), both, 1, 0).astype(BF)


def owner_first_sent(own):
    def source(i, at):
        return (i // own ^ 1 ^ at[1]) * own + i % own

    return source


def pick_rows(at, patches, index, cols):
    pairs = index.shape[0]
    width = 2 * PATCHES * cols
    source = owner_first_sent(pairs // 2)
    return call(
        partial(pick_body, cols),
        (pairs,),
        [
            spec((1, width), lambda i, at: (0, source(i, at))),
            spec((1, ROWS, 1), lambda i, at: (source(i, at), 0, 0)),
        ],
        spec((ROWS, cols), lambda i, at: (i, 0)),
        struct((pairs * ROWS, cols), BF),
        [pltpu.VMEM((width // 128, 128), F32)],
        prefetch=1,
        us=200,
        nbytes=pairs * width * 4,
    )(at, patches, index)


def cot_body(cols, at_ref, cot_ref, rows_ref, scr):
    lanes = cols // 128
    scr[...] = cot_ref[...].astype(F32).reshape(scr.shape)
    parts = [scr[pl.ds(k, PAIR, stride=lanes), :] for k in range(lanes)]
    cot = jnp.concatenate(parts, axis=1)
    rows_ref[...] = jnp.concatenate([cot, jnp.zeros((ROWS - PAIR, cols), F32)], axis=0).astype(BF)


def cot_rows(at, cotangent, pairs, cols):
    width = PAIR * cols
    source = owner_first_sent(pairs // 2)
    return call(
        partial(cot_body, cols),
        (pairs,),
        [spec((1, width), lambda i, at: (0, source(i, at)))],
        spec((ROWS, cols), lambda i, at: (i, 0)),
        struct((pairs * ROWS, cols), BF),
        [pltpu.VMEM((width // 128, 128), F32)],
        prefetch=1,
        us=200,
        nbytes=pairs * width * 4,
    )(at, cotangent)


def own_block(at_ref, keep_ref, got_ref):
    own = pl.num_programs(0) // 2
    mine = pl.program_id(0) // own == at_ref[1]
    return jnp.where(mine, keep_ref[...].astype(F32), got_ref[...].astype(F32))


def put_body(cols, at_ref, keep_ref, got_ref, index_ref, out_ref):
    lanes = cols // 128
    hit = index_ref[0] == lax.broadcasted_iota(jnp.int32, (ROWS, 2 * PATCHES), 1)
    hit = hit.astype(BF)
    rest = own_block(at_ref, keep_ref, got_ref)
    total = None
    for _ in range(3):
        part = rest.astype(BF)
        rest = rest - part.astype(F32)
        term = dot(hit, part, 0, 0)
        total = term if total is None else total + term
    for k in range(lanes):
        out_ref[pl.ds(k, 2 * PATCHES, stride=lanes), :] = total[:, k * 128 : (k + 1) * 128]


def put_rows(at, keep, got, index, cols):
    pairs = index.shape[0]
    own = pairs // 2
    tall = 2 * PATCHES * cols // 128
    rows = spec((ROWS, cols), lambda i, at: (i % own, 0))
    return call(
        partial(put_body, cols),
        (pairs,),
        [rows, rows, spec((1, ROWS, 1), lambda i, at: (i, 0, 0))],
        spec((tall, 128), lambda i, at: (i, 0)),
        struct((pairs * tall, 128), F32),
        prefetch=1,
        us=200,
        nbytes=pairs * (tall * 512 + ROWS * cols * 4),
    )(at, keep, got, index)


def flat_body(cols, at_ref, keep_ref, got_ref, out_ref, scr):
    lanes = cols // 128
    rows = own_block(at_ref, keep_ref, got_ref)
    for k in range(lanes):
        scr[pl.ds(k, PAIR, stride=lanes), :] = rows[:PAIR, k * 128 : (k + 1) * 128]
    out_ref[...] = scr[...].reshape(out_ref.shape).astype(BF)


def flat_rows(at, keep, got, cols):
    own = keep.shape[0] // ROWS
    pairs = 2 * own
    width = PAIR * cols
    rows = spec((ROWS, cols), lambda i, at: (i % own, 0))
    return call(
        partial(flat_body, cols),
        (pairs,),
        [rows, rows],
        spec((1, width), lambda i, at: (0, i)),
        struct((1, pairs * width), BF),
        [pltpu.VMEM((width // 128, 128), F32)],
        prefetch=1,
        us=200,
        nbytes=pairs * width * 6,
    )(at, keep, got)


def stats(rows):
    mean = jnp.mean(rows, 1, keepdims=True)
    off = rows - mean
    inv = lax.rsqrt(jnp.mean(off * off, 1, keepdims=True) + EPS)
    return off * inv, inv


GAIN_ONE, SHIFT_ONE, GAIN_TWO, SHIFT_TWO, BIAS_OUT, BIAS_DOWN = range(6)


def vec_row(vec_ref, i):
    return vec_ref[i : i + 1, :]


def norm_body(rows_ref, vec_ref, out_ref):
    normed, _ = stats(rows_ref[...].astype(F32))
    out_ref[...] = (normed * vec_row(vec_ref, GAIN_ONE) + vec_row(vec_ref, SHIFT_ONE)).astype(BF)


def norm(rows, vec):
    r = rows.shape[0]
    return call(
        norm_body,
        (r // ROWS,),
        [spec((ROWS, D), lambda i: (i, 0)), spec((8, D), lambda i: (0, 0))],
        spec((ROWS, D), lambda i: (i, 0)),
        struct((r, D), BF),
        us=200,
        nbytes=r * D * 4,
    )(rows, vec)


def qkv_body(hidden_ref, w_ref, bias_ref, out_ref):
    out_ref[...] = (dot(hidden_ref[...], w_ref[...], 1, 1) + bias_ref[...]).astype(BF)


def qkv(hidden, w, bias):
    r = hidden.shape[0]
    return call(
        qkv_body,
        (3 * D // TILE,),
        [
            spec((r, D), lambda j: (0, 0)),
            spec((TILE, D), lambda j: (j, 0)),
            spec((1, TILE), lambda j: (0, j)),
        ],
        spec((r, TILE), lambda j: (0, j)),
        struct((r, 3 * D), BF),
        us=0.01,
        nbytes=r * D * 8 + 3 * D * D * 2,
    )(hidden, w, bias)


def same_image():
    at_row = lax.broadcasted_iota(jnp.int32, (ROWS, ROWS), 0)
    at_col = lax.broadcasted_iota(jnp.int32, (ROWS, ROWS), 1)

    def image(at):
        return (at >= VISIBLE).astype(jnp.int32) + (at >= PAIR).astype(jnp.int32)

    return image(at_row) == image(at_col)


def attend_body(triple_ref, mixed_ref, prob_ref):
    keep = same_image()
    left = lax.broadcasted_iota(jnp.int32, (ROWS, 128), 1) < HEAD_DIM
    for pair in range(HEADS // 2):
        q = triple_ref[:, pair * 128 : (pair + 1) * 128]
        k = triple_ref[:, D + pair * 128 : D + (pair + 1) * 128]
        v = triple_ref[:, 2 * D + pair * 128 : 2 * D + (pair + 1) * 128]
        halves = []
        for side in range(2):
            mine = left if side == 0 else jnp.logical_not(left)
            scores = dot(jnp.where(mine, q, jnp.zeros_like(q)), k, 1, 1) * HEAD_DIM**-0.5
            scores = jnp.where(keep, scores, -1e30)
            expo = jnp.exp(scores - jnp.max(scores, 1, keepdims=True))
            prob = expo / jnp.sum(expo, 1, keepdims=True)
            prob_ref[0, 2 * pair + side] = prob
            halves.append(dot(prob.astype(BF), v, 1, 0))
        mixed_ref[:, pair * 128 : (pair + 1) * 128] = jnp.where(left, halves[0], halves[1]).astype(
            BF
        )


def attend(triple):
    groups = triple.shape[0] // ROWS
    return call(
        attend_body,
        (groups,),
        [spec((ROWS, 3 * D), lambda g: (g, 0))],
        [spec((ROWS, D), lambda g: (g, 0)), spec((1, HEADS, ROWS, ROWS), lambda g: (g, 0, 0, 0))],
        [struct((groups * ROWS, D), BF), struct((groups, HEADS, ROWS, ROWS), F32)],
        us=0.01,
        nbytes=groups * ROWS * (8 * D + HEADS * 512),
    )(triple)


def mix_body(mixed_ref, w_ref, rows_ref, vec_ref, middle_ref, hidden_ref):
    branch = dot(mixed_ref[...], w_ref[...], 1, 0) + vec_row(vec_ref, BIAS_OUT)
    middle = rows_ref[...].astype(F32) + branch
    middle_ref[...] = middle
    normed, _ = stats(middle)
    hidden_ref[...] = (
        normed * vec_row(vec_ref, GAIN_TWO) + vec_row(vec_ref, SHIFT_TWO)
    ).astype(BF)


def row_tile(r):
    return r // 2


def mix(mixed, w, rows, vec):
    r = rows.shape[0]
    m = row_tile(r)
    row = spec((m, D), lambda i: (i, 0))
    return call(
        mix_body,
        (r // m,),
        [row, spec((D, D), lambda i: (0, 0)), row, spec((8, D), lambda i: (0, 0))],
        [row, row],
        [struct((r, D), F32), struct((r, D), BF)],
        us=200,
        nbytes=r * D * 10 + D * D * 2,
    )(mixed, w, rows, vec)


def up_body(hidden_ref, w_ref, bias_ref, active_ref, slope_ref):
    inner = dot(hidden_ref[...], w_ref[...], 1, 0) + bias_ref[...]
    phi = 0.5 * (1.0 + lax.erf(inner * (0.5**0.5)))
    active_ref[...] = (inner * phi).astype(BF)
    slope_ref[...] = phi + inner * (jnp.exp(-0.5 * inner * inner) * 0.3989422804014327)


def up(hidden, w, bias):
    r = hidden.shape[0]
    units = w.shape[1]
    tile = spec((r, TILE), lambda j: (0, j))
    return call(
        up_body,
        (units // TILE,),
        [
            spec((r, D), lambda j: (0, 0)),
            spec((D, TILE), lambda j: (0, j)),
            spec((1, TILE), lambda j: (0, j)),
        ],
        [tile, tile],
        [struct((r, units), BF), struct((r, units), F32)],
        us=200,
        nbytes=r * D * 2 + D * units * 2 + r * units * 6,
    )(hidden, w, bias)


def down_body(active_ref, w_ref, vec_ref, middle_ref, out_ref):
    branch = dot(active_ref[...], w_ref[...], 1, 1) + vec_row(vec_ref, BIAS_DOWN)
    out_ref[...] = (middle_ref[...] + branch).astype(BF)


def down(active, w, vec, middle):
    r, units = active.shape
    m = row_tile(r)
    return call(
        down_body,
        (r // m,),
        [
            spec((m, units), lambda i: (i, 0)),
            spec((D, units), lambda i: (0, 0)),
            spec((8, D), lambda i: (0, 0)),
            spec((m, D), lambda i: (i, 0)),
        ],
        spec((m, D), lambda i: (i, 0)),
        struct((r, D), BF),
        us=200,
        nbytes=r * units * 2 + D * units * 2 + r * D * 6,
    )(active, w, vec, middle)


def outer_body(left_ref, right_ref, out_ref, sum_ref, turned):
    @pl.when(pl.program_id(0) == 0)
    def _():
        turned[...] = left_ref[...].T

    right = right_ref[...]
    out_ref[...] = dot(turned[...], right, 1, 0).astype(BF)
    sum_ref[...] = jnp.sum(right.astype(F32), 0, keepdims=True)


def outer(left, right):
    r, width = right.shape
    rows = left.shape[1]
    return call(
        outer_body,
        (width // TILE,),
        [spec((r, rows), lambda j: (0, 0)), spec((r, TILE), lambda j: (0, j))],
        [spec((rows, TILE), lambda j: (0, j)), spec((1, TILE), lambda j: (0, j))],
        [struct((rows, width), BF), struct((1, width), F32)],
        [pltpu.VMEM((rows, r), BF)],
        us=0.01,
        nbytes=r * rows * 2 + r * width * 2 + rows * width * 2,
    )(left, right)


def inner_back_body(cot_ref, w_ref, slope_ref, hidden_ref, grad_ref, gw_ref, gb_ref, turned):
    @pl.when(pl.program_id(0) == 0)
    def _():
        turned[...] = hidden_ref[...].T

    grad = (dot(cot_ref[...], w_ref[...], 1, 0) * slope_ref[...]).astype(BF)
    grad_ref[...] = grad
    gw_ref[...] = dot(turned[...], grad, 1, 0).astype(BF)
    gb_ref[...] = jnp.sum(grad.astype(F32), 0, keepdims=True)


def inner_back(cot, w, slope, hidden):
    r, units = slope.shape
    full = spec((r, D), lambda j: (0, 0))
    col = spec((D, TILE), lambda j: (0, j))
    tile = spec((r, TILE), lambda j: (0, j))
    return call(
        inner_back_body,
        (units // TILE,),
        [full, col, tile, full],
        [tile, col, spec((1, TILE), lambda j: (0, j))],
        [struct((r, units), BF), struct((D, units), BF), struct((1, units), F32)],
        [pltpu.VMEM((D, r), BF)],
        us=200,
        nbytes=r * D * 4 + D * units * 4 + r * units * 6,
    )(cot, w, slope, hidden)


def norm_pull(grad, normed, inv, gain):
    scaled = grad * gain
    return inv * (
        scaled
        - jnp.mean(scaled, 1, keepdims=True)
        - normed * jnp.mean(scaled * normed, 1, keepdims=True)
    )


def middle_back_body(
    grad_ref, w_ref, middle_ref, cot_ref, vec_ref, out_ref, branch_ref, gain_sum, shift_sum, out_sum
):
    grad = dot(grad_ref[...], w_ref[...], 1, 1)
    normed, inv = stats(middle_ref[...])
    total = cot_ref[...].astype(F32) + norm_pull(
        grad, normed, inv, vec_row(vec_ref, GAIN_TWO)
    )
    out_ref[...] = total
    branch = total.astype(BF)
    branch_ref[...] = branch
    sums = (
        (gain_sum, jnp.sum(grad * normed, 0, keepdims=True)),
        (shift_sum, jnp.sum(grad, 0, keepdims=True)),
        (out_sum, jnp.sum(branch.astype(F32), 0, keepdims=True)),
    )
    for ref, value in sums:
        add_up(ref, value)


def add_up(ref, value):
    @pl.when(pl.program_id(0) == 0)
    def _():
        ref[...] = value

    @pl.when(pl.program_id(0) != 0)
    def _():
        ref[...] += value


def middle_back(grad, w, middle, cot, vecs):
    r, units = grad.shape
    m = row_tile(r)
    vec = spec((1, D), lambda i: (0, 0))
    row = spec((m, D), lambda i: (i, 0))
    vec_out = struct((1, D), F32)
    return call(
        middle_back_body,
        (r // m,),
        [
            spec((m, units), lambda i: (i, 0)),
            spec((D, units), lambda i: (0, 0)),
            row,
            row,
            spec((8, D), lambda i: (0, 0)),
        ],
        [row, row, vec, vec, vec],
        [struct((r, D), F32), struct((r, D), BF), vec_out, vec_out, vec_out],
        us=0.01,
        nbytes=r * units * 2 + D * units * 2 + r * D * 12,
    )(grad, w, middle, cot, vecs)


def mixed_back_body(branch_ref, tile_ref, w_ref, mixed_ref, grad_ref, gw_ref, turned):
    @pl.when(pl.program_id(0) == 0)
    def _():
        turned[...] = mixed_ref[...].T

    grad_ref[...] = dot(branch_ref[...], w_ref[...], 1, 1).astype(BF)
    gw_ref[...] = dot(turned[...], tile_ref[...], 1, 0).astype(BF)


def mixed_back(branch, w, mixed):
    r = branch.shape[0]
    full = spec((r, D), lambda j: (0, 0))
    tile = spec((r, TILE), lambda j: (0, j))
    return call(
        mixed_back_body,
        (D // TILE,),
        [full, tile, spec((TILE, D), lambda j: (j, 0)), full],
        [tile, spec((D, TILE), lambda j: (0, j))],
        [struct((r, D), BF), struct((D, D), BF)],
        [pltpu.VMEM((D, r), BF)],
        us=0.01,
        nbytes=r * D * 8 + D * D * 4,
    )(branch, branch, w, mixed)


def attend_back_body(triple_ref, prob_ref, grad_ref, *rest):
    out_ref = rest[-1]
    left = lax.broadcasted_iota(jnp.int32, (ROWS, 128), 1) < HEAD_DIM
    scale = HEAD_DIM**-0.5
    for pair in range(HEADS // 2):
        q = triple_ref[:, pair * 128 : (pair + 1) * 128]
        k = triple_ref[:, D + pair * 128 : D + (pair + 1) * 128]
        v = triple_ref[:, 2 * D + pair * 128 : 2 * D + (pair + 1) * 128]
        grad = grad_ref[:, pair * 128 : (pair + 1) * 128]
        gq, gk, gv = [], [], []
        for side in range(2):
            mine = left if side == 0 else jnp.logical_not(left)
            prob = prob_ref[0, 2 * pair + side]
            gv.append(dot(prob.astype(BF), grad, 0, 0))
            grad_prob = dot(jnp.where(mine, grad, jnp.zeros_like(grad)), v, 1, 1)
            inside = jnp.sum(grad_prob * prob, 1, keepdims=True)
            grad_scores = (prob * (grad_prob - inside)).astype(BF)
            gq.append(dot(grad_scores, k, 1, 0))
            gk.append(dot(grad_scores, q, 0, 0))
        for at, pieces, factor in ((0, gq, scale), (1, gk, scale), (2, gv, None)):
            both = jnp.where(left, pieces[0], pieces[1])
            if factor is not None:
                both = both * factor
            out_ref[:, at * D + pair * 128 : at * D + (pair + 1) * 128] = both.astype(BF)


def attend_back(triple, prob, grad, start, stop, partial_out=None):
    wide = spec((ROWS, 3 * D), lambda g: (g + start, 0))
    count = stop - start
    given = [] if partial_out is None else [partial_out]
    return pl.pallas_call(
        attend_back_body,
        out_shape=struct(triple.shape, BF),
        grid_spec=pltpu.PrefetchScalarGridSpec(
            num_scalar_prefetch=0,
            grid=(count,),
            in_specs=[
                wide,
                spec((1, HEADS, ROWS, ROWS), lambda g: (g + start, 0, 0, 0)),
                spec((ROWS, D), lambda g: (g + start, 0)),
            ]
            + [ANY] * len(given),
            out_specs=wide,
        ),
        input_output_aliases={3: 0} if given else {},
        compiler_params=pltpu.CompilerParams(
            dimension_semantics=("arbitrary",), vmem_limit_bytes=24 * MB
        ),
        cost_estimate=pl.CostEstimate(
            flops=200 * FLOPS_PER_US, bytes_accessed=1024, transcendentals=0
        ),
    )(triple, prob, grad, *given)


def qkv_grad_body(grad_ref, hidden_ref, gw_ref, gb_ref):
    grad = grad_ref[...]
    gw_ref[...] = dot(grad.T, hidden_ref[...], 1, 0).astype(BF)
    gb_ref[...] = jnp.sum(grad.astype(F32), 0, keepdims=True)


def qkv_grad(grad, hidden):
    r, width = grad.shape
    return call(
        qkv_grad_body,
        (width // TILE,),
        [spec((r, TILE), lambda j: (0, j)), spec((r, D), lambda j: (0, 0))],
        [spec((TILE, D), lambda j: (j, 0)), spec((1, TILE), lambda j: (0, j))],
        [struct((width, D), BF), struct((1, width), F32)],
        us=200,
        nbytes=r * width * 2 + r * D * 2 + width * D * 2,
    )(grad, hidden)


def first_back_body(grad_ref, w_ref, rows_ref, middle_ref, vec_ref, out_ref, gain_sum, shift_sum):
    grad = dot(grad_ref[...], w_ref[...], 1, 0)
    normed, inv = stats(rows_ref[...].astype(F32))
    pulled = norm_pull(grad, normed, inv, vec_row(vec_ref, GAIN_ONE))
    out_ref[...] = middle_ref[...] + pulled
    add_up(gain_sum, jnp.sum(grad * normed, 0, keepdims=True))
    add_up(shift_sum, jnp.sum(grad, 0, keepdims=True))


def first_back(grad, w, rows, grad_middle, vecs):
    r, width = grad.shape
    m = row_tile(r)
    vec = spec((1, D), lambda i: (0, 0))
    row = spec((m, D), lambda i: (i, 0))
    vec_out = struct((1, D), F32)
    return call(
        first_back_body,
        (r // m,),
        [
            spec((m, width), lambda i: (i, 0)),
            spec((width, D), lambda i: (0, 0)),
            row,
            row,
            spec((8, D), lambda i: (0, 0)),
        ],
        [row, vec, vec],
        [struct((r, D), F32), vec_out, vec_out],
        us=200,
        nbytes=r * width * 2 + D * width * 2 + r * D * 10,
    )(grad, w, rows, grad_middle, vecs)


WIDE, NARROW, DP = "wide", "narrow", "dp"


def swap(value, axis, bit):
    size = lax.axis_size(axis)
    return lax.ppermute(value, axis, [(i, i ^ bit) for i in range(size)])


def hold(value, *deps):
    return lax.optimization_barrier((value, deps))[0]


class Pieces:
    def __init__(self, stack, tags):
        self.stack, self.tags = stack, tags

    def fetch(self, axis, bit, *deps):
        move = [bit if axis == name else 0 for name in (WIDE, NARROW, DP)]
        tags = [tuple(a ^ b for a, b in zip(tag, move)) for tag in self.tags]
        return Pieces(swap(hold(self.stack, *deps), axis, bit), tags)

    def after(self, *deps):
        return Pieces(hold(self.stack, *deps), self.tags)

    def rows(self, start, stop):
        return Pieces(self.stack[:, start:stop], self.tags)

    def join(self, *others):
        stack = jnp.concatenate([self.stack] + [o.stack for o in others])
        return Pieces(stack, sum([o.tags for o in others], self.tags))


def first_piece(piece):
    return Pieces(piece[None], [(0, 0, 0)])


def dp_sum(total):
    total = total.astype(F32)
    bit = 2
    while bit < lax.axis_size(DP):
        total = total + swap(total.astype(BF), DP, bit).astype(F32)
        bit *= 2
    return total


def qkv_plan(cols, heads_cols, parts, spots=None):
    rows = heads_cols // parts
    spots = spots or [(p * rows, 0) for p in range(3)]

    def plan(w, n, q):
        return [
            (spot, (rows, cols), (p * D + w * heads_cols + q * rows, n * cols))
            for p, spot in enumerate(spots)
        ]

    return plan


def out_plan(cols, heads_cols, parts, spot=(0, 0)):
    rows = heads_cols // parts
    return lambda w, n, q: [(spot, (rows, cols), (w * heads_cols + q * rows, n * cols))]


def flat_plan(cols, units, parts, spot=(0, 0)):
    rows = cols // parts
    return lambda w, n, q: [(spot, (rows, units), (n * cols + q * rows, w * units))]


def prep_body(cols, rows, at_ref, *refs):
    qkv_ref, out_ref, vectors = refs[0], refs[1], refs[2:10]
    piece_ref, held, sem = refs[10], refs[11:-1], refs[-1]
    start = pl.multiple_of(at_ref[2] * rows, 16)
    copies = [
        pltpu.make_async_copy(
            qkv_ref.at[p, pl.ds(start, rows)], piece_ref.at[pl.ds(p * rows, rows)], sem.at[p]
        )
        for p in range(3)
    ]
    copies.append(
        pltpu.make_async_copy(
            out_ref.at[pl.ds(start, rows)], piece_ref.at[pl.ds(3 * rows + 16, rows)], sem.at[3]
        )
    )
    copies += [
        pltpu.make_async_copy(vector, scratch, sem.at[4 + k])
        for k, (vector, scratch) in enumerate(zip(vectors, held))
    ]
    for copy in copies:
        copy.start()
    for copy in copies:
        copy.wait()
    lines = [ref[...].astype(F32).reshape(1, -1) for ref in held[:6]]
    both = held[6][...].astype(F32)
    lines.append(jnp.concatenate([both[:1], both[1:]], axis=1))
    wide_line = held[7][...].astype(F32).reshape(1, -1)
    lines += [wide_line[:, k : k + cols] for k in range(0, wide_line.shape[1], cols)]
    lines.append(jnp.zeros((16 - len(lines), cols), F32))
    piece_ref[3 * rows : 3 * rows + 16, :] = jnp.concatenate(lines, axis=0).astype(BF)


def prep(at, qkv_t, w_out, *vectors):
    cols = qkv_t.shape[2]
    rows = qkv_t.shape[1] // 2
    return pl.pallas_call(
        partial(prep_body, cols, rows),
        out_shape=struct((4 * rows + 16, cols), BF),
        grid_spec=pltpu.PrefetchScalarGridSpec(
            num_scalar_prefetch=1,
            grid=(1,),
            in_specs=[IN_HBM] * (2 + len(vectors)),
            out_specs=pl.BlockSpec(memory_space=pltpu.VMEM),
            scratch_shapes=[pltpu.VMEM(v.shape, BF) for v in vectors]
            + [pltpu.SemaphoreType.DMA((4 + len(vectors),))],
        ),
        compiler_params=pltpu.CompilerParams(vmem_limit_bytes=8 * MB),
        cost_estimate=pl.CostEstimate(
            flops=FLOPS_PER_US // 100, bytes_accessed=1024, transcendentals=0
        ),
    )(at, *[in_hbm(v) for v in (qkv_t, w_out, *vectors)])


def vec_body(wide, narrow, cols, first, tag_lists, at_ref, *refs):
    arrays, (vec_ref, qkv_bias_ref, up_bias_ref, held, sem) = refs[:-5], refs[-5:]
    copies = []
    for array, tags in zip(arrays, tag_lists):
        for k, (dw, dn, _) in enumerate(tags):
            slot = (at_ref[0] ^ dw) * narrow + (at_ref[1] ^ dn)
            source = array.at[k, pl.ds(first, 16)]
            copies.append(pltpu.make_async_copy(source, held.at[slot], sem.at[len(copies)]))
    for copy in copies:
        copy.start()
    for copy in copies:
        copy.wait()
    lines = [held[k].astype(F32) for k in range(wide * narrow)]
    for n in range(narrow):
        vec_ref[:, n * cols : (n + 1) * cols] = lines[n][:8]
    by_wide = [lines[w * narrow] for w in range(wide)]
    half = cols // 2
    q = jnp.concatenate([line[6:7, :half] for line in by_wide], axis=1)
    v = jnp.concatenate([line[6:7, half:] for line in by_wide], axis=1)
    qkv_bias_ref[...] = jnp.concatenate([q, jnp.zeros_like(q), v], axis=1)
    up_bias_ref[...] = jnp.concatenate(
        [line[i : i + 1] for line in by_wide for i in (7, 8)], axis=1
    )


def vectors_of(at, pieces, first, wide, narrow, cols, units):
    vmem = pl.BlockSpec(memory_space=pltpu.VMEM)
    return pl.pallas_call(
        partial(vec_body, wide, narrow, cols, first, [p.tags for p in pieces]),
        out_shape=[struct((8, D), F32), struct((1, 3 * D), F32), struct((1, wide * units), F32)],
        grid_spec=pltpu.PrefetchScalarGridSpec(
            num_scalar_prefetch=1,
            grid=(1,),
            in_specs=[ANY] * len(pieces),
            out_specs=[vmem] * 3,
            scratch_shapes=[
                pltpu.VMEM((wide * narrow, 16, cols), BF),
                pltpu.SemaphoreType.DMA((wide * narrow,)),
            ],
        ),
        compiler_params=pltpu.CompilerParams(vmem_limit_bytes=8 * MB),
        cost_estimate=pl.CostEstimate(flops=FLOPS_PER_US // 100, bytes_accessed=1024, transcendentals=0),
    )(at, *[p.stack for p in pieces])


def pack_body(*refs):
    out = refs[-1]
    at = 0
    for ref in refs[:-1]:
        for k in range(0, ref.shape[1], D):
            out[at : at + 1, :] = ref[:, k : k + D]
            at += 1
    if at < out.shape[0]:
        out[at:, :] = jnp.zeros((out.shape[0] - at, D), F32)


def pack(*rows):
    count = -(-sum(r.shape[1] for r in rows) // (8 * D)) * 8
    vmem = pl.BlockSpec(memory_space=pltpu.VMEM)
    return pl.pallas_call(
        pack_body,
        out_shape=struct((count, D), F32),
        in_specs=[vmem] * len(rows),
        out_specs=vmem,
        compiler_params=pltpu.CompilerParams(vmem_limit_bytes=8 * MB),
        cost_estimate=pl.CostEstimate(flops=FLOPS_PER_US // 100, bytes_accessed=1024, transcendentals=0),
    )(*rows)


ANY = pl.BlockSpec(memory_space=pl.ANY)
IN_HBM = pl.BlockSpec(memory_space=pltpu.HBM)


CORE, DP_INDEX = 2, 3


def build_body(plan, tag_lists, inverse, part_at, at_ref, *refs):
    sem = refs[-1]
    if inverse:
        whole_ref, arrays = refs[0], refs[1:-1]
    else:
        arrays, whole_ref = refs[:-2], refs[-2]
    copies = []
    for array, tags in zip(arrays, tag_lists):
        for k, (dw, dn, dq) in enumerate(tags):
            w, n, q = at_ref[0] ^ dw, at_ref[1] ^ dn, at_ref[part_at] ^ dq
            for (at_row, at_lane), (rows, lanes), (row, lane) in plan(w, n, q):
                piece = array.at[k, pl.ds(at_row, rows), pl.ds(at_lane, lanes)]
                whole = whole_ref.at[
                    pl.ds(pl.multiple_of(row, 16), rows), pl.ds(pl.multiple_of(lane, 128), lanes)
                ]
                ends = (whole, piece) if inverse else (piece, whole)
                copies.append(pltpu.make_async_copy(*ends, sem.at[len(copies)]))
    for copy in copies:
        copy.start()
    for copy in copies:
        copy.wait()


def move_pieces(at, arrays, plan, tag_lists, inverse, part_at, shapes):
    moves = sum(len(tags) for tags in tag_lists) * len(plan(0, 0, 0))
    return pl.pallas_call(
        partial(build_body, plan, tag_lists, inverse, part_at),
        out_shape=[struct(shape, BF) for shape in shapes],
        grid_spec=pltpu.PrefetchScalarGridSpec(
            num_scalar_prefetch=1,
            grid=(1,),
            in_specs=[ANY] * len(arrays),
            out_specs=[ANY] * len(shapes),
            scratch_shapes=[pltpu.SemaphoreType.DMA((moves,))],
        ),
        compiler_params=pltpu.CompilerParams(vmem_limit_bytes=4 * MB),
        cost_estimate=pl.CostEstimate(
            flops=FLOPS_PER_US // 100, bytes_accessed=1024, transcendentals=0
        ),
    )(at, *arrays)


def build_weights(at, pieces, plan, shape, part_at=CORE):
    arrays, tags = [p.stack for p in pieces], [p.tags for p in pieces]
    arrays = [in_hbm(a) for a in arrays]
    return move_pieces(at, arrays, plan, tags, False, part_at, [shape])[0]


def cut_grads(at, grad, plan, tags, shape, part_at=CORE):
    tag_lists = [[(w, n, q ^ dc) for w, n, q in tags] for dc in range(2)]
    return move_pieces(at, [grad], plan, tag_lists, True, part_at, [(len(tags),) + shape] * 2)


class Chain:
    def __init__(self, at, grad, plan, tags, shape, part_at=CORE):
        self.keep, self.send = cut_grads(at, grad, plan, tags, shape, part_at)

    def go(self, axis, bit):
        self.got = swap(self.send, axis, bit)

    def fold(self, *deps):
        self.keep, self.send = halves_summed(self.keep, hold(self.got, *deps))

    def total(self, *deps):
        return self.keep[0].astype(F32) + hold(self.got, *deps)[0].astype(F32)


def doubled(value, bit, index):
    other = swap(value, DP, bit)
    return jnp.where(index == 0, jnp.stack([value, other]), jnp.stack([other, value]))


def halves_summed(kept, got):
    half = kept.shape[0] // 2
    keep = kept[:half].astype(F32) + got[:half].astype(F32)
    send = (kept[half:].astype(F32) + got[half:].astype(F32)).astype(BF)
    return keep, send


def core_half(at, shard):
    rows = shard.shape[0] // 2
    return lax.dynamic_slice_in_dim(shard, at[2] * rows, rows, axis=0)


def quarter(at, shard):
    rows = shard.shape[0] // 4
    return lax.dynamic_slice_in_dim(shard, at[3] * rows, rows, axis=0)


def total_over_all(value, axes):
    for axis in axes:
        bit = 1
        while bit < lax.axis_size(axis):
            value = value + swap(value, axis, bit)
            bit *= 2
    return value


def to_rows(blocks, narrow):
    got = lax.all_to_all(blocks, "narrow", 0, 0, tiled=True)
    return jnp.concatenate([got[n] for n in range(narrow)], axis=1)


def from_rows(rows, narrow):
    cols = rows.shape[1] // narrow
    blocks = jnp.stack([rows[:, n * cols : (n + 1) * cols] for n in range(narrow)])
    got = lax.all_to_all(blocks, "narrow", 0, 0, tiled=True)
    return got.reshape(-1, cols)


def gather_weight(shard, wide, narrow):
    got = lax.all_gather(shard.reshape(-1, 128), ("wide", "narrow"), axis=0, tiled=True)
    return got.reshape((wide, narrow) + shard.shape)


def scatter_grad(blocks):
    shape = blocks.shape[2:]
    got = lax.psum_scatter(
        blocks.reshape(-1, 128), ("wide", "narrow"), scatter_dimension=0, tiled=True
    )
    return lax.psum(got.astype(F32), "dp").reshape(shape)


def on_device(
    wide,
    narrow,
    patches,
    visible,
    w_qkv,
    b_qv,
    w_out,
    b_out,
    w_up,
    b_up,
    w_down,
    b_down,
    gain_one,
    shift_one,
    gain_two,
    shift_two,
    cotangent,
):
    images = visible.shape[0]
    pairs = images // 2
    cols = w_qkv.shape[0]
    heads_cols = w_qkv.shape[2]
    units = w_up.shape[1]
    swaps = cols % 128 == 0 and narrow == 2 and wide == 4 and lax.axis_size(DP) == 4
    swaps = swaps and pairs % 2 == 0

    at = jnp.stack(
        [
            lax.axis_index("wide"),
            lax.axis_index("narrow"),
            lax.axis_index("dp") % 2,
            lax.axis_index("dp"),
        ]
    ).astype(jnp.int32)

    index = (visible.reshape(pairs, 2, VISIBLE) + jnp.array([0, PATCHES])[None, :, None]).reshape(
        pairs, PAIR
    )
    index = jnp.pad(index, ((0, 0), (0, ROWS - PAIR)), constant_values=-1)[:, :, None]

    w_qkv_t = w_qkv.transpose(1, 2, 0)
    if swaps:
        first = first_piece(
            prep(
                at,
                w_qkv_t,
                w_out,
                gain_one,
                shift_one,
                gain_two,
                shift_two,
                b_out,
                b_down,
                b_qv,
                b_up,
            )
        )

        def part_of(whole, side):
            return lax.dynamic_slice_in_dim(whole, side * cols, cols, axis=1)

        def join_cols(keep, got):
            return jnp.where(
                at[1] == 0,
                jnp.concatenate([keep, got], axis=1),
                jnp.concatenate([got, keep], axis=1),
            )

        mine, theirs = at[1], 1 - at[1]
        whole = (D, wide * units)

        first_z = [first.fetch(WIDE, bit) for bit in (1, 2, 3)]
        rows_out = pick_rows(hold(at, first.stack), patches, index, cols)
        own = rows_out.shape[0] // 2
        rows_send = rows_out[:own]
        rows_got = swap(rows_send, NARROW, 1)
        cot_out = cot_rows(hold(at, rows_send), cotangent, pairs, cols)

        first = first.join(*[p.after(cot_out) for p in first_z])
        up_p = first_piece(hold(core_half(at, w_up), first.stack))
        up_z = [up_p.fetch(WIDE, bit) for bit in (1, 2, 3)]
        rows = join_cols(rows_out[own:], hold(rows_got, up_p.stack))
        first_x = first.fetch(NARROW, 1, rows)
        up_p = up_p.join(*[p.after(rows) for p in up_z])

        first = first.join(first_x.after(up_p.stack))
        first_c = first.fetch(DP, 1)
        up_x = up_p.fetch(NARROW, 1)
        down_p = first_piece(hold(quarter(at, w_down), first.stack))
        down_z = [down_p.fetch(WIDE, bit) for bit in (1, 2, 3)]
        vec_at = 3 * heads_cols // 2
        out_at = (vec_at + 16, 0)
        vecs, bias_qkv, bias_up = vectors_of(at, [first], vec_at, wide, narrow, cols, units)
        hidden_one = norm(rows, vecs)
        all_first = [first, first_c.after(hidden_one)]
        qkv_t = build_weights(at, all_first, qkv_plan(cols, heads_cols, 2), (3 * D, D))
        out_w = build_weights(at, all_first, out_plan(cols, heads_cols, 2, out_at), (D, D))
        down_p = down_p.join(*[p.after(qkv_t) for p in down_z])
        down_x = down_p.fetch(NARROW, 1)
        triple = qkv(hold(hidden_one, down_p.stack), qkv_t, bias_qkv)
        mixed, prob = attend(triple)
        half_flat, part_flat = flat_plan(cols, units, 2), flat_plan(cols, units, 4)
        up_x = up_x.after(mixed)
        up_c = up_p.fetch(DP, 1, up_x.stack)
        up_xc = up_x.fetch(DP, 1)
        down_p = down_p.join(down_x.after(mixed))
        down_y = down_p.fetch(DP, 2)
        cot_send = hold(cot_out[:own], down_p.stack)
        cot_got = swap(cot_send, NARROW, 1)
        middle, hidden_two = mix(
            hold(mixed, up_x.stack, down_p.stack, cot_send), out_w, rows, vecs
        )
        up_c, up_xc = up_c.after(hidden_two), up_xc.after(hidden_two)
        up_w = build_weights(at, [up_p, up_x, up_c, up_xc], half_flat, whole)
        active, slope = up(hidden_two, up_w, bias_up)
        cot = join_cols(cot_out[own:], hold(cot_got, active))
        gw_down, _ = outer(cot, active)
        gb_down = jnp.sum(cot, 0, dtype=F32)[None]
        x_first = [(w, n, 0) for n in range(2) for w in (0, 2, 1, 3)]
        y_first = [(w, n, dy) for dy in (0, 2) for n in range(2) for w in (0, 2, 1, 3)]
        g_d = Chain(at, gw_down, half_flat, x_first, (cols // 2, units))
        g_d.go(DP, 1)
        down_y = down_y.after(g_d.send)
        down_c = [p.fetch(DP, 1, down_y.stack) for p in (down_p, down_y)]
        down_w = build_weights(at, [down_p, down_y] + down_c, part_flat, whole, DP_INDEX)
        g_d.fold(down_w)
        g_d.go(NARROW, 1)
        grad_inner, gw_up, gb_up = inner_back(
            cot, hold(down_w, g_d.send), in_hbm(slope), hidden_two
        )

        g_u = Chain(at, gw_up, part_flat, y_first, (cols // 4, units), DP_INDEX)
        g_u.go(DP, 1)
        g_d.fold(g_u.send)
        g_d.go(WIDE, 1)
        result = down(hold(active, g_d.send), down_w, vecs, middle)
        grad_middle, branch, gg_two, gs_two, gb_out = middle_back(
            hold(grad_inner, result), up_w, middle, cot, vecs
        )
        grad_mixed, gw_out = mixed_back(branch, out_w, mixed)

        g_o = Chain(at, gw_out, out_plan(cols, heads_cols, 2), x_first, (heads_cols // 2, cols))
        g_o.go(DP, 1)
        g_u.fold(g_o.send)
        g_u.go(DP, 2)
        g_d.fold(g_o.send)
        g_d.go(WIDE, 2)
        result_got = swap(hold(part_of(result, theirs), g_o.send), NARROW, 1)
        groups = rows.shape[0] // ROWS
        grad_triple = attend_back(
            triple, in_hbm(prob), hold(grad_mixed, g_u.send, g_d.send), 0, groups
        )

        d_sum = g_d.total(grad_triple)
        d_got = swap(d_sum.astype(BF), DP, 2)
        g_u.fold(grad_triple)
        g_u.go(NARROW, 1)
        g_o.fold(grad_triple)
        g_o.go(NARROW, 1)
        result_got = hold(result_got, grad_triple)
        gw_qkv, gb_qkv = qkv_grad(hold(grad_triple, d_sum, g_u.send, g_o.send), hidden_one)

        g_q = Chain(
            at,
            gw_qkv,
            qkv_plan(cols, heads_cols, 4),
            y_first,
            (3 * heads_cols // 4, cols),
            DP_INDEX,
        )
        g_q.go(DP, 1)
        d_sum = d_sum + hold(d_got, g_q.send).astype(F32)
        d_got = swap(d_sum, DP, 1)
        g_u.fold(g_q.send)
        g_u.go(WIDE, 1)
        g_o.fold(g_q.send)
        g_o.go(WIDE, 1)
        grad_rows, gg_one, gs_one = first_back(
            grad_triple, hold(qkv_t, d_sum, g_u.send, g_o.send), rows, grad_middle, vecs
        )

        g_q.fold(grad_rows)
        g_q.go(DP, 2)
        rows_send = part_of(grad_rows, theirs).astype(BF)
        rows_back = swap(rows_send, NARROW, 1)
        g_u.fold(grad_rows)
        g_u.go(WIDE, 2)
        g_o.fold(grad_rows)
        g_o.go(WIDE, 2)
        sums = pack(gg_one, gs_one, gg_two, gs_two, gb_out, gb_down, gb_qkv, gb_up)
        sums_got = swap(sums, DP, 1)
        keep = part_of(result, mine)
        block_output = flat_rows(
            at, hold(keep, g_q.send, rows_send, g_u.send, g_o.send, sums), result_got, cols
        )

        g_q.fold(block_output)
        g_q.go(NARROW, 1)
        u_sum = g_u.total(block_output)
        u_got = swap(u_sum, DP, 2)
        o_sum = g_o.total(block_output)
        o_got = swap(o_sum.astype(BF), DP, 2)
        sums = sums + hold(sums_got, block_output)
        sums_got = swap(sums, DP, 2)
        rows_back = hold(rows_back, block_output, g_q.send, u_sum, o_sum, sums)
        grad_patches = put_rows(at, part_of(grad_rows, mine), rows_back, index, cols)

        def in_order(value, other, index):
            return jnp.where(index == 0, jnp.stack([value, other]), jnp.stack([other, value]))

        g_q.fold(grad_patches)
        g_q.go(WIDE, 1)
        u_sum = in_order(u_sum, hold(u_got, grad_patches), at[3] // 2)
        u_got = swap(u_sum, DP, 1)
        o_sum = o_sum + hold(o_got, grad_patches).astype(F32)
        o_got = swap(o_sum, DP, 1)
        sums = sums + hold(sums_got, grad_patches)
        sums = total_over_all(sums, ("narrow", "wide"))
        g_down = in_order(d_sum, d_got, at[2]).reshape(cols, units)
        g_q.fold()
        g_q.go(WIDE, 2)
        g_up = in_order(u_sum, u_got, at[2]).transpose(1, 0, 2, 3).reshape(cols, units)
        g_out = in_order(o_sum, o_got, at[2]).reshape(heads_cols, cols)
        q_sum = doubled(doubled(g_q.total(), 2, at[3] // 2), 1, at[2])
        g_qkv = q_sum.reshape(2, 2, 3, heads_cols // 4, cols).transpose(4, 2, 1, 0, 3)
        g_qkv = g_qkv.reshape(cols, 3, heads_cols)
        grad_patches = grad_patches.reshape(1, -1)
    else:
        table = patches.reshape(images, PATCHES, cols)
        rows_mine = jnp.take_along_axis(table, visible[:, :, None], axis=1)
        rows_mine = jnp.pad(
            rows_mine.reshape(pairs, PAIR, cols), ((0, 0), (0, ROWS - PAIR), (0, 0))
        )
        cot_mine = jnp.pad(
            cotangent.reshape(pairs, PAIR, cols), ((0, 0), (0, ROWS - PAIR), (0, 0))
        )
        rows = to_rows(rows_mine.reshape(narrow, -1, cols), narrow)
        cot = to_rows(cot_mine.reshape(narrow, -1, cols), narrow)
        vec = jnp.concatenate(
            [gain_one, shift_one, gain_two, shift_two, b_out, b_down, b_qv.reshape(-1), b_up]
        )
        vec = lax.all_gather(vec, ("wide", "narrow"), axis=0, tiled=False).astype(F32)
        qkv_t = gather_weight(w_qkv_t, wide, narrow)
        qkv_t = qkv_t.transpose(2, 0, 3, 1, 4).reshape(3 * D, D)
        out_w = gather_weight(w_out, wide, narrow).transpose(0, 2, 1, 3).reshape(D, D)
        up_w = gather_weight(w_up, wide, narrow).transpose(1, 2, 0, 3).reshape(D, -1)
        down_w = gather_weight(w_down, wide, narrow).transpose(1, 2, 0, 3).reshape(D, -1)
        vec = vec.reshape(wide, narrow, -1)
        vecs = vec[0, :, : 6 * cols].reshape(narrow, 6, cols).transpose(1, 0, 2).reshape(6, D)
        vecs = jnp.pad(vecs, ((0, 2), (0, 0)))
        by_wide = vec[:, 0, 6 * cols :]
        bias_q = by_wide[:, :heads_cols].reshape(1, D)
        bias_v = by_wide[:, heads_cols : 2 * heads_cols].reshape(1, D)
        bias_qkv = jnp.concatenate([bias_q, jnp.zeros((1, D), F32), bias_v], axis=1)
        bias_up = by_wide[:, 2 * heads_cols :].reshape(1, -1)

        hidden_one = norm(rows, vecs)
        triple = qkv(hidden_one, qkv_t, bias_qkv)
        mixed, prob = attend(triple)
        middle, hidden_two = mix(mixed, out_w, rows, vecs)
        active, slope = up(hidden_two, up_w, bias_up)
        result = down(active, down_w, vecs, middle)
        gw_down, _ = outer(cot, active)
        gb_down = jnp.sum(cot, 0, dtype=F32)[None]
        grad_inner, gw_up, gb_up = inner_back(cot, down_w, slope, hidden_two)
        grad_middle, branch, gg_two, gs_two, gb_out = middle_back(
            grad_inner, up_w, middle, cot, vecs
        )
        grad_mixed, gw_out = mixed_back(branch, out_w, mixed)
        grad_triple = attend_back(triple, prob, grad_mixed, 0, rows.shape[0] // ROWS)
        gw_qkv, gb_qkv = qkv_grad(grad_triple, hidden_one)
        grad_rows, gg_one, gs_one = first_back(grad_triple, qkv_t, rows, grad_middle, vecs)
        sums = pack(gg_one, gs_one, gg_two, gs_two, gb_out, gb_down, gb_qkv, gb_up)

        result = from_rows(result, narrow)
        grad_rows = from_rows(grad_rows, narrow)
        block_output = result.reshape(pairs, ROWS, cols)[:, :PAIR].reshape(1, -1)
        grad_rows = grad_rows.reshape(pairs, ROWS, cols)[:, :PAIR].reshape(images, VISIBLE, cols)
        grad_patches = (
            jnp.zeros((images, PATCHES, cols), F32)
            .at[jnp.arange(images)[:, None], visible]
            .set(grad_rows)
            .reshape(1, -1)
        )
        g_down = scatter_grad(gw_down.reshape(narrow, cols, wide, units).transpose(2, 0, 1, 3))
        g_up = scatter_grad(gw_up.reshape(narrow, cols, wide, units).transpose(2, 0, 1, 3))
        g_out = scatter_grad(gw_out.reshape(wide, heads_cols, narrow, cols).transpose(0, 2, 1, 3))
        g_qkv = scatter_grad(
            gw_qkv.reshape(3, wide, heads_cols, narrow, cols).transpose(1, 3, 0, 2, 4)
        )
        g_qkv = g_qkv.transpose(2, 0, 1)
        sums = lax.psum(sums, ("dp", "wide", "narrow"))

    sums = sums.reshape(-1)
    at_narrow = at[1] * cols
    at_wide = at[0]

    def narrow_part(i):
        return lax.dynamic_slice_in_dim(sums, i * D + at_narrow, cols)

    g_bqv = jnp.stack(
        [
            lax.dynamic_slice_in_dim(sums, (6 + i) * D + at_wide * heads_cols, heads_cols)
            for i in (0, 2)
        ]
    )
    g_bup = lax.dynamic_slice_in_dim(sums, 9 * D + at_wide * units, units)
    return (
        block_output,
        grad_patches,
        g_qkv,
        g_bqv,
        g_out,
        narrow_part(4),
        g_up,
        g_bup,
        g_down,
        narrow_part(5),
        narrow_part(0),
        narrow_part(1),
        narrow_part(2),
        narrow_part(3),
    )


def solution(mesh):
    in_specs = (
        P("narrow", ("dp", "wide")),
        P(("dp", "wide"), None),
        P("narrow", None, "wide"),
        P(None, "wide"),
        P("wide", "narrow"),
        P("narrow"),
        P("narrow", "wide"),
        P("wide"),
        P("narrow", "wide"),
        P("narrow"),
        P("narrow"),
        P("narrow"),
        P("narrow"),
        P("narrow"),
        P("narrow", ("dp", "wide")),
    )
    out_specs = (
        P("narrow", ("dp", "wide")),
        P("narrow", ("dp", "wide")),
        P("narrow", None, "wide"),
        P(None, "wide"),
        P("wide", "narrow"),
        P("narrow"),
        P("narrow", "wide"),
        P("wide"),
        P("narrow", "wide"),
        P("narrow"),
        P("narrow"),
        P("narrow"),
        P("narrow"),
        P("narrow"),
    )
    body = partial(on_device, mesh.shape["wide"], mesh.shape["narrow"])
    return jax.shard_map(body, mesh=mesh, in_specs=in_specs, out_specs=out_specs, check_vma=False)
```

```python
from functools import partial

import jax
import jax.numpy as jnp
from jax import lax
from jax.experimental import pallas as pl
from jax.experimental.pallas import tpu as pltpu
from jax.sharding import PartitionSpec as P

D = 768
HEAD_DIM = 64
HEADS = 12
PATCHES = 196
VISIBLE = 49
PAIR = 2 * VISIBLE
ROWS = 112
TILE = 768
EPS = 1e-06
BF = jnp.bfloat16
F32 = jnp.float32
MB = 1024 * 1024


def dot(a, b, ca, cb):
    return lax.dot_general(a, b, (((ca,), (cb,)), ((), ())), preferred_element_type=F32)


FLOPS_PER_US = 540000000


def call(body, grid, ins, outs, shapes, scratch=(), prefetch=0, us=1.0, nbytes=0, vmem=32):
    return pl.pallas_call(
        body,
        out_shape=shapes,
        grid_spec=pltpu.PrefetchScalarGridSpec(
            num_scalar_prefetch=prefetch,
            grid=grid,
            in_specs=ins,
            out_specs=outs,
            scratch_shapes=scratch,
        ),
        compiler_params=pltpu.CompilerParams(
            dimension_semantics=("arbitrary",) * len(grid), vmem_limit_bytes=vmem * MB
        ),
        cost_estimate=pl.CostEstimate(
            flops=int(us * FLOPS_PER_US), bytes_accessed=1024, transcendentals=0
        ),
    )


def in_hbm(value):
    return pltpu.with_memory_space_constraint(value, pltpu.HBM)


def spec(shape, index):
    return pl.BlockSpec(shape, index)


def struct(shape, dtype):
    return jax.ShapeDtypeStruct(shape, dtype)


def pick_body(cols, at_ref, patch_ref, index_ref, rows_ref, wide_ref):
    lanes = cols // 128
    wide_ref[...] = patch_ref[...].astype(F32).reshape(wide_ref.shape)
    parts = [wide_ref[pl.ds(k, 2 * PATCHES, stride=lanes), :] for k in range(lanes)]
    both = jnp.concatenate(parts, axis=1).astype(BF)
    hit = index_ref[0] == lax.broadcasted_iota(jnp.int32, (ROWS, 2 * PATCHES), 1)
    rows_ref[...] = dot(hit.astype(BF), both, 1, 0).astype(BF)


def owner_first_sent(own):
    def source(i, at):
        return (i // own ^ 1 ^ at[1]) * own + i % own

    return source


def pick_rows(at, patches, index, cols):
    pairs = index.shape[0]
    width = 2 * PATCHES * cols
    source = owner_first_sent(pairs // 2)
    return call(
        partial(pick_body, cols),
        (pairs,),
        [
            spec((1, width), lambda i, at: (0, source(i, at))),
            spec((1, ROWS, 1), lambda i, at: (source(i, at), 0, 0)),
        ],
        spec((ROWS, cols), lambda i, at: (i, 0)),
        struct((pairs * ROWS, cols), BF),
        [pltpu.VMEM((width // 128, 128), F32)],
        prefetch=1,
        us=200,
        nbytes=pairs * width * 4,
    )(at, patches, index)


def cot_body(cols, at_ref, cot_ref, rows_ref, scr):
    lanes = cols // 128
    scr[...] = cot_ref[...].astype(F32).reshape(scr.shape)
    parts = [scr[pl.ds(k, PAIR, stride=lanes), :] for k in range(lanes)]
    cot = jnp.concatenate(parts, axis=1)
    rows_ref[...] = jnp.concatenate([cot, jnp.zeros((ROWS - PAIR, cols), F32)], axis=0).astype(BF)


def cot_rows(at, cotangent, pairs, cols):
    width = PAIR * cols
    source = owner_first_sent(pairs // 2)
    return call(
        partial(cot_body, cols),
        (pairs,),
        [spec((1, width), lambda i, at: (0, source(i, at)))],
        spec((ROWS, cols), lambda i, at: (i, 0)),
        struct((pairs * ROWS, cols), BF),
        [pltpu.VMEM((width // 128, 128), F32)],
        prefetch=1,
        us=200,
        nbytes=pairs * width * 4,
    )(at, cotangent)


def own_block(at_ref, keep_ref, got_ref):
    own = pl.num_programs(0) // 2
    mine = pl.program_id(0) // own == at_ref[1]
    return jnp.where(mine, keep_ref[...].astype(F32), got_ref[...].astype(F32))


def put_body(cols, at_ref, keep_ref, got_ref, index_ref, out_ref):
    lanes = cols // 128
    hit = index_ref[0] == lax.broadcasted_iota(jnp.int32, (ROWS, 2 * PATCHES), 1)
    hit = hit.astype(BF)
    rest = own_block(at_ref, keep_ref, got_ref)
    total = None
    for _ in range(3):
        part = rest.astype(BF)
        rest = rest - part.astype(F32)
        term = dot(hit, part, 0, 0)
        total = term if total is None else total + term
    for k in range(lanes):
        out_ref[pl.ds(k, 2 * PATCHES, stride=lanes), :] = total[:, k * 128 : (k + 1) * 128]


def put_rows(at, keep, got, index, cols):
    pairs = index.shape[0]
    own = pairs // 2
    tall = 2 * PATCHES * cols // 128
    rows = spec((ROWS, cols), lambda i, at: (i % own, 0))
    return call(
        partial(put_body, cols),
        (pairs,),
        [rows, rows, spec((1, ROWS, 1), lambda i, at: (i, 0, 0))],
        spec((tall, 128), lambda i, at: (i, 0)),
        struct((pairs * tall, 128), F32),
        prefetch=1,
        us=200,
        nbytes=pairs * (tall * 512 + ROWS * cols * 4),
    )(at, keep, got, index)


def flat_body(cols, at_ref, keep_ref, got_ref, out_ref, scr):
    lanes = cols // 128
    rows = own_block(at_ref, keep_ref, got_ref)
    for k in range(lanes):
        scr[pl.ds(k, PAIR, stride=lanes), :] = rows[:PAIR, k * 128 : (k + 1) * 128]
    out_ref[...] = scr[...].reshape(out_ref.shape).astype(BF)


def flat_rows(at, keep, got, cols):
    own = keep.shape[0] // ROWS
    pairs = 2 * own
    width = PAIR * cols
    rows = spec((ROWS, cols), lambda i, at: (i % own, 0))
    return call(
        partial(flat_body, cols),
        (pairs,),
        [rows, rows],
        spec((1, width), lambda i, at: (0, i)),
        struct((1, pairs * width), BF),
        [pltpu.VMEM((width // 128, 128), F32)],
        prefetch=1,
        us=200,
        nbytes=pairs * width * 6,
    )(at, keep, got)


def stats(rows):
    mean = jnp.mean(rows, 1, keepdims=True)
    off = rows - mean
    inv = lax.rsqrt(jnp.mean(off * off, 1, keepdims=True) + EPS)
    return off * inv, inv


GAIN_ONE, SHIFT_ONE, GAIN_TWO, SHIFT_TWO, BIAS_OUT, BIAS_DOWN = range(6)


def vec_row(vec_ref, i):
    return vec_ref[i : i + 1, :]


def norm_body(rows_ref, vec_ref, out_ref):
    normed, _ = stats(rows_ref[...].astype(F32))
    out_ref[...] = (normed * vec_row(vec_ref, GAIN_ONE) + vec_row(vec_ref, SHIFT_ONE)).astype(BF)


def norm(rows, vec):
    r = rows.shape[0]
    return call(
        norm_body,
        (r // ROWS,),
        [spec((ROWS, D), lambda i: (i, 0)), spec((8, D), lambda i: (0, 0))],
        spec((ROWS, D), lambda i: (i, 0)),
        struct((r, D), BF),
        us=200,
        nbytes=r * D * 4,
    )(rows, vec)


def qkv_body(hidden_ref, w_ref, bias_ref, out_ref):
    out_ref[...] = (dot(hidden_ref[...], w_ref[...], 1, 1) + bias_ref[...]).astype(BF)


def qkv(hidden, w, bias):
    r = hidden.shape[0]
    return call(
        qkv_body,
        (3 * D // TILE,),
        [
            spec((r, D), lambda j: (0, 0)),
            spec((TILE, D), lambda j: (j, 0)),
            spec((1, TILE), lambda j: (0, j)),
        ],
        spec((r, TILE), lambda j: (0, j)),
        struct((r, 3 * D), BF),
        us=0.01,
        nbytes=r * D * 8 + 3 * D * D * 2,
    )(hidden, w, bias)


def same_image():
    at_row = lax.broadcasted_iota(jnp.int32, (ROWS, ROWS), 0)
    at_col = lax.broadcasted_iota(jnp.int32, (ROWS, ROWS), 1)

    def image(at):
        return (at >= VISIBLE).astype(jnp.int32) + (at >= PAIR).astype(jnp.int32)

    return image(at_row) == image(at_col)


def side_by_side(block):
    left = lax.broadcasted_iota(jnp.int32, (ROWS, 128), 1) < HEAD_DIM
    none = jnp.zeros_like(block)
    return jnp.concatenate([jnp.where(left, block, none), jnp.where(left, none, block)])


def both_heads(stack):
    left = lax.broadcasted_iota(jnp.int32, (ROWS, 128), 1) < HEAD_DIM
    return jnp.where(left, stack[:ROWS], stack[ROWS:])


def pair_of(ref, part, pair):
    return ref[:, part * D + pair * 128 : part * D + (pair + 1) * 128]


def attend_body(triple_ref, mixed_ref, prob_ref):
    keep = same_image()[None]
    for pair in range(HEADS // 2):
        q, k, v = (pair_of(triple_ref, part, pair) for part in range(3))
        scores = dot(side_by_side(k), q, 1, 1).reshape(2, ROWS, ROWS) * HEAD_DIM**-0.5
        scores = jnp.where(keep, scores, -1e30)
        expo = jnp.exp(scores - jnp.max(scores, 1, keepdims=True))
        prob = expo / jnp.sum(expo, 1, keepdims=True)
        prob_ref[0, 2 * pair : 2 * pair + 2] = prob
        low = prob.astype(BF).reshape(2 * ROWS, ROWS)
        mixed_ref[:, pair * 128 : (pair + 1) * 128] = dot(low, side_by_side(v), 0, 0).astype(BF)


def attend(triple):
    groups = triple.shape[0] // ROWS
    return call(
        attend_body,
        (groups,),
        [spec((ROWS, 3 * D), lambda g: (g, 0))],
        [spec((ROWS, D), lambda g: (g, 0)), spec((1, HEADS, ROWS, ROWS), lambda g: (g, 0, 0, 0))],
        [struct((groups * ROWS, D), BF), pltpu.HBM((groups, HEADS, ROWS, ROWS), F32)],
        us=0.01,
        nbytes=groups * ROWS * (8 * D + HEADS * 512),
    )(triple)


def mix_body(mixed_ref, w_ref, rows_ref, vec_ref, middle_ref, hidden_ref):
    branch = dot(mixed_ref[...], w_ref[...], 1, 0) + vec_row(vec_ref, BIAS_OUT)
    middle = rows_ref[...].astype(F32) + branch
    middle_ref[...] = middle
    normed, _ = stats(middle)
    hidden_ref[...] = (
        normed * vec_row(vec_ref, GAIN_TWO) + vec_row(vec_ref, SHIFT_TWO)
    ).astype(BF)


def row_tile(r):
    return r // 2


def mix(mixed, w, rows, vec):
    r = rows.shape[0]
    m = row_tile(r)
    row = spec((m, D), lambda i: (i, 0))
    return call(
        mix_body,
        (r // m,),
        [row, spec((D, D), lambda i: (0, 0)), row, spec((8, D), lambda i: (0, 0))],
        [row, row],
        [struct((r, D), F32), struct((r, D), BF)],
        us=200,
        nbytes=r * D * 10 + D * D * 2,
    )(mixed, w, rows, vec)


def up_body(hidden_ref, w_ref, bias_ref, active_ref, slope_ref):
    inner = dot(hidden_ref[...], w_ref[...], 1, 0) + bias_ref[...]
    phi = 0.5 * (1.0 + lax.erf(inner * (0.5**0.5)))
    active_ref[...] = (inner * phi).astype(BF)
    slope_ref[...] = phi + inner * (jnp.exp(-0.5 * inner * inner) * 0.3989422804014327)


def up(hidden, w, bias):
    r = hidden.shape[0]
    units = w.shape[1]
    tile = spec((r, TILE), lambda j: (0, j))
    return call(
        up_body,
        (units // TILE,),
        [
            spec((r, D), lambda j: (0, 0)),
            spec((D, TILE), lambda j: (0, j)),
            spec((1, TILE), lambda j: (0, j)),
        ],
        [tile, tile],
        [pltpu.HBM((r, units), BF), pltpu.HBM((r, units), F32)],
        us=0.01,
        nbytes=r * D * 2 + D * units * 2 + r * units * 6,
    )(hidden, w, bias)


def down_body(active_ref, w_ref, vec_ref, middle_ref, out_ref):
    branch = dot(active_ref[...], w_ref[...], 1, 1) + vec_row(vec_ref, BIAS_DOWN)
    out_ref[...] = (middle_ref[...] + branch).astype(BF)


def down(active, w, vec, middle):
    r, units = active.shape
    m = row_tile(r)
    return call(
        down_body,
        (r // m,),
        [
            spec((m, units), lambda i: (i, 0)),
            spec((D, units), lambda i: (0, 0)),
            spec((8, D), lambda i: (0, 0)),
            spec((m, D), lambda i: (i, 0)),
        ],
        spec((m, D), lambda i: (i, 0)),
        struct((r, D), BF),
        us=200,
        nbytes=r * units * 2 + D * units * 2 + r * D * 6,
    )(active, w, vec, middle)


def outer_body(left_ref, right_ref, out_ref, sum_ref, turned):
    @pl.when(pl.program_id(0) == 0)
    def _():
        turned[...] = left_ref[...].T

    right = right_ref[...]
    out_ref[...] = dot(turned[...], right, 1, 0).astype(BF)
    sum_ref[...] = jnp.sum(right.astype(F32), 0, keepdims=True)


def outer(left, right):
    r, width = right.shape
    rows = left.shape[1]
    return call(
        outer_body,
        (width // TILE,),
        [spec((r, rows), lambda j: (0, 0)), spec((r, TILE), lambda j: (0, j))],
        [spec((rows, TILE), lambda j: (0, j)), spec((1, TILE), lambda j: (0, j))],
        [struct((rows, width), BF), struct((1, width), F32)],
        [pltpu.VMEM((rows, r), BF)],
        us=200,
        nbytes=r * rows * 2 + r * width * 2 + rows * width * 2,
    )(left, right)


def inner_back_body(cot_ref, w_ref, slope_ref, hidden_ref, grad_ref, gw_ref, gb_ref, turned):
    @pl.when(pl.program_id(0) == 0)
    def _():
        turned[...] = hidden_ref[...].T

    grad = (dot(cot_ref[...], w_ref[...], 1, 0) * slope_ref[...]).astype(BF)
    grad_ref[...] = grad
    gw_ref[...] = dot(turned[...], grad, 1, 0).astype(BF)
    gb_ref[...] = jnp.sum(grad.astype(F32), 0, keepdims=True)


def inner_back(cot, w, slope, hidden):
    r, units = slope.shape
    full = spec((r, D), lambda j: (0, 0))
    col = spec((D, TILE), lambda j: (0, j))
    tile = spec((r, TILE), lambda j: (0, j))
    return call(
        inner_back_body,
        (units // TILE,),
        [full, col, tile, full],
        [tile, col, spec((1, TILE), lambda j: (0, j))],
        [pltpu.HBM((r, units), BF), struct((D, units), BF), struct((1, units), F32)],
        [pltpu.VMEM((D, r), BF)],
        us=200,
        nbytes=r * D * 4 + D * units * 4 + r * units * 6,
    )(cot, w, slope, hidden)


def norm_pull(grad, normed, inv, gain):
    scaled = grad * gain
    return inv * (
        scaled
        - jnp.mean(scaled, 1, keepdims=True)
        - normed * jnp.mean(scaled * normed, 1, keepdims=True)
    )


def middle_back_body(
    grad_ref, w_ref, middle_ref, cot_ref, vec_ref, out_ref, branch_ref, gain_sum, shift_sum, out_sum
):
    grad = dot(grad_ref[...], w_ref[...], 1, 1)
    normed, inv = stats(middle_ref[...])
    total = cot_ref[...].astype(F32) + norm_pull(
        grad, normed, inv, vec_row(vec_ref, GAIN_TWO)
    )
    out_ref[...] = total
    branch = total.astype(BF)
    branch_ref[...] = branch
    sums = (
        (gain_sum, jnp.sum(grad * normed, 0, keepdims=True)),
        (shift_sum, jnp.sum(grad, 0, keepdims=True)),
        (out_sum, jnp.sum(branch.astype(F32), 0, keepdims=True)),
    )
    for ref, value in sums:
        add_up(ref, value)


def add_up(ref, value):
    @pl.when(pl.program_id(0) == 0)
    def _():
        ref[...] = value

    @pl.when(pl.program_id(0) != 0)
    def _():
        ref[...] += value


def middle_back(grad, w, middle, cot, vecs):
    r, units = grad.shape
    m = row_tile(r)
    vec = spec((1, D), lambda i: (0, 0))
    row = spec((m, D), lambda i: (i, 0))
    vec_out = struct((1, D), F32)
    return call(
        middle_back_body,
        (r // m,),
        [
            spec((m, units), lambda i: (i, 0)),
            spec((D, units), lambda i: (0, 0)),
            row,
            row,
            spec((8, D), lambda i: (0, 0)),
        ],
        [row, row, vec, vec, vec],
        [struct((r, D), F32), struct((r, D), BF), vec_out, vec_out, vec_out],
        us=0.01,
        nbytes=r * units * 2 + D * units * 2 + r * D * 12,
    )(grad, w, middle, cot, vecs)


def mixed_back_body(branch_ref, tile_ref, w_ref, mixed_ref, grad_ref, gw_ref, turned):
    @pl.when(pl.program_id(0) == 0)
    def _():
        turned[...] = mixed_ref[...].T

    grad_ref[...] = dot(branch_ref[...], w_ref[...], 1, 1).astype(BF)
    gw_ref[...] = dot(turned[...], tile_ref[...], 1, 0).astype(BF)


def mixed_back(branch, w, mixed):
    r = branch.shape[0]
    full = spec((r, D), lambda j: (0, 0))
    tile = spec((r, TILE), lambda j: (0, j))
    return call(
        mixed_back_body,
        (D // TILE,),
        [full, tile, spec((TILE, D), lambda j: (j, 0)), full],
        [tile, spec((D, TILE), lambda j: (0, j))],
        [struct((r, D), BF), struct((D, D), BF)],
        [pltpu.VMEM((D, r), BF)],
        us=0.01,
        nbytes=r * D * 8 + D * D * 4,
    )(branch, branch, w, mixed)


def attend_back_body(triple_ref, prob_ref, grad_ref, *rest):
    out_ref = rest[-1]
    scale = HEAD_DIM**-0.5
    for pair in range(HEADS // 2):
        q, k, v = (pair_of(triple_ref, part, pair) for part in range(3))
        grad = pair_of(grad_ref, 0, pair)
        prob = prob_ref[0, 2 * pair : 2 * pair + 2]
        grad_prob = dot(side_by_side(v), grad, 1, 1).reshape(2, ROWS, ROWS)
        inside = jnp.sum(grad_prob * prob, 1, keepdims=True)
        grad_scores = (prob * (grad_prob - inside)).astype(BF).reshape(2 * ROWS, ROWS)
        grads = (
            dot(grad_scores, side_by_side(k), 0, 0) * scale,
            both_heads(dot(grad_scores, q, 1, 0)) * scale,
            both_heads(dot(prob.astype(BF).reshape(2 * ROWS, ROWS), grad, 1, 0)),
        )
        for part, value in enumerate(grads):
            out_ref[:, part * D + pair * 128 : part * D + (pair + 1) * 128] = value.astype(BF)


def attend_back(triple, prob, grad, start, stop, partial_out=None):
    wide = spec((ROWS, 3 * D), lambda g: (g + start, 0))
    count = stop - start
    given = [] if partial_out is None else [partial_out]
    return pl.pallas_call(
        attend_back_body,
        out_shape=struct(triple.shape, BF),
        grid_spec=pltpu.PrefetchScalarGridSpec(
            num_scalar_prefetch=0,
            grid=(count,),
            in_specs=[
                wide,
                spec((1, HEADS, ROWS, ROWS), lambda g: (g + start, 0, 0, 0)),
                spec((ROWS, D), lambda g: (g + start, 0)),
            ]
            + [ANY] * len(given),
            out_specs=wide,
        ),
        input_output_aliases={3: 0} if given else {},
        compiler_params=pltpu.CompilerParams(
            dimension_semantics=("arbitrary",), vmem_limit_bytes=24 * MB
        ),
        cost_estimate=pl.CostEstimate(
            flops=200 * FLOPS_PER_US, bytes_accessed=1024, transcendentals=0
        ),
    )(triple, prob, grad, *given)


def qkv_grad_body(grad_ref, hidden_ref, gw_ref, gb_ref):
    grad = grad_ref[...]
    gw_ref[...] = dot(grad.T, hidden_ref[...], 1, 0).astype(BF)
    gb_ref[...] = jnp.sum(grad.astype(F32), 0, keepdims=True)


def qkv_grad(grad, hidden):
    r, width = grad.shape
    return call(
        qkv_grad_body,
        (width // TILE,),
        [spec((r, TILE), lambda j: (0, j)), spec((r, D), lambda j: (0, 0))],
        [spec((TILE, D), lambda j: (j, 0)), spec((1, TILE), lambda j: (0, j))],
        [struct((width, D), BF), struct((1, width), F32)],
        us=200,
        nbytes=r * width * 2 + r * D * 2 + width * D * 2,
    )(grad, hidden)


def first_back_body(grad_ref, w_ref, rows_ref, middle_ref, vec_ref, out_ref, gain_sum, shift_sum):
    grad = dot(grad_ref[...], w_ref[...], 1, 0)
    normed, inv = stats(rows_ref[...].astype(F32))
    pulled = norm_pull(grad, normed, inv, vec_row(vec_ref, GAIN_ONE))
    out_ref[...] = middle_ref[...] + pulled
    add_up(gain_sum, jnp.sum(grad * normed, 0, keepdims=True))
    add_up(shift_sum, jnp.sum(grad, 0, keepdims=True))


def first_back(grad, w, rows, grad_middle, vecs):
    r, width = grad.shape
    m = row_tile(r)
    vec = spec((1, D), lambda i: (0, 0))
    row = spec((m, D), lambda i: (i, 0))
    vec_out = struct((1, D), F32)
    return call(
        first_back_body,
        (r // m,),
        [
            spec((m, width), lambda i: (i, 0)),
            spec((width, D), lambda i: (0, 0)),
            row,
            row,
            spec((8, D), lambda i: (0, 0)),
        ],
        [row, vec, vec],
        [struct((r, D), F32), vec_out, vec_out],
        us=0.01,
        nbytes=r * width * 2 + D * width * 2 + r * D * 10,
    )(grad, w, rows, grad_middle, vecs)


WIDE, NARROW, DP = "wide", "narrow", "dp"


def swap(value, axis, bit):
    size = lax.axis_size(axis)
    return lax.ppermute(value, axis, [(i, i ^ bit) for i in range(size)])


def hold(value, *deps):
    return lax.optimization_barrier((value, deps))[0]


class Pieces:
    def __init__(self, stack, tags):
        self.stack, self.tags = stack, tags

    def fetch(self, axis, bit, *deps):
        move = [bit if axis == name else 0 for name in (WIDE, NARROW, DP)]
        tags = [tuple(a ^ b for a, b in zip(tag, move)) for tag in self.tags]
        return Pieces(swap(hold(self.stack, *deps), axis, bit), tags)

    def after(self, *deps):
        return Pieces(hold(self.stack, *deps), self.tags)

    def rows(self, start, stop):
        return Pieces(self.stack[:, start:stop], self.tags)

    def join(self, *others):
        stack = jnp.concatenate([self.stack] + [o.stack for o in others])
        return Pieces(stack, sum([o.tags for o in others], self.tags))


def first_piece(piece):
    return Pieces(piece[None], [(0, 0, 0)])


def dp_sum(total):
    total = total.astype(F32)
    bit = 2
    while bit < lax.axis_size(DP):
        total = total + swap(total.astype(BF), DP, bit).astype(F32)
        bit *= 2
    return total


def qkv_plan(cols, heads_cols, parts, spots):
    rows = heads_cols // parts

    def plan(w, n, q):
        return [
            (0, spot, (rows, cols), (p * D + w * heads_cols + q * rows, n * cols))
            for p, spot in spots.items()
        ]

    return plan


def out_plan(cols, heads_cols, parts, spot, which=0):
    rows = heads_cols // parts
    return lambda w, n, q: [(which, spot, (rows, cols), (w * heads_cols + q * rows, n * cols))]


def flat_plan(cols, units, parts):
    rows = cols // parts
    return lambda w, n, q: [(0, (0, 0), (rows, units), (n * cols + q * rows, w * units))]


def sums_plan(cols, narrow, spot, which):
    return lambda w, n, q: [(which, spot, (16, cols), ((w * narrow + n) * 16, 0))]


def joined(*plans):
    return lambda w, n, q: [move for plan in plans for move in plan(w, n, q)]


def prep_body(cols, rows, at_ref, *refs):
    qkv_ref, out_ref, vectors = refs[0], refs[1], refs[2:10]
    piece_ref, held, sem = refs[10], refs[11:-1], refs[-1]
    start = pl.multiple_of(at_ref[2] * rows, 16)
    copies = [
        pltpu.make_async_copy(
            qkv_ref.at[p, pl.ds(start, rows)], piece_ref.at[pl.ds(p * rows, rows)], sem.at[p]
        )
        for p in range(3)
    ]
    copies.append(
        pltpu.make_async_copy(
            out_ref.at[pl.ds(start, rows)], piece_ref.at[pl.ds(3 * rows + 16, rows)], sem.at[3]
        )
    )
    copies += [
        pltpu.make_async_copy(vector, scratch, sem.at[4 + k])
        for k, (vector, scratch) in enumerate(zip(vectors, held))
    ]
    for copy in copies:
        copy.start()
    for copy in copies:
        copy.wait()
    lines = [ref[...].astype(F32).reshape(1, -1) for ref in held[:6]]
    both = held[6][...].astype(F32)
    lines.append(jnp.concatenate([both[:1], both[1:]], axis=1))
    wide_line = held[7][...].astype(F32).reshape(1, -1)
    lines += [wide_line[:, k : k + cols] for k in range(0, wide_line.shape[1], cols)]
    lines.append(jnp.zeros((16 - len(lines), cols), F32))
    piece_ref[3 * rows : 3 * rows + 16, :] = jnp.concatenate(lines, axis=0).astype(BF)


def prep(at, qkv_t, w_out, *vectors):
    cols = qkv_t.shape[2]
    rows = qkv_t.shape[1] // 2
    return pl.pallas_call(
        partial(prep_body, cols, rows),
        out_shape=struct((4 * rows + 16, cols), BF),
        grid_spec=pltpu.PrefetchScalarGridSpec(
            num_scalar_prefetch=1,
            grid=(1,),
            in_specs=[IN_HBM] * (2 + len(vectors)),
            out_specs=pl.BlockSpec(memory_space=pltpu.VMEM),
            scratch_shapes=[pltpu.VMEM(v.shape, BF) for v in vectors]
            + [pltpu.SemaphoreType.DMA((4 + len(vectors),))],
        ),
        compiler_params=pltpu.CompilerParams(vmem_limit_bytes=8 * MB),
        cost_estimate=pl.CostEstimate(
            flops=FLOPS_PER_US // 100, bytes_accessed=1024, transcendentals=0
        ),
    )(at, *[in_hbm(v) for v in (qkv_t, w_out, *vectors)])


def vec_body(wide, narrow, cols, first, tag_lists, at_ref, *refs):
    arrays, (vec_ref, qkv_bias_ref, up_bias_ref, held, sem) = refs[:-5], refs[-5:]
    copies = []
    for array, tags in zip(arrays, tag_lists):
        for k, (dw, dn, _) in enumerate(tags):
            slot = (at_ref[0] ^ dw) * narrow + (at_ref[1] ^ dn)
            source = array.at[k, pl.ds(first, 16)]
            copies.append(pltpu.make_async_copy(source, held.at[slot], sem.at[len(copies)]))
    for copy in copies:
        copy.start()
    for copy in copies:
        copy.wait()
    lines = [held[k].astype(F32) for k in range(wide * narrow)]
    for n in range(narrow):
        vec_ref[:, n * cols : (n + 1) * cols] = lines[n][:8]
    by_wide = [lines[w * narrow] for w in range(wide)]
    half = cols // 2
    q = jnp.concatenate([line[6:7, :half] for line in by_wide], axis=1)
    v = jnp.concatenate([line[6:7, half:] for line in by_wide], axis=1)
    qkv_bias_ref[...] = jnp.concatenate([q, jnp.zeros_like(q), v], axis=1)
    up_bias_ref[...] = jnp.concatenate(
        [line[i : i + 1] for line in by_wide for i in (7, 8)], axis=1
    )


def vectors_of(at, pieces, first, wide, narrow, cols, units):
    vmem = pl.BlockSpec(memory_space=pltpu.VMEM)
    return pl.pallas_call(
        partial(vec_body, wide, narrow, cols, first, [p.tags for p in pieces]),
        out_shape=[struct((8, D), F32), struct((1, 3 * D), F32), struct((1, wide * units), F32)],
        grid_spec=pltpu.PrefetchScalarGridSpec(
            num_scalar_prefetch=1,
            grid=(1,),
            in_specs=[ANY] * len(pieces),
            out_specs=[vmem] * 3,
            scratch_shapes=[
                pltpu.VMEM((wide * narrow, 16, cols), BF),
                pltpu.SemaphoreType.DMA((wide * narrow,)),
            ],
        ),
        compiler_params=pltpu.CompilerParams(vmem_limit_bytes=8 * MB),
        cost_estimate=pl.CostEstimate(flops=FLOPS_PER_US // 100, bytes_accessed=1024, transcendentals=0),
    )(at, *[p.stack for p in pieces])


def pack_body(*refs):
    out = refs[-1]
    at = 0
    for ref in refs[:-1]:
        for k in range(0, ref.shape[1], D):
            out[at : at + 1, :] = ref[:, k : k + D]
            at += 1
    if at < out.shape[0]:
        out[at:, :] = jnp.zeros((out.shape[0] - at, D), F32)


def pack(*rows):
    count = -(-sum(r.shape[1] for r in rows) // (8 * D)) * 8
    vmem = pl.BlockSpec(memory_space=pltpu.VMEM)
    return pl.pallas_call(
        pack_body,
        out_shape=struct((count, D), F32),
        in_specs=[vmem] * len(rows),
        out_specs=vmem,
        compiler_params=pltpu.CompilerParams(vmem_limit_bytes=8 * MB),
        cost_estimate=pl.CostEstimate(flops=FLOPS_PER_US // 100, bytes_accessed=1024, transcendentals=0),
    )(*rows)


ANY = pl.BlockSpec(memory_space=pl.ANY)
IN_HBM = pl.BlockSpec(memory_space=pltpu.HBM)


CORE, DP_INDEX = 2, 3


def owner_sums_body(wide, narrow, cols, *refs):
    out = refs[-1]
    narrow_refs, qkv_ref, up_ref = refs[:6], refs[6], refs[7]
    part, units = D // wide, up_ref.shape[1] // wide
    for w in range(wide):
        for n in range(narrow):
            lines = [ref[:, n * cols : (n + 1) * cols] for ref in narrow_refs]
            lines.append(
                jnp.concatenate(
                    [qkv_ref[:, p * D + w * part : p * D + (w + 1) * part] for p in (0, 2)], axis=1
                )
            )
            lines += [
                up_ref[:, w * units + k : w * units + k + cols] for k in range(0, units, cols)
            ]
            lines.append(jnp.zeros((16 - len(lines), cols), F32))
            at = (w * narrow + n) * 16
            out[at : at + 16, :] = jnp.concatenate(lines, axis=0).astype(BF)


def owner_sums(wide, narrow, cols, *rows):
    vmem = pl.BlockSpec(memory_space=pltpu.VMEM)
    return pl.pallas_call(
        partial(owner_sums_body, wide, narrow, cols),
        out_shape=struct((wide * narrow * 16, cols), BF),
        in_specs=[vmem] * len(rows),
        out_specs=vmem,
        compiler_params=pltpu.CompilerParams(vmem_limit_bytes=8 * MB),
        cost_estimate=pl.CostEstimate(
            flops=FLOPS_PER_US // 100, bytes_accessed=1024, transcendentals=0
        ),
    )(*rows)


def build_body(plan, tag_lists, inverse, part_at, at_ref, *refs):
    refs, sem = refs[:-1], refs[-1]
    count = len(tag_lists)
    wholes, arrays = (refs[:-count], refs[-count:]) if inverse else (refs[count:], refs[:count])
    copies = []
    for array, tags in zip(arrays, tag_lists):
        for k, (dw, dn, dq) in enumerate(tags):
            w, n, q = at_ref[0] ^ dw, at_ref[1] ^ dn, at_ref[part_at] ^ dq
            for which, (at_row, at_lane), (rows, lanes), (row, lane) in plan(w, n, q):
                piece = array.at[k, pl.ds(at_row, rows), pl.ds(at_lane, lanes)]
                whole = wholes[which].at[
                    pl.ds(pl.multiple_of(row, 16), rows), pl.ds(pl.multiple_of(lane, 128), lanes)
                ]
                ends = (whole, piece) if inverse else (piece, whole)
                copies.append(pltpu.make_async_copy(*ends, sem.at[len(copies)]))
    for copy in copies:
        copy.start()
    for copy in copies:
        copy.wait()


def move_pieces(at, arrays, plan, tag_lists, inverse, part_at, shapes):
    moves = sum(len(tags) for tags in tag_lists) * len(plan(0, 0, 0))
    return pl.pallas_call(
        partial(build_body, plan, tag_lists, inverse, part_at),
        out_shape=[struct(shape, BF) for shape in shapes],
        grid_spec=pltpu.PrefetchScalarGridSpec(
            num_scalar_prefetch=1,
            grid=(1,),
            in_specs=[ANY] * len(arrays),
            out_specs=[ANY] * len(shapes),
            scratch_shapes=[pltpu.SemaphoreType.DMA((moves,))],
        ),
        compiler_params=pltpu.CompilerParams(vmem_limit_bytes=4 * MB),
        cost_estimate=pl.CostEstimate(
            flops=FLOPS_PER_US // 100, bytes_accessed=1024, transcendentals=0
        ),
    )(at, *arrays)


CORE, DP_INDEX = 2, 3


def build_weights(at, pieces, plan, shape, part_at=CORE):
    arrays, tags = [in_hbm(p.stack) for p in pieces], [p.tags for p in pieces]
    return move_pieces(at, arrays, plan, tags, False, part_at, [shape])[0]


def cut_grads(at, grads, plan, tags, shape, part_at=CORE):
    tag_lists = [[(w, n, q ^ dc) for w, n, q in tags] for dc in range(2)]
    return move_pieces(at, grads, plan, tag_lists, True, part_at, [(len(tags),) + shape] * 2)


def fence_body(x_ref, out_ref):
    out_ref[...] = x_ref[...]


def fence(token):
    vmem = pl.BlockSpec(memory_space=pltpu.VMEM)
    return pl.pallas_call(
        fence_body,
        out_shape=struct(token.shape, token.dtype),
        in_specs=[vmem],
        out_specs=vmem,
        compiler_params=pltpu.CompilerParams(vmem_limit_bytes=MB, has_side_effects=True),
        cost_estimate=pl.CostEstimate(
            flops=200 * FLOPS_PER_US, bytes_accessed=1024, transcendentals=0
        ),
    )(token)


class Chain:
    def __init__(self, at, grads, plan, tags, shape, part_at=CORE):
        self.keep, self.send = cut_grads(at, grads, plan, tags, shape, part_at)

    def go(self, axis, bit):
        self.got = swap(self.send, axis, bit)

    def fold(self, *deps):
        self.keep, self.send = halves_summed(self.keep, hold(self.got, *deps))

    def spread(self, *deps):
        got = hold(self.got, *deps)
        order = (0, 2, 1, 3)
        total = [k.astype(F32) + g.astype(F32) for k, g in zip(self.keep, got)]
        self.keep = total[0]
        self.send = [total[order.index(bit)].astype(BF) for bit in range(1, len(total))]
        self.got = [swap(piece, WIDE, bit) for bit, piece in enumerate(self.send, 1)]

    def all_of(self, *deps):
        total = self.keep
        for got in hold(self.got, *deps):
            total = total + got.astype(F32)
        return total

    def total(self, *deps):
        return self.keep[0].astype(F32) + hold(self.got, *deps)[0].astype(F32)


def doubled(value, bit, index):
    other = swap(value, DP, bit)
    return jnp.where(index == 0, jnp.stack([value, other]), jnp.stack([other, value]))


def halves_summed(kept, got):
    half = kept.shape[0] // 2
    keep = kept[:half].astype(F32) + got[:half].astype(F32)
    send = (kept[half:].astype(F32) + got[half:].astype(F32)).astype(BF)
    return keep, send


def core_half(at, shard):
    rows = shard.shape[0] // 2
    return lax.dynamic_slice_in_dim(shard, at[2] * rows, rows, axis=0)


def quarter(at, shard):
    rows = shard.shape[0] // 4
    return lax.dynamic_slice_in_dim(shard, at[3] * rows, rows, axis=0)


def to_rows(blocks, narrow):
    got = lax.all_to_all(blocks, "narrow", 0, 0, tiled=True)
    return jnp.concatenate([got[n] for n in range(narrow)], axis=1)


def from_rows(rows, narrow):
    cols = rows.shape[1] // narrow
    blocks = jnp.stack([rows[:, n * cols : (n + 1) * cols] for n in range(narrow)])
    got = lax.all_to_all(blocks, "narrow", 0, 0, tiled=True)
    return got.reshape(-1, cols)


def gather_weight(shard, wide, narrow):
    got = lax.all_gather(shard.reshape(-1, 128), ("wide", "narrow"), axis=0, tiled=True)
    return got.reshape((wide, narrow) + shard.shape)


def scatter_grad(blocks):
    shape = blocks.shape[2:]
    got = lax.psum_scatter(
        blocks.reshape(-1, 128), ("wide", "narrow"), scatter_dimension=0, tiled=True
    )
    return lax.psum(got.astype(F32), "dp").reshape(shape)


def on_device(
    wide,
    narrow,
    patches,
    visible,
    w_qkv,
    b_qv,
    w_out,
    b_out,
    w_up,
    b_up,
    w_down,
    b_down,
    gain_one,
    shift_one,
    gain_two,
    shift_two,
    cotangent,
):
    images = visible.shape[0]
    pairs = images // 2
    cols = w_qkv.shape[0]
    heads_cols = w_qkv.shape[2]
    units = w_up.shape[1]
    swaps = cols % 128 == 0 and narrow == 2 and wide == 4 and lax.axis_size(DP) == 4
    swaps = swaps and pairs % 2 == 0

    at = jnp.stack(
        [
            lax.axis_index("wide"),
            lax.axis_index("narrow"),
            lax.axis_index("dp") % 2,
            lax.axis_index("dp"),
        ]
    ).astype(jnp.int32)

    index = (visible.reshape(pairs, 2, VISIBLE) + jnp.array([0, PATCHES])[None, :, None]).reshape(
        pairs, PAIR
    )
    index = jnp.pad(index, ((0, 0), (0, ROWS - PAIR)), constant_values=-1)[:, :, None]

    w_qkv_t = w_qkv.transpose(1, 2, 0)
    if swaps:
        first = first_piece(
            prep(
                at,
                w_qkv_t,
                w_out,
                gain_one,
                shift_one,
                gain_two,
                shift_two,
                b_out,
                b_down,
                b_qv,
                b_up,
            )
        )

        def part_of(whole, side):
            return lax.dynamic_slice_in_dim(whole, side * cols, cols, axis=1)

        def join_cols(keep, got):
            return jnp.where(
                at[1] == 0,
                jnp.concatenate([keep, got], axis=1),
                jnp.concatenate([got, keep], axis=1),
            )

        mine, theirs = at[1], 1 - at[1]
        whole = (D, wide * units)

        first_z = [first.fetch(WIDE, bit) for bit in (1, 2, 3)]
        rows_out = pick_rows(hold(at, first.stack), patches, index, cols)
        own = rows_out.shape[0] // 2
        rows_send = rows_out[:own]
        rows_got = swap(rows_send, NARROW, 1)
        cot_out = cot_rows(hold(at, rows_send), cotangent, pairs, cols)

        first = first.join(*[p.after(cot_out) for p in first_z])
        up_p = first_piece(hold(core_half(at, w_up), first.stack))
        up_z = [up_p.fetch(WIDE, bit) for bit in (1, 2, 3)]
        rows = join_cols(rows_out[own:], hold(rows_got, up_p.stack))
        first_x = first.fetch(NARROW, 1, rows)
        up_p = up_p.join(*[p.after(rows) for p in up_z])

        first = first.join(first_x.after(up_p.stack))
        first_c = first.fetch(DP, 1)
        up_x = up_p.fetch(NARROW, 1)
        down_p = first_piece(hold(quarter(at, w_down), first.stack))
        down_z = [down_p.fetch(WIDE, bit) for bit in (1, 2, 3)]
        vec_at = 3 * heads_cols // 2
        out_at = (vec_at + 16, 0)
        vecs, bias_qkv, bias_up = vectors_of(at, [first], vec_at, wide, narrow, cols, units)
        hidden_one = norm(rows, vecs)
        all_first = [first, first_c.after(hidden_one)]
        half = heads_cols // 2
        first_plan = qkv_plan(cols, heads_cols, 2, {p: (p * half, 0) for p in range(3)})
        qkv_t = build_weights(at, all_first, first_plan, (3 * D, D))
        out_w = build_weights(at, all_first, out_plan(cols, heads_cols, 2, out_at), (D, D))
        down_p = down_p.join(*[p.after(qkv_t) for p in down_z])
        down_x = down_p.fetch(NARROW, 1)
        triple = qkv(hold(hidden_one, down_p.stack), qkv_t, bias_qkv)
        mixed, prob = attend(triple)
        half_flat, part_flat = flat_plan(cols, units, 2), flat_plan(cols, units, 4)
        up_x = up_x.after(mixed)
        up_c = up_p.fetch(DP, 1, up_x.stack)
        up_xc = up_x.fetch(DP, 1)
        down_p = down_p.join(down_x.after(mixed))
        down_y = down_p.fetch(DP, 2)
        cot_send = hold(cot_out[:own], down_p.stack)
        cot_got = swap(cot_send, NARROW, 1)
        middle, hidden_two = mix(
            hold(mixed, up_x.stack, down_p.stack, cot_send), out_w, rows, vecs
        )
        up_c, up_xc = up_c.after(hidden_two), up_xc.after(hidden_two)
        up_w = build_weights(at, [up_p, up_x, up_c, up_xc], half_flat, whole)
        active, slope = up(hidden_two, up_w, bias_up)
        cot = join_cols(cot_out[own:], hold(cot_got, active))
        down_y = down_y.after(active)
        down_c = [p.fetch(DP, 1, down_y.stack) for p in (down_p, down_y)]

        x_first = [(w, n, 0) for n in range(2) for w in (0, 2, 1, 3)]
        y_first = [(w, n, dy) for dy in (0, 2) for n in range(2) for w in (0, 2, 1, 3)]
        gw_down, _ = outer(hold(cot, *[p.stack for p in (down_p, down_y)]), active)
        gb_down = jnp.sum(cot, 0, dtype=F32)[None]
        down_c = [p.after(gw_down) for p in down_c]
        down_w = build_weights(at, [down_p, down_y] + down_c, part_flat, whole, DP_INDEX)
        g_d = Chain(at, [hold(gw_down, down_w)], half_flat, x_first, (cols // 2, units))
        g_d.go(DP, 1)
        g_d.fold()
        g_d.go(NARROW, 1)
        grad_inner, gw_up, gb_up = inner_back(
            cot, hold(down_w, g_d.send), in_hbm(slope), hidden_two
        )

        g_u = Chain(at, [gw_up], part_flat, y_first, (cols // 4, units), DP_INDEX)
        g_u.go(DP, 1)
        g_d.fold(g_u.send)
        g_d.go(WIDE, 1)
        result = down(hold(active, g_d.send), down_w, vecs, middle)
        grad_middle, branch, gg_two, gs_two, gb_out = middle_back(
            hold(grad_inner, result), up_w, middle, cot, vecs
        )
        grad_mixed, gw_out = mixed_back(branch, out_w, mixed)

        g_u.fold(grad_mixed)
        g_u.go(DP, 2)
        g_d.fold(grad_mixed)
        g_d.go(WIDE, 2)
        result_send = hold(part_of(result, theirs), grad_mixed)
        result_got = swap(result_send, NARROW, 1)
        groups = rows.shape[0] // ROWS
        grad_triple = attend_back(
            triple, in_hbm(prob), hold(grad_mixed, g_u.send, g_d.send, result_send), 0, groups
        )
        grad_rows, gg_one, gs_one = first_back(grad_triple, qkv_t, rows, grad_middle, vecs)

        d_sum = g_d.total(grad_rows)
        d_got = swap(d_sum.astype(BF), DP, 2)
        g_u.fold(grad_rows)
        g_u.go(NARROW, 1)
        result_got = hold(result_got, grad_rows)
        gw_qkv, gb_qkv = qkv_grad(hold(grad_triple, d_sum, g_u.send, result_got), hidden_one)
        sums = owner_sums(
            wide,
            narrow,
            cols,
            gg_one,
            gs_one,
            gg_two,
            gs_two,
            gb_out,
            gb_down,
            gb_qkv,
            gb_up,
        )

        part = heads_cols // 4
        g_q = Chain(
            at,
            [gw_qkv],
            qkv_plan(cols, heads_cols, 4, {0: (0, 0), 1: (part, 0)}),
            y_first,
            (2 * part, cols),
            DP_INDEX,
        )
        g_q.go(DP, 1)
        rest_plan = joined(
            qkv_plan(cols, heads_cols, 2, {2: (0, 0)}),
            out_plan(cols, heads_cols, 2, (half, 0), 1),
            sums_plan(cols, narrow, (2 * half, 0), 2),
        )
        g_r = Chain(at, [gw_qkv, gw_out, sums], rest_plan, x_first, (2 * half + 16, cols))
        g_r.go(DP, 1)
        d_sum = d_sum + hold(d_got, g_r.send).astype(F32)
        d_got = swap(d_sum, DP, 1)
        g_u.fold(g_r.send)
        g_u.go(WIDE, 1)
        rows_send = hold(part_of(grad_rows, theirs), g_r.send).astype(BF)
        rows_back = swap(rows_send, NARROW, 1)
        keep = hold(part_of(result, mine), g_q.send, d_sum, g_u.send, rows_send)
        block_output = flat_rows(at, keep, result_got, cols)

        g_q.fold(block_output)
        g_q.go(DP, 2)
        g_r.fold(block_output)
        g_r.go(NARROW, 1)
        g_u.fold(g_q.send, g_r.send)
        g_u.go(WIDE, 2)
        rows_back = hold(rows_back, g_u.send)
        grad_patches = put_rows(at, part_of(grad_rows, mine), rows_back, index, cols)

        def in_order(value, other, index):
            return jnp.where(index == 0, jnp.stack([value, other]), jnp.stack([other, value]))

        g_q.fold(grad_patches)
        g_q.go(NARROW, 1)
        g_r.spread(grad_patches)
        u_sum = g_u.total(g_q.send, *g_r.send)
        u_got = swap(u_sum.astype(BF), DP, 2)
        token = fence(hold(vecs, g_q.send, u_sum, *g_r.send))
        g_q.spread(token)
        r_sum = g_r.all_of(token)
        r_got = swap(r_sum.astype(BF), DP, 2)
        u_sum = in_order(u_sum, hold(u_got, token).astype(F32), at[3] // 2)
        u_got = swap(u_sum, DP, 1)
        token = fence(hold(token, r_sum, u_sum, *g_q.send))
        q_sum = g_q.all_of(token)
        q_got = [swap(q_sum.astype(BF), DP, bit) for bit in (1, 2, 3)]
        r_sum = r_sum + hold(r_got, token).astype(F32)
        r_got = swap(r_sum[: 2 * half], DP, 1)
        g_down = in_order(d_sum, d_got, at[2]).reshape(cols, units)
        g_up = in_order(u_sum, hold(u_got, token), at[2]).transpose(1, 0, 2, 3)
        g_up = g_up.reshape(cols, units)
        q_got = [got.astype(F32) for got in q_got]
        pairs_of = [in_order(q_sum, q_got[0], at[2]), in_order(q_got[1], q_got[2], at[2])]
        q_sum = in_order(*pairs_of, at[3] // 2).reshape(4, 2, part, cols)
        g_rest = in_order(r_sum[: 2 * half], r_got, at[2]).reshape(2, 2, half, cols)
        g_out = g_rest[:, 1].reshape(heads_cols, cols)
        g_qkv = jnp.stack(
            [
                q_sum[:, 0].reshape(heads_cols, cols),
                q_sum[:, 1].reshape(heads_cols, cols),
                g_rest[:, 0].reshape(heads_cols, cols),
            ]
        )
        g_qkv = g_qkv.transpose(2, 0, 1)
        grad_patches = grad_patches.reshape(1, -1)
        lines = r_sum[2 * half :]
        vector_grads = [lines[i] for i in range(6)]
        g_bqv = lines[6].reshape(2, heads_cols)
        g_bup = lines[7:9].reshape(units)
    else:
        table = patches.reshape(images, PATCHES, cols)
        rows_mine = jnp.take_along_axis(table, visible[:, :, None], axis=1)
        rows_mine = jnp.pad(
            rows_mine.reshape(pairs, PAIR, cols), ((0, 0), (0, ROWS - PAIR), (0, 0))
        )
        cot_mine = jnp.pad(
            cotangent.reshape(pairs, PAIR, cols), ((0, 0), (0, ROWS - PAIR), (0, 0))
        )
        rows = to_rows(rows_mine.reshape(narrow, -1, cols), narrow)
        cot = to_rows(cot_mine.reshape(narrow, -1, cols), narrow)
        vec = jnp.concatenate(
            [gain_one, shift_one, gain_two, shift_two, b_out, b_down, b_qv.reshape(-1), b_up]
        )
        vec = lax.all_gather(vec, ("wide", "narrow"), axis=0, tiled=False).astype(F32)
        qkv_t = gather_weight(w_qkv_t, wide, narrow)
        qkv_t = qkv_t.transpose(2, 0, 3, 1, 4).reshape(3 * D, D)
        out_w = gather_weight(w_out, wide, narrow).transpose(0, 2, 1, 3).reshape(D, D)
        up_w = gather_weight(w_up, wide, narrow).transpose(1, 2, 0, 3).reshape(D, -1)
        down_w = gather_weight(w_down, wide, narrow).transpose(1, 2, 0, 3).reshape(D, -1)
        vec = vec.reshape(wide, narrow, -1)
        vecs = vec[0, :, : 6 * cols].reshape(narrow, 6, cols).transpose(1, 0, 2).reshape(6, D)
        vecs = jnp.pad(vecs, ((0, 2), (0, 0)))
        by_wide = vec[:, 0, 6 * cols :]
        bias_q = by_wide[:, :heads_cols].reshape(1, D)
        bias_v = by_wide[:, heads_cols : 2 * heads_cols].reshape(1, D)
        bias_qkv = jnp.concatenate([bias_q, jnp.zeros((1, D), F32), bias_v], axis=1)
        bias_up = by_wide[:, 2 * heads_cols :].reshape(1, -1)

        hidden_one = norm(rows, vecs)
        triple = qkv(hidden_one, qkv_t, bias_qkv)
        mixed, prob = attend(triple)
        middle, hidden_two = mix(mixed, out_w, rows, vecs)
        active, slope = up(hidden_two, up_w, bias_up)
        result = down(active, down_w, vecs, middle)
        gw_down, _ = outer(cot, active)
        gb_down = jnp.sum(cot, 0, dtype=F32)[None]
        grad_inner, gw_up, gb_up = inner_back(cot, down_w, slope, hidden_two)
        grad_middle, branch, gg_two, gs_two, gb_out = middle_back(
            grad_inner, up_w, middle, cot, vecs
        )
        grad_mixed, gw_out = mixed_back(branch, out_w, mixed)
        grad_triple = attend_back(triple, prob, grad_mixed, 0, rows.shape[0] // ROWS)
        gw_qkv, gb_qkv = qkv_grad(grad_triple, hidden_one)
        grad_rows, gg_one, gs_one = first_back(grad_triple, qkv_t, rows, grad_middle, vecs)
        sums = pack(gg_one, gs_one, gg_two, gs_two, gb_out, gb_down, gb_qkv, gb_up)

        result = from_rows(result, narrow)
        grad_rows = from_rows(grad_rows, narrow)
        block_output = result.reshape(pairs, ROWS, cols)[:, :PAIR].reshape(1, -1)
        grad_rows = grad_rows.reshape(pairs, ROWS, cols)[:, :PAIR].reshape(images, VISIBLE, cols)
        grad_patches = (
            jnp.zeros((images, PATCHES, cols), F32)
            .at[jnp.arange(images)[:, None], visible]
            .set(grad_rows)
            .reshape(1, -1)
        )
        g_down = scatter_grad(gw_down.reshape(narrow, cols, wide, units).transpose(2, 0, 1, 3))
        g_up = scatter_grad(gw_up.reshape(narrow, cols, wide, units).transpose(2, 0, 1, 3))
        g_out = scatter_grad(gw_out.reshape(wide, heads_cols, narrow, cols).transpose(0, 2, 1, 3))
        g_qkv = scatter_grad(
            gw_qkv.reshape(3, wide, heads_cols, narrow, cols).transpose(1, 3, 0, 2, 4)
        )
        g_qkv = g_qkv.transpose(2, 0, 1)
        sums = lax.psum(sums, ("dp", "wide", "narrow"))
        sums = sums.reshape(-1)
        vector_grads = [
            lax.dynamic_slice_in_dim(sums, i * D + at[1] * cols, cols) for i in range(6)
        ]
        g_bqv = jnp.stack(
            [
                lax.dynamic_slice_in_dim(sums, (6 + i) * D + at[0] * heads_cols, heads_cols)
                for i in (0, 2)
            ]
        )
        g_bup = lax.dynamic_slice_in_dim(sums, 9 * D + at[0] * units, units)

    return (
        block_output,
        grad_patches,
        g_qkv,
        g_bqv,
        g_out,
        vector_grads[4],
        g_up,
        g_bup,
        g_down,
        vector_grads[5],
        vector_grads[0],
        vector_grads[1],
        vector_grads[2],
        vector_grads[3],
    )


def solution(mesh):
    in_specs = (
        P("narrow", ("dp", "wide")),
        P(("dp", "wide"), None),
        P("narrow", None, "wide"),
        P(None, "wide"),
        P("wide", "narrow"),
        P("narrow"),
        P("narrow", "wide"),
        P("wide"),
        P("narrow", "wide"),
        P("narrow"),
        P("narrow"),
        P("narrow"),
        P("narrow"),
        P("narrow"),
        P("narrow", ("dp", "wide")),
    )
    out_specs = (
        P("narrow", ("dp", "wide")),
        P("narrow", ("dp", "wide")),
        P("narrow", None, "wide"),
        P(None, "wide"),
        P("wide", "narrow"),
        P("narrow"),
        P("narrow", "wide"),
        P("wide"),
        P("narrow", "wide"),
        P("narrow"),
        P("narrow"),
        P("narrow"),
        P("narrow"),
        P("narrow"),
    )
    body = partial(on_device, mesh.shape["wide"], mesh.shape["narrow"])
    return jax.shard_map(body, mesh=mesh, in_specs=in_specs, out_specs=out_specs, check_vma=False)
```

```python
from functools import partial

import jax
import jax.numpy as jnp
from jax import lax
from jax.experimental import pallas as pl
from jax.experimental.pallas import tpu as pltpu
from jax.sharding import PartitionSpec as P

D = 768
HEAD_DIM = 64
HEADS = 12
PATCHES = 196
VISIBLE = 49
PAIR = 2 * VISIBLE
ROWS = 112
TILE = 768
EPS = 1e-06
BF = jnp.bfloat16
F32 = jnp.float32
MB = 1024 * 1024


def dot(a, b, ca, cb):
    return lax.dot_general(a, b, (((ca,), (cb,)), ((), ())), preferred_element_type=F32)


FLOPS_PER_US = 540000000


def call(body, grid, ins, outs, shapes, scratch=(), prefetch=0, us=1.0, nbytes=0, vmem=32):
    return pl.pallas_call(
        body,
        out_shape=shapes,
        grid_spec=pltpu.PrefetchScalarGridSpec(
            num_scalar_prefetch=prefetch,
            grid=grid,
            in_specs=ins,
            out_specs=outs,
            scratch_shapes=scratch,
        ),
        compiler_params=pltpu.CompilerParams(
            dimension_semantics=("arbitrary",) * len(grid), vmem_limit_bytes=vmem * MB
        ),
        cost_estimate=pl.CostEstimate(
            flops=int(us * FLOPS_PER_US), bytes_accessed=1024, transcendentals=0
        ),
    )


def in_hbm(value):
    return pltpu.with_memory_space_constraint(value, pltpu.HBM)


def spec(shape, index):
    return pl.BlockSpec(shape, index)


def struct(shape, dtype):
    return jax.ShapeDtypeStruct(shape, dtype)


def together(own):
    return next(count for count in (4, 2, 1) if own % count == 0)


def strided(start, count, lanes):
    return [pl.ds(start + k, count, stride=lanes) for k in range(lanes)]


def one_hot(index):
    return (index == lax.broadcasted_iota(jnp.int32, (ROWS, 2 * PATCHES), 1)).astype(BF)


def pick_body(cols, count, at_ref, patch_ref, index_ref, rows_ref, wide_ref):
    lanes = cols // 128
    wide_ref[...] = patch_ref[...].astype(F32).reshape(wide_ref.shape)
    for j in range(count):
        places = strided(j * 2 * PATCHES * lanes, 2 * PATCHES, lanes)
        both = jnp.concatenate([wide_ref[place, :] for place in places], axis=1).astype(BF)
        rows_ref[j * ROWS : (j + 1) * ROWS, :] = dot(one_hot(index_ref[j]), both, 1, 0).astype(BF)


def owner_first_sent(steps):
    own = steps // 2

    def source(i, at):
        return (i // own ^ 1 ^ at[1]) * own + i % own

    return source


def pick_rows(at, patches, index, cols):
    pairs = index.shape[0]
    count = together(pairs // 2)
    width = 2 * PATCHES * cols * count
    source = owner_first_sent(pairs // count)
    return call(
        partial(pick_body, cols, count),
        (pairs // count,),
        [
            spec((1, width), lambda i, at: (0, source(i, at))),
            spec((count, ROWS, 1), lambda i, at: (source(i, at), 0, 0)),
        ],
        spec((count * ROWS, cols), lambda i, at: (i, 0)),
        struct((pairs * ROWS, cols), BF),
        [pltpu.VMEM((width // 128, 128), F32)],
        prefetch=1,
        us=200,
        nbytes=pairs * width * 4,
    )(at, patches, index)


def cot_body(cols, count, at_ref, cot_ref, rows_ref, scr):
    lanes = cols // 128
    scr[...] = cot_ref[...].astype(F32).reshape(scr.shape)
    for j in range(count):
        places = strided(j * PAIR * lanes, PAIR, lanes)
        cot = jnp.concatenate([scr[place, :] for place in places], axis=1)
        rows_ref[j * ROWS : (j + 1) * ROWS, :] = jnp.concatenate(
            [cot, jnp.zeros((ROWS - PAIR, cols), F32)], axis=0
        ).astype(BF)


def cot_rows(at, cotangent, pairs, cols):
    count = together(pairs // 2)
    width = PAIR * cols * count
    source = owner_first_sent(pairs // count)
    return call(
        partial(cot_body, cols, count),
        (pairs // count,),
        [spec((1, width), lambda i, at: (0, source(i, at)))],
        spec((count * ROWS, cols), lambda i, at: (i, 0)),
        struct((pairs * ROWS, cols), BF),
        [pltpu.VMEM((width // 128, 128), F32)],
        prefetch=1,
        us=200,
        nbytes=pairs * width * 4,
    )(at, cotangent)


def own_block(at_ref, keep_ref, got_ref, j):
    own = pl.num_programs(0) // 2
    mine = pl.program_id(0) // own == at_ref[1]
    rows = slice(j * ROWS, (j + 1) * ROWS)
    return jnp.where(mine, keep_ref[rows, :].astype(F32), got_ref[rows, :].astype(F32))


def put_body(cols, count, at_ref, keep_ref, got_ref, index_ref, out_ref):
    lanes = cols // 128
    for j in range(count):
        hit = one_hot(index_ref[j])
        rest = own_block(at_ref, keep_ref, got_ref, j)
        parts = []
        for _ in range(3):
            parts.append(rest.astype(BF))
            rest = rest - parts[-1].astype(F32)
        total = dot(jnp.concatenate([hit] * 3), jnp.concatenate(parts), 0, 0)
        for k, place in enumerate(strided(j * 2 * PATCHES * lanes, 2 * PATCHES, lanes)):
            out_ref[place, :] = total[:, k * 128 : (k + 1) * 128]


def put_rows(at, keep, got, index, cols):
    pairs = index.shape[0]
    count = together(pairs // 2)
    own = pairs // count // 2
    tall = count * 2 * PATCHES * cols // 128
    rows = spec((count * ROWS, cols), lambda i, at: (i % own, 0))
    return call(
        partial(put_body, cols, count),
        (pairs // count,),
        [rows, rows, spec((count, ROWS, 1), lambda i, at: (i, 0, 0))],
        spec((tall, 128), lambda i, at: (i, 0)),
        struct((pairs // count * tall, 128), F32),
        prefetch=1,
        us=200,
        nbytes=pairs * (tall * 512 + ROWS * cols * 4),
    )(at, keep, got, index)


def flat_body(cols, count, at_ref, keep_ref, got_ref, out_ref, scr):
    lanes = cols // 128
    for j in range(count):
        rows = own_block(at_ref, keep_ref, got_ref, j)
        for k, place in enumerate(strided(j * PAIR * lanes, PAIR, lanes)):
            scr[place, :] = rows[:PAIR, k * 128 : (k + 1) * 128]
    out_ref[...] = scr[...].reshape(out_ref.shape).astype(BF)


def flat_rows(at, keep, got, cols):
    pairs = 2 * (keep.shape[0] // ROWS)
    count = together(pairs // 2)
    own = pairs // count // 2
    width = PAIR * cols * count
    rows = spec((count * ROWS, cols), lambda i, at: (i % own, 0))
    return call(
        partial(flat_body, cols, count),
        (pairs // count,),
        [rows, rows],
        spec((1, width), lambda i, at: (0, i)),
        struct((1, pairs // count * width), BF),
        [pltpu.VMEM((width // 128, 128), F32)],
        prefetch=1,
        us=200,
        nbytes=pairs * width * 6,
    )(at, keep, got)


def stats(rows):
    mean = jnp.mean(rows, 1, keepdims=True)
    off = rows - mean
    inv = lax.rsqrt(jnp.mean(off * off, 1, keepdims=True) + EPS)
    return off * inv, inv


GAIN_ONE, SHIFT_ONE, GAIN_TWO, SHIFT_TWO, BIAS_OUT, BIAS_DOWN = range(6)


def vec_row(vec_ref, i):
    return vec_ref[i : i + 1, :]


def norm_body(rows_ref, vec_ref, out_ref):
    normed, _ = stats(rows_ref[...].astype(F32))
    out_ref[...] = (normed * vec_row(vec_ref, GAIN_ONE) + vec_row(vec_ref, SHIFT_ONE)).astype(BF)


def norm(rows, vec):
    r = rows.shape[0]
    return call(
        norm_body,
        (r // ROWS,),
        [spec((ROWS, D), lambda i: (i, 0)), spec((8, D), lambda i: (0, 0))],
        spec((ROWS, D), lambda i: (i, 0)),
        struct((r, D), BF),
        us=200,
        nbytes=r * D * 4,
    )(rows, vec)


def qkv_body(hidden_ref, w_ref, bias_ref, out_ref):
    out_ref[...] = (dot(hidden_ref[...], w_ref[...], 1, 1) + bias_ref[...]).astype(BF)


def qkv(hidden, w, bias):
    r = hidden.shape[0]
    return call(
        qkv_body,
        (3 * D // TILE,),
        [
            spec((r, D), lambda j: (0, 0)),
            spec((TILE, D), lambda j: (j, 0)),
            spec((1, TILE), lambda j: (0, j)),
        ],
        spec((r, TILE), lambda j: (0, j)),
        struct((r, 3 * D), BF),
        us=13,
        nbytes=r * D * 8 + 3 * D * D * 2,
    )(hidden, w, bias)


def same_image():
    at_row = lax.broadcasted_iota(jnp.int32, (ROWS, ROWS), 0)
    at_col = lax.broadcasted_iota(jnp.int32, (ROWS, ROWS), 1)

    def image(at):
        return (at >= VISIBLE).astype(jnp.int32) + (at >= PAIR).astype(jnp.int32)

    return image(at_row) == image(at_col)


def side_by_side(block):
    left = lax.broadcasted_iota(jnp.int32, (ROWS, 128), 1) < HEAD_DIM
    none = jnp.zeros_like(block)
    return jnp.concatenate([jnp.where(left, block, none), jnp.where(left, none, block)])


def both_heads(stack):
    left = lax.broadcasted_iota(jnp.int32, (ROWS, 128), 1) < HEAD_DIM
    return jnp.where(left, stack[:ROWS], stack[ROWS:])


def pair_of(ref, part, pair):
    return ref[:, part * D + pair * 128 : part * D + (pair + 1) * 128]


def attend_body(triple_ref, mixed_ref, prob_ref):
    keep = same_image()[None]
    for pair in range(HEADS // 2):
        q, k, v = (pair_of(triple_ref, part, pair) for part in range(3))
        scores = dot(side_by_side(k), q, 1, 1).reshape(2, ROWS, ROWS) * HEAD_DIM**-0.5
        scores = jnp.where(keep, scores, -1e30)
        expo = jnp.exp(scores - jnp.max(scores, 1, keepdims=True))
        prob = expo / jnp.sum(expo, 1, keepdims=True)
        prob_ref[0, 2 * pair : 2 * pair + 2] = prob
        low = prob.astype(BF).reshape(2 * ROWS, ROWS)
        mixed_ref[:, pair * 128 : (pair + 1) * 128] = dot(low, side_by_side(v), 0, 0).astype(BF)


def attend(triple):
    groups = triple.shape[0] // ROWS
    return call(
        attend_body,
        (groups,),
        [spec((ROWS, 3 * D), lambda g: (g, 0))],
        [spec((ROWS, D), lambda g: (g, 0)), spec((1, HEADS, ROWS, ROWS), lambda g: (g, 0, 0, 0))],
        [struct((groups * ROWS, D), BF), pltpu.HBM((groups, HEADS, ROWS, ROWS), F32)],
        us=200,
        nbytes=groups * ROWS * (8 * D + HEADS * 512),
    )(triple)


def mix_body(mixed_ref, w_ref, rows_ref, vec_ref, middle_ref, hidden_ref):
    branch = dot(mixed_ref[...], w_ref[...], 1, 0) + vec_row(vec_ref, BIAS_OUT)
    middle = rows_ref[...].astype(F32) + branch
    middle_ref[...] = middle
    normed, _ = stats(middle)
    hidden_ref[...] = (
        normed * vec_row(vec_ref, GAIN_TWO) + vec_row(vec_ref, SHIFT_TWO)
    ).astype(BF)


def row_tile(r):
    return r // 2


def mix(mixed, w, rows, vec):
    r = rows.shape[0]
    m = row_tile(r)
    row = spec((m, D), lambda i: (i, 0))
    return call(
        mix_body,
        (r // m,),
        [row, spec((D, D), lambda i: (0, 0)), row, spec((8, D), lambda i: (0, 0))],
        [row, row],
        [struct((r, D), F32), struct((r, D), BF)],
        us=16,
        nbytes=r * D * 10 + D * D * 2,
    )(mixed, w, rows, vec)


def up_body(hidden_ref, w_ref, bias_ref, active_ref, slope_ref):
    inner = dot(hidden_ref[...], w_ref[...], 1, 0) + bias_ref[...]
    phi = 0.5 * (1.0 + lax.erf(inner * (0.5**0.5)))
    active_ref[...] = (inner * phi).astype(BF)
    slope_ref[...] = phi + inner * (jnp.exp(-0.5 * inner * inner) * 0.3989422804014327)


def up(hidden, w, bias):
    r = hidden.shape[0]
    units = w.shape[1]
    tile = spec((r, TILE), lambda j: (0, j))
    return call(
        up_body,
        (units // TILE,),
        [
            spec((r, D), lambda j: (0, 0)),
            spec((D, TILE), lambda j: (0, j)),
            spec((1, TILE), lambda j: (0, j)),
        ],
        [tile, tile],
        [pltpu.HBM((r, units), BF), pltpu.HBM((r, units), F32)],
        us=0.01,
        nbytes=r * D * 2 + D * units * 2 + r * units * 6,
    )(hidden, w, bias)


def down_body(active_ref, w_ref, vec_ref, middle_ref, out_ref):
    branch = dot(active_ref[...], w_ref[...], 1, 1) + vec_row(vec_ref, BIAS_DOWN)
    out_ref[...] = (middle_ref[...] + branch).astype(BF)


def down(active, w, vec, middle):
    r, units = active.shape
    m = row_tile(r)
    return call(
        down_body,
        (r // m,),
        [
            spec((m, units), lambda i: (i, 0)),
            spec((D, units), lambda i: (0, 0)),
            spec((8, D), lambda i: (0, 0)),
            spec((m, D), lambda i: (i, 0)),
        ],
        spec((m, D), lambda i: (i, 0)),
        struct((r, D), BF),
        us=0.01,
        nbytes=r * units * 2 + D * units * 2 + r * D * 6,
    )(active, w, vec, middle)


def outer_body(left_ref, right_ref, out_ref, sum_ref, turned):
    @pl.when(pl.program_id(0) == 0)
    def _():
        turned[...] = left_ref[...].T

    right = right_ref[...]
    out_ref[...] = dot(turned[...], right, 1, 0).astype(BF)
    sum_ref[...] = jnp.sum(right.astype(F32), 0, keepdims=True)


def outer(left, right):
    r, width = right.shape
    rows = left.shape[1]
    return call(
        outer_body,
        (width // TILE,),
        [spec((r, rows), lambda j: (0, 0)), spec((r, TILE), lambda j: (0, j))],
        [spec((rows, TILE), lambda j: (0, j)), spec((1, TILE), lambda j: (0, j))],
        [struct((rows, width), BF), struct((1, width), F32)],
        [pltpu.VMEM((rows, r), BF)],
        us=0.01,
        nbytes=r * rows * 2 + r * width * 2 + rows * width * 2,
    )(left, right)


def inner_back_body(cot_ref, w_ref, slope_ref, hidden_ref, grad_ref, gw_ref, gb_ref, turned):
    @pl.when(pl.program_id(0) == 0)
    def _():
        turned[...] = hidden_ref[...].T

    grad = (dot(cot_ref[...], w_ref[...], 1, 0) * slope_ref[...]).astype(BF)
    grad_ref[...] = grad
    gw_ref[...] = dot(turned[...], grad, 1, 0).astype(BF)
    gb_ref[...] = jnp.sum(grad.astype(F32), 0, keepdims=True)


def inner_back(cot, w, slope, hidden):
    r, units = slope.shape
    full = spec((r, D), lambda j: (0, 0))
    col = spec((D, TILE), lambda j: (0, j))
    tile = spec((r, TILE), lambda j: (0, j))
    return call(
        inner_back_body,
        (units // TILE,),
        [full, col, tile, full],
        [tile, col, spec((1, TILE), lambda j: (0, j))],
        [pltpu.HBM((r, units), BF), struct((D, units), BF), struct((1, units), F32)],
        [pltpu.VMEM((D, r), BF)],
        us=200,
        nbytes=r * D * 4 + D * units * 4 + r * units * 6,
    )(cot, w, slope, hidden)


def norm_pull(grad, normed, inv, gain):
    scaled = grad * gain
    return inv * (
        scaled
        - jnp.mean(scaled, 1, keepdims=True)
        - normed * jnp.mean(scaled * normed, 1, keepdims=True)
    )


def middle_back_body(
    grad_ref, w_ref, middle_ref, cot_ref, vec_ref, out_ref, branch_ref, gain_sum, shift_sum, out_sum
):
    grad = dot(grad_ref[...], w_ref[...], 1, 1)
    normed, inv = stats(middle_ref[...])
    total = cot_ref[...].astype(F32) + norm_pull(
        grad, normed, inv, vec_row(vec_ref, GAIN_TWO)
    )
    out_ref[...] = total
    branch = total.astype(BF)
    branch_ref[...] = branch
    sums = (
        (gain_sum, jnp.sum(grad * normed, 0, keepdims=True)),
        (shift_sum, jnp.sum(grad, 0, keepdims=True)),
        (out_sum, jnp.sum(branch.astype(F32), 0, keepdims=True)),
    )
    for ref, value in sums:
        add_up(ref, value)


def add_up(ref, value):
    @pl.when(pl.program_id(0) == 0)
    def _():
        ref[...] = value

    @pl.when(pl.program_id(0) != 0)
    def _():
        ref[...] += value


def middle_back(grad, w, middle, cot, vecs):
    r, units = grad.shape
    m = row_tile(r)
    vec = spec((1, D), lambda i: (0, 0))
    row = spec((m, D), lambda i: (i, 0))
    vec_out = struct((1, D), F32)
    return call(
        middle_back_body,
        (r // m,),
        [
            spec((m, units), lambda i: (i, 0)),
            spec((D, units), lambda i: (0, 0)),
            row,
            row,
            spec((8, D), lambda i: (0, 0)),
        ],
        [row, row, vec, vec, vec],
        [struct((r, D), F32), struct((r, D), BF), vec_out, vec_out, vec_out],
        us=200,
        nbytes=r * units * 2 + D * units * 2 + r * D * 12,
    )(grad, w, middle, cot, vecs)


def mixed_back_body(branch_ref, tile_ref, w_ref, mixed_ref, grad_ref, gw_ref, turned):
    @pl.when(pl.program_id(0) == 0)
    def _():
        turned[...] = mixed_ref[...].T

    grad_ref[...] = dot(branch_ref[...], w_ref[...], 1, 1).astype(BF)
    gw_ref[...] = dot(turned[...], tile_ref[...], 1, 0).astype(BF)


def mixed_back(branch, w, mixed):
    r = branch.shape[0]
    full = spec((r, D), lambda j: (0, 0))
    tile = spec((r, TILE), lambda j: (0, j))
    return call(
        mixed_back_body,
        (D // TILE,),
        [full, tile, spec((TILE, D), lambda j: (j, 0)), full],
        [tile, spec((D, TILE), lambda j: (0, j))],
        [struct((r, D), BF), struct((D, D), BF)],
        [pltpu.VMEM((D, r), BF)],
        us=0.01,
        nbytes=r * D * 8 + D * D * 4,
    )(branch, branch, w, mixed)


def attend_back_body(triple_ref, prob_ref, grad_ref, *rest):
    out_ref = rest[-1]
    scale = HEAD_DIM**-0.5
    for pair in range(HEADS // 2):
        q, k, v = (pair_of(triple_ref, part, pair) for part in range(3))
        grad = pair_of(grad_ref, 0, pair)
        prob = prob_ref[0, 2 * pair : 2 * pair + 2]
        grad_prob = dot(side_by_side(v), grad, 1, 1).reshape(2, ROWS, ROWS)
        inside = jnp.sum(grad_prob * prob, 1, keepdims=True)
        grad_scores = (prob * (grad_prob - inside)).astype(BF).reshape(2 * ROWS, ROWS)
        grads = (
            dot(grad_scores, side_by_side(k), 0, 0) * scale,
            both_heads(dot(grad_scores, q, 1, 0)) * scale,
            both_heads(dot(prob.astype(BF).reshape(2 * ROWS, ROWS), grad, 1, 0)),
        )
        for part, value in enumerate(grads):
            out_ref[:, part * D + pair * 128 : part * D + (pair + 1) * 128] = value.astype(BF)


def attend_back(triple, prob, grad, start, stop, partial_out=None):
    wide = spec((ROWS, 3 * D), lambda g: (g + start, 0))
    count = stop - start
    given = [] if partial_out is None else [partial_out]
    return pl.pallas_call(
        attend_back_body,
        out_shape=struct(triple.shape, BF),
        grid_spec=pltpu.PrefetchScalarGridSpec(
            num_scalar_prefetch=0,
            grid=(count,),
            in_specs=[
                wide,
                spec((1, HEADS, ROWS, ROWS), lambda g: (g + start, 0, 0, 0)),
                spec((ROWS, D), lambda g: (g + start, 0)),
            ]
            + [ANY] * len(given),
            out_specs=wide,
        ),
        input_output_aliases={3: 0} if given else {},
        compiler_params=pltpu.CompilerParams(
            dimension_semantics=("arbitrary",), vmem_limit_bytes=24 * MB
        ),
        cost_estimate=pl.CostEstimate(
            flops=FLOPS_PER_US // 100, bytes_accessed=1024, transcendentals=0
        ),
    )(triple, prob, grad, *given)


def qkv_grad_body(grad_ref, hidden_ref, gw_ref, gb_ref):
    grad = grad_ref[...]
    gw_ref[...] = dot(grad.T, hidden_ref[...], 1, 0).astype(BF)
    gb_ref[...] = jnp.sum(grad.astype(F32), 0, keepdims=True)


def qkv_grad(grad, hidden):
    r, width = grad.shape
    return call(
        qkv_grad_body,
        (width // TILE,),
        [spec((r, TILE), lambda j: (0, j)), spec((r, D), lambda j: (0, 0))],
        [spec((TILE, D), lambda j: (j, 0)), spec((1, TILE), lambda j: (0, j))],
        [struct((width, D), BF), struct((1, width), F32)],
        us=200,
        nbytes=r * width * 2 + r * D * 2 + width * D * 2,
    )(grad, hidden)


def first_back_body(grad_ref, w_ref, rows_ref, middle_ref, vec_ref, out_ref, gain_sum, shift_sum):
    grad = dot(grad_ref[...], w_ref[...], 1, 0)
    normed, inv = stats(rows_ref[...].astype(F32))
    pulled = norm_pull(grad, normed, inv, vec_row(vec_ref, GAIN_ONE))
    out_ref[...] = middle_ref[...] + pulled
    add_up(gain_sum, jnp.sum(grad * normed, 0, keepdims=True))
    add_up(shift_sum, jnp.sum(grad, 0, keepdims=True))


def first_back(grad, w, rows, grad_middle, vecs):
    r, width = grad.shape
    m = row_tile(r)
    vec = spec((1, D), lambda i: (0, 0))
    row = spec((m, D), lambda i: (i, 0))
    vec_out = struct((1, D), F32)
    return call(
        first_back_body,
        (r // m,),
        [
            spec((m, width), lambda i: (i, 0)),
            spec((width, D), lambda i: (0, 0)),
            row,
            row,
            spec((8, D), lambda i: (0, 0)),
        ],
        [row, vec, vec],
        [struct((r, D), F32), vec_out, vec_out],
        us=0.01,
        nbytes=r * width * 2 + D * width * 2 + r * D * 10,
    )(grad, w, rows, grad_middle, vecs)


WIDE, NARROW, DP = "wide", "narrow", "dp"


def swap(value, axis, bit):
    size = lax.axis_size(axis)
    return lax.ppermute(value, axis, [(i, i ^ bit) for i in range(size)])


def hold(value, *deps):
    return lax.optimization_barrier((value, deps))[0]


class Pieces:
    def __init__(self, stack, tags):
        self.stack, self.tags = stack, tags

    def fetch(self, axis, bit, *deps):
        move = [bit if axis == name else 0 for name in (WIDE, NARROW, DP)]
        tags = [tuple(a ^ b for a, b in zip(tag, move)) for tag in self.tags]
        return Pieces(swap(hold(self.stack, *deps), axis, bit), tags)

    def after(self, *deps):
        return Pieces(hold(self.stack, *deps), self.tags)

    def rows(self, start, stop):
        return Pieces(self.stack[:, start:stop], self.tags)

    def join(self, *others):
        stack = jnp.concatenate([self.stack] + [o.stack for o in others])
        return Pieces(stack, sum([o.tags for o in others], self.tags))


def first_piece(piece):
    return Pieces(piece[None], [(0, 0, 0)])


def dp_sum(total):
    total = total.astype(F32)
    bit = 2
    while bit < lax.axis_size(DP):
        total = total + swap(total.astype(BF), DP, bit).astype(F32)
        bit *= 2
    return total


def qkv_plan(cols, heads_cols, parts, spots):
    rows = heads_cols // parts

    def plan(w, n, q):
        return [
            (0, spot, (rows, cols), (p * D + w * heads_cols + q * rows, n * cols))
            for p, spot in spots.items()
        ]

    return plan


def out_plan(cols, heads_cols, parts, spot, which=0):
    rows = heads_cols // parts
    return lambda w, n, q: [(which, spot, (rows, cols), (w * heads_cols + q * rows, n * cols))]


def flat_plan(cols, units, rows, base=0):
    return lambda w, n, q: [(0, (0, 0), (rows, units), (n * cols + base + q * rows, w * units))]


def sums_plan(cols, narrow, spot, which):
    return lambda w, n, q: [(which, spot, (16, cols), ((w * narrow + n) * 16, 0))]


def joined(*plans):
    return lambda w, n, q: [move for plan in plans for move in plan(w, n, q)]


def prep_body(cols, at_ref, *refs):
    (qkv_ref, out_ref, up_ref, down_ref), vectors = refs[:4], refs[4:12]
    first_ref, second_ref, up_a_ref, up_b_ref, down_part_ref = refs[12:17]
    held, sem = refs[17:-1], refs[-1]
    core, q = at_ref[2], at_ref[3]

    def block(ref, index, rows, base=0):
        return ref.at[pl.ds(pl.multiple_of(base + index * rows, 16), rows)]

    half = qkv_ref.shape[1] // 2
    ends = [
        (block(qkv_ref.at[0], core, half), first_ref.at[pl.ds(0, half)]),
        (block(out_ref, core, half), first_ref.at[pl.ds(half + 16, half)]),
    ]
    part = half // 2
    ends += [
        (block(qkv_ref.at[1 + p], q, part), second_ref.at[pl.ds(p * part, part)]) for p in range(2)
    ]
    ends.append((block(up_ref, core, up_a_ref.shape[0]), up_a_ref))
    ends.append((block(up_ref, q, up_b_ref.shape[0], up_ref.shape[0] // 2), up_b_ref))
    ends.append((block(down_ref, q, down_part_ref.shape[0]), down_part_ref))
    ends += list(zip(vectors, held))
    copies = [pltpu.make_async_copy(a, b, sem.at[k]) for k, (a, b) in enumerate(ends)]
    for copy in copies:
        copy.start()
    for copy in copies:
        copy.wait()
    lines = [ref[...].astype(F32).reshape(1, -1) for ref in held[:6]]
    both = held[6][...].astype(F32)
    lines.append(jnp.concatenate([both[:1], both[1:]], axis=1))
    wide_line = held[7][...].astype(F32).reshape(1, -1)
    lines += [wide_line[:, k : k + cols] for k in range(0, wide_line.shape[1], cols)]
    lines.append(jnp.zeros((16 - len(lines), cols), F32))
    first_ref[half : half + 16, :] = jnp.concatenate(lines, axis=0).astype(BF)


def prep(at, qkv_t, w_out, w_up, w_down, *vectors):
    cols, half = qkv_t.shape[2], qkv_t.shape[1] // 2
    rows, units = w_up.shape
    shapes = [
        (2 * half + 16, cols),
        (half, cols),
        (rows // 4, units),
        (rows // 8, units),
        (rows // 4, units),
    ]
    return pl.pallas_call(
        partial(prep_body, cols),
        out_shape=[struct(shape, BF) for shape in shapes],
        grid_spec=pltpu.PrefetchScalarGridSpec(
            num_scalar_prefetch=1,
            grid=(1,),
            in_specs=[IN_HBM] * (4 + len(vectors)),
            out_specs=[pl.BlockSpec(memory_space=pltpu.VMEM)] * len(shapes),
            scratch_shapes=[pltpu.VMEM(v.shape, BF) for v in vectors]
            + [pltpu.SemaphoreType.DMA((7 + len(vectors),))],
        ),
        compiler_params=pltpu.CompilerParams(vmem_limit_bytes=8 * MB),
        cost_estimate=pl.CostEstimate(
            flops=FLOPS_PER_US // 100, bytes_accessed=1024, transcendentals=0
        ),
    )(at, *[in_hbm(v) for v in (qkv_t, w_out, w_up, w_down, *vectors)])


def vec_body(wide, narrow, cols, first, tag_lists, at_ref, *refs):
    arrays, (vec_ref, qkv_bias_ref, up_bias_ref, held, sem) = refs[:-5], refs[-5:]
    copies = []
    for array, tags in zip(arrays, tag_lists):
        for k, (dw, dn, _) in enumerate(tags):
            slot = (at_ref[0] ^ dw) * narrow + (at_ref[1] ^ dn)
            source = array.at[k, pl.ds(first, 16)]
            copies.append(pltpu.make_async_copy(source, held.at[slot], sem.at[len(copies)]))
    for copy in copies:
        copy.start()
    for copy in copies:
        copy.wait()
    lines = [held[k].astype(F32) for k in range(wide * narrow)]
    for n in range(narrow):
        vec_ref[:, n * cols : (n + 1) * cols] = lines[n][:8]
    by_wide = [lines[w * narrow] for w in range(wide)]
    half = cols // 2
    q = jnp.concatenate([line[6:7, :half] for line in by_wide], axis=1)
    v = jnp.concatenate([line[6:7, half:] for line in by_wide], axis=1)
    qkv_bias_ref[...] = jnp.concatenate([q, jnp.zeros_like(q), v], axis=1)
    up_bias_ref[...] = jnp.concatenate(
        [line[i : i + 1] for line in by_wide for i in (7, 8)], axis=1
    )


def vectors_of(at, pieces, first, wide, narrow, cols, units):
    vmem = pl.BlockSpec(memory_space=pltpu.VMEM)
    return pl.pallas_call(
        partial(vec_body, wide, narrow, cols, first, [p.tags for p in pieces]),
        out_shape=[struct((8, D), F32), struct((1, 3 * D), F32), struct((1, wide * units), F32)],
        grid_spec=pltpu.PrefetchScalarGridSpec(
            num_scalar_prefetch=1,
            grid=(1,),
            in_specs=[ANY] * len(pieces),
            out_specs=[vmem] * 3,
            scratch_shapes=[
                pltpu.VMEM((wide * narrow, 16, cols), BF),
                pltpu.SemaphoreType.DMA((wide * narrow,)),
            ],
        ),
        compiler_params=pltpu.CompilerParams(vmem_limit_bytes=8 * MB),
        cost_estimate=pl.CostEstimate(flops=FLOPS_PER_US // 100, bytes_accessed=1024, transcendentals=0),
    )(at, *[p.stack for p in pieces])


def pack_body(*refs):
    out = refs[-1]
    at = 0
    for ref in refs[:-1]:
        for k in range(0, ref.shape[1], D):
            out[at : at + 1, :] = ref[:, k : k + D]
            at += 1
    if at < out.shape[0]:
        out[at:, :] = jnp.zeros((out.shape[0] - at, D), F32)


def pack(*rows):
    count = -(-sum(r.shape[1] for r in rows) // (8 * D)) * 8
    vmem = pl.BlockSpec(memory_space=pltpu.VMEM)
    return pl.pallas_call(
        pack_body,
        out_shape=struct((count, D), F32),
        in_specs=[vmem] * len(rows),
        out_specs=vmem,
        compiler_params=pltpu.CompilerParams(vmem_limit_bytes=8 * MB),
        cost_estimate=pl.CostEstimate(flops=FLOPS_PER_US // 100, bytes_accessed=1024, transcendentals=0),
    )(*rows)


ANY = pl.BlockSpec(memory_space=pl.ANY)
IN_HBM = pl.BlockSpec(memory_space=pltpu.HBM)


CORE, DP_INDEX = 2, 3


def owner_sums_body(wide, narrow, cols, *refs):
    out = refs[-1]
    narrow_refs, qkv_ref, up_ref = refs[:6], refs[6], refs[7]
    part, units = D // wide, up_ref.shape[1] // wide
    for w in range(wide):
        for n in range(narrow):
            lines = [ref[:, n * cols : (n + 1) * cols] for ref in narrow_refs]
            lines.append(
                jnp.concatenate(
                    [qkv_ref[:, p * D + w * part : p * D + (w + 1) * part] for p in (0, 2)], axis=1
                )
            )
            lines += [
                up_ref[:, w * units + k : w * units + k + cols] for k in range(0, units, cols)
            ]
            lines.append(jnp.zeros((16 - len(lines), cols), F32))
            at = (w * narrow + n) * 16
            out[at : at + 16, :] = jnp.concatenate(lines, axis=0).astype(BF)


def owner_sums(wide, narrow, cols, *rows):
    vmem = pl.BlockSpec(memory_space=pltpu.VMEM)
    return pl.pallas_call(
        partial(owner_sums_body, wide, narrow, cols),
        out_shape=struct((wide * narrow * 16, cols), BF),
        in_specs=[vmem] * len(rows),
        out_specs=vmem,
        compiler_params=pltpu.CompilerParams(vmem_limit_bytes=8 * MB),
        cost_estimate=pl.CostEstimate(
            flops=FLOPS_PER_US // 100, bytes_accessed=1024, transcendentals=0
        ),
    )(*rows)


def build_body(plans, tag_lists, inverse, parts_by, at_ref, *refs):
    refs, sem = refs[:-1], refs[-1]
    count = len(tag_lists)
    wholes, arrays = (refs[:-count], refs[-count:]) if inverse else (refs[count:], refs[:count])
    copies = []
    for array, tags, plan, by in zip(arrays, tag_lists, plans, parts_by):
        for k, (dw, dn, dq) in enumerate(tags):
            w, n, q = at_ref[0] ^ dw, at_ref[1] ^ dn, at_ref[by] ^ dq
            for which, (at_row, at_lane), (rows, lanes), (row, lane) in plan(w, n, q):
                piece = array.at[k, pl.ds(at_row, rows), pl.ds(at_lane, lanes)]
                whole = wholes[which].at[
                    pl.ds(pl.multiple_of(row, 16), rows), pl.ds(pl.multiple_of(lane, 128), lanes)
                ]
                ends = (whole, piece) if inverse else (piece, whole)
                copies.append(pltpu.make_async_copy(*ends, sem.at[len(copies)]))
    for copy in copies:
        copy.start()
    for copy in copies:
        copy.wait()


def move_pieces(at, arrays, plans, tag_lists, inverse, parts_by, shapes):
    moves = sum(len(tags) * len(plan(0, 0, 0)) for tags, plan in zip(tag_lists, plans))
    return pl.pallas_call(
        partial(build_body, plans, tag_lists, inverse, parts_by),
        out_shape=[struct(shape, BF) for shape in shapes],
        grid_spec=pltpu.PrefetchScalarGridSpec(
            num_scalar_prefetch=1,
            grid=(1,),
            in_specs=[ANY] * len(arrays),
            out_specs=[ANY] * len(shapes),
            scratch_shapes=[pltpu.SemaphoreType.DMA((moves,))],
        ),
        compiler_params=pltpu.CompilerParams(vmem_limit_bytes=4 * MB),
        cost_estimate=pl.CostEstimate(
            flops=FLOPS_PER_US // 100, bytes_accessed=1024, transcendentals=0
        ),
    )(at, *arrays)


CORE, DP_INDEX = 2, 3


def build_weights(at, shape, *groups):
    lists = [(p, plan, by) for pieces, plan, by in groups for p in pieces]
    arrays, tags = [p.stack for p, _, _ in lists], [p.tags for p, _, _ in lists]
    plans, parts_by = [plan for _, plan, _ in lists], [by for _, _, by in lists]
    return move_pieces(at, arrays, plans, tags, False, parts_by, [shape])[0]


def cut_grads(at, grads, plan, tags, shape, part_at=CORE, split=False):
    half = len(tags) // 2
    some = (tags[:half], tags[half:]) if split else (tags,)
    tag_lists = [[(w, n, q ^ dc) for w, n, q in part] for dc in range(2) for part in some]
    shapes = [(len(part),) + shape for part in tag_lists]
    count = len(tag_lists)
    out = move_pieces(
        at, grads, [plan] * count, tag_lists, True, [part_at] * count, shapes
    )
    return (out[:2], out[2:]) if split else out


def fence_body(x_ref, out_ref):
    out_ref[...] = x_ref[...]


def fence(token, us=200):
    vmem = pl.BlockSpec(memory_space=pltpu.VMEM)
    return pl.pallas_call(
        fence_body,
        out_shape=struct(token.shape, token.dtype),
        in_specs=[vmem],
        out_specs=vmem,
        compiler_params=pltpu.CompilerParams(vmem_limit_bytes=MB, has_side_effects=True),
        cost_estimate=pl.CostEstimate(
            flops=us * FLOPS_PER_US, bytes_accessed=1024, transcendentals=0
        ),
    )(token)


class Chain:
    def __init__(self, *args, **options):
        self.keep, self.send = cut_grads(*args, **options)

    def go(self, axis, bit):
        if isinstance(self.send, (list, tuple)):
            self.got = [swap(part, axis, bit) for part in self.send]
        else:
            self.got = swap(self.send, axis, bit)

    def fold(self, *deps):
        self.keep, self.send = halves_summed(self.keep, hold(self.got, *deps))

    def spread(self, *deps):
        got = hold(self.got, *deps)
        order = (0, 2, 1, 3)
        total = [k.astype(F32) + g.astype(F32) for k, g in zip(self.keep, got)]
        self.keep = total[0]
        self.send = [total[order.index(bit)].astype(BF) for bit in range(1, len(total))]
        self.got = [swap(piece, WIDE, bit) for bit, piece in enumerate(self.send, 1)]

    def all_of(self, *deps):
        total = self.keep
        for got in hold(self.got, *deps):
            total = total + got.astype(F32)
        return total

    def total(self, *deps):
        return self.keep[0].astype(F32) + hold(self.got, *deps)[0].astype(F32)


def doubled(value, bit, index):
    other = swap(value, DP, bit)
    return jnp.where(index == 0, jnp.stack([value, other]), jnp.stack([other, value]))


def halves_summed(kept, got):
    def halves(stack):
        if isinstance(stack, (list, tuple)):
            return stack
        half = stack.shape[0] // 2
        return stack[:half], stack[half:]

    first, second = [a.astype(F32) + b.astype(F32) for a, b in zip(halves(kept), halves(got))]
    return first, second.astype(BF)


def core_half(at, shard):
    rows = shard.shape[0] // 2
    return lax.dynamic_slice_in_dim(shard, at[2] * rows, rows, axis=0)


def quarter(at, shard):
    rows = shard.shape[0] // 4
    return lax.dynamic_slice_in_dim(shard, at[3] * rows, rows, axis=0)


def to_rows(blocks, narrow):
    got = lax.all_to_all(blocks, "narrow", 0, 0, tiled=True)
    return jnp.concatenate([got[n] for n in range(narrow)], axis=1)


def from_rows(rows, narrow):
    cols = rows.shape[1] // narrow
    blocks = jnp.stack([rows[:, n * cols : (n + 1) * cols] for n in range(narrow)])
    got = lax.all_to_all(blocks, "narrow", 0, 0, tiled=True)
    return got.reshape(-1, cols)


def gather_weight(shard, wide, narrow):
    got = lax.all_gather(shard.reshape(-1, 128), ("wide", "narrow"), axis=0, tiled=True)
    return got.reshape((wide, narrow) + shard.shape)


def scatter_grad(blocks):
    shape = blocks.shape[2:]
    got = lax.psum_scatter(
        blocks.reshape(-1, 128), ("wide", "narrow"), scatter_dimension=0, tiled=True
    )
    return lax.psum(got.astype(F32), "dp").reshape(shape)


def on_device(
    wide,
    narrow,
    patches,
    visible,
    w_qkv,
    b_qv,
    w_out,
    b_out,
    w_up,
    b_up,
    w_down,
    b_down,
    gain_one,
    shift_one,
    gain_two,
    shift_two,
    cotangent,
):
    images = visible.shape[0]
    pairs = images // 2
    cols = w_qkv.shape[0]
    heads_cols = w_qkv.shape[2]
    units = w_up.shape[1]
    swaps = cols % 128 == 0 and narrow == 2 and wide == 4 and lax.axis_size(DP) == 4
    swaps = swaps and pairs % 2 == 0

    at = jnp.stack(
        [
            lax.axis_index("wide"),
            lax.axis_index("narrow"),
            lax.axis_index("dp") % 2,
            lax.axis_index("dp"),
        ]
    ).astype(jnp.int32)

    index = (visible.reshape(pairs, 2, VISIBLE) + jnp.array([0, PATCHES])[None, :, None]).reshape(
        pairs, PAIR
    )
    index = jnp.pad(index, ((0, 0), (0, ROWS - PAIR)), constant_values=-1)[:, :, None]

    w_qkv_t = w_qkv.transpose(1, 2, 0)
    if swaps:
        pieces = prep(
            at,
            w_qkv_t,
            w_out,
            w_up,
            w_down,
            gain_one,
            shift_one,
            gain_two,
            shift_two,
            b_out,
            b_down,
            b_qv,
            b_up,
        )
        a_p, b_p, u_p, v_p, d_p = [first_piece(piece) for piece in pieces]

        def part_of(whole, side):
            return lax.dynamic_slice_in_dim(whole, side * cols, cols, axis=1)

        def join_cols(keep, got):
            return jnp.where(
                at[1] == 0,
                jnp.concatenate([keep, got], axis=1),
                jnp.concatenate([got, keep], axis=1),
            )

        mine, theirs = at[1], 1 - at[1]
        whole = (D, wide * units)

        b_z = [b_p.fetch(WIDE, bit) for bit in (1, 2, 3)]
        a_x, d_x = a_p.fetch(NARROW, 1), d_p.fetch(NARROW, 1)
        token = fence(hold(at, a_p.stack, b_p.stack, d_p.stack))
        a_p, d_p = a_p.join(a_x.after(token)), d_p.join(d_x.after(token))
        b_p = b_p.join(*[p.after(token) for p in b_z])

        b_x, a_z = b_p.fetch(NARROW, 1), a_p.fetch(WIDE, 2)
        rows_out = pick_rows(
            hold(at, a_p.stack, b_p.stack, d_p.stack), patches, index, cols
        )
        own = rows_out.shape[0] // 2
        rows_send = rows_out[:own]
        a_p, b_p = a_p.join(a_z.after(rows_send)), b_p.join(b_x.after(rows_send))

        b_y, a_z = b_p.fetch(DP, 2), a_p.fetch(WIDE, 1)
        v_z = v_p.fetch(WIDE, 2, rows_send)
        rows_got = swap(rows_send, NARROW, 1)
        cot_out = cot_rows(hold(at, rows_send, a_p.stack, b_p.stack), cotangent, pairs, cols)
        a_p, b_p = a_p.join(a_z.after(cot_out)), b_p.join(b_y.after(cot_out))
        v_p = v_p.join(v_z.after(cot_out))
        rows = join_cols(rows_out[own:], hold(rows_got, cot_out))

        started = [a_p.stack, b_p.stack, v_p.stack, rows]
        a_c, b_c = a_p.fetch(DP, 1, *started), b_p.fetch(DP, 1, *started)
        u_z, v_z = u_p.fetch(WIDE, 2, *started), v_p.fetch(WIDE, 1, *started)
        cot_send = hold(cot_out[:own], *started)
        cot_got = swap(cot_send, NARROW, 1)
        half = heads_cols // 2
        vecs, bias_qkv, bias_up = vectors_of(at, [a_p], half, wide, narrow, cols, units)
        hidden_one = norm(hold(rows, *started, cot_send), vecs)
        u_p, v_p = u_p.join(u_z.after(hidden_one)), v_p.join(v_z.after(hidden_one))
        a_c, b_c = a_c.after(hidden_one), b_c.after(hidden_one)

        u_z, v_x = u_p.fetch(WIDE, 1), v_p.fetch(NARROW, 1)
        started = [u_p.stack, v_p.stack]
        d_z = d_p.fetch(WIDE, 2, *started)
        part = heads_cols // 4
        qkv_t = build_weights(
            at,
            (3 * D, D),
            ([a_p, a_c], qkv_plan(cols, heads_cols, 2, {0: (0, 0)}), CORE),
            (
                [b_p, b_c],
                qkv_plan(cols, heads_cols, 4, {1: (0, 0), 2: (part, 0)}),
                DP_INDEX,
            ),
        )
        out_w = build_weights(
            at, (D, D), ([a_p, a_c], out_plan(cols, heads_cols, 2, (half + 16, 0)), CORE)
        )
        triple = qkv(hold(hidden_one, *started), qkv_t, bias_qkv)
        u_p, v_p = u_p.join(u_z.after(triple)), v_p.join(v_x.after(triple))
        d_p = d_p.join(d_z.after(triple))
        cot = join_cols(cot_out[own:], hold(cot_got, triple))

        u_x, v_y, d_z = u_p.fetch(NARROW, 1), v_p.fetch(DP, 2), d_p.fetch(WIDE, 1)
        mixed, prob = attend(hold(triple, u_p.stack, v_p.stack, d_p.stack, cot))
        d_p = d_p.join(d_z.after(mixed))
        u_x, v_y = u_x.after(mixed), v_y.after(mixed)

        u_all, v_all = [u_p, u_x], [v_p, v_y]
        started = [d_p.stack, u_x.stack, v_y.stack]
        d_y = d_p.fetch(DP, 2)
        u_c = [p.fetch(DP, 1, *started) for p in u_all]
        v_c = [p.fetch(DP, 1, *started) for p in v_all]
        middle, hidden_two = mix(hold(mixed, *started), out_w, rows, vecs)
        half_flat = flat_plan(cols, units, cols // 2)
        part_flat = flat_plan(cols, units, cols // 4)
        up_w = build_weights(
            at,
            whole,
            (u_all + [p.after(hidden_two) for p in u_c], part_flat, CORE),
            (
                v_all + [p.after(hidden_two) for p in v_c],
                flat_plan(cols, units, cols // 8, cols // 2),
                DP_INDEX,
            ),
        )
        active, slope = up(hidden_two, up_w, bias_up)

        x_first = [(w, n, 0) for n in range(2) for w in (0, 2, 1, 3)]
        y_first = [(w, n, dy) for dy in (0, 2) for n in range(2) for w in (0, 2, 1, 3)]
        gw_down, _ = outer(cot, in_hbm(active))
        gb_down = jnp.sum(cot, 0, dtype=F32)[None]
        d_y = d_y.after(gw_down)
        d_c = [p.fetch(DP, 1, d_y.stack) for p in (d_p, d_y)]
        g_d = Chain(
            at,
            [hold(gw_down, d_y.stack)],
            half_flat,
            x_first,
            (cols // 2, units),
            split=True,
        )
        g_d.go(DP, 1)
        d_c = [p.after(*g_d.send) for p in d_c]
        down_w = build_weights(at, whole, ([d_p, d_y] + d_c, part_flat, DP_INDEX))
        g_d.fold(down_w)
        g_d.go(NARROW, 1)
        grad_inner, gw_up, gb_up = inner_back(
            cot, hold(down_w, g_d.send), in_hbm(slope), hidden_two
        )

        result = down(hold(in_hbm(active), grad_inner), down_w, vecs, middle)
        g_u = Chain(
            at,
            [hold(gw_up, result)],
            part_flat,
            y_first,
            (cols // 4, units),
            DP_INDEX,
            split=True,
        )
        g_u.go(DP, 1)
        g_d.fold(*g_u.send)
        g_d.go(WIDE, 1)
        g_u.fold(g_d.send)
        g_u.go(DP, 2)
        grad_middle, branch, gg_two, gs_two, gb_out = middle_back(
            hold(grad_inner, g_d.send, g_u.send), up_w, middle, cot, vecs
        )
        grad_mixed, gw_out = mixed_back(branch, out_w, mixed)

        g_d.fold(grad_mixed)
        g_d.go(WIDE, 2)
        result_send = hold(part_of(result, theirs), grad_mixed)
        result_got = swap(result_send, NARROW, 1)
        groups = rows.shape[0] // ROWS
        grad_triple = attend_back(
            triple, in_hbm(prob), hold(grad_mixed, g_d.send, result_send), 0, groups
        )
        grad_rows, gg_one, gs_one = first_back(grad_triple, qkv_t, rows, grad_middle, vecs)

        d_sum = g_d.total(grad_rows)
        d_got = swap(d_sum.astype(BF), DP, 2)
        g_u.fold(grad_rows)
        g_u.go(NARROW, 1)
        result_got = hold(result_got, grad_rows)
        gw_qkv, gb_qkv = qkv_grad(hold(grad_triple, d_sum, g_u.send, result_got), hidden_one)
        sums = owner_sums(
            wide,
            narrow,
            cols,
            gg_one,
            gs_one,
            gg_two,
            gs_two,
            gb_out,
            gb_down,
            gb_qkv,
            gb_up,
        )

        part = heads_cols // 4
        g_q = Chain(
            at,
            [gw_qkv],
            qkv_plan(cols, heads_cols, 4, {p: (p * part, 0) for p in range(3)}),
            y_first,
            (3 * part, cols),
            DP_INDEX,
        )
        g_q.go(DP, 1)
        rest_plan = joined(
            out_plan(cols, heads_cols, 2, (0, 0), 0), sums_plan(cols, narrow, (half, 0), 1)
        )
        g_r = Chain(at, [gw_out, sums], rest_plan, x_first, (half + 16, cols))
        g_r.go(DP, 1)
        d_sum = d_sum + hold(d_got, g_r.send).astype(F32)
        d_got = swap(d_sum, DP, 1)
        g_u.fold(g_r.send)
        g_u.go(WIDE, 1)
        rows_send = hold(part_of(grad_rows, theirs), g_r.send).astype(BF)
        rows_back = swap(rows_send, NARROW, 1)
        keep = hold(part_of(result, mine), g_q.send, d_sum, g_u.send, rows_send)
        block_output = flat_rows(at, keep, result_got, cols)

        g_q.fold(block_output)
        g_q.go(DP, 2)
        g_r.fold(block_output)
        g_r.go(NARROW, 1)
        g_u.fold(g_q.send, g_r.send)
        g_u.go(WIDE, 2)
        rows_back = hold(rows_back, g_u.send)
        grad_patches = put_rows(at, part_of(grad_rows, mine), rows_back, index, cols)

        def in_order(value, other, index):
            return jnp.where(index == 0, jnp.stack([value, other]), jnp.stack([other, value]))

        g_q.fold(grad_patches)
        g_q.go(NARROW, 1)
        g_r.spread(grad_patches)
        u_sum = g_u.total(g_q.send, *g_r.send)
        token = fence(hold(vecs, g_q.send, u_sum, *g_r.send))
        g_q.spread(token)
        r_sum = g_r.all_of(token)
        r_got = swap(r_sum.astype(BF), DP, 2)
        u_got = swap(u_sum.astype(BF), DP, 2)
        token = fence(hold(token, r_sum, u_sum, *g_q.send))
        q_sum = g_q.all_of(token)
        q_got = [swap(q_sum.astype(BF), DP, bit) for bit in (1, 2, 3)]
        r_sum = r_sum + hold(r_got, token).astype(F32)
        r_got = swap(r_sum[:half], DP, 1)
        u_sum = in_order(u_sum, hold(u_got, token).astype(F32), at[3] // 2)
        u_got = swap(u_sum, DP, 1)
        g_down = in_order(d_sum, d_got, at[2]).reshape(cols, units)
        g_up = in_order(u_sum, u_got, at[2]).transpose(1, 0, 2, 3).reshape(cols, units)
        q_got = [got.astype(F32) for got in q_got]
        pairs_of = [in_order(q_sum, q_got[0], at[2]), in_order(q_got[1], q_got[2], at[2])]
        q_sum = in_order(*pairs_of, at[3] // 2).reshape(4, 3, part, cols)
        g_out = in_order(r_sum[:half], r_got, at[2]).reshape(heads_cols, cols)
        g_qkv = q_sum.transpose(3, 1, 0, 2).reshape(cols, 3, heads_cols)
        grad_patches = grad_patches.reshape(1, -1)
        lines = r_sum[half:]
        vector_grads = [lines[i] for i in range(6)]
        g_bqv = lines[6].reshape(2, heads_cols)
        g_bup = lines[7:9].reshape(units)
    else:
        table = patches.reshape(images, PATCHES, cols)
        rows_mine = jnp.take_along_axis(table, visible[:, :, None], axis=1)
        rows_mine = jnp.pad(
            rows_mine.reshape(pairs, PAIR, cols), ((0, 0), (0, ROWS - PAIR), (0, 0))
        )
        cot_mine = jnp.pad(
            cotangent.reshape(pairs, PAIR, cols), ((0, 0), (0, ROWS - PAIR), (0, 0))
        )
        rows = to_rows(rows_mine.reshape(narrow, -1, cols), narrow)
        cot = to_rows(cot_mine.reshape(narrow, -1, cols), narrow)
        vec = jnp.concatenate(
            [gain_one, shift_one, gain_two, shift_two, b_out, b_down, b_qv.reshape(-1), b_up]
        )
        vec = lax.all_gather(vec, ("wide", "narrow"), axis=0, tiled=False).astype(F32)
        qkv_t = gather_weight(w_qkv_t, wide, narrow)
        qkv_t = qkv_t.transpose(2, 0, 3, 1, 4).reshape(3 * D, D)
        out_w = gather_weight(w_out, wide, narrow).transpose(0, 2, 1, 3).reshape(D, D)
        up_w = gather_weight(w_up, wide, narrow).transpose(1, 2, 0, 3).reshape(D, -1)
        down_w = gather_weight(w_down, wide, narrow).transpose(1, 2, 0, 3).reshape(D, -1)
        vec = vec.reshape(wide, narrow, -1)
        vecs = vec[0, :, : 6 * cols].reshape(narrow, 6, cols).transpose(1, 0, 2).reshape(6, D)
        vecs = jnp.pad(vecs, ((0, 2), (0, 0)))
        by_wide = vec[:, 0, 6 * cols :]
        bias_q = by_wide[:, :heads_cols].reshape(1, D)
        bias_v = by_wide[:, heads_cols : 2 * heads_cols].reshape(1, D)
        bias_qkv = jnp.concatenate([bias_q, jnp.zeros((1, D), F32), bias_v], axis=1)
        bias_up = by_wide[:, 2 * heads_cols :].reshape(1, -1)

        hidden_one = norm(rows, vecs)
        triple = qkv(hidden_one, qkv_t, bias_qkv)
        mixed, prob = attend(triple)
        middle, hidden_two = mix(mixed, out_w, rows, vecs)
        active, slope = up(hidden_two, up_w, bias_up)
        result = down(active, down_w, vecs, middle)
        gw_down, _ = outer(cot, active)
        gb_down = jnp.sum(cot, 0, dtype=F32)[None]
        grad_inner, gw_up, gb_up = inner_back(cot, down_w, slope, hidden_two)
        grad_middle, branch, gg_two, gs_two, gb_out = middle_back(
            grad_inner, up_w, middle, cot, vecs
        )
        grad_mixed, gw_out = mixed_back(branch, out_w, mixed)
        grad_triple = attend_back(triple, prob, grad_mixed, 0, rows.shape[0] // ROWS)
        gw_qkv, gb_qkv = qkv_grad(grad_triple, hidden_one)
        grad_rows, gg_one, gs_one = first_back(grad_triple, qkv_t, rows, grad_middle, vecs)
        sums = pack(gg_one, gs_one, gg_two, gs_two, gb_out, gb_down, gb_qkv, gb_up)

        result = from_rows(result, narrow)
        grad_rows = from_rows(grad_rows, narrow)
        block_output = result.reshape(pairs, ROWS, cols)[:, :PAIR].reshape(1, -1)
        grad_rows = grad_rows.reshape(pairs, ROWS, cols)[:, :PAIR].reshape(images, VISIBLE, cols)
        grad_patches = (
            jnp.zeros((images, PATCHES, cols), F32)
            .at[jnp.arange(images)[:, None], visible]
            .set(grad_rows)
            .reshape(1, -1)
        )
        g_down = scatter_grad(gw_down.reshape(narrow, cols, wide, units).transpose(2, 0, 1, 3))
        g_up = scatter_grad(gw_up.reshape(narrow, cols, wide, units).transpose(2, 0, 1, 3))
        g_out = scatter_grad(gw_out.reshape(wide, heads_cols, narrow, cols).transpose(0, 2, 1, 3))
        g_qkv = scatter_grad(
            gw_qkv.reshape(3, wide, heads_cols, narrow, cols).transpose(1, 3, 0, 2, 4)
        )
        g_qkv = g_qkv.transpose(2, 0, 1)
        sums = lax.psum(sums, ("dp", "wide", "narrow"))
        sums = sums.reshape(-1)
        vector_grads = [
            lax.dynamic_slice_in_dim(sums, i * D + at[1] * cols, cols) for i in range(6)
        ]
        g_bqv = jnp.stack(
            [
                lax.dynamic_slice_in_dim(sums, (6 + i) * D + at[0] * heads_cols, heads_cols)
                for i in (0, 2)
            ]
        )
        g_bup = lax.dynamic_slice_in_dim(sums, 9 * D + at[0] * units, units)

    return (
        block_output,
        grad_patches,
        g_qkv,
        g_bqv,
        g_out,
        vector_grads[4],
        g_up,
        g_bup,
        g_down,
        vector_grads[5],
        vector_grads[0],
        vector_grads[1],
        vector_grads[2],
        vector_grads[3],
    )


def solution(mesh):
    in_specs = (
        P("narrow", ("dp", "wide")),
        P(("dp", "wide"), None),
        P("narrow", None, "wide"),
        P(None, "wide"),
        P("wide", "narrow"),
        P("narrow"),
        P("narrow", "wide"),
        P("wide"),
        P("narrow", "wide"),
        P("narrow"),
        P("narrow"),
        P("narrow"),
        P("narrow"),
        P("narrow"),
        P("narrow", ("dp", "wide")),
    )
    out_specs = (
        P("narrow", ("dp", "wide")),
        P("narrow", ("dp", "wide")),
        P("narrow", None, "wide"),
        P(None, "wide"),
        P("wide", "narrow"),
        P("narrow"),
        P("narrow", "wide"),
        P("wide"),
        P("narrow", "wide"),
        P("narrow"),
        P("narrow"),
        P("narrow"),
        P("narrow"),
        P("narrow"),
    )
    body = partial(on_device, mesh.shape["wide"], mesh.shape["narrow"])
    return jax.shard_map(body, mesh=mesh, in_specs=in_specs, out_specs=out_specs, check_vma=False)
```

```python
from functools import partial

import jax
import jax.numpy as jnp
from jax import lax
from jax.experimental import pallas as pl
from jax.experimental.pallas import tpu as pltpu
from jax.sharding import PartitionSpec as P

D = 768
HEAD_DIM = 64
HEADS = 12
PATCHES = 196
VISIBLE = 49
PAIR = 2 * VISIBLE
ROWS = 112
TILE = 768
EPS = 1e-06
BF = jnp.bfloat16
F32 = jnp.float32
MB = 1024 * 1024


def dot(a, b, ca, cb):
    return lax.dot_general(a, b, (((ca,), (cb,)), ((), ())), preferred_element_type=F32)


FLOPS_PER_US = 540000000


def call(body, grid, ins, outs, shapes, scratch=(), prefetch=0, us=1.0, nbytes=0, vmem=32):
    return pl.pallas_call(
        body,
        out_shape=shapes,
        grid_spec=pltpu.PrefetchScalarGridSpec(
            num_scalar_prefetch=prefetch,
            grid=grid,
            in_specs=ins,
            out_specs=outs,
            scratch_shapes=scratch,
        ),
        compiler_params=pltpu.CompilerParams(
            dimension_semantics=("arbitrary",) * len(grid), vmem_limit_bytes=vmem * MB
        ),
        cost_estimate=pl.CostEstimate(
            flops=int(us * FLOPS_PER_US), bytes_accessed=1024, transcendentals=0
        ),
    )


def in_hbm(value):
    return pltpu.with_memory_space_constraint(value, pltpu.HBM)


def spec(shape, index):
    return pl.BlockSpec(shape, index)


def struct(shape, dtype):
    return jax.ShapeDtypeStruct(shape, dtype)


def together(own):
    return next(count for count in (4, 2, 1) if own % count == 0)


def strided(start, count, lanes):
    return [pl.ds(start + k, count, stride=lanes) for k in range(lanes)]


def one_hot(index):
    return (index == lax.broadcasted_iota(jnp.int32, (ROWS, 2 * PATCHES), 1)).astype(BF)


def pick_body(cols, count, at_ref, patch_ref, index_ref, rows_ref, wide_ref):
    lanes = cols // 128
    wide_ref[...] = patch_ref[...].astype(F32).reshape(wide_ref.shape)
    for j in range(count):
        places = strided(j * 2 * PATCHES * lanes, 2 * PATCHES, lanes)
        both = jnp.concatenate([wide_ref[place, :] for place in places], axis=1).astype(BF)
        rows_ref[j * ROWS : (j + 1) * ROWS, :] = dot(one_hot(index_ref[j]), both, 1, 0).astype(BF)


def owner_first_sent(steps):
    own = steps // 2

    def source(i, at):
        return (i // own ^ 1 ^ at[1]) * own + i % own

    return source


def pick_rows(at, patches, index, cols):
    pairs = index.shape[0]
    count = together(pairs // 2)
    width = 2 * PATCHES * cols * count
    source = owner_first_sent(pairs // count)
    return call(
        partial(pick_body, cols, count),
        (pairs // count,),
        [
            spec((1, width), lambda i, at: (0, source(i, at))),
            spec((count, ROWS, 1), lambda i, at: (source(i, at), 0, 0)),
        ],
        spec((count * ROWS, cols), lambda i, at: (i, 0)),
        struct((pairs * ROWS, cols), BF),
        [pltpu.VMEM((width // 128, 128), F32)],
        prefetch=1,
        us=200,
        nbytes=pairs * width * 4,
    )(at, patches, index)


def cot_body(cols, count, at_ref, cot_ref, rows_ref, scr):
    lanes = cols // 128
    scr[...] = cot_ref[...].astype(F32).reshape(scr.shape)
    for j in range(count):
        places = strided(j * PAIR * lanes, PAIR, lanes)
        cot = jnp.concatenate([scr[place, :] for place in places], axis=1)
        rows_ref[j * ROWS : (j + 1) * ROWS, :] = jnp.concatenate(
            [cot, jnp.zeros((ROWS - PAIR, cols), F32)], axis=0
        ).astype(BF)


def cot_rows(at, cotangent, pairs, cols):
    count = together(pairs // 2)
    width = PAIR * cols * count
    source = owner_first_sent(pairs // count)
    return call(
        partial(cot_body, cols, count),
        (pairs // count,),
        [spec((1, width), lambda i, at: (0, source(i, at)))],
        spec((count * ROWS, cols), lambda i, at: (i, 0)),
        struct((pairs * ROWS, cols), BF),
        [pltpu.VMEM((width // 128, 128), F32)],
        prefetch=1,
        us=200,
        nbytes=pairs * width * 4,
    )(at, cotangent)


def own_block(at_ref, keep_ref, got_ref, j):
    own = pl.num_programs(0) // 2
    mine = pl.program_id(0) // own == at_ref[1]
    rows = slice(j * ROWS, (j + 1) * ROWS)
    return jnp.where(mine, keep_ref[rows, :].astype(F32), got_ref[rows, :].astype(F32))


def put_body(cols, count, at_ref, keep_ref, got_ref, index_ref, out_ref):
    lanes = cols // 128
    for j in range(count):
        hit = one_hot(index_ref[j])
        rest = own_block(at_ref, keep_ref, got_ref, j)
        parts = []
        for _ in range(3):
            parts.append(rest.astype(BF))
            rest = rest - parts[-1].astype(F32)
        total = dot(jnp.concatenate([hit] * 3), jnp.concatenate(parts), 0, 0)
        for k, place in enumerate(strided(j * 2 * PATCHES * lanes, 2 * PATCHES, lanes)):
            out_ref[place, :] = total[:, k * 128 : (k + 1) * 128]


def put_rows(at, keep, got, index, cols):
    pairs = index.shape[0]
    count = together(pairs // 2)
    own = pairs // count // 2
    tall = count * 2 * PATCHES * cols // 128
    rows = spec((count * ROWS, cols), lambda i, at: (i % own, 0))
    return call(
        partial(put_body, cols, count),
        (pairs // count,),
        [rows, rows, spec((count, ROWS, 1), lambda i, at: (i, 0, 0))],
        spec((tall, 128), lambda i, at: (i, 0)),
        struct((pairs // count * tall, 128), F32),
        prefetch=1,
        us=200,
        nbytes=pairs * (tall * 512 + ROWS * cols * 4),
    )(at, keep, got, index)


def flat_body(cols, count, at_ref, keep_ref, got_ref, out_ref, scr):
    lanes = cols // 128
    for j in range(count):
        rows = own_block(at_ref, keep_ref, got_ref, j)
        for k, place in enumerate(strided(j * PAIR * lanes, PAIR, lanes)):
            scr[place, :] = rows[:PAIR, k * 128 : (k + 1) * 128]
    out_ref[...] = scr[...].reshape(out_ref.shape).astype(BF)


def flat_rows(at, keep, got, cols):
    pairs = 2 * (keep.shape[0] // ROWS)
    count = together(pairs // 2)
    own = pairs // count // 2
    width = PAIR * cols * count
    rows = spec((count * ROWS, cols), lambda i, at: (i % own, 0))
    return call(
        partial(flat_body, cols, count),
        (pairs // count,),
        [rows, rows],
        spec((1, width), lambda i, at: (0, i)),
        struct((1, pairs // count * width), BF),
        [pltpu.VMEM((width // 128, 128), F32)],
        prefetch=1,
        us=200,
        nbytes=pairs * width * 6,
    )(at, keep, got)


def stats(rows):
    mean = jnp.mean(rows, 1, keepdims=True)
    off = rows - mean
    inv = lax.rsqrt(jnp.mean(off * off, 1, keepdims=True) + EPS)
    return off * inv, inv


GAIN_ONE, SHIFT_ONE, GAIN_TWO, SHIFT_TWO, BIAS_OUT, BIAS_DOWN = range(6)


def vec_row(vec_ref, i):
    return vec_ref[i : i + 1, :]


def norm_body(rows_ref, vec_ref, out_ref):
    normed, _ = stats(rows_ref[...].astype(F32))
    out_ref[...] = (normed * vec_row(vec_ref, GAIN_ONE) + vec_row(vec_ref, SHIFT_ONE)).astype(BF)


def norm(rows, vec):
    r = rows.shape[0]
    return call(
        norm_body,
        (r // ROWS,),
        [spec((ROWS, D), lambda i: (i, 0)), spec((8, D), lambda i: (0, 0))],
        spec((ROWS, D), lambda i: (i, 0)),
        struct((r, D), BF),
        us=200,
        nbytes=r * D * 4,
    )(rows, vec)


def qkv_body(hidden_ref, w_ref, bias_ref, out_ref):
    out_ref[...] = (dot(hidden_ref[...], w_ref[...], 1, 1) + bias_ref[...]).astype(BF)


def qkv(hidden, w, bias):
    r = hidden.shape[0]
    return call(
        qkv_body,
        (3 * D // TILE,),
        [
            spec((r, D), lambda j: (0, 0)),
            spec((TILE, D), lambda j: (j, 0)),
            spec((1, TILE), lambda j: (0, j)),
        ],
        spec((r, TILE), lambda j: (0, j)),
        struct((r, 3 * D), BF),
        us=13,
        nbytes=r * D * 8 + 3 * D * D * 2,
    )(hidden, w, bias)


def same_image():
    at_row = lax.broadcasted_iota(jnp.int32, (ROWS, ROWS), 0)
    at_col = lax.broadcasted_iota(jnp.int32, (ROWS, ROWS), 1)

    def image(at):
        return (at >= VISIBLE).astype(jnp.int32) + (at >= PAIR).astype(jnp.int32)

    return image(at_row) == image(at_col)


def side_by_side(block):
    left = lax.broadcasted_iota(jnp.int32, (ROWS, 128), 1) < HEAD_DIM
    none = jnp.zeros_like(block)
    return jnp.concatenate([jnp.where(left, block, none), jnp.where(left, none, block)])


def both_heads(stack):
    left = lax.broadcasted_iota(jnp.int32, (ROWS, 128), 1) < HEAD_DIM
    return jnp.where(left, stack[:ROWS], stack[ROWS:])


def pair_of(ref, part, pair):
    return ref[:, part * D + pair * 128 : part * D + (pair + 1) * 128]


def attend_body(triple_ref, mixed_ref, prob_ref):
    keep = same_image()[None]
    for pair in range(HEADS // 2):
        q, k, v = (pair_of(triple_ref, part, pair) for part in range(3))
        scores = dot(side_by_side(k), q, 1, 1).reshape(2, ROWS, ROWS) * HEAD_DIM**-0.5
        scores = jnp.where(keep, scores, -1e30)
        expo = jnp.exp(scores - jnp.max(scores, 1, keepdims=True))
        prob = expo / jnp.sum(expo, 1, keepdims=True)
        prob_ref[0, 2 * pair : 2 * pair + 2] = prob
        low = prob.astype(BF).reshape(2 * ROWS, ROWS)
        mixed_ref[:, pair * 128 : (pair + 1) * 128] = dot(low, side_by_side(v), 0, 0).astype(BF)


def attend(triple):
    groups = triple.shape[0] // ROWS
    return call(
        attend_body,
        (groups,),
        [spec((ROWS, 3 * D), lambda g: (g, 0))],
        [spec((ROWS, D), lambda g: (g, 0)), spec((1, HEADS, ROWS, ROWS), lambda g: (g, 0, 0, 0))],
        [struct((groups * ROWS, D), BF), pltpu.HBM((groups, HEADS, ROWS, ROWS), F32)],
        us=200,
        nbytes=groups * ROWS * (8 * D + HEADS * 512),
    )(triple)


def mix_body(mixed_ref, w_ref, rows_ref, vec_ref, middle_ref, hidden_ref):
    branch = dot(mixed_ref[...], w_ref[...], 1, 0) + vec_row(vec_ref, BIAS_OUT)
    middle = rows_ref[...].astype(F32) + branch
    middle_ref[...] = middle
    normed, _ = stats(middle)
    hidden_ref[...] = (
        normed * vec_row(vec_ref, GAIN_TWO) + vec_row(vec_ref, SHIFT_TWO)
    ).astype(BF)


def row_tile(r):
    return r // 2


def mix(mixed, w, rows, vec):
    r = rows.shape[0]
    m = r // 4 if r % 64 == 0 else row_tile(r)
    row = spec((m, D), lambda i: (i, 0))
    return call(
        mix_body,
        (r // m,),
        [row, spec((D, D), lambda i: (0, 0)), row, spec((8, D), lambda i: (0, 0))],
        [row, row],
        [struct((r, D), F32), struct((r, D), BF)],
        us=16,
        nbytes=r * D * 10 + D * D * 2,
    )(mixed, w, rows, vec)


def up_body(hidden_ref, w_ref, bias_ref, active_ref, slope_ref):
    half = hidden_ref.shape[0] // 2

    def step(i, carry):
        rows = pl.ds(pl.multiple_of(i * half, 16), half)
        inner = dot(hidden_ref[rows, :], w_ref[...], 1, 0) + bias_ref[...]
        phi = 0.5 * (1.0 + lax.erf(inner * (0.5**0.5)))
        active_ref[rows, :] = (inner * phi).astype(BF)
        slope_ref[rows, :] = phi + inner * (jnp.exp(-0.5 * inner * inner) * 0.3989422804014327)
        return carry

    lax.fori_loop(0, 2, step, 0)


def up(hidden, w, bias):
    r = hidden.shape[0]
    units = w.shape[1]
    tile = spec((r, TILE), lambda j: (0, j))
    return call(
        up_body,
        (units // TILE,),
        [
            spec((r, D), lambda j: (0, 0)),
            spec((D, TILE), lambda j: (0, j)),
            spec((1, TILE), lambda j: (0, j)),
        ],
        [tile, tile],
        [pltpu.HBM((r, units), BF), pltpu.HBM((r, units), F32)],
        us=0.01,
        nbytes=r * D * 2 + D * units * 2 + r * units * 6,
    )(hidden, w, bias)


def down_body(active_ref, w_ref, vec_ref, middle_ref, out_ref):
    branch = dot(active_ref[...], w_ref[...], 1, 1) + vec_row(vec_ref, BIAS_DOWN)
    out_ref[...] = (middle_ref[...] + branch).astype(BF)


def down(active, w, vec, middle):
    r, units = active.shape
    m = row_tile(r)
    return call(
        down_body,
        (r // m,),
        [
            spec((m, units), lambda i: (i, 0)),
            spec((D, units), lambda i: (0, 0)),
            spec((8, D), lambda i: (0, 0)),
            spec((m, D), lambda i: (i, 0)),
        ],
        spec((m, D), lambda i: (i, 0)),
        struct((r, D), BF),
        us=0.01,
        nbytes=r * units * 2 + D * units * 2 + r * D * 6,
    )(active, w, vec, middle)


def outer_body(left_ref, right_ref, out_ref, turned):
    @pl.when(pl.program_id(0) == 0)
    def _():
        turned[...] = left_ref[...].T

    out_ref[...] = dot(turned[...], right_ref[...], 1, 0).astype(BF)


def outer(left, right):
    r, width = right.shape
    rows = left.shape[1]
    return call(
        outer_body,
        (width // TILE,),
        [spec((r, rows), lambda j: (0, 0)), spec((r, TILE), lambda j: (0, j))],
        spec((rows, TILE), lambda j: (0, j)),
        struct((rows, width), BF),
        [pltpu.VMEM((rows, r), BF)],
        us=0.01,
        nbytes=r * rows * 2 + r * width * 2 + rows * width * 2,
    )(left, right)


def inner_back_body(cot_ref, w_ref, slope_ref, hidden_ref, grad_ref, gw_ref, gb_ref, turned):
    @pl.when(pl.program_id(0) == 0)
    def _():
        turned[...] = hidden_ref[...].T

    grad = (dot(cot_ref[...], w_ref[...], 1, 0) * slope_ref[...]).astype(BF)
    grad_ref[...] = grad
    gw_ref[...] = dot(turned[...], grad, 1, 0).astype(BF)
    gb_ref[...] = jnp.sum(grad.astype(F32), 0, keepdims=True)


def inner_back(cot, w, slope, hidden):
    r, units = slope.shape
    full = spec((r, D), lambda j: (0, 0))
    col = spec((D, TILE), lambda j: (0, j))
    tile = spec((r, TILE), lambda j: (0, j))
    return call(
        inner_back_body,
        (units // TILE,),
        [full, col, tile, full],
        [tile, col, spec((1, TILE), lambda j: (0, j))],
        [pltpu.HBM((r, units), BF), struct((D, units), BF), struct((1, units), F32)],
        [pltpu.VMEM((D, r), BF)],
        us=200,
        nbytes=r * D * 4 + D * units * 4 + r * units * 6,
    )(cot, w, slope, hidden)


def norm_pull(grad, normed, inv, gain):
    scaled = grad * gain
    return inv * (
        scaled
        - jnp.mean(scaled, 1, keepdims=True)
        - normed * jnp.mean(scaled * normed, 1, keepdims=True)
    )


def middle_back_body(
    grad_ref, w_ref, middle_ref, cot_ref, vec_ref, out_ref, branch_ref, gain_sum, shift_sum, out_sum
):
    grad = dot(grad_ref[...], w_ref[...], 1, 1)
    normed, inv = stats(middle_ref[...])
    total = cot_ref[...].astype(F32) + norm_pull(
        grad, normed, inv, vec_row(vec_ref, GAIN_TWO)
    )
    out_ref[...] = total
    branch = total.astype(BF)
    branch_ref[...] = branch
    sums = (
        (gain_sum, jnp.sum(grad * normed, 0, keepdims=True)),
        (shift_sum, jnp.sum(grad, 0, keepdims=True)),
        (out_sum, jnp.sum(branch.astype(F32), 0, keepdims=True)),
    )
    for ref, value in sums:
        add_up(ref, value)


def add_up(ref, value):
    @pl.when(pl.program_id(0) == 0)
    def _():
        ref[...] = value

    @pl.when(pl.program_id(0) != 0)
    def _():
        ref[...] += value


def middle_back(grad, w, middle, cot, vecs):
    r, units = grad.shape
    m = row_tile(r)
    vec = spec((1, D), lambda i: (0, 0))
    row = spec((m, D), lambda i: (i, 0))
    vec_out = struct((1, D), F32)
    return call(
        middle_back_body,
        (r // m,),
        [
            spec((m, units), lambda i: (i, 0)),
            spec((D, units), lambda i: (0, 0)),
            row,
            row,
            spec((8, D), lambda i: (0, 0)),
        ],
        [row, row, vec, vec, vec],
        [struct((r, D), F32), struct((r, D), BF), vec_out, vec_out, vec_out],
        us=200,
        nbytes=r * units * 2 + D * units * 2 + r * D * 12,
    )(grad, w, middle, cot, vecs)


def mixed_back_body(branch_ref, tile_ref, w_ref, mixed_ref, grad_ref, gw_ref, turned):
    @pl.when(pl.program_id(0) == 0)
    def _():
        turned[...] = mixed_ref[...].T

    grad_ref[...] = dot(branch_ref[...], w_ref[...], 1, 1).astype(BF)
    gw_ref[...] = dot(turned[...], tile_ref[...], 1, 0).astype(BF)


def mixed_back(branch, w, mixed):
    r = branch.shape[0]
    full = spec((r, D), lambda j: (0, 0))
    tile = spec((r, TILE), lambda j: (0, j))
    return call(
        mixed_back_body,
        (D // TILE,),
        [full, tile, spec((TILE, D), lambda j: (j, 0)), full],
        [tile, spec((D, TILE), lambda j: (0, j))],
        [struct((r, D), BF), struct((D, D), BF)],
        [pltpu.VMEM((D, r), BF)],
        us=0.01,
        nbytes=r * D * 8 + D * D * 4,
    )(branch, branch, w, mixed)


def attend_back_body(triple_ref, prob_ref, grad_ref, *rest):
    out_ref = rest[-1]
    scale = HEAD_DIM**-0.5
    for pair in range(HEADS // 2):
        q, k, v = (pair_of(triple_ref, part, pair) for part in range(3))
        grad = pair_of(grad_ref, 0, pair)
        prob = prob_ref[0, 2 * pair : 2 * pair + 2]
        grad_prob = dot(side_by_side(v), grad, 1, 1).reshape(2, ROWS, ROWS)
        inside = jnp.sum(grad_prob * prob, 1, keepdims=True)
        grad_scores = (prob * (grad_prob - inside)).astype(BF).reshape(2 * ROWS, ROWS)
        grads = (
            dot(grad_scores, side_by_side(k), 0, 0) * scale,
            both_heads(dot(grad_scores, q, 1, 0)) * scale,
            both_heads(dot(prob.astype(BF).reshape(2 * ROWS, ROWS), grad, 1, 0)),
        )
        for part, value in enumerate(grads):
            out_ref[:, part * D + pair * 128 : part * D + (pair + 1) * 128] = value.astype(BF)


def attend_back(triple, prob, grad, start, stop, partial_out=None):
    wide = spec((ROWS, 3 * D), lambda g: (g + start, 0))
    count = stop - start
    given = [] if partial_out is None else [partial_out]
    return pl.pallas_call(
        attend_back_body,
        out_shape=struct(triple.shape, BF),
        grid_spec=pltpu.PrefetchScalarGridSpec(
            num_scalar_prefetch=0,
            grid=(count,),
            in_specs=[
                wide,
                spec((1, HEADS, ROWS, ROWS), lambda g: (g + start, 0, 0, 0)),
                spec((ROWS, D), lambda g: (g + start, 0)),
            ]
            + [ANY] * len(given),
            out_specs=wide,
        ),
        input_output_aliases={3: 0} if given else {},
        compiler_params=pltpu.CompilerParams(
            dimension_semantics=("arbitrary",), vmem_limit_bytes=24 * MB
        ),
        cost_estimate=pl.CostEstimate(
            flops=FLOPS_PER_US // 100, bytes_accessed=1024, transcendentals=0
        ),
    )(triple, prob, grad, *given)


def qkv_grad_body(grad_ref, hidden_ref, gw_ref, gb_ref):
    grad = grad_ref[...]
    gw_ref[...] = dot(grad.T, hidden_ref[...], 1, 0).astype(BF)
    gb_ref[...] = jnp.sum(grad.astype(F32), 0, keepdims=True)


def qkv_grad(grad, hidden):
    r, width = grad.shape
    return call(
        qkv_grad_body,
        (width // TILE,),
        [spec((r, TILE), lambda j: (0, j)), spec((r, D), lambda j: (0, 0))],
        [spec((TILE, D), lambda j: (j, 0)), spec((1, TILE), lambda j: (0, j))],
        [struct((width, D), BF), struct((1, width), F32)],
        us=200,
        nbytes=r * width * 2 + r * D * 2 + width * D * 2,
    )(grad, hidden)


def first_back_body(grad_ref, w_ref, rows_ref, middle_ref, vec_ref, out_ref, gain_sum, shift_sum):
    grad = dot(grad_ref[...], w_ref[...], 1, 0)
    normed, inv = stats(rows_ref[...].astype(F32))
    pulled = norm_pull(grad, normed, inv, vec_row(vec_ref, GAIN_ONE))
    out_ref[...] = middle_ref[...] + pulled
    add_up(gain_sum, jnp.sum(grad * normed, 0, keepdims=True))
    add_up(shift_sum, jnp.sum(grad, 0, keepdims=True))


def first_back(grad, w, rows, grad_middle, vecs):
    r, width = grad.shape
    m = r // 4 if r % 64 == 0 else row_tile(r)
    vec = spec((1, D), lambda i: (0, 0))
    row = spec((m, D), lambda i: (i, 0))
    vec_out = struct((1, D), F32)
    return call(
        first_back_body,
        (r // m,),
        [
            spec((m, width), lambda i: (i, 0)),
            spec((width, D), lambda i: (0, 0)),
            row,
            row,
            spec((8, D), lambda i: (0, 0)),
        ],
        [row, vec, vec],
        [struct((r, D), F32), vec_out, vec_out],
        us=0.01,
        nbytes=r * width * 2 + D * width * 2 + r * D * 10,
    )(grad, w, rows, grad_middle, vecs)


WIDE, NARROW, DP = "wide", "narrow", "dp"


def swap(value, axis, bit):
    size = lax.axis_size(axis)
    return lax.ppermute(value, axis, [(i, i ^ bit) for i in range(size)])


def hold(value, *deps):
    return lax.optimization_barrier((value, deps))[0]


class Pieces:
    def __init__(self, stack, tags):
        self.stack, self.tags = stack, tags

    def fetch(self, axis, bit, *deps):
        move = [bit if axis == name else 0 for name in (WIDE, NARROW, DP)]
        tags = [tuple(a ^ b for a, b in zip(tag, move)) for tag in self.tags]
        return Pieces(swap(hold(self.stack, *deps), axis, bit), tags)

    def after(self, *deps):
        return Pieces(hold(self.stack, *deps), self.tags)

    def rows(self, start, stop):
        return Pieces(self.stack[:, start:stop], self.tags)

    def join(self, *others):
        stack = jnp.concatenate([self.stack] + [o.stack for o in others])
        return Pieces(stack, sum([o.tags for o in others], self.tags))


def first_piece(piece):
    return Pieces(piece[None], [(0, 0, 0)])


def dp_sum(total):
    total = total.astype(F32)
    bit = 2
    while bit < lax.axis_size(DP):
        total = total + swap(total.astype(BF), DP, bit).astype(F32)
        bit *= 2
    return total


def qkv_plan(cols, heads_cols, parts, spots):
    rows = heads_cols // parts

    def plan(w, n, q):
        return [
            (0, spot, (rows, cols), (p * D + w * heads_cols + q * rows, n * cols))
            for p, spot in spots.items()
        ]

    return plan


def out_plan(cols, heads_cols, parts, spot, which=0):
    rows = heads_cols // parts
    return lambda w, n, q: [(which, spot, (rows, cols), (w * heads_cols + q * rows, n * cols))]


def flat_plan(cols, units, rows, base=0):
    return lambda w, n, q: [(0, (0, 0), (rows, units), (n * cols + base + q * rows, w * units))]


def sums_plan(cols, narrow, spot, which):
    return lambda w, n, q: [(which, spot, (16, cols), ((w * narrow + n) * 16, 0))]


def joined(*plans):
    return lambda w, n, q: [move for plan in plans for move in plan(w, n, q)]


def prep_body(cols, at_ref, *refs):
    (qkv_ref, out_ref, up_ref, down_ref), vectors = refs[:4], refs[4:12]
    first_ref, second_ref, up_a_ref, up_b_ref, down_part_ref = refs[12:17]
    held, sem = refs[17:-1], refs[-1]
    core, q = at_ref[2], at_ref[3]

    def block(ref, index, rows, base=0):
        return ref.at[pl.ds(pl.multiple_of(base + index * rows, 16), rows)]

    half = qkv_ref.shape[1] // 2
    ends = [
        (block(qkv_ref.at[0], core, half), first_ref.at[pl.ds(0, half)]),
        (block(out_ref, core, half), first_ref.at[pl.ds(half + 16, half)]),
    ]
    part = half // 2
    ends += [
        (block(qkv_ref.at[1 + p], q, part), second_ref.at[pl.ds(p * part, part)]) for p in range(2)
    ]
    ends.append((block(up_ref, core, up_a_ref.shape[0]), up_a_ref))
    ends.append((block(up_ref, q, up_b_ref.shape[0], up_ref.shape[0] // 2), up_b_ref))
    ends.append((block(down_ref, q, down_part_ref.shape[0]), down_part_ref))
    ends += list(zip(vectors, held))
    copies = [pltpu.make_async_copy(a, b, sem.at[k]) for k, (a, b) in enumerate(ends)]
    for copy in copies:
        copy.start()
    for copy in copies:
        copy.wait()
    lines = [ref[...].astype(F32).reshape(1, -1) for ref in held[:6]]
    both = held[6][...].astype(F32)
    lines.append(jnp.concatenate([both[:1], both[1:]], axis=1))
    wide_line = held[7][...].astype(F32).reshape(1, -1)
    lines += [wide_line[:, k : k + cols] for k in range(0, wide_line.shape[1], cols)]
    lines.append(jnp.zeros((16 - len(lines), cols), F32))
    first_ref[half : half + 16, :] = jnp.concatenate(lines, axis=0).astype(BF)


def prep(at, qkv_t, w_out, w_up, w_down, *vectors):
    cols, half = qkv_t.shape[2], qkv_t.shape[1] // 2
    rows, units = w_up.shape
    shapes = [
        (2 * half + 16, cols),
        (half, cols),
        (rows // 4, units),
        (rows // 8, units),
        (rows // 4, units),
    ]
    return pl.pallas_call(
        partial(prep_body, cols),
        out_shape=[struct(shape, BF) for shape in shapes],
        grid_spec=pltpu.PrefetchScalarGridSpec(
            num_scalar_prefetch=1,
            grid=(1,),
            in_specs=[IN_HBM] * (4 + len(vectors)),
            out_specs=[pl.BlockSpec(memory_space=pltpu.VMEM)] * len(shapes),
            scratch_shapes=[pltpu.VMEM(v.shape, BF) for v in vectors]
            + [pltpu.SemaphoreType.DMA((7 + len(vectors),))],
        ),
        compiler_params=pltpu.CompilerParams(vmem_limit_bytes=8 * MB),
        cost_estimate=pl.CostEstimate(
            flops=FLOPS_PER_US // 100, bytes_accessed=1024, transcendentals=0
        ),
    )(at, *[in_hbm(v) for v in (qkv_t, w_out, w_up, w_down, *vectors)])


def vec_body(wide, narrow, cols, first, tag_lists, at_ref, *refs):
    arrays, (vec_ref, qkv_bias_ref, up_bias_ref, held, sem) = refs[:-5], refs[-5:]
    copies = []
    for array, tags in zip(arrays, tag_lists):
        for k, (dw, dn, _) in enumerate(tags):
            slot = (at_ref[0] ^ dw) * narrow + (at_ref[1] ^ dn)
            source = array.at[k, pl.ds(first, 16)]
            copies.append(pltpu.make_async_copy(source, held.at[slot], sem.at[len(copies)]))
    for copy in copies:
        copy.start()
    for copy in copies:
        copy.wait()
    lines = [held[k].astype(F32) for k in range(wide * narrow)]
    for n in range(narrow):
        vec_ref[:, n * cols : (n + 1) * cols] = lines[n][:8]
    by_wide = [lines[w * narrow] for w in range(wide)]
    half = cols // 2
    q = jnp.concatenate([line[6:7, :half] for line in by_wide], axis=1)
    v = jnp.concatenate([line[6:7, half:] for line in by_wide], axis=1)
    qkv_bias_ref[...] = jnp.concatenate([q, jnp.zeros_like(q), v], axis=1)
    up_bias_ref[...] = jnp.concatenate(
        [line[i : i + 1] for line in by_wide for i in (7, 8)], axis=1
    )


def vectors_of(at, pieces, first, wide, narrow, cols, units):
    vmem = pl.BlockSpec(memory_space=pltpu.VMEM)
    return pl.pallas_call(
        partial(vec_body, wide, narrow, cols, first, [p.tags for p in pieces]),
        out_shape=[struct((8, D), F32), struct((1, 3 * D), F32), struct((1, wide * units), F32)],
        grid_spec=pltpu.PrefetchScalarGridSpec(
            num_scalar_prefetch=1,
            grid=(1,),
            in_specs=[ANY] * len(pieces),
            out_specs=[vmem] * 3,
            scratch_shapes=[
                pltpu.VMEM((wide * narrow, 16, cols), BF),
                pltpu.SemaphoreType.DMA((wide * narrow,)),
            ],
        ),
        compiler_params=pltpu.CompilerParams(vmem_limit_bytes=8 * MB),
        cost_estimate=pl.CostEstimate(flops=FLOPS_PER_US // 100, bytes_accessed=1024, transcendentals=0),
    )(at, *[p.stack for p in pieces])


def pack_body(*refs):
    out = refs[-1]
    at = 0
    for ref in refs[:-1]:
        for k in range(0, ref.shape[1], D):
            out[at : at + 1, :] = ref[:, k : k + D]
            at += 1
    if at < out.shape[0]:
        out[at:, :] = jnp.zeros((out.shape[0] - at, D), F32)


def pack(*rows):
    count = -(-sum(r.shape[1] for r in rows) // (8 * D)) * 8
    vmem = pl.BlockSpec(memory_space=pltpu.VMEM)
    return pl.pallas_call(
        pack_body,
        out_shape=struct((count, D), F32),
        in_specs=[vmem] * len(rows),
        out_specs=vmem,
        compiler_params=pltpu.CompilerParams(vmem_limit_bytes=8 * MB),
        cost_estimate=pl.CostEstimate(flops=FLOPS_PER_US // 100, bytes_accessed=1024, transcendentals=0),
    )(*rows)


ANY = pl.BlockSpec(memory_space=pl.ANY)
IN_HBM = pl.BlockSpec(memory_space=pltpu.HBM)


CORE, DP_INDEX = 2, 3


def owner_sums_body(wide, narrow, cols, *refs):
    out = refs[-1]
    narrow_refs, qkv_ref, up_ref = refs[:6], refs[6], refs[7]
    part, units = D // wide, up_ref.shape[1] // wide
    for w in range(wide):
        for n in range(narrow):
            lines = [ref[:, n * cols : (n + 1) * cols] for ref in narrow_refs]
            lines.append(
                jnp.concatenate(
                    [qkv_ref[:, p * D + w * part : p * D + (w + 1) * part] for p in (0, 2)], axis=1
                )
            )
            lines += [
                up_ref[:, w * units + k : w * units + k + cols] for k in range(0, units, cols)
            ]
            lines.append(jnp.zeros((16 - len(lines), cols), F32))
            at = (w * narrow + n) * 16
            out[at : at + 16, :] = jnp.concatenate(lines, axis=0).astype(BF)


def owner_sums(wide, narrow, cols, *rows):
    vmem = pl.BlockSpec(memory_space=pltpu.VMEM)
    return pl.pallas_call(
        partial(owner_sums_body, wide, narrow, cols),
        out_shape=struct((wide * narrow * 16, cols), BF),
        in_specs=[vmem] * len(rows),
        out_specs=vmem,
        compiler_params=pltpu.CompilerParams(vmem_limit_bytes=8 * MB),
        cost_estimate=pl.CostEstimate(
            flops=FLOPS_PER_US // 100, bytes_accessed=1024, transcendentals=0
        ),
    )(*rows)


def build_body(plans, counts, inverse, parts_by, at_ref, tag_ref, *refs):
    refs, sem = refs[:-1], refs[-1]
    lists = len(counts)
    wholes, arrays = (refs[:-lists], refs[-lists:]) if inverse else (refs[lists:], refs[:lists])

    def each(act):
        first, slot = 0, 0
        for array, plan, count, by in zip(arrays, plans, counts, parts_by):
            moves = len(plan(0, 0, 0))

            def step(k, carry, array=array, plan=plan, by=by, first=first, slot=slot, moves=moves):
                w, n, q = (
                    at_ref[axis] ^ tag_ref[i, first + k] for i, axis in enumerate((0, 1, by))
                )
                for m, (which, (at_row, at_lane), (rows, lanes), (row, lane)) in enumerate(
                    plan(w, n, q)
                ):
                    piece = array.at[k, pl.ds(at_row, rows), pl.ds(at_lane, lanes)]
                    whole = wholes[which].at[
                        pl.ds(pl.multiple_of(row, 16), rows),
                        pl.ds(pl.multiple_of(lane, 128), lanes),
                    ]
                    ends = (whole, piece) if inverse else (piece, whole)
                    act(pltpu.make_async_copy(*ends, sem.at[slot + k * moves + m]))
                return carry

            lax.fori_loop(0, count, step, 0)
            first, slot = first + count, slot + count * moves

    each(lambda copy: copy.start())
    each(lambda copy: copy.wait())


def move_pieces(at, arrays, plans, tag_lists, inverse, parts_by, shapes):
    counts = [len(tags) for tags in tag_lists]
    moves = sum(count * len(plan(0, 0, 0)) for count, plan in zip(counts, plans))
    table = jnp.array([tag for tags in tag_lists for tag in tags], jnp.int32).T
    return pl.pallas_call(
        partial(build_body, plans, counts, inverse, parts_by),
        out_shape=[struct(shape, BF) for shape in shapes],
        grid_spec=pltpu.PrefetchScalarGridSpec(
            num_scalar_prefetch=2,
            grid=(1,),
            in_specs=[ANY] * len(arrays),
            out_specs=[ANY] * len(shapes),
            scratch_shapes=[pltpu.SemaphoreType.DMA((moves,))],
        ),
        compiler_params=pltpu.CompilerParams(vmem_limit_bytes=4 * MB),
        cost_estimate=pl.CostEstimate(
            flops=FLOPS_PER_US // 100, bytes_accessed=1024, transcendentals=0
        ),
    )(at, table, *arrays)


CORE, DP_INDEX = 2, 3


def owner_sums_body(wide, narrow, cols, *refs):
    out = refs[-1]
    narrow_refs, qkv_ref, up_ref = refs[:6], refs[6], refs[7]
    part, units = D // wide, up_ref.shape[1] // wide
    for w in range(wide):
        for n in range(narrow):
            lines = [ref[:, n * cols : (n + 1) * cols] for ref in narrow_refs]
            lines.append(
                jnp.concatenate(
                    [qkv_ref[:, p * D + w * part : p * D + (w + 1) * part] for p in (0, 2)], axis=1
                )
            )
            lines += [
                up_ref[:, w * units + k : w * units + k + cols] for k in range(0, units, cols)
            ]
            lines.append(jnp.zeros((16 - len(lines), cols), F32))
            at = (w * narrow + n) * 16
            out[at : at + 16, :] = jnp.concatenate(lines, axis=0).astype(BF)


def owner_sums(wide, narrow, cols, *rows):
    vmem = pl.BlockSpec(memory_space=pltpu.VMEM)
    return pl.pallas_call(
        partial(owner_sums_body, wide, narrow, cols),
        out_shape=struct((wide * narrow * 16, cols), BF),
        in_specs=[vmem] * len(rows),
        out_specs=vmem,
        compiler_params=pltpu.CompilerParams(vmem_limit_bytes=8 * MB),
        cost_estimate=pl.CostEstimate(
            flops=FLOPS_PER_US // 100, bytes_accessed=1024, transcendentals=0
        ),
    )(*rows)


def build_body(plans, tag_lists, inverse, parts_by, at_ref, *refs):
    refs, sem = refs[:-1], refs[-1]
    count = len(tag_lists)
    wholes, arrays = (refs[:-count], refs[-count:]) if inverse else (refs[count:], refs[:count])
    copies = []
    for array, tags, plan, by in zip(arrays, tag_lists, plans, parts_by):
        for k, (dw, dn, dq) in enumerate(tags):
            w, n, q = at_ref[0] ^ dw, at_ref[1] ^ dn, at_ref[by] ^ dq
            for which, (at_row, at_lane), (rows, lanes), (row, lane) in plan(w, n, q):
                piece = array.at[k, pl.ds(at_row, rows), pl.ds(at_lane, lanes)]
                whole = wholes[which].at[
                    pl.ds(pl.multiple_of(row, 16), rows), pl.ds(pl.multiple_of(lane, 128), lanes)
                ]
                ends = (whole, piece) if inverse else (piece, whole)
                copies.append(pltpu.make_async_copy(*ends, sem.at[len(copies)]))
    for copy in copies:
        copy.start()
    for copy in copies:
        copy.wait()


def move_pieces(at, arrays, plans, tag_lists, inverse, parts_by, shapes):
    moves = sum(len(tags) * len(plan(0, 0, 0)) for tags, plan in zip(tag_lists, plans))
    return pl.pallas_call(
        partial(build_body, plans, tag_lists, inverse, parts_by),
        out_shape=[struct(shape, BF) for shape in shapes],
        grid_spec=pltpu.PrefetchScalarGridSpec(
            num_scalar_prefetch=1,
            grid=(1,),
            in_specs=[ANY] * len(arrays),
            out_specs=[ANY] * len(shapes),
            scratch_shapes=[pltpu.SemaphoreType.DMA((moves,))],
        ),
        compiler_params=pltpu.CompilerParams(vmem_limit_bytes=4 * MB),
        cost_estimate=pl.CostEstimate(
            flops=FLOPS_PER_US // 100, bytes_accessed=1024, transcendentals=0
        ),
    )(at, *arrays)


CORE, DP_INDEX = 2, 3


def build_weights(at, shape, *groups):
    lists = [(p, plan, by) for pieces, plan, by in groups for p in pieces]
    arrays, tags = [p.stack for p, _, _ in lists], [p.tags for p, _, _ in lists]
    plans, parts_by = [plan for _, plan, _ in lists], [by for _, _, by in lists]
    return move_pieces(at, arrays, plans, tags, False, parts_by, [shape])[0]


def cut_grads(at, grads, plan, tags, shape, part_at=CORE, split=False):
    half = len(tags) // 2
    some = (tags[:half], tags[half:]) if split else (tags,)
    tag_lists = [[(w, n, q ^ dc) for w, n, q in part] for dc in range(2) for part in some]
    shapes = [(len(part),) + shape for part in tag_lists]
    count = len(tag_lists)
    out = move_pieces(
        at, grads, [plan] * count, tag_lists, True, [part_at] * count, shapes
    )
    return (out[:2], out[2:]) if split else out


def fence_body(x_ref, out_ref):
    out_ref[...] = x_ref[...]


def fence(token, us=200):
    vmem = pl.BlockSpec(memory_space=pltpu.VMEM)
    return pl.pallas_call(
        fence_body,
        out_shape=struct(token.shape, token.dtype),
        in_specs=[vmem],
        out_specs=vmem,
        compiler_params=pltpu.CompilerParams(vmem_limit_bytes=MB, has_side_effects=True),
        cost_estimate=pl.CostEstimate(
            flops=us * FLOPS_PER_US, bytes_accessed=1024, transcendentals=0
        ),
    )(token)


class Chain:
    def __init__(self, *args, **options):
        self.keep, self.send = cut_grads(*args, **options)

    def go(self, axis, bit):
        if isinstance(self.send, (list, tuple)):
            self.got = [swap(part, axis, bit) for part in self.send]
        else:
            self.got = swap(self.send, axis, bit)

    def fold(self, *deps):
        self.keep, self.send = halves_summed(self.keep, hold(self.got, *deps))

    def spread(self, *deps):
        got = hold(self.got, *deps)
        order = (0, 2, 1, 3)
        total = [k.astype(F32) + g.astype(F32) for k, g in zip(self.keep, got)]
        self.keep = total[0]
        self.send = [total[order.index(bit)].astype(BF) for bit in range(1, len(total))]
        self.got = [swap(piece, WIDE, bit) for bit, piece in enumerate(self.send, 1)]

    def all_of(self, *deps):
        total = self.keep
        for got in hold(self.got, *deps):
            total = total + got.astype(F32)
        return total

    def total(self, *deps):
        return self.keep[0].astype(F32) + hold(self.got, *deps)[0].astype(F32)


def doubled(value, bit, index):
    other = swap(value, DP, bit)
    return jnp.where(index == 0, jnp.stack([value, other]), jnp.stack([other, value]))


def halves_summed(kept, got):
    def halves(stack):
        if isinstance(stack, (list, tuple)):
            return stack
        half = stack.shape[0] // 2
        return stack[:half], stack[half:]

    first, second = [a.astype(F32) + b.astype(F32) for a, b in zip(halves(kept), halves(got))]
    return first, second.astype(BF)


def core_half(at, shard):
    rows = shard.shape[0] // 2
    return lax.dynamic_slice_in_dim(shard, at[2] * rows, rows, axis=0)


def quarter(at, shard):
    rows = shard.shape[0] // 4
    return lax.dynamic_slice_in_dim(shard, at[3] * rows, rows, axis=0)


def to_rows(blocks, narrow):
    got = lax.all_to_all(blocks, "narrow", 0, 0, tiled=True)
    return jnp.concatenate([got[n] for n in range(narrow)], axis=1)


def from_rows(rows, narrow):
    cols = rows.shape[1] // narrow
    blocks = jnp.stack([rows[:, n * cols : (n + 1) * cols] for n in range(narrow)])
    got = lax.all_to_all(blocks, "narrow", 0, 0, tiled=True)
    return got.reshape(-1, cols)


def gather_weight(shard, wide, narrow):
    got = lax.all_gather(shard.reshape(-1, 128), ("wide", "narrow"), axis=0, tiled=True)
    return got.reshape((wide, narrow) + shard.shape)


def scatter_grad(blocks):
    shape = blocks.shape[2:]
    got = lax.psum_scatter(
        blocks.reshape(-1, 128), ("wide", "narrow"), scatter_dimension=0, tiled=True
    )
    return lax.psum(got.astype(F32), "dp").reshape(shape)


def on_device(
    wide,
    narrow,
    patches,
    visible,
    w_qkv,
    b_qv,
    w_out,
    b_out,
    w_up,
    b_up,
    w_down,
    b_down,
    gain_one,
    shift_one,
    gain_two,
    shift_two,
    cotangent,
):
    images = visible.shape[0]
    pairs = images // 2
    cols = w_qkv.shape[0]
    heads_cols = w_qkv.shape[2]
    units = w_up.shape[1]
    swaps = cols % 128 == 0 and narrow == 2 and wide == 4 and lax.axis_size(DP) == 4
    swaps = swaps and pairs % 2 == 0

    at = jnp.stack(
        [
            lax.axis_index("wide"),
            lax.axis_index("narrow"),
            lax.axis_index("dp") % 2,
            lax.axis_index("dp"),
        ]
    ).astype(jnp.int32)

    index = (visible.reshape(pairs, 2, VISIBLE) + jnp.array([0, PATCHES])[None, :, None]).reshape(
        pairs, PAIR
    )
    index = jnp.pad(index, ((0, 0), (0, ROWS - PAIR)), constant_values=-1)[:, :, None]

    w_qkv_t = w_qkv.transpose(1, 2, 0)
    if swaps:
        pieces = prep(
            at,
            w_qkv_t,
            w_out,
            w_up,
            w_down,
            gain_one,
            shift_one,
            gain_two,
            shift_two,
            b_out,
            b_down,
            b_qv,
            b_up,
        )
        a_p, b_p, u_p, v_p, d_p = [first_piece(piece) for piece in pieces]

        def part_of(whole, side):
            return lax.dynamic_slice_in_dim(whole, side * cols, cols, axis=1)

        def join_cols(keep, got):
            return jnp.where(
                at[1] == 0,
                jnp.concatenate([keep, got], axis=1),
                jnp.concatenate([got, keep], axis=1),
            )

        mine, theirs = at[1], 1 - at[1]
        whole = (D, wide * units)

        b_z = [b_p.fetch(WIDE, bit) for bit in (1, 2, 3)]
        a_x, d_x = a_p.fetch(NARROW, 1), d_p.fetch(NARROW, 1)
        token = fence(hold(at, a_p.stack, b_p.stack, d_p.stack))
        a_p, d_p = a_p.join(a_x.after(token)), d_p.join(d_x.after(token))
        b_p = b_p.join(*[p.after(token) for p in b_z])

        b_x, a_z = b_p.fetch(NARROW, 1), a_p.fetch(WIDE, 2)
        rows_out = pick_rows(
            hold(at, a_p.stack, b_p.stack, d_p.stack), patches, index, cols
        )
        own = rows_out.shape[0] // 2
        rows_send = rows_out[:own]
        a_p, b_p = a_p.join(a_z.after(rows_send)), b_p.join(b_x.after(rows_send))

        b_y, a_z = b_p.fetch(DP, 2), a_p.fetch(WIDE, 1)
        v_z = v_p.fetch(WIDE, 2, rows_send)
        rows_got = swap(rows_send, NARROW, 1)
        cot_out = cot_rows(hold(at, rows_send, a_p.stack, b_p.stack), cotangent, pairs, cols)
        a_p, b_p = a_p.join(a_z.after(cot_out)), b_p.join(b_y.after(cot_out))
        v_p = v_p.join(v_z.after(cot_out))
        rows = join_cols(rows_out[own:], hold(rows_got, cot_out))

        started = [a_p.stack, b_p.stack, v_p.stack, rows]
        a_c, b_c = a_p.fetch(DP, 1, *started), b_p.fetch(DP, 1, *started)
        u_z, v_z = u_p.fetch(WIDE, 2, *started), v_p.fetch(WIDE, 1, *started)
        cot_send = hold(cot_out[:own], *started)
        cot_got = swap(cot_send, NARROW, 1)
        half = heads_cols // 2
        vecs, bias_qkv, bias_up = vectors_of(at, [a_p], half, wide, narrow, cols, units)
        hidden_one = norm(hold(rows, *started, cot_send), vecs)
        u_p, v_p = u_p.join(u_z.after(hidden_one)), v_p.join(v_z.after(hidden_one))
        a_c, b_c = a_c.after(hidden_one), b_c.after(hidden_one)

        u_z, v_x = u_p.fetch(WIDE, 1), v_p.fetch(NARROW, 1)
        started = [u_p.stack, v_p.stack]
        d_z = d_p.fetch(WIDE, 2, *started)
        part = heads_cols // 4
        qkv_t = build_weights(
            at,
            (3 * D, D),
            ([a_p, a_c], qkv_plan(cols, heads_cols, 2, {0: (0, 0)}), CORE),
            (
                [b_p, b_c],
                qkv_plan(cols, heads_cols, 4, {1: (0, 0), 2: (part, 0)}),
                DP_INDEX,
            ),
        )
        out_w = build_weights(
            at, (D, D), ([a_p, a_c], out_plan(cols, heads_cols, 2, (half + 16, 0)), CORE)
        )
        triple = qkv(hold(hidden_one, *started), qkv_t, bias_qkv)
        u_p, v_p = u_p.join(u_z.after(triple)), v_p.join(v_x.after(triple))
        d_p = d_p.join(d_z.after(triple))
        cot = join_cols(cot_out[own:], hold(cot_got, triple))

        u_x, v_y, d_z = u_p.fetch(NARROW, 1), v_p.fetch(DP, 2), d_p.fetch(WIDE, 1)
        mixed, prob = attend(hold(triple, u_p.stack, v_p.stack, d_p.stack, cot))
        d_p = d_p.join(d_z.after(mixed))
        u_x, v_y = u_x.after(mixed), v_y.after(mixed)

        u_all, v_all = [u_p, u_x], [v_p, v_y]
        started = [d_p.stack, u_x.stack, v_y.stack]
        d_y = d_p.fetch(DP, 2)
        u_c = [p.fetch(DP, 1, *started) for p in u_all]
        v_c = [p.fetch(DP, 1, *started) for p in v_all]
        middle, hidden_two = mix(hold(mixed, *started), out_w, rows, vecs)
        half_flat = flat_plan(cols, units, cols // 2)
        part_flat = flat_plan(cols, units, cols // 4)
        up_w = build_weights(
            at,
            whole,
            (u_all + [p.after(hidden_two) for p in u_c], part_flat, CORE),
            (
                v_all + [p.after(hidden_two) for p in v_c],
                flat_plan(cols, units, cols // 8, cols // 2),
                DP_INDEX,
            ),
        )
        active, slope = up(hidden_two, up_w, bias_up)

        x_first = [(w, n, 0) for n in range(2) for w in (0, 2, 1, 3)]
        y_first = [(w, n, dy) for dy in (0, 2) for n in range(2) for w in (0, 2, 1, 3)]
        gw_down = outer(cot, in_hbm(active))
        gb_down = jnp.sum(cot, 0, dtype=F32)[None]
        d_y = d_y.after(gw_down)
        d_c = [p.fetch(DP, 1, d_y.stack) for p in (d_p, d_y)]
        g_d = Chain(
            at,
            [hold(gw_down, d_y.stack)],
            half_flat,
            x_first,
            (cols // 2, units),
            split=True,
        )
        g_d.go(DP, 1)
        d_c = [p.after(*g_d.send) for p in d_c]
        down_w = build_weights(at, whole, ([d_p, d_y] + d_c, part_flat, DP_INDEX))
        g_d.fold(down_w)
        g_d.go(NARROW, 1)
        grad_inner, gw_up, gb_up = inner_back(
            cot, hold(down_w, g_d.send), in_hbm(slope), hidden_two
        )

        result = down(hold(in_hbm(active), grad_inner), down_w, vecs, middle)
        g_u = Chain(
            at,
            [hold(gw_up, result)],
            part_flat,
            y_first,
            (cols // 4, units),
            DP_INDEX,
            split=True,
        )
        g_u.go(DP, 1)
        g_d.fold(*g_u.send)
        g_d.go(WIDE, 1)
        g_u.fold(g_d.send)
        g_u.go(DP, 2)
        grad_middle, branch, gg_two, gs_two, gb_out = middle_back(
            hold(grad_inner, g_d.send, g_u.send), up_w, middle, cot, vecs
        )
        grad_mixed, gw_out = mixed_back(branch, out_w, mixed)

        g_d.fold(grad_mixed)
        g_d.go(WIDE, 2)
        result_send = hold(part_of(result, theirs), grad_mixed)
        result_got = swap(result_send, NARROW, 1)
        groups = rows.shape[0] // ROWS
        grad_triple = attend_back(
            triple, in_hbm(prob), hold(grad_mixed, g_d.send, result_send), 0, groups
        )
        grad_rows, gg_one, gs_one = first_back(grad_triple, qkv_t, rows, grad_middle, vecs)

        d_sum = g_d.total(grad_rows)
        d_got = swap(d_sum.astype(BF), DP, 2)
        g_u.fold(grad_rows)
        g_u.go(NARROW, 1)
        result_got = hold(result_got, grad_rows)
        gw_qkv, gb_qkv = qkv_grad(hold(grad_triple, d_sum, g_u.send, result_got), hidden_one)
        sums = owner_sums(
            wide,
            narrow,
            cols,
            gg_one,
            gs_one,
            gg_two,
            gs_two,
            gb_out,
            gb_down,
            gb_qkv,
            gb_up,
        )

        part = heads_cols // 4
        g_q = Chain(
            at,
            [gw_qkv],
            qkv_plan(cols, heads_cols, 4, {p: (p * part, 0) for p in range(3)}),
            y_first,
            (3 * part, cols),
            DP_INDEX,
        )
        g_q.go(DP, 1)
        rest_plan = joined(
            out_plan(cols, heads_cols, 2, (0, 0), 0), sums_plan(cols, narrow, (half, 0), 1)
        )
        g_r = Chain(at, [gw_out, sums], rest_plan, x_first, (half + 16, cols))
        g_r.go(DP, 1)
        d_sum = d_sum + hold(d_got, g_r.send).astype(F32)
        d_got = swap(d_sum, DP, 1)
        g_u.fold(g_r.send)
        g_u.go(WIDE, 1)
        rows_send = hold(part_of(grad_rows, theirs), g_r.send).astype(BF)
        rows_back = swap(rows_send, NARROW, 1)
        keep = hold(part_of(result, mine), g_q.send, d_sum, g_u.send, rows_send)
        block_output = flat_rows(at, keep, result_got, cols)

        g_q.fold(block_output)
        g_q.go(DP, 2)
        g_r.fold(block_output)
        g_r.go(NARROW, 1)
        g_u.fold(g_q.send, g_r.send)
        g_u.go(WIDE, 2)
        rows_back = hold(rows_back, g_u.send)
        grad_patches = put_rows(at, part_of(grad_rows, mine), rows_back, index, cols)

        def in_order(value, other, index):
            return jnp.where(index == 0, jnp.stack([value, other]), jnp.stack([other, value]))

        g_q.fold(grad_patches)
        g_q.go(NARROW, 1)
        g_r.spread(grad_patches)
        u_sum = g_u.total(g_q.send, *g_r.send)
        token = fence(hold(vecs, g_q.send, u_sum, *g_r.send))
        g_q.spread(token)
        r_sum = g_r.all_of(token)
        r_got = swap(r_sum.astype(BF), DP, 2)
        u_got = swap(u_sum.astype(BF), DP, 2)
        token = fence(hold(token, r_sum, u_sum, *g_q.send))
        q_sum = g_q.all_of(token)
        q_got = [swap(q_sum.astype(BF), DP, bit) for bit in (1, 2, 3)]
        r_sum = r_sum + hold(r_got, token).astype(F32)
        r_got = swap(r_sum[:half], DP, 1)
        u_sum = in_order(u_sum, hold(u_got, token).astype(F32), at[3] // 2)
        u_got = swap(u_sum, DP, 1)
        g_down = in_order(d_sum, d_got, at[2]).reshape(cols, units)
        g_up = in_order(u_sum, u_got, at[2]).transpose(1, 0, 2, 3).reshape(cols, units)
        q_got = [got.astype(F32) for got in q_got]
        pairs_of = [in_order(q_sum, q_got[0], at[2]), in_order(q_got[1], q_got[2], at[2])]
        q_sum = in_order(*pairs_of, at[3] // 2).reshape(4, 3, part, cols)
        g_out = in_order(r_sum[:half], r_got, at[2]).reshape(heads_cols, cols)
        g_qkv = q_sum.transpose(3, 1, 0, 2).reshape(cols, 3, heads_cols)
        grad_patches = grad_patches.reshape(1, -1)
        lines = r_sum[half:]
        vector_grads = [lines[i] for i in range(6)]
        g_bqv = lines[6].reshape(2, heads_cols)
        g_bup = lines[7:9].reshape(units)
    else:
        table = patches.reshape(images, PATCHES, cols)
        rows_mine = jnp.take_along_axis(table, visible[:, :, None], axis=1)
        rows_mine = jnp.pad(
            rows_mine.reshape(pairs, PAIR, cols), ((0, 0), (0, ROWS - PAIR), (0, 0))
        )
        cot_mine = jnp.pad(
            cotangent.reshape(pairs, PAIR, cols), ((0, 0), (0, ROWS - PAIR), (0, 0))
        )
        rows = to_rows(rows_mine.reshape(narrow, -1, cols), narrow)
        cot = to_rows(cot_mine.reshape(narrow, -1, cols), narrow)
        vec = jnp.concatenate(
            [gain_one, shift_one, gain_two, shift_two, b_out, b_down, b_qv.reshape(-1), b_up]
        )
        vec = lax.all_gather(vec, ("wide", "narrow"), axis=0, tiled=False).astype(F32)
        qkv_t = gather_weight(w_qkv_t, wide, narrow)
        qkv_t = qkv_t.transpose(2, 0, 3, 1, 4).reshape(3 * D, D)
        out_w = gather_weight(w_out, wide, narrow).transpose(0, 2, 1, 3).reshape(D, D)
        up_w = gather_weight(w_up, wide, narrow).transpose(1, 2, 0, 3).reshape(D, -1)
        down_w = gather_weight(w_down, wide, narrow).transpose(1, 2, 0, 3).reshape(D, -1)
        vec = vec.reshape(wide, narrow, -1)
        vecs = vec[0, :, : 6 * cols].reshape(narrow, 6, cols).transpose(1, 0, 2).reshape(6, D)
        vecs = jnp.pad(vecs, ((0, 2), (0, 0)))
        by_wide = vec[:, 0, 6 * cols :]
        bias_q = by_wide[:, :heads_cols].reshape(1, D)
        bias_v = by_wide[:, heads_cols : 2 * heads_cols].reshape(1, D)
        bias_qkv = jnp.concatenate([bias_q, jnp.zeros((1, D), F32), bias_v], axis=1)
        bias_up = by_wide[:, 2 * heads_cols :].reshape(1, -1)

        hidden_one = norm(rows, vecs)
        triple = qkv(hidden_one, qkv_t, bias_qkv)
        mixed, prob = attend(triple)
        middle, hidden_two = mix(mixed, out_w, rows, vecs)
        active, slope = up(hidden_two, up_w, bias_up)
        result = down(active, down_w, vecs, middle)
        gw_down = outer(cot, active)
        gb_down = jnp.sum(cot, 0, dtype=F32)[None]
        grad_inner, gw_up, gb_up = inner_back(cot, down_w, slope, hidden_two)
        grad_middle, branch, gg_two, gs_two, gb_out = middle_back(
            grad_inner, up_w, middle, cot, vecs
        )
        grad_mixed, gw_out = mixed_back(branch, out_w, mixed)
        grad_triple = attend_back(triple, prob, grad_mixed, 0, rows.shape[0] // ROWS)
        gw_qkv, gb_qkv = qkv_grad(grad_triple, hidden_one)
        grad_rows, gg_one, gs_one = first_back(grad_triple, qkv_t, rows, grad_middle, vecs)
        sums = pack(gg_one, gs_one, gg_two, gs_two, gb_out, gb_down, gb_qkv, gb_up)

        result = from_rows(result, narrow)
        grad_rows = from_rows(grad_rows, narrow)
        block_output = result.reshape(pairs, ROWS, cols)[:, :PAIR].reshape(1, -1)
        grad_rows = grad_rows.reshape(pairs, ROWS, cols)[:, :PAIR].reshape(images, VISIBLE, cols)
        grad_patches = (
            jnp.zeros((images, PATCHES, cols), F32)
            .at[jnp.arange(images)[:, None], visible]
            .set(grad_rows)
            .reshape(1, -1)
        )
        g_down = scatter_grad(gw_down.reshape(narrow, cols, wide, units).transpose(2, 0, 1, 3))
        g_up = scatter_grad(gw_up.reshape(narrow, cols, wide, units).transpose(2, 0, 1, 3))
        g_out = scatter_grad(gw_out.reshape(wide, heads_cols, narrow, cols).transpose(0, 2, 1, 3))
        g_qkv = scatter_grad(
            gw_qkv.reshape(3, wide, heads_cols, narrow, cols).transpose(1, 3, 0, 2, 4)
        )
        g_qkv = g_qkv.transpose(2, 0, 1)
        sums = lax.psum(sums, ("dp", "wide", "narrow"))
        sums = sums.reshape(-1)
        vector_grads = [
            lax.dynamic_slice_in_dim(sums, i * D + at[1] * cols, cols) for i in range(6)
        ]
        g_bqv = jnp.stack(
            [
                lax.dynamic_slice_in_dim(sums, (6 + i) * D + at[0] * heads_cols, heads_cols)
                for i in (0, 2)
            ]
        )
        g_bup = lax.dynamic_slice_in_dim(sums, 9 * D + at[0] * units, units)

    return (
        block_output,
        grad_patches,
        g_qkv,
        g_bqv,
        g_out,
        vector_grads[4],
        g_up,
        g_bup,
        g_down,
        vector_grads[5],
        vector_grads[0],
        vector_grads[1],
        vector_grads[2],
        vector_grads[3],
    )


def solution(mesh):
    in_specs = (
        P("narrow", ("dp", "wide")),
        P(("dp", "wide"), None),
        P("narrow", None, "wide"),
        P(None, "wide"),
        P("wide", "narrow"),
        P("narrow"),
        P("narrow", "wide"),
        P("wide"),
        P("narrow", "wide"),
        P("narrow"),
        P("narrow"),
        P("narrow"),
        P("narrow"),
        P("narrow"),
        P("narrow", ("dp", "wide")),
    )
    out_specs = (
        P("narrow", ("dp", "wide")),
        P("narrow", ("dp", "wide")),
        P("narrow", None, "wide"),
        P(None, "wide"),
        P("wide", "narrow"),
        P("narrow"),
        P("narrow", "wide"),
        P("wide"),
        P("narrow", "wide"),
        P("narrow"),
        P("narrow"),
        P("narrow"),
        P("narrow"),
        P("narrow"),
    )
    body = partial(on_device, mesh.shape["wide"], mesh.shape["narrow"])
    return jax.shard_map(body, mesh=mesh, in_specs=in_specs, out_specs=out_specs, check_vma=False)
```

```python
from functools import partial

import jax
import jax.numpy as jnp
from jax import lax
from jax.experimental import pallas as pl
from jax.experimental.pallas import tpu as pltpu
from jax.sharding import PartitionSpec as P

D = 768
HEAD_DIM = 64
HEADS = 12
PATCHES = 196
VISIBLE = 49
PAIR = 2 * VISIBLE
ROWS = 112
TILE = 768
EPS = 1e-06
BF = jnp.bfloat16
F32 = jnp.float32
MB = 1024 * 1024


def dot(a, b, ca, cb):
    return lax.dot_general(a, b, (((ca,), (cb,)), ((), ())), preferred_element_type=F32)


FLOPS_PER_US = 540000000


def call(body, grid, ins, outs, shapes, scratch=(), prefetch=0, us=1.0, nbytes=0, vmem=32):
    return pl.pallas_call(
        body,
        out_shape=shapes,
        grid_spec=pltpu.PrefetchScalarGridSpec(
            num_scalar_prefetch=prefetch,
            grid=grid,
            in_specs=ins,
            out_specs=outs,
            scratch_shapes=scratch,
        ),
        compiler_params=pltpu.CompilerParams(
            dimension_semantics=("arbitrary",) * len(grid), vmem_limit_bytes=vmem * MB
        ),
        cost_estimate=pl.CostEstimate(
            flops=int(us * FLOPS_PER_US), bytes_accessed=1024, transcendentals=0
        ),
    )


def in_hbm(value):
    return pltpu.with_memory_space_constraint(value, pltpu.HBM)


def spec(shape, index):
    return pl.BlockSpec(shape, index)


def struct(shape, dtype):
    return jax.ShapeDtypeStruct(shape, dtype)


def together(own):
    return next(count for count in (4, 2, 1) if own % count == 0)


def strided(start, count, lanes):
    return [pl.ds(start + k, count, stride=lanes) for k in range(lanes)]


def one_hot(index):
    return (index == lax.broadcasted_iota(jnp.int32, (ROWS, 2 * PATCHES), 1)).astype(BF)


def pick_body(cols, count, at_ref, patch_ref, index_ref, rows_ref, wide_ref):
    lanes = cols // 128
    wide_ref[...] = patch_ref[...].astype(F32).reshape(wide_ref.shape)
    for j in range(count):
        places = strided(j * 2 * PATCHES * lanes, 2 * PATCHES, lanes)
        both = jnp.concatenate([wide_ref[place, :] for place in places], axis=1).astype(BF)
        rows_ref[j * ROWS : (j + 1) * ROWS, :] = dot(one_hot(index_ref[j]), both, 1, 0).astype(BF)


def owner_first_sent(steps):
    own = steps // 2

    def source(i, at):
        return (i // own ^ 1 ^ at[1]) * own + i % own

    return source


def pick_rows(at, patches, index, cols):
    pairs = index.shape[0]
    count = together(pairs // 2)
    width = 2 * PATCHES * cols * count
    source = owner_first_sent(pairs // count)
    return call(
        partial(pick_body, cols, count),
        (pairs // count,),
        [
            spec((1, width), lambda i, at: (0, source(i, at))),
            spec((count, ROWS, 1), lambda i, at: (source(i, at), 0, 0)),
        ],
        spec((count * ROWS, cols), lambda i, at: (i, 0)),
        struct((pairs * ROWS, cols), BF),
        [pltpu.VMEM((width // 128, 128), F32)],
        prefetch=1,
        us=200,
        nbytes=pairs * width * 4,
    )(at, patches, index)


def cot_body(cols, count, at_ref, cot_ref, rows_ref, scr):
    lanes = cols // 128
    scr[...] = cot_ref[...].astype(F32).reshape(scr.shape)
    for j in range(count):
        places = strided(j * PAIR * lanes, PAIR, lanes)
        cot = jnp.concatenate([scr[place, :] for place in places], axis=1)
        rows_ref[j * ROWS : (j + 1) * ROWS, :] = jnp.concatenate(
            [cot, jnp.zeros((ROWS - PAIR, cols), F32)], axis=0
        ).astype(BF)


def cot_rows(at, cotangent, pairs, cols):
    count = together(pairs // 2)
    width = PAIR * cols * count
    source = owner_first_sent(pairs // count)
    return call(
        partial(cot_body, cols, count),
        (pairs // count,),
        [spec((1, width), lambda i, at: (0, source(i, at)))],
        spec((count * ROWS, cols), lambda i, at: (i, 0)),
        struct((pairs * ROWS, cols), BF),
        [pltpu.VMEM((width // 128, 128), F32)],
        prefetch=1,
        us=200,
        nbytes=pairs * width * 4,
    )(at, cotangent)


def own_block(at_ref, keep_ref, got_ref, j):
    own = pl.num_programs(0) // 2
    mine = pl.program_id(0) // own == at_ref[1]
    rows = slice(j * ROWS, (j + 1) * ROWS)
    return jnp.where(mine, keep_ref[rows, :].astype(F32), got_ref[rows, :].astype(F32))


def put_body(cols, count, at_ref, keep_ref, got_ref, index_ref, out_ref):
    lanes = cols // 128
    for j in range(count):
        hit = one_hot(index_ref[j])
        rest = own_block(at_ref, keep_ref, got_ref, j)
        parts = []
        for _ in range(3):
            parts.append(rest.astype(BF))
            rest = rest - parts[-1].astype(F32)
        total = dot(jnp.concatenate([hit] * 3), jnp.concatenate(parts), 0, 0)
        for k, place in enumerate(strided(j * 2 * PATCHES * lanes, 2 * PATCHES, lanes)):
            out_ref[place, :] = total[:, k * 128 : (k + 1) * 128]


def put_rows(at, keep, got, index, cols):
    pairs = index.shape[0]
    count = together(pairs // 2)
    own = pairs // count // 2
    tall = count * 2 * PATCHES * cols // 128
    rows = spec((count * ROWS, cols), lambda i, at: (i % own, 0))
    return call(
        partial(put_body, cols, count),
        (pairs // count,),
        [rows, rows, spec((count, ROWS, 1), lambda i, at: (i, 0, 0))],
        spec((tall, 128), lambda i, at: (i, 0)),
        struct((pairs // count * tall, 128), F32),
        prefetch=1,
        us=200,
        nbytes=pairs * (tall * 512 + ROWS * cols * 4),
    )(at, keep, got, index)


def flat_body(cols, count, at_ref, keep_ref, got_ref, out_ref, scr):
    lanes = cols // 128
    for j in range(count):
        rows = own_block(at_ref, keep_ref, got_ref, j)
        for k, place in enumerate(strided(j * PAIR * lanes, PAIR, lanes)):
            scr[place, :] = rows[:PAIR, k * 128 : (k + 1) * 128]
    out_ref[...] = scr[...].reshape(out_ref.shape).astype(BF)


def flat_rows(at, keep, got, cols):
    pairs = 2 * (keep.shape[0] // ROWS)
    count = together(pairs // 2)
    own = pairs // count // 2
    width = PAIR * cols * count
    rows = spec((count * ROWS, cols), lambda i, at: (i % own, 0))
    return call(
        partial(flat_body, cols, count),
        (pairs // count,),
        [rows, rows],
        spec((1, width), lambda i, at: (0, i)),
        struct((1, pairs // count * width), BF),
        [pltpu.VMEM((width // 128, 128), F32)],
        prefetch=1,
        us=200,
        nbytes=pairs * width * 6,
    )(at, keep, got)


def stats(rows):
    mean = jnp.mean(rows, 1, keepdims=True)
    off = rows - mean
    inv = lax.rsqrt(jnp.mean(off * off, 1, keepdims=True) + EPS)
    return off * inv, inv


GAIN_ONE, SHIFT_ONE, GAIN_TWO, SHIFT_TWO, BIAS_OUT, BIAS_DOWN = range(6)


def vec_row(vec_ref, i):
    return vec_ref[i : i + 1, :]


def norm_body(rows_ref, vec_ref, out_ref):
    normed, _ = stats(rows_ref[...].astype(F32))
    out_ref[...] = (normed * vec_row(vec_ref, GAIN_ONE) + vec_row(vec_ref, SHIFT_ONE)).astype(BF)


def norm(rows, vec):
    r = rows.shape[0]
    return call(
        norm_body,
        (r // ROWS,),
        [spec((ROWS, D), lambda i: (i, 0)), spec((8, D), lambda i: (0, 0))],
        spec((ROWS, D), lambda i: (i, 0)),
        struct((r, D), BF),
        us=200,
        nbytes=r * D * 4,
    )(rows, vec)


def qkv_body(hidden_ref, w_ref, bias_ref, out_ref):
    out_ref[...] = (dot(hidden_ref[...], w_ref[...], 1, 1) + bias_ref[...]).astype(BF)


def qkv(hidden, w, bias):
    r = hidden.shape[0]
    return call(
        qkv_body,
        (3 * D // TILE,),
        [
            spec((r, D), lambda j: (0, 0)),
            spec((TILE, D), lambda j: (j, 0)),
            spec((1, TILE), lambda j: (0, j)),
        ],
        spec((r, TILE), lambda j: (0, j)),
        struct((r, 3 * D), BF),
        us=13,
        nbytes=r * D * 8 + 3 * D * D * 2,
    )(hidden, w, bias)


def same_image():
    at_row = lax.broadcasted_iota(jnp.int32, (ROWS, ROWS), 0)
    at_col = lax.broadcasted_iota(jnp.int32, (ROWS, ROWS), 1)

    def image(at):
        return (at >= VISIBLE).astype(jnp.int32) + (at >= PAIR).astype(jnp.int32)

    return image(at_row) == image(at_col)


def side_by_side(block):
    left = lax.broadcasted_iota(jnp.int32, (ROWS, 128), 1) < HEAD_DIM
    none = jnp.zeros_like(block)
    return jnp.concatenate([jnp.where(left, block, none), jnp.where(left, none, block)])


def both_heads(stack):
    left = lax.broadcasted_iota(jnp.int32, (ROWS, 128), 1) < HEAD_DIM
    return jnp.where(left, stack[:ROWS], stack[ROWS:])


def pair_of(ref, part, pair):
    return ref[:, part * D + pair * 128 : part * D + (pair + 1) * 128]


def attend_body(triple_ref, mixed_ref, prob_ref):
    keep = same_image()[None]
    for pair in range(HEADS // 2):
        q, k, v = (pair_of(triple_ref, part, pair) for part in range(3))
        scores = dot(side_by_side(k), q, 1, 1).reshape(2, ROWS, ROWS) * HEAD_DIM**-0.5
        scores = jnp.where(keep, scores, -1e30)
        expo = jnp.exp(scores - jnp.max(scores, 1, keepdims=True))
        prob = expo / jnp.sum(expo, 1, keepdims=True)
        prob_ref[0, 2 * pair : 2 * pair + 2] = prob
        low = prob.astype(BF).reshape(2 * ROWS, ROWS)
        mixed_ref[:, pair * 128 : (pair + 1) * 128] = dot(low, side_by_side(v), 0, 0).astype(BF)


def attend(triple):
    groups = triple.shape[0] // ROWS
    return call(
        attend_body,
        (groups,),
        [spec((ROWS, 3 * D), lambda g: (g, 0))],
        [spec((ROWS, D), lambda g: (g, 0)), spec((1, HEADS, ROWS, ROWS), lambda g: (g, 0, 0, 0))],
        [struct((groups * ROWS, D), BF), pltpu.HBM((groups, HEADS, ROWS, ROWS), F32)],
        us=200,
        nbytes=groups * ROWS * (8 * D + HEADS * 512),
    )(triple)


def mix_body(mixed_ref, w_ref, rows_ref, vec_ref, middle_ref, hidden_ref):
    branch = dot(mixed_ref[...], w_ref[...], 1, 0) + vec_row(vec_ref, BIAS_OUT)
    middle = rows_ref[...].astype(F32) + branch
    middle_ref[...] = middle
    normed, _ = stats(middle)
    hidden_ref[...] = (
        normed * vec_row(vec_ref, GAIN_TWO) + vec_row(vec_ref, SHIFT_TWO)
    ).astype(BF)


def row_tile(r):
    return r // 2


def mix(mixed, w, rows, vec):
    r = rows.shape[0]
    m = r // 4 if r % 64 == 0 else row_tile(r)
    row = spec((m, D), lambda i: (i, 0))
    return call(
        mix_body,
        (r // m,),
        [row, spec((D, D), lambda i: (0, 0)), row, spec((8, D), lambda i: (0, 0))],
        [row, row],
        [struct((r, D), F32), struct((r, D), BF)],
        us=16,
        nbytes=r * D * 10 + D * D * 2,
    )(mixed, w, rows, vec)


def up_body(hidden_ref, w_ref, bias_ref, active_ref, slope_ref):
    inner = dot(hidden_ref[...], w_ref[...], 1, 0) + bias_ref[...]
    phi = 0.5 * (1.0 + lax.erf(inner * (0.5**0.5)))
    active_ref[...] = (inner * phi).astype(BF)
    slope_ref[...] = phi + inner * (jnp.exp(-0.5 * inner * inner) * 0.3989422804014327)


def up(hidden, w, bias):
    r = hidden.shape[0]
    units = w.shape[1]
    tile = spec((r, TILE), lambda j: (0, j))
    return call(
        up_body,
        (units // TILE,),
        [
            spec((r, D), lambda j: (0, 0)),
            spec((D, TILE), lambda j: (0, j)),
            spec((1, TILE), lambda j: (0, j)),
        ],
        [tile, tile],
        [pltpu.HBM((r, units), BF), pltpu.HBM((r, units), F32)],
        us=0.01,
        nbytes=r * D * 2 + D * units * 2 + r * units * 6,
    )(hidden, w, bias)


def down_body(active_ref, w_ref, vec_ref, middle_ref, out_ref):
    branch = dot(active_ref[...], w_ref[...], 1, 1) + vec_row(vec_ref, BIAS_DOWN)
    out_ref[...] = (middle_ref[...] + branch).astype(BF)


def down(active, w, vec, middle):
    r, units = active.shape
    m = row_tile(r)
    return call(
        down_body,
        (r // m,),
        [
            spec((m, units), lambda i: (i, 0)),
            spec((D, units), lambda i: (0, 0)),
            spec((8, D), lambda i: (0, 0)),
            spec((m, D), lambda i: (i, 0)),
        ],
        spec((m, D), lambda i: (i, 0)),
        struct((r, D), BF),
        us=0.01,
        nbytes=r * units * 2 + D * units * 2 + r * D * 6,
    )(active, w, vec, middle)


def outer_body(left_ref, right_ref, out_ref, turned):
    @pl.when(pl.program_id(0) == 0)
    def _():
        turned[...] = left_ref[...].T

    out_ref[...] = dot(turned[...], right_ref[...], 1, 0).astype(BF)


def outer(left, right):
    r, width = right.shape
    rows = left.shape[1]
    return call(
        outer_body,
        (width // TILE,),
        [spec((r, rows), lambda j: (0, 0)), spec((r, TILE), lambda j: (0, j))],
        spec((rows, TILE), lambda j: (0, j)),
        struct((rows, width), BF),
        [pltpu.VMEM((rows, r), BF)],
        us=0.01,
        nbytes=r * rows * 2 + r * width * 2 + rows * width * 2,
    )(left, right)


def inner_back_body(cot_ref, w_ref, slope_ref, hidden_ref, grad_ref, gw_ref, gb_ref, turned):
    @pl.when(pl.program_id(0) == 0)
    def _():
        turned[...] = hidden_ref[...].T

    grad = (dot(cot_ref[...], w_ref[...], 1, 0) * slope_ref[...]).astype(BF)
    grad_ref[...] = grad
    gw_ref[...] = dot(turned[...], grad, 1, 0).astype(BF)
    gb_ref[...] = jnp.sum(grad.astype(F32), 0, keepdims=True)


def inner_back(cot, w, slope, hidden):
    r, units = slope.shape
    full = spec((r, D), lambda j: (0, 0))
    col = spec((D, TILE), lambda j: (0, j))
    tile = spec((r, TILE), lambda j: (0, j))
    return call(
        inner_back_body,
        (units // TILE,),
        [full, col, tile, full],
        [tile, col, spec((1, TILE), lambda j: (0, j))],
        [pltpu.HBM((r, units), BF), struct((D, units), BF), struct((1, units), F32)],
        [pltpu.VMEM((D, r), BF)],
        us=200,
        nbytes=r * D * 4 + D * units * 4 + r * units * 6,
    )(cot, w, slope, hidden)


def place(w):
    return w % 2 * 2 + w // 2


def turn_blocks(left_ref, plain, turned, offsets):
    plain[...] = left_ref[...].T
    rows = plain.shape[0] // len(offsets)
    for i, offset in enumerate(offsets):
        turned[i * rows : (i + 1) * rows, :] = plain[pl.ds(pl.multiple_of(offset, 16), rows), :]


def outer_pieces_body(cols, at_ref, left_ref, right_ref, *refs):
    outs, (plain, turned) = refs[:4], refs[4:]

    @pl.when(pl.program_id(0) == 0)
    def _():
        offsets = [
            (n ^ at_ref[1]) * cols + (at_ref[2] ^ side) * (cols // 2)
            for side in range(2)
            for n in range(2)
        ]
        turn_blocks(left_ref, plain, turned, offsets)

    grad = dot(turned[...], right_ref[...], 1, 0).astype(BF)
    half = cols // 2
    for i, out in enumerate(outs):
        out[...] = grad[i * half : (i + 1) * half].reshape(out.shape)


def outer_pieces(at, left, right, cols, wide):
    r, width = right.shape
    rows, units = left.shape[1], width // wide
    shape = (wide, cols // 2, units)
    block = spec((1, cols // 2, units), lambda j, at: (place(j ^ at[0]), 0, 0))
    out = call(
        partial(outer_pieces_body, cols),
        (wide,),
        [spec((r, rows), lambda j, at: (0, 0)), spec((r, units), lambda j, at: (0, j))],
        [block] * 4,
        [pltpu.HBM(shape, BF)] * 2 + [struct(shape, BF)] * 2,
        [pltpu.VMEM((rows, r), BF)] * 2,
        prefetch=1,
        us=0.01,
        nbytes=r * rows * 2 + r * width * 2 + rows * width * 2,
    )(at, left, right)
    return out[:2], out[2:]


def inner_back_pieces_body(cols, at_ref, cot_ref, w_ref, slope_ref, hidden_ref, *refs):
    grad_ref, outs, gb_ref, plain, turned = refs[0], refs[1:5], refs[5], refs[6], refs[7]
    part = cols // 4

    @pl.when(pl.program_id(0) == 0)
    def _():
        offsets = [
            (n ^ at_ref[1]) * cols + (at_ref[3] ^ (2 * dy) ^ side) * part
            for side in range(2)
            for dy in range(2)
            for n in range(2)
        ]
        turn_blocks(hidden_ref, plain, turned, offsets)

    grad = (dot(cot_ref[...], w_ref[...], 1, 0) * slope_ref[...]).astype(BF)
    grad_ref[...] = grad
    gb_ref[...] = jnp.sum(grad.astype(F32), 0, keepdims=True)
    outer_grad = dot(turned[...], grad, 1, 0).astype(BF)
    for i, out in enumerate(outs):
        out[...] = outer_grad[2 * i * part : 2 * (i + 1) * part].reshape(out.shape)


def inner_back_pieces(at, cot, w, slope, hidden, cols, wide):
    r, width = slope.shape
    units, part = width // wide, cols // 4
    shape = (2, wide, part, units)
    full = spec((r, D), lambda j, at: (0, 0))
    tile = spec((r, units), lambda j, at: (0, j))
    block = spec((2, 1, part, units), lambda j, at: (0, place(j ^ at[0]), 0, 0))
    out = call(
        partial(inner_back_pieces_body, cols),
        (wide,),
        [full, spec((D, units), lambda j, at: (0, j)), tile, full],
        [tile] + [block] * 4 + [spec((1, units), lambda j, at: (0, j))],
        [pltpu.HBM((r, width), BF)]
        + [pltpu.HBM(shape, BF)] * 2
        + [struct(shape, BF)] * 2
        + [struct((1, width), F32)],
        [pltpu.VMEM((D, r), BF)] * 2,
        prefetch=1,
        us=200,
        nbytes=r * D * 4 + D * width * 4 + r * width * 6,
    )(at, cot, w, slope, hidden)
    pieces = [piece.reshape(2 * wide, part, units) for piece in out[1:5]]
    return out[0], pieces[:2], pieces[2:], out[5]


def norm_pull(grad, normed, inv, gain):
    scaled = grad * gain
    return inv * (
        scaled
        - jnp.mean(scaled, 1, keepdims=True)
        - normed * jnp.mean(scaled * normed, 1, keepdims=True)
    )


def middle_back_body(
    grad_ref, w_ref, middle_ref, cot_ref, vec_ref, out_ref, branch_ref, gain_sum, shift_sum, out_sum
):
    grad = dot(grad_ref[...], w_ref[...], 1, 1)
    normed, inv = stats(middle_ref[...])
    total = cot_ref[...].astype(F32) + norm_pull(
        grad, normed, inv, vec_row(vec_ref, GAIN_TWO)
    )
    out_ref[...] = total
    branch = total.astype(BF)
    branch_ref[...] = branch
    sums = (
        (gain_sum, jnp.sum(grad * normed, 0, keepdims=True)),
        (shift_sum, jnp.sum(grad, 0, keepdims=True)),
        (out_sum, jnp.sum(branch.astype(F32), 0, keepdims=True)),
    )
    for ref, value in sums:
        add_up(ref, value)


def add_up(ref, value):
    @pl.when(pl.program_id(0) == 0)
    def _():
        ref[...] = value

    @pl.when(pl.program_id(0) != 0)
    def _():
        ref[...] += value


def middle_back(grad, w, middle, cot, vecs):
    r, units = grad.shape
    m = row_tile(r)
    vec = spec((1, D), lambda i: (0, 0))
    row = spec((m, D), lambda i: (i, 0))
    vec_out = struct((1, D), F32)
    return call(
        middle_back_body,
        (r // m,),
        [
            spec((m, units), lambda i: (i, 0)),
            spec((D, units), lambda i: (0, 0)),
            row,
            row,
            spec((8, D), lambda i: (0, 0)),
        ],
        [row, row, vec, vec, vec],
        [struct((r, D), F32), struct((r, D), BF), vec_out, vec_out, vec_out],
        us=200,
        nbytes=r * units * 2 + D * units * 2 + r * D * 12,
    )(grad, w, middle, cot, vecs)


def mixed_back_body(branch_ref, tile_ref, w_ref, mixed_ref, grad_ref, gw_ref, turned):
    @pl.when(pl.program_id(0) == 0)
    def _():
        turned[...] = mixed_ref[...].T

    grad_ref[...] = dot(branch_ref[...], w_ref[...], 1, 1).astype(BF)
    gw_ref[...] = dot(turned[...], tile_ref[...], 1, 0).astype(BF)


def mixed_back(branch, w, mixed):
    r = branch.shape[0]
    full = spec((r, D), lambda j: (0, 0))
    tile = spec((r, TILE), lambda j: (0, j))
    return call(
        mixed_back_body,
        (D // TILE,),
        [full, tile, spec((TILE, D), lambda j: (j, 0)), full],
        [tile, spec((D, TILE), lambda j: (0, j))],
        [struct((r, D), BF), struct((D, D), BF)],
        [pltpu.VMEM((D, r), BF)],
        us=0.01,
        nbytes=r * D * 8 + D * D * 4,
    )(branch, branch, w, mixed)


def attend_back_body(triple_ref, prob_ref, grad_ref, *rest):
    out_ref = rest[-1]
    scale = HEAD_DIM**-0.5
    for pair in range(HEADS // 2):
        q, k, v = (pair_of(triple_ref, part, pair) for part in range(3))
        grad = pair_of(grad_ref, 0, pair)
        prob = prob_ref[0, 2 * pair : 2 * pair + 2]
        grad_prob = dot(side_by_side(v), grad, 1, 1).reshape(2, ROWS, ROWS)
        inside = jnp.sum(grad_prob * prob, 1, keepdims=True)
        grad_scores = (prob * (grad_prob - inside)).astype(BF).reshape(2 * ROWS, ROWS)
        grads = (
            dot(grad_scores, side_by_side(k), 0, 0) * scale,
            both_heads(dot(grad_scores, q, 1, 0)) * scale,
            both_heads(dot(prob.astype(BF).reshape(2 * ROWS, ROWS), grad, 1, 0)),
        )
        for part, value in enumerate(grads):
            out_ref[:, part * D + pair * 128 : part * D + (pair + 1) * 128] = value.astype(BF)


def attend_back(triple, prob, grad, start, stop, partial_out=None):
    wide = spec((ROWS, 3 * D), lambda g: (g + start, 0))
    count = stop - start
    given = [] if partial_out is None else [partial_out]
    return pl.pallas_call(
        attend_back_body,
        out_shape=struct(triple.shape, BF),
        grid_spec=pltpu.PrefetchScalarGridSpec(
            num_scalar_prefetch=0,
            grid=(count,),
            in_specs=[
                wide,
                spec((1, HEADS, ROWS, ROWS), lambda g: (g + start, 0, 0, 0)),
                spec((ROWS, D), lambda g: (g + start, 0)),
            ]
            + [ANY] * len(given),
            out_specs=wide,
        ),
        input_output_aliases={3: 0} if given else {},
        compiler_params=pltpu.CompilerParams(
            dimension_semantics=("arbitrary",), vmem_limit_bytes=24 * MB
        ),
        cost_estimate=pl.CostEstimate(
            flops=FLOPS_PER_US // 100, bytes_accessed=1024, transcendentals=0
        ),
    )(triple, prob, grad, *given)


def qkv_grad_body(grad_ref, hidden_ref, gw_ref, gb_ref):
    grad = grad_ref[...]
    gw_ref[...] = dot(grad.T, hidden_ref[...], 1, 0).astype(BF)
    gb_ref[...] = jnp.sum(grad.astype(F32), 0, keepdims=True)


def qkv_grad(grad, hidden):
    r, width = grad.shape
    return call(
        qkv_grad_body,
        (width // TILE,),
        [spec((r, TILE), lambda j: (0, j)), spec((r, D), lambda j: (0, 0))],
        [spec((TILE, D), lambda j: (j, 0)), spec((1, TILE), lambda j: (0, j))],
        [struct((width, D), BF), struct((1, width), F32)],
        us=200,
        nbytes=r * width * 2 + r * D * 2 + width * D * 2,
    )(grad, hidden)


def first_back_body(grad_ref, w_ref, rows_ref, middle_ref, vec_ref, out_ref, gain_sum, shift_sum):
    grad = dot(grad_ref[...], w_ref[...], 1, 0)
    normed, inv = stats(rows_ref[...].astype(F32))
    pulled = norm_pull(grad, normed, inv, vec_row(vec_ref, GAIN_ONE))
    out_ref[...] = middle_ref[...] + pulled
    add_up(gain_sum, jnp.sum(grad * normed, 0, keepdims=True))
    add_up(shift_sum, jnp.sum(grad, 0, keepdims=True))


def first_back(grad, w, rows, grad_middle, vecs):
    r, width = grad.shape
    m = r // 4 if r % 64 == 0 else row_tile(r)
    vec = spec((1, D), lambda i: (0, 0))
    row = spec((m, D), lambda i: (i, 0))
    vec_out = struct((1, D), F32)
    return call(
        first_back_body,
        (r // m,),
        [
            spec((m, width), lambda i: (i, 0)),
            spec((width, D), lambda i: (0, 0)),
            row,
            row,
            spec((8, D), lambda i: (0, 0)),
        ],
        [row, vec, vec],
        [struct((r, D), F32), vec_out, vec_out],
        us=0.01,
        nbytes=r * width * 2 + D * width * 2 + r * D * 10,
    )(grad, w, rows, grad_middle, vecs)


WIDE, NARROW, DP = "wide", "narrow", "dp"


def swap(value, axis, bit):
    size = lax.axis_size(axis)
    return lax.ppermute(value, axis, [(i, i ^ bit) for i in range(size)])


def hold(value, *deps):
    return lax.optimization_barrier((value, deps))[0]


class Pieces:
    def __init__(self, stack, tags):
        self.stack, self.tags = stack, tags

    def fetch(self, axis, bit, *deps):
        move = [bit if axis == name else 0 for name in (WIDE, NARROW, DP)]
        tags = [tuple(a ^ b for a, b in zip(tag, move)) for tag in self.tags]
        return Pieces(swap(hold(self.stack, *deps), axis, bit), tags)

    def after(self, *deps):
        return Pieces(hold(self.stack, *deps), self.tags)

    def rows(self, start, stop):
        return Pieces(self.stack[:, start:stop], self.tags)

    def join(self, *others):
        stack = jnp.concatenate([self.stack] + [o.stack for o in others])
        return Pieces(stack, sum([o.tags for o in others], self.tags))


def first_piece(piece):
    return Pieces(piece[None], [(0, 0, 0)])


def dp_sum(total):
    total = total.astype(F32)
    bit = 2
    while bit < lax.axis_size(DP):
        total = total + swap(total.astype(BF), DP, bit).astype(F32)
        bit *= 2
    return total


def qkv_plan(cols, heads_cols, parts, spots):
    rows = heads_cols // parts

    def plan(w, n, q):
        return [
            (0, spot, (rows, cols), (p * D + w * heads_cols + q * rows, n * cols))
            for p, spot in spots.items()
        ]

    return plan


def out_plan(cols, heads_cols, parts, spot, which=0):
    rows = heads_cols // parts
    return lambda w, n, q: [(which, spot, (rows, cols), (w * heads_cols + q * rows, n * cols))]


def flat_plan(cols, units, rows, base=0):
    return lambda w, n, q: [(0, (0, 0), (rows, units), (n * cols + base + q * rows, w * units))]


def sums_plan(cols, narrow, spot, which):
    return lambda w, n, q: [(which, spot, (16, cols), ((w * narrow + n) * 16, 0))]


def joined(*plans):
    return lambda w, n, q: [move for plan in plans for move in plan(w, n, q)]


def prep_body(cols, at_ref, *refs):
    (qkv_ref, out_ref, up_ref, down_ref), vectors = refs[:4], refs[4:12]
    first_ref, second_ref, up_a_ref, up_b_ref, down_part_ref = refs[12:17]
    held, sem = refs[17:-1], refs[-1]
    core, q = at_ref[2], at_ref[3]

    def block(ref, index, rows, base=0):
        return ref.at[pl.ds(pl.multiple_of(base + index * rows, 16), rows)]

    half = qkv_ref.shape[1] // 2
    ends = [
        (block(qkv_ref.at[0], core, half), first_ref.at[pl.ds(0, half)]),
        (block(out_ref, core, half), first_ref.at[pl.ds(half + 16, half)]),
    ]
    part = half // 2
    ends += [
        (block(qkv_ref.at[1 + p], q, part), second_ref.at[pl.ds(p * part, part)]) for p in range(2)
    ]
    ends.append((block(up_ref, core, up_a_ref.shape[0]), up_a_ref))
    ends.append((block(up_ref, q, up_b_ref.shape[0], up_ref.shape[0] // 2), up_b_ref))
    ends.append((block(down_ref, q, down_part_ref.shape[0]), down_part_ref))
    ends += list(zip(vectors, held))
    copies = [pltpu.make_async_copy(a, b, sem.at[k]) for k, (a, b) in enumerate(ends)]
    for copy in copies:
        copy.start()
    for copy in copies:
        copy.wait()
    lines = [ref[...].astype(F32).reshape(1, -1) for ref in held[:6]]
    both = held[6][...].astype(F32)
    lines.append(jnp.concatenate([both[:1], both[1:]], axis=1))
    wide_line = held[7][...].astype(F32).reshape(1, -1)
    lines += [wide_line[:, k : k + cols] for k in range(0, wide_line.shape[1], cols)]
    lines.append(jnp.zeros((16 - len(lines), cols), F32))
    first_ref[half : half + 16, :] = jnp.concatenate(lines, axis=0).astype(BF)


def prep(at, qkv_t, w_out, w_up, w_down, *vectors):
    cols, half = qkv_t.shape[2], qkv_t.shape[1] // 2
    rows, units = w_up.shape
    shapes = [
        (2 * half + 16, cols),
        (half, cols),
        (rows // 4, units),
        (rows // 8, units),
        (rows // 4, units),
    ]
    return pl.pallas_call(
        partial(prep_body, cols),
        out_shape=[struct(shape, BF) for shape in shapes],
        grid_spec=pltpu.PrefetchScalarGridSpec(
            num_scalar_prefetch=1,
            grid=(1,),
            in_specs=[IN_HBM] * (4 + len(vectors)),
            out_specs=[pl.BlockSpec(memory_space=pltpu.VMEM)] * len(shapes),
            scratch_shapes=[pltpu.VMEM(v.shape, BF) for v in vectors]
            + [pltpu.SemaphoreType.DMA((7 + len(vectors),))],
        ),
        compiler_params=pltpu.CompilerParams(vmem_limit_bytes=8 * MB),
        cost_estimate=pl.CostEstimate(
            flops=FLOPS_PER_US // 100, bytes_accessed=1024, transcendentals=0
        ),
    )(at, *[in_hbm(v) for v in (qkv_t, w_out, w_up, w_down, *vectors)])


def vec_body(wide, narrow, cols, first, tag_lists, at_ref, *refs):
    arrays, (vec_ref, qkv_bias_ref, up_bias_ref, held, sem) = refs[:-5], refs[-5:]
    copies = []
    for array, tags in zip(arrays, tag_lists):
        for k, (dw, dn, _) in enumerate(tags):
            slot = (at_ref[0] ^ dw) * narrow + (at_ref[1] ^ dn)
            source = array.at[k, pl.ds(first, 16)]
            copies.append(pltpu.make_async_copy(source, held.at[slot], sem.at[len(copies)]))
    for copy in copies:
        copy.start()
    for copy in copies:
        copy.wait()
    lines = [held[k].astype(F32) for k in range(wide * narrow)]
    for n in range(narrow):
        vec_ref[:, n * cols : (n + 1) * cols] = lines[n][:8]
    by_wide = [lines[w * narrow] for w in range(wide)]
    half = cols // 2
    q = jnp.concatenate([line[6:7, :half] for line in by_wide], axis=1)
    v = jnp.concatenate([line[6:7, half:] for line in by_wide], axis=1)
    qkv_bias_ref[...] = jnp.concatenate([q, jnp.zeros_like(q), v], axis=1)
    up_bias_ref[...] = jnp.concatenate(
        [line[i : i + 1] for line in by_wide for i in (7, 8)], axis=1
    )


def vectors_of(at, pieces, first, wide, narrow, cols, units):
    vmem = pl.BlockSpec(memory_space=pltpu.VMEM)
    return pl.pallas_call(
        partial(vec_body, wide, narrow, cols, first, [p.tags for p in pieces]),
        out_shape=[struct((8, D), F32), struct((1, 3 * D), F32), struct((1, wide * units), F32)],
        grid_spec=pltpu.PrefetchScalarGridSpec(
            num_scalar_prefetch=1,
            grid=(1,),
            in_specs=[ANY] * len(pieces),
            out_specs=[vmem] * 3,
            scratch_shapes=[
                pltpu.VMEM((wide * narrow, 16, cols), BF),
                pltpu.SemaphoreType.DMA((wide * narrow,)),
            ],
        ),
        compiler_params=pltpu.CompilerParams(vmem_limit_bytes=8 * MB),
        cost_estimate=pl.CostEstimate(flops=FLOPS_PER_US // 100, bytes_accessed=1024, transcendentals=0),
    )(at, *[p.stack for p in pieces])


def pack_body(*refs):
    out = refs[-1]
    at = 0
    for ref in refs[:-1]:
        for k in range(0, ref.shape[1], D):
            out[at : at + 1, :] = ref[:, k : k + D]
            at += 1
    if at < out.shape[0]:
        out[at:, :] = jnp.zeros((out.shape[0] - at, D), F32)


def pack(*rows):
    count = -(-sum(r.shape[1] for r in rows) // (8 * D)) * 8
    vmem = pl.BlockSpec(memory_space=pltpu.VMEM)
    return pl.pallas_call(
        pack_body,
        out_shape=struct((count, D), F32),
        in_specs=[vmem] * len(rows),
        out_specs=vmem,
        compiler_params=pltpu.CompilerParams(vmem_limit_bytes=8 * MB),
        cost_estimate=pl.CostEstimate(flops=FLOPS_PER_US // 100, bytes_accessed=1024, transcendentals=0),
    )(*rows)


ANY = pl.BlockSpec(memory_space=pl.ANY)
IN_HBM = pl.BlockSpec(memory_space=pltpu.HBM)


def owner_sums_body(wide, narrow, cols, *refs):
    out = refs[-1]
    narrow_refs, qkv_ref, up_ref = refs[:6], refs[6], refs[7]
    part, units = D // wide, up_ref.shape[1] // wide
    for w in range(wide):
        for n in range(narrow):
            lines = [ref[:, n * cols : (n + 1) * cols] for ref in narrow_refs]
            lines.append(
                jnp.concatenate(
                    [qkv_ref[:, p * D + w * part : p * D + (w + 1) * part] for p in (0, 2)], axis=1
                )
            )
            lines += [
                up_ref[:, w * units + k : w * units + k + cols] for k in range(0, units, cols)
            ]
            lines.append(jnp.zeros((16 - len(lines), cols), F32))
            at = (w * narrow + n) * 16
            out[at : at + 16, :] = jnp.concatenate(lines, axis=0).astype(BF)


def owner_sums(wide, narrow, cols, *rows):
    vmem = pl.BlockSpec(memory_space=pltpu.VMEM)
    return pl.pallas_call(
        partial(owner_sums_body, wide, narrow, cols),
        out_shape=struct((wide * narrow * 16, cols), BF),
        in_specs=[vmem] * len(rows),
        out_specs=vmem,
        compiler_params=pltpu.CompilerParams(vmem_limit_bytes=8 * MB),
        cost_estimate=pl.CostEstimate(
            flops=FLOPS_PER_US // 100, bytes_accessed=1024, transcendentals=0
        ),
    )(*rows)


def build_body(plans, counts, inverse, parts_by, at_ref, tag_ref, *refs):
    refs, sem = refs[:-1], refs[-1]
    lists = len(counts)
    wholes, arrays = (refs[:-lists], refs[-lists:]) if inverse else (refs[lists:], refs[:lists])

    def each(act):
        first, slot = 0, 0
        for array, plan, count, by in zip(arrays, plans, counts, parts_by):
            moves = len(plan(0, 0, 0))

            def step(k, carry, array=array, plan=plan, by=by, first=first, slot=slot, moves=moves):
                w, n, q = (
                    at_ref[axis] ^ tag_ref[i, first + k] for i, axis in enumerate((0, 1, by))
                )
                for m, (which, (at_row, at_lane), (rows, lanes), (row, lane)) in enumerate(
                    plan(w, n, q)
                ):
                    piece = array.at[k, pl.ds(at_row, rows), pl.ds(at_lane, lanes)]
                    whole = wholes[which].at[
                        pl.ds(pl.multiple_of(row, 16), rows),
                        pl.ds(pl.multiple_of(lane, 128), lanes),
                    ]
                    ends = (whole, piece) if inverse else (piece, whole)
                    act(pltpu.make_async_copy(*ends, sem.at[slot + k * moves + m]))
                return carry

            lax.fori_loop(0, count, step, 0, unroll=4)
            first, slot = first + count, slot + count * moves

    each(lambda copy: copy.start())
    each(lambda copy: copy.wait())


def move_pieces(at, arrays, plans, tag_lists, inverse, parts_by, shapes, pinned=0):
    counts = [len(tags) for tags in tag_lists]
    moves = sum(count * len(plan(0, 0, 0)) for count, plan in zip(counts, plans))
    table = jnp.array([tag for tags in tag_lists for tag in tags], jnp.int32).T
    return pl.pallas_call(
        partial(build_body, plans, counts, inverse, parts_by),
        out_shape=[
            pltpu.HBM(shape, BF) if i < pinned else struct(shape, BF)
            for i, shape in enumerate(shapes)
        ],
        grid_spec=pltpu.PrefetchScalarGridSpec(
            num_scalar_prefetch=2,
            grid=(1,),
            in_specs=[ANY] * len(arrays),
            out_specs=[ANY] * len(shapes),
            scratch_shapes=[pltpu.SemaphoreType.DMA((moves,))],
        ),
        compiler_params=pltpu.CompilerParams(vmem_limit_bytes=4 * MB),
        cost_estimate=pl.CostEstimate(
            flops=FLOPS_PER_US // 100, bytes_accessed=1024, transcendentals=0
        ),
    )(at, table, *arrays)


CORE, DP_INDEX = 2, 3


def build_weights(at, shape, *groups):
    lists = [(p, plan, by) for pieces, plan, by in groups for p in pieces]
    arrays, tags = [p.stack for p, _, _ in lists], [p.tags for p, _, _ in lists]
    plans, parts_by = [plan for _, plan, _ in lists], [by for _, _, by in lists]
    return move_pieces(at, arrays, plans, tags, False, parts_by, [shape])[0]


def cut_grads(at, grads, plan, tags, shape, part_at=CORE):
    lists = [[(w, n, q ^ dc) for w, n, q in tags] for dc in range(2)]
    shapes = [(len(tags),) + shape] * 2
    return move_pieces(at, grads, [plan] * 2, lists, True, [part_at] * 2, shapes, 1)


def fence_body(x_ref, out_ref):
    out_ref[...] = x_ref[...]


def fence(token, us=200):
    vmem = pl.BlockSpec(memory_space=pltpu.VMEM)
    return pl.pallas_call(
        fence_body,
        out_shape=struct(token.shape, token.dtype),
        in_specs=[vmem],
        out_specs=vmem,
        compiler_params=pltpu.CompilerParams(vmem_limit_bytes=MB, has_side_effects=True),
        cost_estimate=pl.CostEstimate(
            flops=us * FLOPS_PER_US, bytes_accessed=1024, transcendentals=0
        ),
    )(token)


class Chain:
    def __init__(self, keep, send):
        self.keep, self.send = keep, send

    def go(self, axis, bit):
        if isinstance(self.send, (list, tuple)):
            self.got = [swap(part, axis, bit) for part in self.send]
        else:
            self.got = swap(self.send, axis, bit)

    def fold(self, *deps):
        self.keep, self.send = halves_summed(self.keep, hold(self.got, *deps))

    def spread(self, *deps):
        got = hold(self.got, *deps)
        order = (0, 2, 1, 3)
        total = [k.astype(F32) + g.astype(F32) for k, g in zip(self.keep, got)]
        self.keep = total[0]
        self.send = [total[order.index(bit)].astype(BF) for bit in range(1, len(total))]
        self.got = [swap(piece, WIDE, bit) for bit, piece in enumerate(self.send, 1)]

    def all_of(self, *deps):
        total = self.keep
        for got in hold(self.got, *deps):
            total = total + got.astype(F32)
        return total

    def total(self, *deps):
        return self.keep[0].astype(F32) + hold(self.got, *deps)[0].astype(F32)


def doubled(value, bit, index):
    other = swap(value, DP, bit)
    return jnp.where(index == 0, jnp.stack([value, other]), jnp.stack([other, value]))


def halves_summed(kept, got):
    def halves(stack):
        if isinstance(stack, (list, tuple)):
            return stack
        half = stack.shape[0] // 2
        return stack[:half], stack[half:]

    first, second = [a.astype(F32) + b.astype(F32) for a, b in zip(halves(kept), halves(got))]
    return first, second.astype(BF)


def core_half(at, shard):
    rows = shard.shape[0] // 2
    return lax.dynamic_slice_in_dim(shard, at[2] * rows, rows, axis=0)


def quarter(at, shard):
    rows = shard.shape[0] // 4
    return lax.dynamic_slice_in_dim(shard, at[3] * rows, rows, axis=0)


def to_rows(blocks, narrow):
    got = lax.all_to_all(blocks, "narrow", 0, 0, tiled=True)
    return jnp.concatenate([got[n] for n in range(narrow)], axis=1)


def from_rows(rows, narrow):
    cols = rows.shape[1] // narrow
    blocks = jnp.stack([rows[:, n * cols : (n + 1) * cols] for n in range(narrow)])
    got = lax.all_to_all(blocks, "narrow", 0, 0, tiled=True)
    return got.reshape(-1, cols)


def gather_weight(shard, wide, narrow):
    got = lax.all_gather(shard.reshape(-1, 128), ("wide", "narrow"), axis=0, tiled=True)
    return got.reshape((wide, narrow) + shard.shape)


def scatter_grad(blocks):
    shape = blocks.shape[2:]
    got = lax.psum_scatter(
        blocks.reshape(-1, 128), ("wide", "narrow"), scatter_dimension=0, tiled=True
    )
    return lax.psum(got.astype(F32), "dp").reshape(shape)


def on_device(
    wide,
    narrow,
    patches,
    visible,
    w_qkv,
    b_qv,
    w_out,
    b_out,
    w_up,
    b_up,
    w_down,
    b_down,
    gain_one,
    shift_one,
    gain_two,
    shift_two,
    cotangent,
):
    images = visible.shape[0]
    pairs = images // 2
    cols = w_qkv.shape[0]
    heads_cols = w_qkv.shape[2]
    units = w_up.shape[1]
    swaps = cols % 128 == 0 and narrow == 2 and wide == 4 and lax.axis_size(DP) == 4
    swaps = swaps and pairs % 2 == 0

    at = jnp.stack(
        [
            lax.axis_index("wide"),
            lax.axis_index("narrow"),
            lax.axis_index("dp") % 2,
            lax.axis_index("dp"),
        ]
    ).astype(jnp.int32)

    index = (visible.reshape(pairs, 2, VISIBLE) + jnp.array([0, PATCHES])[None, :, None]).reshape(
        pairs, PAIR
    )
    index = jnp.pad(index, ((0, 0), (0, ROWS - PAIR)), constant_values=-1)[:, :, None]

    w_qkv_t = w_qkv.transpose(1, 2, 0)
    if swaps:
        pieces = prep(
            at,
            w_qkv_t,
            w_out,
            w_up,
            w_down,
            gain_one,
            shift_one,
            gain_two,
            shift_two,
            b_out,
            b_down,
            b_qv,
            b_up,
        )
        a_p, b_p, u_p, v_p, d_p = [first_piece(piece) for piece in pieces]

        def part_of(whole, side):
            return lax.dynamic_slice_in_dim(whole, side * cols, cols, axis=1)

        def join_cols(keep, got):
            return jnp.where(
                at[1] == 0,
                jnp.concatenate([keep, got], axis=1),
                jnp.concatenate([got, keep], axis=1),
            )

        mine, theirs = at[1], 1 - at[1]
        whole = (D, wide * units)

        b_z = [b_p.fetch(WIDE, bit) for bit in (1, 2, 3)]
        a_x, d_x = a_p.fetch(NARROW, 1), d_p.fetch(NARROW, 1)
        token = fence(hold(at, a_p.stack, b_p.stack, d_p.stack))
        a_p, d_p = a_p.join(a_x.after(token)), d_p.join(d_x.after(token))
        b_p = b_p.join(*[p.after(token) for p in b_z])

        b_x, a_z = b_p.fetch(NARROW, 1), a_p.fetch(WIDE, 2)
        rows_out = pick_rows(
            hold(at, a_p.stack, b_p.stack, d_p.stack), in_hbm(patches), index, cols
        )
        own = rows_out.shape[0] // 2
        rows_send = rows_out[:own]
        a_p, b_p = a_p.join(a_z.after(rows_send)), b_p.join(b_x.after(rows_send))

        b_y, a_z = b_p.fetch(DP, 2), a_p.fetch(WIDE, 1)
        v_z = v_p.fetch(WIDE, 2, rows_send)
        rows_got = swap(rows_send, NARROW, 1)
        cot_out = cot_rows(hold(at, rows_send, a_p.stack, b_p.stack), cotangent, pairs, cols)
        a_p, b_p = a_p.join(a_z.after(cot_out)), b_p.join(b_y.after(cot_out))
        v_p = v_p.join(v_z.after(cot_out))
        rows = join_cols(rows_out[own:], hold(rows_got, cot_out))

        started = [a_p.stack, b_p.stack, v_p.stack, rows]
        a_c, b_c = a_p.fetch(DP, 1, *started), b_p.fetch(DP, 1, *started)
        u_z, v_z = u_p.fetch(WIDE, 2, *started), v_p.fetch(WIDE, 1, *started)
        cot_send = hold(cot_out[:own], *started)
        cot_got = swap(cot_send, NARROW, 1)
        half = heads_cols // 2
        vecs, bias_qkv, bias_up = vectors_of(at, [a_p], half, wide, narrow, cols, units)
        hidden_one = norm(hold(rows, *started, cot_send), vecs)
        u_p, v_p = u_p.join(u_z.after(hidden_one)), v_p.join(v_z.after(hidden_one))
        a_c, b_c = a_c.after(hidden_one), b_c.after(hidden_one)

        u_z, v_x = u_p.fetch(WIDE, 1), v_p.fetch(NARROW, 1)
        started = [u_p.stack, v_p.stack]
        d_z = d_p.fetch(WIDE, 2, *started)
        part = heads_cols // 4
        qkv_t = build_weights(
            at,
            (3 * D, D),
            ([a_p, a_c], qkv_plan(cols, heads_cols, 2, {0: (0, 0)}), CORE),
            (
                [b_p, b_c],
                qkv_plan(cols, heads_cols, 4, {1: (0, 0), 2: (part, 0)}),
                DP_INDEX,
            ),
        )
        out_w = build_weights(
            at, (D, D), ([a_p, a_c], out_plan(cols, heads_cols, 2, (half + 16, 0)), CORE)
        )
        triple = qkv(hold(hidden_one, *started), qkv_t, bias_qkv)
        u_p, v_p = u_p.join(u_z.after(triple)), v_p.join(v_x.after(triple))
        d_p = d_p.join(d_z.after(triple))
        cot = join_cols(cot_out[own:], hold(cot_got, triple))

        u_x, v_y, d_z = u_p.fetch(NARROW, 1), v_p.fetch(DP, 2), d_p.fetch(WIDE, 1)
        mixed, prob = attend(hold(triple, u_p.stack, v_p.stack, d_p.stack, cot))
        d_p = d_p.join(d_z.after(mixed))
        u_x, v_y = u_x.after(mixed), v_y.after(mixed)

        u_all, v_all = [u_p, u_x], [v_p, v_y]
        started = [d_p.stack, u_x.stack, v_y.stack]
        d_y = d_p.fetch(DP, 2)
        u_c = [p.fetch(DP, 1, *started) for p in u_all]
        v_c = [p.fetch(DP, 1, *started) for p in v_all]
        middle, hidden_two = mix(hold(mixed, *started), out_w, rows, vecs)
        half_flat = flat_plan(cols, units, cols // 2)
        part_flat = flat_plan(cols, units, cols // 4)
        up_w = build_weights(
            at,
            whole,
            (u_all + [p.after(hidden_two) for p in u_c], part_flat, CORE),
            (
                v_all + [p.after(hidden_two) for p in v_c],
                flat_plan(cols, units, cols // 8, cols // 2),
                DP_INDEX,
            ),
        )
        active, slope = up(hidden_two, up_w, bias_up)

        x_first = [(w, n, 0) for n in range(2) for w in (0, 2, 1, 3)]
        y_first = [(w, n, dy) for dy in (0, 2) for n in range(2) for w in (0, 2, 1, 3)]
        gd_keep, gd_send = outer_pieces(at, cot, in_hbm(active), cols, wide)
        gb_down = jnp.sum(cot, 0, dtype=F32)[None]
        d_y = d_y.after(*gd_send)
        d_c = [p.fetch(DP, 1, d_y.stack) for p in (d_p, d_y)]
        g_d = Chain(gd_keep, [hold(piece, d_y.stack) for piece in gd_send])
        g_d.go(DP, 1)
        d_c = [p.after(*g_d.send) for p in d_c]
        down_w = build_weights(at, whole, ([d_p, d_y] + d_c, part_flat, DP_INDEX))
        g_d.fold(down_w)
        g_d.go(NARROW, 1)
        grad_inner, gu_keep, gu_send, gb_up = inner_back_pieces(
            at, cot, hold(down_w, g_d.send), in_hbm(slope), hidden_two, cols, wide
        )

        result = down(hold(in_hbm(active), grad_inner), down_w, vecs, middle)
        g_u = Chain(gu_keep, [hold(piece, result) for piece in gu_send])
        g_u.go(DP, 1)
        g_d.fold(*g_u.send)
        g_d.go(WIDE, 1)
        g_u.fold(g_d.send)
        g_u.go(DP, 2)
        grad_middle, branch, gg_two, gs_two, gb_out = middle_back(
            hold(grad_inner, g_d.send, g_u.send), up_w, middle, cot, vecs
        )
        grad_mixed, gw_out = mixed_back(branch, out_w, mixed)

        g_d.fold(grad_mixed)
        g_d.go(WIDE, 2)
        result_send = hold(part_of(result, theirs), grad_mixed)
        result_got = swap(result_send, NARROW, 1)
        groups = rows.shape[0] // ROWS
        grad_triple = attend_back(
            triple, in_hbm(prob), hold(grad_mixed, g_d.send, result_send), 0, groups
        )
        grad_rows, gg_one, gs_one = first_back(grad_triple, qkv_t, rows, grad_middle, vecs)

        d_sum = g_d.total(grad_rows)
        d_got = swap(d_sum.astype(BF), DP, 2)
        g_u.fold(grad_rows)
        g_u.go(NARROW, 1)
        result_got = hold(result_got, grad_rows)
        gw_qkv, gb_qkv = qkv_grad(hold(grad_triple, d_sum, g_u.send, result_got), hidden_one)
        sums = owner_sums(
            wide,
            narrow,
            cols,
            gg_one,
            gs_one,
            gg_two,
            gs_two,
            gb_out,
            gb_down,
            gb_qkv,
            gb_up,
        )

        part = heads_cols // 4
        g_q = cut_grads(
            at,
            [gw_qkv],
            qkv_plan(cols, heads_cols, 4, {p: (p * part, 0) for p in range(3)}),
            y_first,
            (3 * part, cols),
            DP_INDEX,
        )
        g_q = Chain(*g_q)
        g_q.go(DP, 1)
        rest_plan = joined(
            out_plan(cols, heads_cols, 2, (0, 0), 0), sums_plan(cols, narrow, (half, 0), 1)
        )
        g_r = Chain(*cut_grads(at, [gw_out, sums], rest_plan, x_first, (half + 16, cols)))
        g_r.go(DP, 1)
        d_sum = d_sum + hold(d_got, g_r.send).astype(F32)
        d_got = swap(d_sum, DP, 1)
        g_u.fold(g_r.send)
        g_u.go(WIDE, 1)
        rows_send = hold(part_of(grad_rows, theirs), g_r.send).astype(BF)
        rows_back = swap(rows_send, NARROW, 1)
        token = fence(hold(vecs, g_q.send, d_sum, g_u.send, rows_send))

        g_q.fold(token)
        g_q.go(DP, 2)
        g_r.fold(token, g_q.send)
        g_r.go(NARROW, 1)
        g_u.fold(g_q.send, g_r.send)
        g_u.go(WIDE, 2)
        rows_back = hold(rows_back, g_u.send)
        grad_patches = put_rows(at, part_of(grad_rows, mine), rows_back, index, cols)

        def in_order(value, other, index):
            return jnp.where(index == 0, jnp.stack([value, other]), jnp.stack([other, value]))

        g_q.fold(grad_patches)
        g_q.go(NARROW, 1)
        g_r.spread(grad_patches, g_q.send)
        u_sum = g_u.total(g_q.send, *g_r.send)
        keep = hold(part_of(result, mine), g_q.send, u_sum, *g_r.send)
        block_output = flat_rows(at, keep, result_got, cols)
        g_q.spread(block_output)
        r_sum = g_r.all_of(block_output)
        r_got = swap(r_sum.astype(BF), DP, 2)
        u_got = swap(u_sum.astype(BF), DP, 2)
        token = fence(hold(token, r_sum, u_sum, *g_q.send))
        q_sum = g_q.all_of(token)
        q_got = [swap(q_sum.astype(BF), DP, bit) for bit in (1, 2, 3)]
        r_sum = r_sum + hold(r_got, q_sum).astype(F32)
        r_got = swap(r_sum[:half], DP, 1)
        u_sum = in_order(u_sum, hold(u_got, token).astype(F32), at[3] // 2)
        u_got = swap(u_sum, DP, 1)
        g_down = in_order(d_sum, d_got, at[2]).reshape(cols, units)
        g_up = in_order(u_sum, u_got, at[2]).transpose(1, 0, 2, 3).reshape(cols, units)
        q_got = [got.astype(F32) for got in q_got]
        pairs_of = [in_order(q_sum, q_got[0], at[2]), in_order(q_got[1], q_got[2], at[2])]
        q_sum = in_order(*pairs_of, at[3] // 2).reshape(4, 3, part, cols)
        g_out = in_order(r_sum[:half], r_got, at[2]).reshape(heads_cols, cols)
        g_qkv = q_sum.transpose(3, 1, 0, 2).reshape(cols, 3, heads_cols)
        grad_patches = grad_patches.reshape(1, -1)
        lines = r_sum[half:]
        vector_grads = [lines[i] for i in range(6)]
        g_bqv = lines[6].reshape(2, heads_cols)
        g_bup = lines[7:9].reshape(units)
    else:
        table = patches.reshape(images, PATCHES, cols)
        rows_mine = jnp.take_along_axis(table, visible[:, :, None], axis=1)
        rows_mine = jnp.pad(
            rows_mine.reshape(pairs, PAIR, cols), ((0, 0), (0, ROWS - PAIR), (0, 0))
        )
        cot_mine = jnp.pad(
            cotangent.reshape(pairs, PAIR, cols), ((0, 0), (0, ROWS - PAIR), (0, 0))
        )
        rows = to_rows(rows_mine.reshape(narrow, -1, cols), narrow)
        cot = to_rows(cot_mine.reshape(narrow, -1, cols), narrow)
        vec = jnp.concatenate(
            [gain_one, shift_one, gain_two, shift_two, b_out, b_down, b_qv.reshape(-1), b_up]
        )
        vec = lax.all_gather(vec, ("wide", "narrow"), axis=0, tiled=False).astype(F32)
        qkv_t = gather_weight(w_qkv_t, wide, narrow)
        qkv_t = qkv_t.transpose(2, 0, 3, 1, 4).reshape(3 * D, D)
        out_w = gather_weight(w_out, wide, narrow).transpose(0, 2, 1, 3).reshape(D, D)
        up_w = gather_weight(w_up, wide, narrow).transpose(1, 2, 0, 3).reshape(D, -1)
        down_w = gather_weight(w_down, wide, narrow).transpose(1, 2, 0, 3).reshape(D, -1)
        vec = vec.reshape(wide, narrow, -1)
        vecs = vec[0, :, : 6 * cols].reshape(narrow, 6, cols).transpose(1, 0, 2).reshape(6, D)
        vecs = jnp.pad(vecs, ((0, 2), (0, 0)))
        by_wide = vec[:, 0, 6 * cols :]
        bias_q = by_wide[:, :heads_cols].reshape(1, D)
        bias_v = by_wide[:, heads_cols : 2 * heads_cols].reshape(1, D)
        bias_qkv = jnp.concatenate([bias_q, jnp.zeros((1, D), F32), bias_v], axis=1)
        bias_up = by_wide[:, 2 * heads_cols :].reshape(1, -1)

        hidden_one = norm(rows, vecs)
        triple = qkv(hidden_one, qkv_t, bias_qkv)
        mixed, prob = attend(triple)
        middle, hidden_two = mix(mixed, out_w, rows, vecs)
        active, slope = up(hidden_two, up_w, bias_up)
        result = down(active, down_w, vecs, middle)
        gw_down = outer(cot, active)
        gb_down = jnp.sum(cot, 0, dtype=F32)[None]
        grad_inner, gw_up, gb_up = inner_back(cot, down_w, slope, hidden_two)
        grad_middle, branch, gg_two, gs_two, gb_out = middle_back(
            grad_inner, up_w, middle, cot, vecs
        )
        grad_mixed, gw_out = mixed_back(branch, out_w, mixed)
        grad_triple = attend_back(triple, prob, grad_mixed, 0, rows.shape[0] // ROWS)
        gw_qkv, gb_qkv = qkv_grad(grad_triple, hidden_one)
        grad_rows, gg_one, gs_one = first_back(grad_triple, qkv_t, rows, grad_middle, vecs)
        sums = pack(gg_one, gs_one, gg_two, gs_two, gb_out, gb_down, gb_qkv, gb_up)

        result = from_rows(result, narrow)
        grad_rows = from_rows(grad_rows, narrow)
        block_output = result.reshape(pairs, ROWS, cols)[:, :PAIR].reshape(1, -1)
        grad_rows = grad_rows.reshape(pairs, ROWS, cols)[:, :PAIR].reshape(images, VISIBLE, cols)
        grad_patches = (
            jnp.zeros((images, PATCHES, cols), F32)
            .at[jnp.arange(images)[:, None], visible]
            .set(grad_rows)
            .reshape(1, -1)
        )
        g_down = scatter_grad(gw_down.reshape(narrow, cols, wide, units).transpose(2, 0, 1, 3))
        g_up = scatter_grad(gw_up.reshape(narrow, cols, wide, units).transpose(2, 0, 1, 3))
        g_out = scatter_grad(gw_out.reshape(wide, heads_cols, narrow, cols).transpose(0, 2, 1, 3))
        g_qkv = scatter_grad(
            gw_qkv.reshape(3, wide, heads_cols, narrow, cols).transpose(1, 3, 0, 2, 4)
        )
        g_qkv = g_qkv.transpose(2, 0, 1)
        sums = lax.psum(sums, ("dp", "wide", "narrow"))
        sums = sums.reshape(-1)
        vector_grads = [
            lax.dynamic_slice_in_dim(sums, i * D + at[1] * cols, cols) for i in range(6)
        ]
        g_bqv = jnp.stack(
            [
                lax.dynamic_slice_in_dim(sums, (6 + i) * D + at[0] * heads_cols, heads_cols)
                for i in (0, 2)
            ]
        )
        g_bup = lax.dynamic_slice_in_dim(sums, 9 * D + at[0] * units, units)

    return (
        block_output,
        grad_patches,
        g_qkv,
        g_bqv,
        g_out,
        vector_grads[4],
        g_up,
        g_bup,
        g_down,
        vector_grads[5],
        vector_grads[0],
        vector_grads[1],
        vector_grads[2],
        vector_grads[3],
    )


def solution(mesh):
    in_specs = (
        P("narrow", ("dp", "wide")),
        P(("dp", "wide"), None),
        P("narrow", None, "wide"),
        P(None, "wide"),
        P("wide", "narrow"),
        P("narrow"),
        P("narrow", "wide"),
        P("wide"),
        P("narrow", "wide"),
        P("narrow"),
        P("narrow"),
        P("narrow"),
        P("narrow"),
        P("narrow"),
        P("narrow", ("dp", "wide")),
    )
    out_specs = (
        P("narrow", ("dp", "wide")),
        P("narrow", ("dp", "wide")),
        P("narrow", None, "wide"),
        P(None, "wide"),
        P("wide", "narrow"),
        P("narrow"),
        P("narrow", "wide"),
        P("wide"),
        P("narrow", "wide"),
        P("narrow"),
        P("narrow"),
        P("narrow"),
        P("narrow"),
        P("narrow"),
    )
    body = partial(on_device, mesh.shape["wide"], mesh.shape["narrow"])
    return jax.shard_map(body, mesh=mesh, in_specs=in_specs, out_specs=out_specs, check_vma=False)
```

```python
from functools import partial

import jax
import jax.numpy as jnp
from jax import lax
from jax.experimental import pallas as pl
from jax.experimental.pallas import tpu as pltpu
from jax.sharding import PartitionSpec as P

D = 768
HEAD_DIM = 64
HEADS = 12
PATCHES = 196
VISIBLE = 49
PAIR = 2 * VISIBLE
ROWS = 112
TILE = 768
EPS = 1e-06
BF = jnp.bfloat16
F32 = jnp.float32
MB = 1024 * 1024


def dot(a, b, ca, cb):
    return lax.dot_general(a, b, (((ca,), (cb,)), ((), ())), preferred_element_type=F32)


FLOPS_PER_US = 540000000


def call(body, grid, ins, outs, shapes, scratch=(), prefetch=0, us=1.0, nbytes=0, vmem=32):
    return pl.pallas_call(
        body,
        out_shape=shapes,
        grid_spec=pltpu.PrefetchScalarGridSpec(
            num_scalar_prefetch=prefetch,
            grid=grid,
            in_specs=ins,
            out_specs=outs,
            scratch_shapes=scratch,
        ),
        compiler_params=pltpu.CompilerParams(
            dimension_semantics=("arbitrary",) * len(grid), vmem_limit_bytes=vmem * MB
        ),
        cost_estimate=pl.CostEstimate(
            flops=int(us * FLOPS_PER_US), bytes_accessed=1024, transcendentals=0
        ),
    )


def in_hbm(value):
    return pltpu.with_memory_space_constraint(value, pltpu.HBM)


def spec(shape, index):
    return pl.BlockSpec(shape, index)


def struct(shape, dtype):
    return jax.ShapeDtypeStruct(shape, dtype)


def together(own):
    return next(count for count in (4, 2, 1) if own % count == 0)


def strided(start, count, lanes):
    return [pl.ds(start + k, count, stride=lanes) for k in range(lanes)]


def one_hot(index):
    return (index == lax.broadcasted_iota(jnp.int32, (ROWS, 2 * PATCHES), 1)).astype(BF)


def pick_body(cols, count, at_ref, patch_ref, index_ref, rows_ref, wide_ref):
    lanes = cols // 128
    wide_ref[...] = patch_ref[...].astype(F32).reshape(wide_ref.shape)
    for j in range(count):
        places = strided(j * 2 * PATCHES * lanes, 2 * PATCHES, lanes)
        both = jnp.concatenate([wide_ref[place, :] for place in places], axis=1).astype(BF)
        rows_ref[j * ROWS : (j + 1) * ROWS, :] = dot(one_hot(index_ref[j]), both, 1, 0).astype(BF)


def owner_first_sent(steps):
    own = steps // 2

    def source(i, at):
        return (i // own ^ 1 ^ at[1]) * own + i % own

    return source


def pick_rows(at, patches, index, cols):
    pairs = index.shape[0]
    count = together(pairs // 2)
    width = 2 * PATCHES * cols * count
    source = owner_first_sent(pairs // count)
    return call(
        partial(pick_body, cols, count),
        (pairs // count,),
        [
            spec((1, width), lambda i, at: (0, source(i, at))),
            spec((count, ROWS, 1), lambda i, at: (source(i, at), 0, 0)),
        ],
        spec((count * ROWS, cols), lambda i, at: (i, 0)),
        struct((pairs * ROWS, cols), BF),
        [pltpu.VMEM((width // 128, 128), F32)],
        prefetch=1,
        us=200,
        nbytes=pairs * width * 4,
    )(at, patches, index)


def cot_body(cols, count, at_ref, cot_ref, rows_ref, scr):
    lanes = cols // 128
    scr[...] = cot_ref[...].astype(F32).reshape(scr.shape)
    for j in range(count):
        places = strided(j * PAIR * lanes, PAIR, lanes)
        cot = jnp.concatenate([scr[place, :] for place in places], axis=1)
        rows_ref[j * ROWS : (j + 1) * ROWS, :] = jnp.concatenate(
            [cot, jnp.zeros((ROWS - PAIR, cols), F32)], axis=0
        ).astype(BF)


def cot_rows(at, cotangent, pairs, cols):
    count = together(pairs // 2)
    width = PAIR * cols * count
    source = owner_first_sent(pairs // count)
    return call(
        partial(cot_body, cols, count),
        (pairs // count,),
        [spec((1, width), lambda i, at: (0, source(i, at)))],
        spec((count * ROWS, cols), lambda i, at: (i, 0)),
        struct((pairs * ROWS, cols), BF),
        [pltpu.VMEM((width // 128, 128), F32)],
        prefetch=1,
        us=200,
        nbytes=pairs * width * 4,
    )(at, cotangent)


def own_block(at_ref, keep_ref, got_ref, j):
    own = pl.num_programs(0) // 2
    mine = pl.program_id(0) // own == at_ref[1]
    rows = slice(j * ROWS, (j + 1) * ROWS)
    return jnp.where(mine, keep_ref[rows, :].astype(F32), got_ref[rows, :].astype(F32))


def put_body(cols, count, at_ref, keep_ref, got_ref, index_ref, out_ref):
    lanes = cols // 128
    for j in range(count):
        hit = one_hot(index_ref[j])
        rest = own_block(at_ref, keep_ref, got_ref, j)
        parts = []
        for _ in range(3):
            parts.append(rest.astype(BF))
            rest = rest - parts[-1].astype(F32)
        total = dot(jnp.concatenate([hit] * 3), jnp.concatenate(parts), 0, 0)
        for k, place in enumerate(strided(j * 2 * PATCHES * lanes, 2 * PATCHES, lanes)):
            out_ref[place, :] = total[:, k * 128 : (k + 1) * 128]


def put_rows(at, keep, got, index, cols):
    pairs = index.shape[0]
    count = together(pairs // 2)
    own = pairs // count // 2
    tall = count * 2 * PATCHES * cols // 128
    rows = spec((count * ROWS, cols), lambda i, at: (i % own, 0))
    return call(
        partial(put_body, cols, count),
        (pairs // count,),
        [rows, rows, spec((count, ROWS, 1), lambda i, at: (i, 0, 0))],
        spec((tall, 128), lambda i, at: (i, 0)),
        struct((pairs // count * tall, 128), F32),
        prefetch=1,
        us=200,
        nbytes=pairs * (tall * 512 + ROWS * cols * 4),
    )(at, keep, got, index)


def flat_body(cols, count, at_ref, keep_ref, got_ref, out_ref, scr):
    lanes = cols // 128
    for j in range(count):
        rows = own_block(at_ref, keep_ref, got_ref, j)
        for k, place in enumerate(strided(j * PAIR * lanes, PAIR, lanes)):
            scr[place, :] = rows[:PAIR, k * 128 : (k + 1) * 128]
    out_ref[...] = scr[...].reshape(out_ref.shape).astype(BF)


def flat_rows(at, keep, got, cols):
    pairs = 2 * (keep.shape[0] // ROWS)
    count = together(pairs // 2)
    own = pairs // count // 2
    width = PAIR * cols * count
    rows = spec((count * ROWS, cols), lambda i, at: (i % own, 0))
    return call(
        partial(flat_body, cols, count),
        (pairs // count,),
        [rows, rows],
        spec((1, width), lambda i, at: (0, i)),
        struct((1, pairs // count * width), BF),
        [pltpu.VMEM((width // 128, 128), F32)],
        prefetch=1,
        us=200,
        nbytes=pairs * width * 6,
    )(at, keep, got)


def stats(rows):
    mean = jnp.mean(rows, 1, keepdims=True)
    off = rows - mean
    inv = lax.rsqrt(jnp.mean(off * off, 1, keepdims=True) + EPS)
    return off * inv, inv


GAIN_ONE, SHIFT_ONE, GAIN_TWO, SHIFT_TWO, BIAS_OUT, BIAS_DOWN = range(6)


def vec_row(vec_ref, i):
    return vec_ref[i : i + 1, :]


def norm_body(rows_ref, vec_ref, out_ref):
    normed, _ = stats(rows_ref[...].astype(F32))
    out_ref[...] = (normed * vec_row(vec_ref, GAIN_ONE) + vec_row(vec_ref, SHIFT_ONE)).astype(BF)


def norm(rows, vec):
    r = rows.shape[0]
    return call(
        norm_body,
        (r // ROWS,),
        [spec((ROWS, D), lambda i: (i, 0)), spec((8, D), lambda i: (0, 0))],
        spec((ROWS, D), lambda i: (i, 0)),
        struct((r, D), BF),
        us=200,
        nbytes=r * D * 4,
    )(rows, vec)


def qkv_body(hidden_ref, w_ref, bias_ref, out_ref):
    out_ref[...] = (dot(hidden_ref[...], w_ref[...], 1, 1) + bias_ref[...]).astype(BF)


def qkv(hidden, w, bias):
    r = hidden.shape[0]
    return call(
        qkv_body,
        (3 * D // TILE,),
        [
            spec((r, D), lambda j: (0, 0)),
            spec((TILE, D), lambda j: (j, 0)),
            spec((1, TILE), lambda j: (0, j)),
        ],
        spec((r, TILE), lambda j: (0, j)),
        struct((r, 3 * D), BF),
        us=13,
        nbytes=r * D * 8 + 3 * D * D * 2,
    )(hidden, w, bias)


def same_image():
    at_row = lax.broadcasted_iota(jnp.int32, (ROWS, ROWS), 0)
    at_col = lax.broadcasted_iota(jnp.int32, (ROWS, ROWS), 1)

    def image(at):
        return (at >= VISIBLE).astype(jnp.int32) + (at >= PAIR).astype(jnp.int32)

    return image(at_row) == image(at_col)


def side_by_side(block):
    left = lax.broadcasted_iota(jnp.int32, (ROWS, 128), 1) < HEAD_DIM
    none = jnp.zeros_like(block)
    return jnp.concatenate([jnp.where(left, block, none), jnp.where(left, none, block)])


def both_heads(stack):
    left = lax.broadcasted_iota(jnp.int32, (ROWS, 128), 1) < HEAD_DIM
    return jnp.where(left, stack[:ROWS], stack[ROWS:])


def pair_of(ref, part, pair):
    return ref[:, part * D + pair * 128 : part * D + (pair + 1) * 128]


def attend_body(triple_ref, mixed_ref, prob_ref):
    keep = same_image()[None]
    for pair in range(HEADS // 2):
        q, k, v = (pair_of(triple_ref, part, pair) for part in range(3))
        scores = dot(side_by_side(k), q, 1, 1).reshape(2, ROWS, ROWS) * HEAD_DIM**-0.5
        scores = jnp.where(keep, scores, -1e30)
        expo = jnp.exp(scores - jnp.max(scores, 1, keepdims=True))
        prob = expo / jnp.sum(expo, 1, keepdims=True)
        prob_ref[0, 2 * pair : 2 * pair + 2] = prob
        low = prob.astype(BF).reshape(2 * ROWS, ROWS)
        mixed_ref[:, pair * 128 : (pair + 1) * 128] = dot(low, side_by_side(v), 0, 0).astype(BF)


def attend(triple):
    groups = triple.shape[0] // ROWS
    return call(
        attend_body,
        (groups,),
        [spec((ROWS, 3 * D), lambda g: (g, 0))],
        [spec((ROWS, D), lambda g: (g, 0)), spec((1, HEADS, ROWS, ROWS), lambda g: (g, 0, 0, 0))],
        [struct((groups * ROWS, D), BF), pltpu.HBM((groups, HEADS, ROWS, ROWS), F32)],
        us=200,
        nbytes=groups * ROWS * (8 * D + HEADS * 512),
    )(triple)


def mix_body(mixed_ref, w_ref, rows_ref, vec_ref, middle_ref, hidden_ref):
    branch = dot(mixed_ref[...], w_ref[...], 1, 0) + vec_row(vec_ref, BIAS_OUT)
    middle = rows_ref[...].astype(F32) + branch
    middle_ref[...] = middle
    normed, _ = stats(middle)
    hidden_ref[...] = (
        normed * vec_row(vec_ref, GAIN_TWO) + vec_row(vec_ref, SHIFT_TWO)
    ).astype(BF)


def row_tile(r):
    return r // 2


def mix(mixed, w, rows, vec):
    r = rows.shape[0]
    m = r // 4 if r % 64 == 0 else row_tile(r)
    row = spec((m, D), lambda i: (i, 0))
    return call(
        mix_body,
        (r // m,),
        [row, spec((D, D), lambda i: (0, 0)), row, spec((8, D), lambda i: (0, 0))],
        [row, row],
        [struct((r, D), F32), struct((r, D), BF)],
        us=16,
        nbytes=r * D * 10 + D * D * 2,
    )(mixed, w, rows, vec)


def up_body(hidden_ref, w_ref, bias_ref, active_ref, slope_ref):
    inner = dot(hidden_ref[...], w_ref[...], 1, 0) + bias_ref[...]
    phi = 0.5 * (1.0 + lax.erf(inner * (0.5**0.5)))
    active_ref[...] = (inner * phi).astype(BF)
    slope_ref[...] = phi + inner * (jnp.exp(-0.5 * inner * inner) * 0.3989422804014327)


def up(hidden, w, bias):
    r = hidden.shape[0]
    units = w.shape[1]
    tile = spec((r, TILE), lambda j: (0, j))
    return call(
        up_body,
        (units // TILE,),
        [
            spec((r, D), lambda j: (0, 0)),
            spec((D, TILE), lambda j: (0, j)),
            spec((1, TILE), lambda j: (0, j)),
        ],
        [tile, tile],
        [pltpu.HBM((r, units), BF), pltpu.HBM((r, units), F32)],
        us=0.01,
        nbytes=r * D * 2 + D * units * 2 + r * units * 6,
    )(hidden, w, bias)


def down_body(active_ref, w_ref, vec_ref, middle_ref, out_ref):
    branch = dot(active_ref[...], w_ref[...], 1, 1) + vec_row(vec_ref, BIAS_DOWN)
    out_ref[...] = (middle_ref[...] + branch).astype(BF)


def down(active, w, vec, middle):
    r, units = active.shape
    m = row_tile(r)
    return call(
        down_body,
        (r // m,),
        [
            spec((m, units), lambda i: (i, 0)),
            spec((D, units), lambda i: (0, 0)),
            spec((8, D), lambda i: (0, 0)),
            spec((m, D), lambda i: (i, 0)),
        ],
        spec((m, D), lambda i: (i, 0)),
        struct((r, D), BF),
        us=0.01,
        nbytes=r * units * 2 + D * units * 2 + r * D * 6,
    )(active, w, vec, middle)


def outer_body(left_ref, right_ref, out_ref, turned):
    @pl.when(pl.program_id(0) == 0)
    def _():
        turned[...] = left_ref[...].T

    out_ref[...] = dot(turned[...], right_ref[...], 1, 0).astype(BF)


def outer(left, right):
    r, width = right.shape
    rows = left.shape[1]
    return call(
        outer_body,
        (width // TILE,),
        [spec((r, rows), lambda j: (0, 0)), spec((r, TILE), lambda j: (0, j))],
        spec((rows, TILE), lambda j: (0, j)),
        struct((rows, width), BF),
        [pltpu.VMEM((rows, r), BF)],
        us=0.01,
        nbytes=r * rows * 2 + r * width * 2 + rows * width * 2,
    )(left, right)


def inner_back_body(cot_ref, w_ref, slope_ref, hidden_ref, grad_ref, gw_ref, gb_ref, turned):
    @pl.when(pl.program_id(0) == 0)
    def _():
        turned[...] = hidden_ref[...].T

    grad = (dot(cot_ref[...], w_ref[...], 1, 0) * slope_ref[...]).astype(BF)
    grad_ref[...] = grad
    gw_ref[...] = dot(turned[...], grad, 1, 0).astype(BF)
    gb_ref[...] = jnp.sum(grad.astype(F32), 0, keepdims=True)


def inner_back(cot, w, slope, hidden):
    r, units = slope.shape
    full = spec((r, D), lambda j: (0, 0))
    col = spec((D, TILE), lambda j: (0, j))
    tile = spec((r, TILE), lambda j: (0, j))
    return call(
        inner_back_body,
        (units // TILE,),
        [full, col, tile, full],
        [tile, col, spec((1, TILE), lambda j: (0, j))],
        [pltpu.HBM((r, units), BF), struct((D, units), BF), struct((1, units), F32)],
        [pltpu.VMEM((D, r), BF)],
        us=200,
        nbytes=r * D * 4 + D * units * 4 + r * units * 6,
    )(cot, w, slope, hidden)


def place(w):
    return w % 2 * 2 + w // 2


def turn_blocks(left_ref, plain, turned, offsets):
    plain[...] = left_ref[...].T
    rows = plain.shape[0] // len(offsets)
    for i, offset in enumerate(offsets):
        turned[i * rows : (i + 1) * rows, :] = plain[pl.ds(pl.multiple_of(offset, 16), rows), :]


def outer_pieces_body(cols, at_ref, left_ref, right_ref, *refs):
    outs, (plain, turned) = refs[:4], refs[4:]

    @pl.when(pl.program_id(0) == 0)
    def _():
        offsets = [
            (n ^ at_ref[1]) * cols + (at_ref[2] ^ side) * (cols // 2)
            for side in range(2)
            for n in range(2)
        ]
        turn_blocks(left_ref, plain, turned, offsets)

    grad = dot(turned[...], right_ref[...], 1, 0).astype(BF)
    half = cols // 2
    for i, out in enumerate(outs):
        out[...] = grad[i * half : (i + 1) * half].reshape(out.shape)


def outer_pieces(at, left, right, cols, wide):
    r, width = right.shape
    rows, units = left.shape[1], width // wide
    shape = (wide, cols // 2, units)
    block = spec((1, cols // 2, units), lambda j, at: (place(j ^ at[0]), 0, 0))
    out = call(
        partial(outer_pieces_body, cols),
        (wide,),
        [spec((r, rows), lambda j, at: (0, 0)), spec((r, units), lambda j, at: (0, j))],
        [block] * 4,
        [pltpu.HBM(shape, BF)] * 2 + [struct(shape, BF)] * 2,
        [pltpu.VMEM((rows, r), BF)] * 2,
        prefetch=1,
        us=0.01,
        nbytes=r * rows * 2 + r * width * 2 + rows * width * 2,
    )(at, left, right)
    return out[:2], out[2:]


def inner_back_pieces_body(cols, at_ref, cot_ref, w_ref, slope_ref, hidden_ref, *refs):
    grad_ref, outs, gb_ref, plain, turned = refs[0], refs[1:5], refs[5], refs[6], refs[7]
    part = cols // 4

    @pl.when(pl.program_id(0) == 0)
    def _():
        offsets = [
            (n ^ at_ref[1]) * cols + (at_ref[3] ^ (2 * dy) ^ side) * part
            for side in range(2)
            for dy in range(2)
            for n in range(2)
        ]
        turn_blocks(hidden_ref, plain, turned, offsets)

    grad = (dot(cot_ref[...], w_ref[...], 1, 0) * slope_ref[...]).astype(BF)
    grad_ref[...] = grad
    gb_ref[...] = jnp.sum(grad.astype(F32), 0, keepdims=True)
    outer_grad = dot(turned[...], grad, 1, 0).astype(BF)
    for i, out in enumerate(outs):
        out[...] = outer_grad[2 * i * part : 2 * (i + 1) * part].reshape(out.shape)


def inner_back_pieces(at, cot, w, slope, hidden, cols, wide):
    r, width = slope.shape
    units, part = width // wide, cols // 4
    shape = (2, wide, part, units)
    full = spec((r, D), lambda j, at: (0, 0))
    tile = spec((r, units), lambda j, at: (0, j))
    block = spec((2, 1, part, units), lambda j, at: (0, place(j ^ at[0]), 0, 0))
    out = call(
        partial(inner_back_pieces_body, cols),
        (wide,),
        [full, spec((D, units), lambda j, at: (0, j)), tile, full],
        [tile] + [block] * 4 + [spec((1, units), lambda j, at: (0, j))],
        [pltpu.HBM((r, width), BF)]
        + [pltpu.HBM(shape, BF)] * 2
        + [struct(shape, BF)] * 2
        + [struct((1, width), F32)],
        [pltpu.VMEM((D, r), BF)] * 2,
        prefetch=1,
        us=200,
        nbytes=r * D * 4 + D * width * 4 + r * width * 6,
    )(at, cot, w, slope, hidden)
    pieces = [piece.reshape(2 * wide, part, units) for piece in out[1:5]]
    return out[0], pieces[:2], pieces[2:], out[5]


def norm_pull(grad, normed, inv, gain):
    scaled = grad * gain
    return inv * (
        scaled
        - jnp.mean(scaled, 1, keepdims=True)
        - normed * jnp.mean(scaled * normed, 1, keepdims=True)
    )


def middle_back_body(
    grad_ref, w_ref, middle_ref, cot_ref, vec_ref, out_ref, branch_ref, gain_sum, shift_sum, out_sum
):
    grad = dot(grad_ref[...], w_ref[...], 1, 1)
    normed, inv = stats(middle_ref[...])
    total = cot_ref[...].astype(F32) + norm_pull(
        grad, normed, inv, vec_row(vec_ref, GAIN_TWO)
    )
    out_ref[...] = total
    branch = total.astype(BF)
    branch_ref[...] = branch
    sums = (
        (gain_sum, jnp.sum(grad * normed, 0, keepdims=True)),
        (shift_sum, jnp.sum(grad, 0, keepdims=True)),
        (out_sum, jnp.sum(branch.astype(F32), 0, keepdims=True)),
    )
    for ref, value in sums:
        add_up(ref, value)


def add_up(ref, value):
    @pl.when(pl.program_id(0) == 0)
    def _():
        ref[...] = value

    @pl.when(pl.program_id(0) != 0)
    def _():
        ref[...] += value


def middle_back(grad, w, middle, cot, vecs):
    r, units = grad.shape
    m = row_tile(r)
    vec = spec((1, D), lambda i: (0, 0))
    row = spec((m, D), lambda i: (i, 0))
    vec_out = struct((1, D), F32)
    return call(
        middle_back_body,
        (r // m,),
        [
            spec((m, units), lambda i: (i, 0)),
            spec((D, units), lambda i: (0, 0)),
            row,
            row,
            spec((8, D), lambda i: (0, 0)),
        ],
        [row, row, vec, vec, vec],
        [struct((r, D), F32), struct((r, D), BF), vec_out, vec_out, vec_out],
        us=200,
        nbytes=r * units * 2 + D * units * 2 + r * D * 12,
    )(grad, w, middle, cot, vecs)


def mixed_back_body(branch_ref, tile_ref, w_ref, mixed_ref, grad_ref, gw_ref, turned):
    @pl.when(pl.program_id(0) == 0)
    def _():
        turned[...] = mixed_ref[...].T

    grad_ref[...] = dot(branch_ref[...], w_ref[...], 1, 1).astype(BF)
    gw_ref[...] = dot(turned[...], tile_ref[...], 1, 0).astype(BF)


def mixed_back(branch, w, mixed):
    r = branch.shape[0]
    full = spec((r, D), lambda j: (0, 0))
    tile = spec((r, TILE), lambda j: (0, j))
    return call(
        mixed_back_body,
        (D // TILE,),
        [full, tile, spec((TILE, D), lambda j: (j, 0)), full],
        [tile, spec((D, TILE), lambda j: (0, j))],
        [struct((r, D), BF), struct((D, D), BF)],
        [pltpu.VMEM((D, r), BF)],
        us=0.01,
        nbytes=r * D * 8 + D * D * 4,
    )(branch, branch, w, mixed)


def attend_back_body(triple_ref, prob_ref, grad_ref, *rest):
    out_ref = rest[-1]
    scale = HEAD_DIM**-0.5
    for pair in range(HEADS // 2):
        q, k, v = (pair_of(triple_ref, part, pair) for part in range(3))
        grad = pair_of(grad_ref, 0, pair)
        prob = prob_ref[0, 2 * pair : 2 * pair + 2]
        grad_prob = dot(side_by_side(v), grad, 1, 1).reshape(2, ROWS, ROWS)
        inside = jnp.sum(grad_prob * prob, 1, keepdims=True)
        grad_scores = (prob * (grad_prob - inside)).astype(BF).reshape(2 * ROWS, ROWS)
        grads = (
            dot(grad_scores, side_by_side(k), 0, 0) * scale,
            both_heads(dot(grad_scores, q, 1, 0)) * scale,
            both_heads(dot(prob.astype(BF).reshape(2 * ROWS, ROWS), grad, 1, 0)),
        )
        for part, value in enumerate(grads):
            out_ref[:, part * D + pair * 128 : part * D + (pair + 1) * 128] = value.astype(BF)


def attend_back(triple, prob, grad, start, stop, partial_out=None):
    wide = spec((ROWS, 3 * D), lambda g: (g + start, 0))
    count = stop - start
    given = [] if partial_out is None else [partial_out]
    return pl.pallas_call(
        attend_back_body,
        out_shape=struct(triple.shape, BF),
        grid_spec=pltpu.PrefetchScalarGridSpec(
            num_scalar_prefetch=0,
            grid=(count,),
            in_specs=[
                wide,
                spec((1, HEADS, ROWS, ROWS), lambda g: (g + start, 0, 0, 0)),
                spec((ROWS, D), lambda g: (g + start, 0)),
            ]
            + [ANY] * len(given),
            out_specs=wide,
        ),
        input_output_aliases={3: 0} if given else {},
        compiler_params=pltpu.CompilerParams(
            dimension_semantics=("arbitrary",), vmem_limit_bytes=24 * MB
        ),
        cost_estimate=pl.CostEstimate(
            flops=FLOPS_PER_US // 100, bytes_accessed=1024, transcendentals=0
        ),
    )(triple, prob, grad, *given)


def qkv_grad_body(grad_ref, hidden_ref, gw_ref, gb_ref):
    grad = grad_ref[...]
    gw_ref[...] = dot(grad.T, hidden_ref[...], 1, 0).astype(BF)
    gb_ref[...] = jnp.sum(grad.astype(F32), 0, keepdims=True)


def qkv_grad(grad, hidden):
    r, width = grad.shape
    return call(
        qkv_grad_body,
        (width // TILE,),
        [spec((r, TILE), lambda j: (0, j)), spec((r, D), lambda j: (0, 0))],
        [spec((TILE, D), lambda j: (j, 0)), spec((1, TILE), lambda j: (0, j))],
        [struct((width, D), BF), struct((1, width), F32)],
        us=200,
        nbytes=r * width * 2 + r * D * 2 + width * D * 2,
    )(grad, hidden)


def first_back_body(grad_ref, w_ref, rows_ref, middle_ref, vec_ref, out_ref, gain_sum, shift_sum):
    grad = dot(grad_ref[...], w_ref[...], 1, 0)
    normed, inv = stats(rows_ref[...].astype(F32))
    pulled = norm_pull(grad, normed, inv, vec_row(vec_ref, GAIN_ONE))
    out_ref[...] = middle_ref[...] + pulled
    add_up(gain_sum, jnp.sum(grad * normed, 0, keepdims=True))
    add_up(shift_sum, jnp.sum(grad, 0, keepdims=True))


def first_back(grad, w, rows, grad_middle, vecs):
    r, width = grad.shape
    m = r // 4 if r % 64 == 0 else row_tile(r)
    vec = spec((1, D), lambda i: (0, 0))
    row = spec((m, D), lambda i: (i, 0))
    vec_out = struct((1, D), F32)
    return call(
        first_back_body,
        (r // m,),
        [
            spec((m, width), lambda i: (i, 0)),
            spec((width, D), lambda i: (0, 0)),
            row,
            row,
            spec((8, D), lambda i: (0, 0)),
        ],
        [row, vec, vec],
        [struct((r, D), F32), vec_out, vec_out],
        us=0.01,
        nbytes=r * width * 2 + D * width * 2 + r * D * 10,
    )(grad, w, rows, grad_middle, vecs)


WIDE, NARROW, DP = "wide", "narrow", "dp"


def swap(value, axis, bit):
    size = lax.axis_size(axis)
    return lax.ppermute(value, axis, [(i, i ^ bit) for i in range(size)])


def hold(value, *deps):
    return lax.optimization_barrier((value, deps))[0]


class Pieces:
    def __init__(self, stack, tags):
        self.stack, self.tags = stack, tags

    def fetch(self, axis, bit, *deps):
        move = [bit if axis == name else 0 for name in (WIDE, NARROW, DP)]
        tags = [tuple(a ^ b for a, b in zip(tag, move)) for tag in self.tags]
        return Pieces(swap(hold(self.stack, *deps), axis, bit), tags)

    def after(self, *deps):
        return Pieces(hold(self.stack, *deps), self.tags)

    def rows(self, start, stop):
        return Pieces(self.stack[:, start:stop], self.tags)

    def join(self, *others):
        stack = jnp.concatenate([self.stack] + [o.stack for o in others])
        return Pieces(stack, sum([o.tags for o in others], self.tags))


def first_piece(piece):
    return Pieces(piece[None], [(0, 0, 0)])


def qkv_plan(cols, heads_cols, parts, spots):
    rows = heads_cols // parts

    def plan(w, n, q):
        return [
            (0, spot, (rows, cols), (p * D + w * heads_cols + q * rows, n * cols))
            for p, spot in spots.items()
        ]

    return plan


def out_plan(cols, heads_cols, parts, spot, which=0):
    rows = heads_cols // parts
    return lambda w, n, q: [(which, spot, (rows, cols), (w * heads_cols + q * rows, n * cols))]


def flat_plan(cols, units, rows, base=0):
    return lambda w, n, q: [(0, (0, 0), (rows, units), (n * cols + base + q * rows, w * units))]


def sums_plan(cols, narrow, spot, which):
    return lambda w, n, q: [(which, spot, (16, cols), ((w * narrow + n) * 16, 0))]


def joined(*plans):
    return lambda w, n, q: [move for plan in plans for move in plan(w, n, q)]


def prep_body(cols, at_ref, *refs):
    (qkv_ref, out_ref, up_ref, down_ref), vectors = refs[:4], refs[4:12]
    first_ref, second_ref, up_a_ref, up_b_ref, down_part_ref = refs[12:17]
    held, sem = refs[17:-1], refs[-1]
    core, q = at_ref[2], at_ref[3]

    def block(ref, index, rows, base=0):
        return ref.at[pl.ds(pl.multiple_of(base + index * rows, 16), rows)]

    half = qkv_ref.shape[1] // 2
    ends = [
        (block(qkv_ref.at[0], core, half), first_ref.at[pl.ds(0, half)]),
        (block(out_ref, core, half), first_ref.at[pl.ds(half + 16, half)]),
    ]
    part = half // 2
    ends += [
        (block(qkv_ref.at[1 + p], q, part), second_ref.at[pl.ds(p * part, part)]) for p in range(2)
    ]
    ends.append((block(up_ref, core, up_a_ref.shape[0]), up_a_ref))
    ends.append((block(up_ref, q, up_b_ref.shape[0], up_ref.shape[0] // 2), up_b_ref))
    ends.append((block(down_ref, q, down_part_ref.shape[0]), down_part_ref))
    ends += list(zip(vectors, held))
    copies = [pltpu.make_async_copy(a, b, sem.at[k]) for k, (a, b) in enumerate(ends)]
    for copy in copies:
        copy.start()
    for copy in copies:
        copy.wait()
    lines = [ref[...].astype(F32).reshape(1, -1) for ref in held[:6]]
    both = held[6][...].astype(F32)
    lines.append(jnp.concatenate([both[:1], both[1:]], axis=1))
    wide_line = held[7][...].astype(F32).reshape(1, -1)
    lines += [wide_line[:, k : k + cols] for k in range(0, wide_line.shape[1], cols)]
    lines.append(jnp.zeros((16 - len(lines), cols), F32))
    first_ref[half : half + 16, :] = jnp.concatenate(lines, axis=0).astype(BF)


def prep(at, qkv_t, w_out, w_up, w_down, *vectors):
    cols, half = qkv_t.shape[2], qkv_t.shape[1] // 2
    rows, units = w_up.shape
    shapes = [
        (2 * half + 16, cols),
        (half, cols),
        (rows // 4, units),
        (rows // 8, units),
        (rows // 4, units),
    ]
    return pl.pallas_call(
        partial(prep_body, cols),
        out_shape=[struct(shape, BF) for shape in shapes],
        grid_spec=pltpu.PrefetchScalarGridSpec(
            num_scalar_prefetch=1,
            grid=(1,),
            in_specs=[IN_HBM] * (4 + len(vectors)),
            out_specs=[pl.BlockSpec(memory_space=pltpu.VMEM)] * len(shapes),
            scratch_shapes=[pltpu.VMEM(v.shape, BF) for v in vectors]
            + [pltpu.SemaphoreType.DMA((7 + len(vectors),))],
        ),
        compiler_params=pltpu.CompilerParams(vmem_limit_bytes=8 * MB),
        cost_estimate=pl.CostEstimate(
            flops=FLOPS_PER_US // 100, bytes_accessed=1024, transcendentals=0
        ),
    )(at, *[in_hbm(v) for v in (qkv_t, w_out, w_up, w_down, *vectors)])


def vec_body(wide, narrow, cols, first, tag_lists, at_ref, *refs):
    arrays, (vec_ref, qkv_bias_ref, up_bias_ref, held, sem) = refs[:-5], refs[-5:]
    copies = []
    for array, tags in zip(arrays, tag_lists):
        for k, (dw, dn, _) in enumerate(tags):
            slot = (at_ref[0] ^ dw) * narrow + (at_ref[1] ^ dn)
            source = array.at[k, pl.ds(first, 16)]
            copies.append(pltpu.make_async_copy(source, held.at[slot], sem.at[len(copies)]))
    for copy in copies:
        copy.start()
    for copy in copies:
        copy.wait()
    lines = [held[k].astype(F32) for k in range(wide * narrow)]
    for n in range(narrow):
        vec_ref[:, n * cols : (n + 1) * cols] = lines[n][:8]
    by_wide = [lines[w * narrow] for w in range(wide)]
    half = cols // 2
    q = jnp.concatenate([line[6:7, :half] for line in by_wide], axis=1)
    v = jnp.concatenate([line[6:7, half:] for line in by_wide], axis=1)
    qkv_bias_ref[...] = jnp.concatenate([q, jnp.zeros_like(q), v], axis=1)
    up_bias_ref[...] = jnp.concatenate(
        [line[i : i + 1] for line in by_wide for i in (7, 8)], axis=1
    )


def vectors_of(at, pieces, first, wide, narrow, cols, units):
    vmem = pl.BlockSpec(memory_space=pltpu.VMEM)
    return pl.pallas_call(
        partial(vec_body, wide, narrow, cols, first, [p.tags for p in pieces]),
        out_shape=[struct((8, D), F32), struct((1, 3 * D), F32), struct((1, wide * units), F32)],
        grid_spec=pltpu.PrefetchScalarGridSpec(
            num_scalar_prefetch=1,
            grid=(1,),
            in_specs=[ANY] * len(pieces),
            out_specs=[vmem] * 3,
            scratch_shapes=[
                pltpu.VMEM((wide * narrow, 16, cols), BF),
                pltpu.SemaphoreType.DMA((wide * narrow,)),
            ],
        ),
        compiler_params=pltpu.CompilerParams(vmem_limit_bytes=8 * MB),
        cost_estimate=pl.CostEstimate(flops=FLOPS_PER_US // 100, bytes_accessed=1024, transcendentals=0),
    )(at, *[p.stack for p in pieces])


def pack_body(*refs):
    out = refs[-1]
    at = 0
    for ref in refs[:-1]:
        for k in range(0, ref.shape[1], D):
            out[at : at + 1, :] = ref[:, k : k + D]
            at += 1
    if at < out.shape[0]:
        out[at:, :] = jnp.zeros((out.shape[0] - at, D), F32)


def pack(*rows):
    count = -(-sum(r.shape[1] for r in rows) // (8 * D)) * 8
    vmem = pl.BlockSpec(memory_space=pltpu.VMEM)
    return pl.pallas_call(
        pack_body,
        out_shape=struct((count, D), F32),
        in_specs=[vmem] * len(rows),
        out_specs=vmem,
        compiler_params=pltpu.CompilerParams(vmem_limit_bytes=8 * MB),
        cost_estimate=pl.CostEstimate(flops=FLOPS_PER_US // 100, bytes_accessed=1024, transcendentals=0),
    )(*rows)


ANY = pl.BlockSpec(memory_space=pl.ANY)
IN_HBM = pl.BlockSpec(memory_space=pltpu.HBM)


def owner_sums_body(wide, narrow, cols, *refs):
    out = refs[-1]
    narrow_refs, qkv_ref, up_ref = refs[:6], refs[6], refs[7]
    part, units = D // wide, up_ref.shape[1] // wide
    for w in range(wide):
        for n in range(narrow):
            lines = [ref[:, n * cols : (n + 1) * cols] for ref in narrow_refs]
            lines.append(
                jnp.concatenate(
                    [qkv_ref[:, p * D + w * part : p * D + (w + 1) * part] for p in (0, 2)], axis=1
                )
            )
            lines += [
                up_ref[:, w * units + k : w * units + k + cols] for k in range(0, units, cols)
            ]
            lines.append(jnp.zeros((16 - len(lines), cols), F32))
            at = (w * narrow + n) * 16
            out[at : at + 16, :] = jnp.concatenate(lines, axis=0).astype(BF)


def owner_sums(wide, narrow, cols, *rows):
    vmem = pl.BlockSpec(memory_space=pltpu.VMEM)
    return pl.pallas_call(
        partial(owner_sums_body, wide, narrow, cols),
        out_shape=struct((wide * narrow * 16, cols), BF),
        in_specs=[vmem] * len(rows),
        out_specs=vmem,
        compiler_params=pltpu.CompilerParams(vmem_limit_bytes=8 * MB),
        cost_estimate=pl.CostEstimate(
            flops=FLOPS_PER_US // 100, bytes_accessed=1024, transcendentals=0
        ),
    )(*rows)


def build_body(plans, counts, inverse, parts_by, at_ref, tag_ref, *refs):
    refs, sem = refs[:-1], refs[-1]
    lists = len(counts)
    wholes, arrays = (refs[:-lists], refs[-lists:]) if inverse else (refs[lists:], refs[:lists])

    def each(act):
        first, slot = 0, 0
        for array, plan, count, by in zip(arrays, plans, counts, parts_by):
            moves = len(plan(0, 0, 0))

            def step(k, carry, array=array, plan=plan, by=by, first=first, slot=slot, moves=moves):
                w, n, q = (
                    at_ref[axis] ^ tag_ref[i, first + k] for i, axis in enumerate((0, 1, by))
                )
                for m, (which, (at_row, at_lane), (rows, lanes), (row, lane)) in enumerate(
                    plan(w, n, q)
                ):
                    piece = array.at[k, pl.ds(at_row, rows), pl.ds(at_lane, lanes)]
                    whole = wholes[which].at[
                        pl.ds(pl.multiple_of(row, 16), rows),
                        pl.ds(pl.multiple_of(lane, 128), lanes),
                    ]
                    ends = (whole, piece) if inverse else (piece, whole)
                    act(pltpu.make_async_copy(*ends, sem.at[slot + k * moves + m]))
                return carry

            lax.fori_loop(0, count, step, 0, unroll=4)
            first, slot = first + count, slot + count * moves

    each(lambda copy: copy.start())
    each(lambda copy: copy.wait())


def move_pieces(at, arrays, plans, tag_lists, inverse, parts_by, shapes, pinned=0):
    counts = [len(tags) for tags in tag_lists]
    moves = sum(count * len(plan(0, 0, 0)) for count, plan in zip(counts, plans))
    table = jnp.array([tag for tags in tag_lists for tag in tags], jnp.int32).T
    return pl.pallas_call(
        partial(build_body, plans, counts, inverse, parts_by),
        out_shape=[
            pltpu.HBM(shape, BF) if i < pinned else struct(shape, BF)
            for i, shape in enumerate(shapes)
        ],
        grid_spec=pltpu.PrefetchScalarGridSpec(
            num_scalar_prefetch=2,
            grid=(1,),
            in_specs=[ANY] * len(arrays),
            out_specs=[ANY] * len(shapes),
            scratch_shapes=[pltpu.SemaphoreType.DMA((moves,))],
        ),
        compiler_params=pltpu.CompilerParams(vmem_limit_bytes=4 * MB),
        cost_estimate=pl.CostEstimate(
            flops=FLOPS_PER_US // 100, bytes_accessed=1024, transcendentals=0
        ),
    )(at, table, *arrays)


CORE, DP_INDEX = 2, 3


def build_weights(at, shape, *groups):
    lists = [(p, plan, by) for pieces, plan, by in groups for p in pieces]
    arrays, tags = [p.stack for p, _, _ in lists], [p.tags for p, _, _ in lists]
    plans, parts_by = [plan for _, plan, _ in lists], [by for _, _, by in lists]
    return move_pieces(at, arrays, plans, tags, False, parts_by, [shape])[0]


def cut_grads(at, grads, plan, tags, shape, part_at=CORE):
    lists = [[(w, n, q ^ dc) for w, n, q in tags] for dc in range(2)]
    shapes = [(len(tags),) + shape] * 2
    return move_pieces(at, grads, [plan] * 2, lists, True, [part_at] * 2, shapes, 1)


def fence_body(x_ref, out_ref):
    out_ref[...] = x_ref[...]


def fence(token, us=200):
    vmem = pl.BlockSpec(memory_space=pltpu.VMEM)
    return pl.pallas_call(
        fence_body,
        out_shape=struct(token.shape, token.dtype),
        in_specs=[vmem],
        out_specs=vmem,
        compiler_params=pltpu.CompilerParams(vmem_limit_bytes=MB, has_side_effects=True),
        cost_estimate=pl.CostEstimate(
            flops=us * FLOPS_PER_US, bytes_accessed=1024, transcendentals=0
        ),
    )(token)


class Chain:
    def __init__(self, keep, send):
        self.keep, self.send = keep, send

    def go(self, axis, bit):
        if isinstance(self.send, (list, tuple)):
            self.got = [swap(part, axis, bit) for part in self.send]
        else:
            self.got = swap(self.send, axis, bit)

    def fold(self, *deps):
        self.keep, self.send = halves_summed(self.keep, hold(self.got, *deps))

    def spread(self, *deps):
        got = hold(self.got, *deps)
        order = (0, 2, 1, 3)
        total = [k.astype(F32) + g.astype(F32) for k, g in zip(self.keep, got)]
        self.keep = total[0]
        self.send = [total[order.index(bit)].astype(BF) for bit in range(1, len(total))]
        self.got = [swap(piece, WIDE, bit) for bit, piece in enumerate(self.send, 1)]

    def all_of(self, *deps):
        total = self.keep
        for got in hold(self.got, *deps):
            total = total + got.astype(F32)
        return total

    def total(self, *deps):
        return self.keep[0].astype(F32) + hold(self.got, *deps)[0].astype(F32)


def halves_summed(kept, got):
    def halves(stack):
        if isinstance(stack, (list, tuple)):
            return stack
        half = stack.shape[0] // 2
        return stack[:half], stack[half:]

    first, second = [a.astype(F32) + b.astype(F32) for a, b in zip(halves(kept), halves(got))]
    return first, second.astype(BF)


def quarter(at, shard):
    rows = shard.shape[0] // 4
    return lax.dynamic_slice_in_dim(shard, at[3] * rows, rows, axis=0)


def to_rows(blocks, narrow):
    got = lax.all_to_all(blocks, "narrow", 0, 0, tiled=True)
    return jnp.concatenate([got[n] for n in range(narrow)], axis=1)


def from_rows(rows, narrow):
    cols = rows.shape[1] // narrow
    blocks = jnp.stack([rows[:, n * cols : (n + 1) * cols] for n in range(narrow)])
    got = lax.all_to_all(blocks, "narrow", 0, 0, tiled=True)
    return got.reshape(-1, cols)


def gather_weight(shard, wide, narrow):
    got = lax.all_gather(shard.reshape(-1, 128), ("wide", "narrow"), axis=0, tiled=True)
    return got.reshape((wide, narrow) + shard.shape)


def scatter_grad(blocks):
    shape = blocks.shape[2:]
    got = lax.psum_scatter(
        blocks.reshape(-1, 128), ("wide", "narrow"), scatter_dimension=0, tiled=True
    )
    return lax.psum(got.astype(F32), "dp").reshape(shape)


def on_device(
    wide,
    narrow,
    patches,
    visible,
    w_qkv,
    b_qv,
    w_out,
    b_out,
    w_up,
    b_up,
    w_down,
    b_down,
    gain_one,
    shift_one,
    gain_two,
    shift_two,
    cotangent,
):
    images = visible.shape[0]
    pairs = images // 2
    cols = w_qkv.shape[0]
    heads_cols = w_qkv.shape[2]
    units = w_up.shape[1]
    swaps = cols % 128 == 0 and narrow == 2 and wide == 4 and lax.axis_size(DP) == 4
    swaps = swaps and pairs % 2 == 0

    at = jnp.stack(
        [
            lax.axis_index("wide"),
            lax.axis_index("narrow"),
            lax.axis_index("dp") % 2,
            lax.axis_index("dp"),
        ]
    ).astype(jnp.int32)

    index = (visible.reshape(pairs, 2, VISIBLE) + jnp.array([0, PATCHES])[None, :, None]).reshape(
        pairs, PAIR
    )
    index = jnp.pad(index, ((0, 0), (0, ROWS - PAIR)), constant_values=-1)[:, :, None]

    w_qkv_t = w_qkv.transpose(1, 2, 0)
    if swaps:
        pieces = prep(
            at,
            w_qkv_t,
            w_out,
            w_up,
            w_down,
            gain_one,
            shift_one,
            gain_two,
            shift_two,
            b_out,
            b_down,
            b_qv,
            b_up,
        )
        a_p, b_p, u_p, v_p, d_p = [first_piece(piece) for piece in pieces]

        def part_of(whole, side):
            return lax.dynamic_slice_in_dim(whole, side * cols, cols, axis=1)

        def join_cols(keep, got):
            return jnp.where(
                at[1] == 0,
                jnp.concatenate([keep, got], axis=1),
                jnp.concatenate([got, keep], axis=1),
            )

        mine, theirs = at[1], 1 - at[1]
        whole = (D, wide * units)

        b_z = [b_p.fetch(WIDE, bit) for bit in (1, 2, 3)]
        a_x, d_x = a_p.fetch(NARROW, 1), d_p.fetch(NARROW, 1)
        token = fence(hold(at, a_p.stack, b_p.stack, d_p.stack))
        a_p, d_p = a_p.join(a_x.after(token)), d_p.join(d_x.after(token))
        b_p = b_p.join(*[p.after(token) for p in b_z])

        b_x, a_z = b_p.fetch(NARROW, 1), a_p.fetch(WIDE, 2)
        rows_out = pick_rows(
            hold(at, a_p.stack, b_p.stack, d_p.stack), in_hbm(patches), index, cols
        )
        own = rows_out.shape[0] // 2
        rows_send = rows_out[:own]
        a_p, b_p = a_p.join(a_z.after(rows_send)), b_p.join(b_x.after(rows_send))

        b_y, a_z = b_p.fetch(DP, 2), a_p.fetch(WIDE, 1)
        v_z = v_p.fetch(WIDE, 2, rows_send)
        rows_got = swap(rows_send, NARROW, 1)
        cot_out = cot_rows(hold(at, rows_send, a_p.stack, b_p.stack), cotangent, pairs, cols)
        a_p, b_p = a_p.join(a_z.after(cot_out)), b_p.join(b_y.after(cot_out))
        v_p = v_p.join(v_z.after(cot_out))
        rows = join_cols(rows_out[own:], hold(rows_got, cot_out))

        started = [a_p.stack, b_p.stack, v_p.stack, rows]
        a_c, b_c = a_p.fetch(DP, 1, *started), b_p.fetch(DP, 1, *started)
        u_z, v_z = u_p.fetch(WIDE, 2, *started), v_p.fetch(WIDE, 1, *started)
        cot_send = hold(cot_out[:own], *started)
        cot_got = swap(cot_send, NARROW, 1)
        half = heads_cols // 2
        vecs, bias_qkv, bias_up = vectors_of(at, [a_p], half, wide, narrow, cols, units)
        hidden_one = norm(hold(rows, *started, cot_send), vecs)
        u_p, v_p = u_p.join(u_z.after(hidden_one)), v_p.join(v_z.after(hidden_one))
        a_c, b_c = a_c.after(hidden_one), b_c.after(hidden_one)

        u_z, v_x = u_p.fetch(WIDE, 1), v_p.fetch(NARROW, 1)
        started = [u_p.stack, v_p.stack]
        d_z = d_p.fetch(WIDE, 2, *started)
        part = heads_cols // 4
        qkv_t = build_weights(
            at,
            (3 * D, D),
            ([a_p, a_c], qkv_plan(cols, heads_cols, 2, {0: (0, 0)}), CORE),
            (
                [b_p, b_c],
                qkv_plan(cols, heads_cols, 4, {1: (0, 0), 2: (part, 0)}),
                DP_INDEX,
            ),
        )
        out_w = build_weights(
            at, (D, D), ([a_p, a_c], out_plan(cols, heads_cols, 2, (half + 16, 0)), CORE)
        )
        triple = qkv(hold(hidden_one, *started), qkv_t, bias_qkv)
        u_p, v_p = u_p.join(u_z.after(triple)), v_p.join(v_x.after(triple))
        d_p = d_p.join(d_z.after(triple))
        cot = join_cols(cot_out[own:], hold(cot_got, triple))

        u_x, v_y, d_z = u_p.fetch(NARROW, 1), v_p.fetch(DP, 2), d_p.fetch(WIDE, 1)
        mixed, prob = attend(hold(triple, u_p.stack, v_p.stack, d_p.stack, cot))
        d_p = d_p.join(d_z.after(mixed))
        u_x, v_y = u_x.after(mixed), v_y.after(mixed)

        u_all, v_all = [u_p, u_x], [v_p, v_y]
        started = [d_p.stack, u_x.stack, v_y.stack]
        d_y = d_p.fetch(DP, 2)
        u_c = [p.fetch(DP, 1, *started) for p in u_all]
        v_c = [p.fetch(DP, 1, *started) for p in v_all]
        middle, hidden_two = mix(hold(mixed, *started), out_w, rows, vecs)
        half_flat = flat_plan(cols, units, cols // 2)
        part_flat = flat_plan(cols, units, cols // 4)
        up_w = build_weights(
            at,
            whole,
            (u_all + [p.after(hidden_two) for p in u_c], part_flat, CORE),
            (
                v_all + [p.after(hidden_two) for p in v_c],
                flat_plan(cols, units, cols // 8, cols // 2),
                DP_INDEX,
            ),
        )
        active, slope = up(hidden_two, up_w, bias_up)

        x_first = [(w, n, 0) for n in range(2) for w in (0, 2, 1, 3)]
        y_first = [(w, n, dy) for dy in (0, 2) for n in range(2) for w in (0, 2, 1, 3)]
        gd_keep, gd_send = outer_pieces(at, cot, in_hbm(active), cols, wide)
        gb_down = jnp.sum(cot, 0, dtype=F32)[None]
        d_y = d_y.after(*gd_send)
        d_c = [p.fetch(DP, 1, d_y.stack) for p in (d_p, d_y)]
        g_d = Chain(gd_keep, [hold(piece, d_y.stack) for piece in gd_send])
        g_d.go(DP, 1)
        d_c = [p.after(*g_d.send) for p in d_c]
        down_w = build_weights(at, whole, ([d_p, d_y] + d_c, part_flat, DP_INDEX))
        g_d.fold(down_w)
        g_d.go(NARROW, 1)
        grad_inner, gu_keep, gu_send, gb_up = inner_back_pieces(
            at, cot, hold(down_w, g_d.send), in_hbm(slope), hidden_two, cols, wide
        )

        result = down(hold(in_hbm(active), grad_inner), down_w, vecs, middle)
        g_u = Chain(gu_keep, [hold(piece, result) for piece in gu_send])
        g_u.go(DP, 1)
        g_d.fold(*g_u.send)
        g_d.go(WIDE, 1)
        g_u.fold(g_d.send)
        g_u.go(DP, 2)
        grad_middle, branch, gg_two, gs_two, gb_out = middle_back(
            hold(grad_inner, g_d.send, g_u.send), up_w, middle, cot, vecs
        )
        grad_mixed, gw_out = mixed_back(branch, out_w, mixed)

        g_d.fold(grad_mixed)
        g_d.go(WIDE, 2)
        result_send = hold(part_of(result, theirs), grad_mixed)
        result_got = swap(result_send, NARROW, 1)
        groups = rows.shape[0] // ROWS
        grad_triple = attend_back(
            triple, in_hbm(prob), hold(grad_mixed, g_d.send, result_send), 0, groups
        )
        grad_rows, gg_one, gs_one = first_back(grad_triple, qkv_t, rows, grad_middle, vecs)

        d_sum = g_d.total(grad_rows)
        d_got = swap(d_sum.astype(BF), DP, 2)
        g_u.fold(grad_rows)
        g_u.go(NARROW, 1)
        result_got = hold(result_got, grad_rows)
        gw_qkv, gb_qkv = qkv_grad(hold(grad_triple, d_sum, g_u.send, result_got), hidden_one)
        sums = owner_sums(
            wide,
            narrow,
            cols,
            gg_one,
            gs_one,
            gg_two,
            gs_two,
            gb_out,
            gb_down,
            gb_qkv,
            gb_up,
        )

        part = heads_cols // 4
        g_q = cut_grads(
            at,
            [gw_qkv],
            qkv_plan(cols, heads_cols, 4, {p: (p * part, 0) for p in range(3)}),
            y_first,
            (3 * part, cols),
            DP_INDEX,
        )
        g_q = Chain(*g_q)
        g_q.go(DP, 1)
        rest_plan = joined(
            out_plan(cols, heads_cols, 2, (0, 0), 0), sums_plan(cols, narrow, (half, 0), 1)
        )
        g_r = Chain(*cut_grads(at, [gw_out, sums], rest_plan, x_first, (half + 16, cols)))
        g_r.go(DP, 1)
        d_sum = d_sum + hold(d_got, g_r.send).astype(F32)
        d_got = swap(d_sum, DP, 1)
        g_u.fold(g_r.send)
        g_u.go(WIDE, 1)
        rows_send = hold(part_of(grad_rows, theirs), g_r.send).astype(BF)
        rows_back = swap(rows_send, NARROW, 1)
        token = fence(hold(vecs, g_q.send, d_sum, g_u.send, rows_send))

        g_q.fold(token)
        g_q.go(DP, 2)
        g_r.fold(token, g_q.send)
        g_r.go(NARROW, 1)
        g_u.fold(g_q.send, g_r.send)
        g_u.go(WIDE, 2)
        rows_back = hold(rows_back, g_u.send)
        grad_patches = put_rows(at, part_of(grad_rows, mine), rows_back, index, cols)

        def in_order(value, other, index):
            return jnp.where(index == 0, jnp.stack([value, other]), jnp.stack([other, value]))

        g_q.fold(grad_patches)
        g_q.go(NARROW, 1)
        g_r.spread(grad_patches, g_q.send)
        u_sum = g_u.total(g_q.send, *g_r.send)
        keep = hold(part_of(result, mine), g_q.send, u_sum, *g_r.send)
        block_output = flat_rows(at, keep, result_got, cols)
        g_q.spread(block_output)
        r_sum = g_r.all_of(block_output)
        r_got = swap(r_sum.astype(BF), DP, 2)
        u_got = swap(u_sum.astype(BF), DP, 2)
        token = fence(hold(token, r_sum, u_sum, *g_q.send))
        q_sum = g_q.all_of(token)
        q_got = [swap(q_sum.astype(BF), DP, bit) for bit in (1, 2, 3)]
        r_sum = r_sum + hold(r_got, q_sum).astype(F32)
        r_got = swap(r_sum[:half], DP, 1)
        u_sum = in_order(u_sum, hold(u_got, token).astype(F32), at[3] // 2)
        u_got = swap(u_sum, DP, 1)
        g_down = in_order(d_sum, d_got, at[2]).reshape(cols, units)
        g_up = in_order(u_sum, u_got, at[2]).transpose(1, 0, 2, 3).reshape(cols, units)
        q_got = [got.astype(F32) for got in q_got]
        pairs_of = [in_order(q_sum, q_got[0], at[2]), in_order(q_got[1], q_got[2], at[2])]
        q_sum = in_order(*pairs_of, at[3] // 2).reshape(4, 3, part, cols)
        g_out = in_order(r_sum[:half], r_got, at[2]).reshape(heads_cols, cols)
        g_qkv = q_sum.transpose(3, 1, 0, 2).reshape(cols, 3, heads_cols)
        grad_patches = grad_patches.reshape(1, -1)
        lines = r_sum[half:]
        vector_grads = [lines[i] for i in range(6)]
        g_bqv = lines[6].reshape(2, heads_cols)
        g_bup = lines[7:9].reshape(units)
    else:
        table = patches.reshape(images, PATCHES, cols)
        rows_mine = jnp.take_along_axis(table, visible[:, :, None], axis=1)
        rows_mine = jnp.pad(
            rows_mine.reshape(pairs, PAIR, cols), ((0, 0), (0, ROWS - PAIR), (0, 0))
        )
        cot_mine = jnp.pad(
            cotangent.reshape(pairs, PAIR, cols), ((0, 0), (0, ROWS - PAIR), (0, 0))
        )
        rows = to_rows(rows_mine.reshape(narrow, -1, cols), narrow)
        cot = to_rows(cot_mine.reshape(narrow, -1, cols), narrow)
        vec = jnp.concatenate(
            [gain_one, shift_one, gain_two, shift_two, b_out, b_down, b_qv.reshape(-1), b_up]
        )
        vec = lax.all_gather(vec, ("wide", "narrow"), axis=0, tiled=False).astype(F32)
        qkv_t = gather_weight(w_qkv_t, wide, narrow)
        qkv_t = qkv_t.transpose(2, 0, 3, 1, 4).reshape(3 * D, D)
        out_w = gather_weight(w_out, wide, narrow).transpose(0, 2, 1, 3).reshape(D, D)
        up_w = gather_weight(w_up, wide, narrow).transpose(1, 2, 0, 3).reshape(D, -1)
        down_w = gather_weight(w_down, wide, narrow).transpose(1, 2, 0, 3).reshape(D, -1)
        vec = vec.reshape(wide, narrow, -1)
        vecs = vec[0, :, : 6 * cols].reshape(narrow, 6, cols).transpose(1, 0, 2).reshape(6, D)
        vecs = jnp.pad(vecs, ((0, 2), (0, 0)))
        by_wide = vec[:, 0, 6 * cols :]
        bias_q = by_wide[:, :heads_cols].reshape(1, D)
        bias_v = by_wide[:, heads_cols : 2 * heads_cols].reshape(1, D)
        bias_qkv = jnp.concatenate([bias_q, jnp.zeros((1, D), F32), bias_v], axis=1)
        bias_up = by_wide[:, 2 * heads_cols :].reshape(1, -1)

        hidden_one = norm(rows, vecs)
        triple = qkv(hidden_one, qkv_t, bias_qkv)
        mixed, prob = attend(triple)
        middle, hidden_two = mix(mixed, out_w, rows, vecs)
        active, slope = up(hidden_two, up_w, bias_up)
        result = down(active, down_w, vecs, middle)
        gw_down = outer(cot, active)
        gb_down = jnp.sum(cot, 0, dtype=F32)[None]
        grad_inner, gw_up, gb_up = inner_back(cot, down_w, slope, hidden_two)
        grad_middle, branch, gg_two, gs_two, gb_out = middle_back(
            grad_inner, up_w, middle, cot, vecs
        )
        grad_mixed, gw_out = mixed_back(branch, out_w, mixed)
        grad_triple = attend_back(triple, prob, grad_mixed, 0, rows.shape[0] // ROWS)
        gw_qkv, gb_qkv = qkv_grad(grad_triple, hidden_one)
        grad_rows, gg_one, gs_one = first_back(grad_triple, qkv_t, rows, grad_middle, vecs)
        sums = pack(gg_one, gs_one, gg_two, gs_two, gb_out, gb_down, gb_qkv, gb_up)

        result = from_rows(result, narrow)
        grad_rows = from_rows(grad_rows, narrow)
        block_output = result.reshape(pairs, ROWS, cols)[:, :PAIR].reshape(1, -1)
        grad_rows = grad_rows.reshape(pairs, ROWS, cols)[:, :PAIR].reshape(images, VISIBLE, cols)
        grad_patches = (
            jnp.zeros((images, PATCHES, cols), F32)
            .at[jnp.arange(images)[:, None], visible]
            .set(grad_rows)
            .reshape(1, -1)
        )
        g_down = scatter_grad(gw_down.reshape(narrow, cols, wide, units).transpose(2, 0, 1, 3))
        g_up = scatter_grad(gw_up.reshape(narrow, cols, wide, units).transpose(2, 0, 1, 3))
        g_out = scatter_grad(gw_out.reshape(wide, heads_cols, narrow, cols).transpose(0, 2, 1, 3))
        g_qkv = scatter_grad(
            gw_qkv.reshape(3, wide, heads_cols, narrow, cols).transpose(1, 3, 0, 2, 4)
        )
        g_qkv = g_qkv.transpose(2, 0, 1)
        sums = lax.psum(sums, ("dp", "wide", "narrow"))
        sums = sums.reshape(-1)
        vector_grads = [
            lax.dynamic_slice_in_dim(sums, i * D + at[1] * cols, cols) for i in range(6)
        ]
        g_bqv = jnp.stack(
            [
                lax.dynamic_slice_in_dim(sums, (6 + i) * D + at[0] * heads_cols, heads_cols)
                for i in (0, 2)
            ]
        )
        g_bup = lax.dynamic_slice_in_dim(sums, 9 * D + at[0] * units, units)

    return (
        block_output,
        grad_patches,
        g_qkv,
        g_bqv,
        g_out,
        vector_grads[4],
        g_up,
        g_bup,
        g_down,
        vector_grads[5],
        vector_grads[0],
        vector_grads[1],
        vector_grads[2],
        vector_grads[3],
    )


def solution(mesh):
    in_specs = (
        P("narrow", ("dp", "wide")),
        P(("dp", "wide"), None),
        P("narrow", None, "wide"),
        P(None, "wide"),
        P("wide", "narrow"),
        P("narrow"),
        P("narrow", "wide"),
        P("wide"),
        P("narrow", "wide"),
        P("narrow"),
        P("narrow"),
        P("narrow"),
        P("narrow"),
        P("narrow"),
        P("narrow", ("dp", "wide")),
    )
    out_specs = (
        P("narrow", ("dp", "wide")),
        P("narrow", ("dp", "wide")),
        P("narrow", None, "wide"),
        P(None, "wide"),
        P("wide", "narrow"),
        P("narrow"),
        P("narrow", "wide"),
        P("wide"),
        P("narrow", "wide"),
        P("narrow"),
        P("narrow"),
        P("narrow"),
        P("narrow"),
        P("narrow"),
    )
    body = partial(on_device, mesh.shape["wide"], mesh.shape["narrow"])
    return jax.shard_map(body, mesh=mesh, in_specs=in_specs, out_specs=out_specs, check_vma=False)
```

```python
from functools import partial

import jax
import jax.numpy as jnp
from jax import lax
from jax.experimental import pallas as pl
from jax.experimental.pallas import tpu as pltpu
from jax.sharding import PartitionSpec as P

D = 768
HEAD_DIM = 64
HEADS = 12
PATCHES = 196
VISIBLE = 49
PAIR = 2 * VISIBLE
ROWS = 112
TILE = 768
EPS = 1e-06
BF = jnp.bfloat16
F32 = jnp.float32
MB = 1024 * 1024


def dot(a, b, ca, cb):
    return lax.dot_general(a, b, (((ca,), (cb,)), ((), ())), preferred_element_type=F32)


FLOPS_PER_US = 540000000


def call(body, grid, ins, outs, shapes, scratch=(), prefetch=0, us=1.0, nbytes=0, vmem=32):
    return pl.pallas_call(
        body,
        out_shape=shapes,
        grid_spec=pltpu.PrefetchScalarGridSpec(
            num_scalar_prefetch=prefetch,
            grid=grid,
            in_specs=ins,
            out_specs=outs,
            scratch_shapes=scratch,
        ),
        compiler_params=pltpu.CompilerParams(
            dimension_semantics=("arbitrary",) * len(grid), vmem_limit_bytes=vmem * MB
        ),
        cost_estimate=pl.CostEstimate(
            flops=int(us * FLOPS_PER_US), bytes_accessed=1024, transcendentals=0
        ),
    )


def in_hbm(value):
    return pltpu.with_memory_space_constraint(value, pltpu.HBM)


def spec(shape, index):
    return pl.BlockSpec(shape, index)


def struct(shape, dtype):
    return jax.ShapeDtypeStruct(shape, dtype)


def together(own):
    return next(count for count in (4, 2, 1) if own % count == 0)


def strided(start, count, lanes):
    return [pl.ds(start + k, count, stride=lanes) for k in range(lanes)]


def one_hot(index):
    return (index == lax.broadcasted_iota(jnp.int32, (ROWS, 2 * PATCHES), 1)).astype(BF)


def pick_body(cols, count, at_ref, patch_ref, index_ref, rows_ref, wide_ref):
    lanes = cols // 128
    wide_ref[...] = patch_ref[...].astype(F32).reshape(wide_ref.shape)
    for j in range(count):
        places = strided(j * 2 * PATCHES * lanes, 2 * PATCHES, lanes)
        both = jnp.concatenate([wide_ref[place, :] for place in places], axis=1).astype(BF)
        rows_ref[j * ROWS : (j + 1) * ROWS, :] = dot(one_hot(index_ref[j]), both, 1, 0).astype(BF)


def owner_first_sent(steps):
    own = steps // 2

    def source(i, at):
        return (i // own ^ 1 ^ at[1]) * own + i % own

    return source


def pick_rows(at, patches, index, cols):
    pairs = index.shape[0]
    count = together(pairs // 2)
    width = 2 * PATCHES * cols * count
    source = owner_first_sent(pairs // count)
    return call(
        partial(pick_body, cols, count),
        (pairs // count,),
        [
            spec((1, width), lambda i, at: (0, source(i, at))),
            spec((count, ROWS, 1), lambda i, at: (source(i, at), 0, 0)),
        ],
        spec((count * ROWS, cols), lambda i, at: (i, 0)),
        struct((pairs * ROWS, cols), BF),
        [pltpu.VMEM((width // 128, 128), F32)],
        prefetch=1,
        us=200,
        vmem=16,
        nbytes=pairs * width * 4,
    )(at, patches, index)


def cot_body(cols, count, at_ref, cot_ref, rows_ref, scr):
    lanes = cols // 128
    scr[...] = cot_ref[...].astype(F32).reshape(scr.shape)
    for j in range(count):
        places = strided(j * PAIR * lanes, PAIR, lanes)
        cot = jnp.concatenate([scr[place, :] for place in places], axis=1)
        rows_ref[j * ROWS : (j + 1) * ROWS, :] = jnp.concatenate(
            [cot, jnp.zeros((ROWS - PAIR, cols), F32)], axis=0
        ).astype(BF)


def cot_rows(at, cotangent, pairs, cols):
    count = together(pairs // 2)
    width = PAIR * cols * count
    source = owner_first_sent(pairs // count)
    return call(
        partial(cot_body, cols, count),
        (pairs // count,),
        [spec((1, width), lambda i, at: (0, source(i, at)))],
        spec((count * ROWS, cols), lambda i, at: (i, 0)),
        struct((pairs * ROWS, cols), BF),
        [pltpu.VMEM((width // 128, 128), F32)],
        prefetch=1,
        us=200,
        vmem=12,
        nbytes=pairs * width * 4,
    )(at, cotangent)


def own_block(at_ref, keep_ref, got_ref, j):
    own = pl.num_programs(0) // 2
    mine = pl.program_id(0) // own == at_ref[1]
    rows = slice(j * ROWS, (j + 1) * ROWS)
    return jnp.where(mine, keep_ref[rows, :].astype(F32), got_ref[rows, :].astype(F32))


def put_body(cols, count, at_ref, keep_ref, got_ref, index_ref, out_ref):
    lanes = cols // 128
    for j in range(count):
        hit = one_hot(index_ref[j])
        rest = own_block(at_ref, keep_ref, got_ref, j)
        parts = []
        for _ in range(3):
            parts.append(rest.astype(BF))
            rest = rest - parts[-1].astype(F32)
        total = dot(jnp.concatenate([hit] * 3), jnp.concatenate(parts), 0, 0)
        for k, place in enumerate(strided(j * 2 * PATCHES * lanes, 2 * PATCHES, lanes)):
            out_ref[place, :] = total[:, k * 128 : (k + 1) * 128]


def put_rows(at, keep, got, index, cols):
    pairs = index.shape[0]
    count = together(pairs // 2)
    own = pairs // count // 2
    tall = count * 2 * PATCHES * cols // 128
    rows = spec((count * ROWS, cols), lambda i, at: (i % own, 0))
    return call(
        partial(put_body, cols, count),
        (pairs // count,),
        [rows, rows, spec((count, ROWS, 1), lambda i, at: (i, 0, 0))],
        spec((tall, 128), lambda i, at: (i, 0)),
        struct((pairs // count * tall, 128), F32),
        prefetch=1,
        us=200,
        vmem=14,
        nbytes=pairs * (tall * 512 + ROWS * cols * 4),
    )(at, keep, got, index)


def flat_body(cols, count, at_ref, keep_ref, got_ref, out_ref, scr):
    lanes = cols // 128
    for j in range(count):
        rows = own_block(at_ref, keep_ref, got_ref, j)
        for k, place in enumerate(strided(j * PAIR * lanes, PAIR, lanes)):
            scr[place, :] = rows[:PAIR, k * 128 : (k + 1) * 128]
    out_ref[...] = scr[...].reshape(out_ref.shape).astype(BF)


def flat_rows(at, keep, got, cols):
    pairs = 2 * (keep.shape[0] // ROWS)
    count = together(pairs // 2)
    own = pairs // count // 2
    width = PAIR * cols * count
    rows = spec((count * ROWS, cols), lambda i, at: (i % own, 0))
    return call(
        partial(flat_body, cols, count),
        (pairs // count,),
        [rows, rows],
        spec((1, width), lambda i, at: (0, i)),
        struct((1, pairs // count * width), BF),
        [pltpu.VMEM((width // 128, 128), F32)],
        prefetch=1,
        us=200,
        vmem=12,
        nbytes=pairs * width * 6,
    )(at, keep, got)


def stats(rows):
    mean = jnp.mean(rows, 1, keepdims=True)
    off = rows - mean
    inv = lax.rsqrt(jnp.mean(off * off, 1, keepdims=True) + EPS)
    return off * inv, inv


GAIN_ONE, SHIFT_ONE, GAIN_TWO, SHIFT_TWO, BIAS_OUT, BIAS_DOWN = range(6)


def vec_row(vec_ref, i):
    return vec_ref[i : i + 1, :]


def norm_body(rows_ref, vec_ref, out_ref):
    normed, _ = stats(rows_ref[...].astype(F32))
    out_ref[...] = (normed * vec_row(vec_ref, GAIN_ONE) + vec_row(vec_ref, SHIFT_ONE)).astype(BF)


def norm(rows, vec):
    r = rows.shape[0]
    return call(
        norm_body,
        (r // ROWS,),
        [spec((ROWS, D), lambda i: (i, 0)), spec((8, D), lambda i: (0, 0))],
        spec((ROWS, D), lambda i: (i, 0)),
        struct((r, D), BF),
        us=200,
        vmem=10,
        nbytes=r * D * 4,
    )(rows, vec)


def qkv_body(hidden_ref, w_ref, bias_ref, out_ref):
    out_ref[...] = (dot(hidden_ref[...], w_ref[...], 1, 1) + bias_ref[...]).astype(BF)


def qkv(hidden, w, bias):
    r = hidden.shape[0]
    return call(
        qkv_body,
        (3 * D // TILE,),
        [
            spec((r, D), lambda j: (0, 0)),
            spec((TILE, D), lambda j: (j, 0)),
            spec((1, TILE), lambda j: (0, j)),
        ],
        spec((r, TILE), lambda j: (0, j)),
        struct((r, 3 * D), BF),
        us=13,
        vmem=16,
        nbytes=r * D * 8 + 3 * D * D * 2,
    )(hidden, w, bias)


def same_image():
    at_row = lax.broadcasted_iota(jnp.int32, (ROWS, ROWS), 0)
    at_col = lax.broadcasted_iota(jnp.int32, (ROWS, ROWS), 1)

    def image(at):
        return (at >= VISIBLE).astype(jnp.int32) + (at >= PAIR).astype(jnp.int32)

    return image(at_row) == image(at_col)


def side_by_side(block):
    left = lax.broadcasted_iota(jnp.int32, (ROWS, 128), 1) < HEAD_DIM
    none = jnp.zeros_like(block)
    return jnp.concatenate([jnp.where(left, block, none), jnp.where(left, none, block)])


def both_heads(stack):
    left = lax.broadcasted_iota(jnp.int32, (ROWS, 128), 1) < HEAD_DIM
    return jnp.where(left, stack[:ROWS], stack[ROWS:])


def pair_of(ref, part, pair):
    return ref[:, part * D + pair * 128 : part * D + (pair + 1) * 128]


def attend_body(triple_ref, mixed_ref, prob_ref):
    keep = same_image()[None]
    for pair in range(HEADS // 2):
        q, k, v = (pair_of(triple_ref, part, pair) for part in range(3))
        scores = dot(side_by_side(k), q, 1, 1).reshape(2, ROWS, ROWS) * HEAD_DIM**-0.5
        scores = jnp.where(keep, scores, -1e30)
        expo = jnp.exp(scores - jnp.max(scores, 1, keepdims=True))
        prob = expo / jnp.sum(expo, 1, keepdims=True)
        prob_ref[0, 2 * pair : 2 * pair + 2] = prob
        low = prob.astype(BF).reshape(2 * ROWS, ROWS)
        mixed_ref[:, pair * 128 : (pair + 1) * 128] = dot(low, side_by_side(v), 0, 0).astype(BF)


def attend(triple):
    groups = triple.shape[0] // ROWS
    return call(
        attend_body,
        (groups,),
        [spec((ROWS, 3 * D), lambda g: (g, 0))],
        [spec((ROWS, D), lambda g: (g, 0)), spec((1, HEADS, ROWS, ROWS), lambda g: (g, 0, 0, 0))],
        [struct((groups * ROWS, D), BF), pltpu.HBM((groups, HEADS, ROWS, ROWS), F32)],
        us=200,
        vmem=16,
        nbytes=groups * ROWS * (8 * D + HEADS * 512),
    )(triple)


def mix_body(mixed_ref, w_ref, rows_ref, vec_ref, middle_ref, hidden_ref):
    branch = dot(mixed_ref[...], w_ref[...], 1, 0) + vec_row(vec_ref, BIAS_OUT)
    middle = rows_ref[...].astype(F32) + branch
    middle_ref[...] = middle
    normed, _ = stats(middle)
    hidden_ref[...] = (
        normed * vec_row(vec_ref, GAIN_TWO) + vec_row(vec_ref, SHIFT_TWO)
    ).astype(BF)


def row_tile(r):
    return r // 2


def mix(mixed, w, rows, vec):
    r = rows.shape[0]
    m = r // 4 if r % 64 == 0 else row_tile(r)
    row = spec((m, D), lambda i: (i, 0))
    return call(
        mix_body,
        (r // m,),
        [row, spec((D, D), lambda i: (0, 0)), row, spec((8, D), lambda i: (0, 0))],
        [row, row],
        [struct((r, D), F32), struct((r, D), BF)],
        us=16,
        vmem=16,
        nbytes=r * D * 10 + D * D * 2,
    )(mixed, w, rows, vec)


def up_body(hidden_ref, w_ref, bias_ref, active_ref, slope_ref):
    inner = dot(hidden_ref[...], w_ref[...], 1, 0) + bias_ref[...]
    phi = 0.5 * (1.0 + lax.erf(inner * (0.5**0.5)))
    active_ref[...] = (inner * phi).astype(BF)
    slope_ref[...] = phi + inner * (jnp.exp(-0.5 * inner * inner) * 0.3989422804014327)


def up(hidden, w, bias):
    r = hidden.shape[0]
    units = w.shape[1]
    tile = spec((r, TILE), lambda j: (0, j))
    return call(
        up_body,
        (units // TILE,),
        [
            spec((r, D), lambda j: (0, 0)),
            spec((D, TILE), lambda j: (0, j)),
            spec((1, TILE), lambda j: (0, j)),
        ],
        [tile, tile],
        [pltpu.HBM((r, units), BF), pltpu.HBM((r, units), F32)],
        us=0.01,
        nbytes=r * D * 2 + D * units * 2 + r * units * 6,
    )(hidden, w, bias)


def down_body(active_ref, w_ref, vec_ref, middle_ref, out_ref):
    branch = dot(active_ref[...], w_ref[...], 1, 1) + vec_row(vec_ref, BIAS_DOWN)
    out_ref[...] = (middle_ref[...] + branch).astype(BF)


def down(active, w, vec, middle):
    r, units = active.shape
    m = row_tile(r)
    return call(
        down_body,
        (r // m,),
        [
            spec((m, units), lambda i: (i, 0)),
            spec((D, units), lambda i: (0, 0)),
            spec((8, D), lambda i: (0, 0)),
            spec((m, D), lambda i: (i, 0)),
        ],
        spec((m, D), lambda i: (i, 0)),
        struct((r, D), BF),
        us=0.01,
        nbytes=r * units * 2 + D * units * 2 + r * D * 6,
    )(active, w, vec, middle)


def outer_body(left_ref, right_ref, out_ref, turned):
    @pl.when(pl.program_id(0) == 0)
    def _():
        turned[...] = left_ref[...].T

    out_ref[...] = dot(turned[...], right_ref[...], 1, 0).astype(BF)


def outer(left, right):
    r, width = right.shape
    rows = left.shape[1]
    return call(
        outer_body,
        (width // TILE,),
        [spec((r, rows), lambda j: (0, 0)), spec((r, TILE), lambda j: (0, j))],
        spec((rows, TILE), lambda j: (0, j)),
        struct((rows, width), BF),
        [pltpu.VMEM((rows, r), BF)],
        us=0.01,
        nbytes=r * rows * 2 + r * width * 2 + rows * width * 2,
    )(left, right)


def inner_back_body(cot_ref, w_ref, slope_ref, hidden_ref, grad_ref, gw_ref, gb_ref, turned):
    @pl.when(pl.program_id(0) == 0)
    def _():
        turned[...] = hidden_ref[...].T

    grad = (dot(cot_ref[...], w_ref[...], 1, 0) * slope_ref[...]).astype(BF)
    grad_ref[...] = grad
    gw_ref[...] = dot(turned[...], grad, 1, 0).astype(BF)
    gb_ref[...] = jnp.sum(grad.astype(F32), 0, keepdims=True)


def inner_back(cot, w, slope, hidden):
    r, units = slope.shape
    full = spec((r, D), lambda j: (0, 0))
    col = spec((D, TILE), lambda j: (0, j))
    tile = spec((r, TILE), lambda j: (0, j))
    return call(
        inner_back_body,
        (units // TILE,),
        [full, col, tile, full],
        [tile, col, spec((1, TILE), lambda j: (0, j))],
        [pltpu.HBM((r, units), BF), struct((D, units), BF), struct((1, units), F32)],
        [pltpu.VMEM((D, r), BF)],
        us=200,
        nbytes=r * D * 4 + D * units * 4 + r * units * 6,
    )(cot, w, slope, hidden)


def place(w):
    return w % 2 * 2 + w // 2


def turn_blocks(left_ref, plain, turned, offsets):
    plain[...] = left_ref[...].T
    rows = plain.shape[0] // len(offsets)
    for i, offset in enumerate(offsets):
        turned[i * rows : (i + 1) * rows, :] = plain[pl.ds(pl.multiple_of(offset, 16), rows), :]


def outer_pieces_body(cols, at_ref, left_ref, right_ref, *refs):
    outs, (plain, turned) = refs[:4], refs[4:]

    @pl.when(pl.program_id(0) == 0)
    def _():
        offsets = [
            (n ^ at_ref[1]) * cols + (at_ref[2] ^ side) * (cols // 2)
            for side in range(2)
            for n in range(2)
        ]
        turn_blocks(left_ref, plain, turned, offsets)

    grad = dot(turned[...], right_ref[...], 1, 0).astype(BF)
    half = cols // 2
    for i, out in enumerate(outs):
        out[...] = grad[i * half : (i + 1) * half].reshape(out.shape)


def outer_pieces(at, left, right, cols, wide):
    r, width = right.shape
    rows, units = left.shape[1], width // wide
    shape = (wide, cols // 2, units)
    block = spec((1, cols // 2, units), lambda j, at: (place(j ^ at[0]), 0, 0))
    out = call(
        partial(outer_pieces_body, cols),
        (wide,),
        [spec((r, rows), lambda j, at: (0, 0)), spec((r, units), lambda j, at: (0, j))],
        [block] * 4,
        [pltpu.HBM(shape, BF)] * 2 + [struct(shape, BF)] * 2,
        [pltpu.VMEM((rows, r), BF)] * 2,
        prefetch=1,
        us=0.01,
        nbytes=r * rows * 2 + r * width * 2 + rows * width * 2,
    )(at, left, right)
    return out[:2], out[2:]


def inner_back_pieces_body(cols, at_ref, cot_ref, w_ref, slope_ref, hidden_ref, *refs):
    grad_ref, outs, gb_ref, plain, turned = refs[0], refs[1:5], refs[5], refs[6], refs[7]
    part = cols // 4

    @pl.when(pl.program_id(0) == 0)
    def _():
        offsets = [
            (n ^ at_ref[1]) * cols + (at_ref[3] ^ (2 * dy) ^ side) * part
            for side in range(2)
            for dy in range(2)
            for n in range(2)
        ]
        turn_blocks(hidden_ref, plain, turned, offsets)

    grad = (dot(cot_ref[...], w_ref[...], 1, 0) * slope_ref[...]).astype(BF)
    grad_ref[...] = grad
    gb_ref[...] = jnp.sum(grad.astype(F32), 0, keepdims=True)
    outer_grad = dot(turned[...], grad, 1, 0).astype(BF)
    for i, out in enumerate(outs):
        out[...] = outer_grad[2 * i * part : 2 * (i + 1) * part].reshape(out.shape)


def inner_back_pieces(at, cot, w, slope, hidden, cols, wide):
    r, width = slope.shape
    units, part = width // wide, cols // 4
    shape = (2, wide, part, units)
    full = spec((r, D), lambda j, at: (0, 0))
    tile = spec((r, units), lambda j, at: (0, j))
    block = spec((2, 1, part, units), lambda j, at: (0, place(j ^ at[0]), 0, 0))
    out = call(
        partial(inner_back_pieces_body, cols),
        (wide,),
        [full, spec((D, units), lambda j, at: (0, j)), tile, full],
        [tile] + [block] * 4 + [spec((1, units), lambda j, at: (0, j))],
        [pltpu.HBM((r, width), BF)]
        + [pltpu.HBM(shape, BF)] * 2
        + [struct(shape, BF)] * 2
        + [struct((1, width), F32)],
        [pltpu.VMEM((D, r), BF)] * 2,
        prefetch=1,
        us=200,
        nbytes=r * D * 4 + D * width * 4 + r * width * 6,
    )(at, cot, w, slope, hidden)
    pieces = [piece.reshape(2 * wide, part, units) for piece in out[1:5]]
    return out[0], pieces[:2], pieces[2:], out[5]


def norm_pull(grad, normed, inv, gain):
    scaled = grad * gain
    return inv * (
        scaled
        - jnp.mean(scaled, 1, keepdims=True)
        - normed * jnp.mean(scaled * normed, 1, keepdims=True)
    )


def middle_back_body(
    grad_ref, w_ref, middle_ref, cot_ref, vec_ref, out_ref, branch_ref, gain_sum, shift_sum, out_sum
):
    grad = dot(grad_ref[...], w_ref[...], 1, 1)
    normed, inv = stats(middle_ref[...])
    total = cot_ref[...].astype(F32) + norm_pull(
        grad, normed, inv, vec_row(vec_ref, GAIN_TWO)
    )
    out_ref[...] = total
    branch = total.astype(BF)
    branch_ref[...] = branch
    sums = (
        (gain_sum, jnp.sum(grad * normed, 0, keepdims=True)),
        (shift_sum, jnp.sum(grad, 0, keepdims=True)),
        (out_sum, jnp.sum(branch.astype(F32), 0, keepdims=True)),
    )
    for ref, value in sums:
        add_up(ref, value)


def add_up(ref, value):
    @pl.when(pl.program_id(0) == 0)
    def _():
        ref[...] = value

    @pl.when(pl.program_id(0) != 0)
    def _():
        ref[...] += value


def middle_back(grad, w, middle, cot, vecs):
    r, units = grad.shape
    m = row_tile(r)
    vec = spec((1, D), lambda i: (0, 0))
    row = spec((m, D), lambda i: (i, 0))
    vec_out = struct((1, D), F32)
    return call(
        middle_back_body,
        (r // m,),
        [
            spec((m, units), lambda i: (i, 0)),
            spec((D, units), lambda i: (0, 0)),
            row,
            row,
            spec((8, D), lambda i: (0, 0)),
        ],
        [row, row, vec, vec, vec],
        [struct((r, D), F32), struct((r, D), BF), vec_out, vec_out, vec_out],
        us=200,
        nbytes=r * units * 2 + D * units * 2 + r * D * 12,
    )(grad, w, middle, cot, vecs)


def mixed_back_body(branch_ref, tile_ref, w_ref, mixed_ref, grad_ref, gw_ref, turned):
    @pl.when(pl.program_id(0) == 0)
    def _():
        turned[...] = mixed_ref[...].T

    grad_ref[...] = dot(branch_ref[...], w_ref[...], 1, 1).astype(BF)
    gw_ref[...] = dot(turned[...], tile_ref[...], 1, 0).astype(BF)


def mixed_back(branch, w, mixed):
    r = branch.shape[0]
    full = spec((r, D), lambda j: (0, 0))
    tile = spec((r, TILE), lambda j: (0, j))
    return call(
        mixed_back_body,
        (D // TILE,),
        [full, tile, spec((TILE, D), lambda j: (j, 0)), full],
        [tile, spec((D, TILE), lambda j: (0, j))],
        [struct((r, D), BF), struct((D, D), BF)],
        [pltpu.VMEM((D, r), BF)],
        us=0.01,
        vmem=16,
        nbytes=r * D * 8 + D * D * 4,
    )(branch, branch, w, mixed)


def attend_back_body(triple_ref, prob_ref, grad_ref, *rest):
    out_ref = rest[-1]
    scale = HEAD_DIM**-0.5
    for pair in range(HEADS // 2):
        q, k, v = (pair_of(triple_ref, part, pair) for part in range(3))
        grad = pair_of(grad_ref, 0, pair)
        prob = prob_ref[0, 2 * pair : 2 * pair + 2]
        grad_prob = dot(side_by_side(v), grad, 1, 1).reshape(2, ROWS, ROWS)
        inside = jnp.sum(grad_prob * prob, 1, keepdims=True)
        grad_scores = (prob * (grad_prob - inside)).astype(BF).reshape(2 * ROWS, ROWS)
        grads = (
            dot(grad_scores, side_by_side(k), 0, 0) * scale,
            both_heads(dot(grad_scores, q, 1, 0)) * scale,
            both_heads(dot(prob.astype(BF).reshape(2 * ROWS, ROWS), grad, 1, 0)),
        )
        for part, value in enumerate(grads):
            out_ref[:, part * D + pair * 128 : part * D + (pair + 1) * 128] = value.astype(BF)


def attend_back(triple, prob, grad, start, stop, partial_out=None):
    wide = spec((ROWS, 3 * D), lambda g: (g + start, 0))
    count = stop - start
    given = [] if partial_out is None else [partial_out]
    return pl.pallas_call(
        attend_back_body,
        out_shape=struct(triple.shape, BF),
        grid_spec=pltpu.PrefetchScalarGridSpec(
            num_scalar_prefetch=0,
            grid=(count,),
            in_specs=[
                wide,
                spec((1, HEADS, ROWS, ROWS), lambda g: (g + start, 0, 0, 0)),
                spec((ROWS, D), lambda g: (g + start, 0)),
            ]
            + [ANY] * len(given),
            out_specs=wide,
        ),
        input_output_aliases={3: 0} if given else {},
        compiler_params=pltpu.CompilerParams(
            dimension_semantics=("arbitrary",), vmem_limit_bytes=16 * MB
        ),
        cost_estimate=pl.CostEstimate(
            flops=FLOPS_PER_US // 100, bytes_accessed=1024, transcendentals=0
        ),
    )(triple, prob, grad, *given)


def qkv_grad_body(grad_ref, hidden_ref, gw_ref, gb_ref):
    grad = grad_ref[...]
    gw_ref[...] = dot(grad.T, hidden_ref[...], 1, 0).astype(BF)
    gb_ref[...] = jnp.sum(grad.astype(F32), 0, keepdims=True)


def qkv_grad(grad, hidden):
    r, width = grad.shape
    return call(
        qkv_grad_body,
        (width // TILE,),
        [spec((r, TILE), lambda j: (0, j)), spec((r, D), lambda j: (0, 0))],
        [spec((TILE, D), lambda j: (j, 0)), spec((1, TILE), lambda j: (0, j))],
        [struct((width, D), BF), struct((1, width), F32)],
        us=200,
        vmem=16,
        nbytes=r * width * 2 + r * D * 2 + width * D * 2,
    )(grad, hidden)


def first_back_body(grad_ref, w_ref, rows_ref, middle_ref, vec_ref, out_ref, gain_sum, shift_sum):
    grad = dot(grad_ref[...], w_ref[...], 1, 0)
    normed, inv = stats(rows_ref[...].astype(F32))
    pulled = norm_pull(grad, normed, inv, vec_row(vec_ref, GAIN_ONE))
    out_ref[...] = middle_ref[...] + pulled
    add_up(gain_sum, jnp.sum(grad * normed, 0, keepdims=True))
    add_up(shift_sum, jnp.sum(grad, 0, keepdims=True))


def first_back(grad, w, rows, grad_middle, vecs):
    r, width = grad.shape
    m = r // 4 if r % 64 == 0 else row_tile(r)
    vec = spec((1, D), lambda i: (0, 0))
    row = spec((m, D), lambda i: (i, 0))
    vec_out = struct((1, D), F32)
    return call(
        first_back_body,
        (r // m,),
        [
            spec((m, width), lambda i: (i, 0)),
            spec((width, D), lambda i: (0, 0)),
            row,
            row,
            spec((8, D), lambda i: (0, 0)),
        ],
        [row, vec, vec],
        [struct((r, D), F32), vec_out, vec_out],
        us=0.01,
        vmem=22,
        nbytes=r * width * 2 + D * width * 2 + r * D * 10,
    )(grad, w, rows, grad_middle, vecs)


WIDE, NARROW, DP = "wide", "narrow", "dp"


def swap(value, axis, bit):
    size = lax.axis_size(axis)
    return lax.ppermute(value, axis, [(i, i ^ bit) for i in range(size)])


def hold(value, *deps):
    return lax.optimization_barrier((value, deps))[0]


class Pieces:
    def __init__(self, stack, tags):
        self.stack, self.tags = stack, tags

    def fetch(self, axis, bit, *deps):
        move = [bit if axis == name else 0 for name in (WIDE, NARROW, DP)]
        tags = [tuple(a ^ b for a, b in zip(tag, move)) for tag in self.tags]
        return Pieces(swap(hold(self.stack, *deps), axis, bit), tags)

    def after(self, *deps):
        return Pieces(hold(self.stack, *deps), self.tags)

    def rows(self, start, stop):
        return Pieces(self.stack[:, start:stop], self.tags)

    def join(self, *others):
        stack = jnp.concatenate([self.stack] + [o.stack for o in others])
        return Pieces(stack, sum([o.tags for o in others], self.tags))


def first_piece(piece):
    return Pieces(piece[None], [(0, 0, 0)])


def qkv_plan(cols, heads_cols, parts, spots):
    rows = heads_cols // parts

    def plan(w, n, q):
        return [
            (0, spot, (rows, cols), (p * D + w * heads_cols + q * rows, n * cols))
            for p, spot in spots.items()
        ]

    return plan


def out_plan(cols, heads_cols, parts, spot, which=0):
    rows = heads_cols // parts
    return lambda w, n, q: [(which, spot, (rows, cols), (w * heads_cols + q * rows, n * cols))]


def flat_plan(cols, units, rows, base=0):
    return lambda w, n, q: [(0, (0, 0), (rows, units), (n * cols + base + q * rows, w * units))]


def sums_plan(cols, narrow, spot, which):
    return lambda w, n, q: [(which, spot, (16, cols), ((w * narrow + n) * 16, 0))]


def joined(*plans):
    return lambda w, n, q: [move for plan in plans for move in plan(w, n, q)]


def prep_body(cols, at_ref, *refs):
    (qkv_ref, out_ref, up_ref, down_ref), vectors = refs[:4], refs[4:12]
    first_ref, second_ref, up_a_ref, up_b_ref, down_part_ref = refs[12:17]
    held, sem = refs[17:-1], refs[-1]
    core, q = at_ref[2], at_ref[3]

    def block(ref, index, rows, base=0):
        return ref.at[pl.ds(pl.multiple_of(base + index * rows, 16), rows)]

    half = qkv_ref.shape[1] // 2
    ends = [
        (block(qkv_ref.at[0], core, half), first_ref.at[pl.ds(0, half)]),
        (block(out_ref, core, half), first_ref.at[pl.ds(half + 16, half)]),
    ]
    part = half // 2
    ends += [
        (block(qkv_ref.at[1 + p], q, part), second_ref.at[pl.ds(p * part, part)]) for p in range(2)
    ]
    ends.append((block(up_ref, core, up_a_ref.shape[0]), up_a_ref))
    ends.append((block(up_ref, q, up_b_ref.shape[0], up_ref.shape[0] // 2), up_b_ref))
    ends.append((block(down_ref, q, down_part_ref.shape[0]), down_part_ref))
    ends += list(zip(vectors, held))
    copies = [pltpu.make_async_copy(a, b, sem.at[k]) for k, (a, b) in enumerate(ends)]
    for copy in copies:
        copy.start()
    for copy in copies:
        copy.wait()
    lines = [ref[...].astype(F32).reshape(1, -1) for ref in held[:6]]
    both = held[6][...].astype(F32)
    lines.append(jnp.concatenate([both[:1], both[1:]], axis=1))
    wide_line = held[7][...].astype(F32).reshape(1, -1)
    lines += [wide_line[:, k : k + cols] for k in range(0, wide_line.shape[1], cols)]
    lines.append(jnp.zeros((16 - len(lines), cols), F32))
    first_ref[half : half + 16, :] = jnp.concatenate(lines, axis=0).astype(BF)


def prep(at, qkv_t, w_out, w_up, w_down, *vectors):
    cols, half = qkv_t.shape[2], qkv_t.shape[1] // 2
    rows, units = w_up.shape
    shapes = [
        (2 * half + 16, cols),
        (half, cols),
        (rows // 4, units),
        (rows // 8, units),
        (rows // 4, units),
    ]
    return pl.pallas_call(
        partial(prep_body, cols),
        out_shape=[struct(shape, BF) for shape in shapes],
        grid_spec=pltpu.PrefetchScalarGridSpec(
            num_scalar_prefetch=1,
            grid=(1,),
            in_specs=[IN_HBM] * (4 + len(vectors)),
            out_specs=[pl.BlockSpec(memory_space=pltpu.VMEM)] * len(shapes),
            scratch_shapes=[pltpu.VMEM(v.shape, BF) for v in vectors]
            + [pltpu.SemaphoreType.DMA((7 + len(vectors),))],
        ),
        compiler_params=pltpu.CompilerParams(vmem_limit_bytes=8 * MB),
        cost_estimate=pl.CostEstimate(
            flops=FLOPS_PER_US // 100, bytes_accessed=1024, transcendentals=0
        ),
    )(at, *[in_hbm(v) for v in (qkv_t, w_out, w_up, w_down, *vectors)])


def vec_body(wide, narrow, cols, first, tag_lists, at_ref, *refs):
    arrays, (vec_ref, qkv_bias_ref, up_bias_ref, held, sem) = refs[:-5], refs[-5:]
    copies = []
    for array, tags in zip(arrays, tag_lists):
        for k, (dw, dn, _) in enumerate(tags):
            slot = (at_ref[0] ^ dw) * narrow + (at_ref[1] ^ dn)
            source = array.at[k, pl.ds(first, 16)]
            copies.append(pltpu.make_async_copy(source, held.at[slot], sem.at[len(copies)]))
    for copy in copies:
        copy.start()
    for copy in copies:
        copy.wait()
    lines = [held[k].astype(F32) for k in range(wide * narrow)]
    for n in range(narrow):
        vec_ref[:, n * cols : (n + 1) * cols] = lines[n][:8]
    by_wide = [lines[w * narrow] for w in range(wide)]
    half = cols // 2
    q = jnp.concatenate([line[6:7, :half] for line in by_wide], axis=1)
    v = jnp.concatenate([line[6:7, half:] for line in by_wide], axis=1)
    qkv_bias_ref[...] = jnp.concatenate([q, jnp.zeros_like(q), v], axis=1)
    up_bias_ref[...] = jnp.concatenate(
        [line[i : i + 1] for line in by_wide for i in (7, 8)], axis=1
    )


def vectors_of(at, pieces, first, wide, narrow, cols, units):
    vmem = pl.BlockSpec(memory_space=pltpu.VMEM)
    return pl.pallas_call(
        partial(vec_body, wide, narrow, cols, first, [p.tags for p in pieces]),
        out_shape=[struct((8, D), F32), struct((1, 3 * D), F32), struct((1, wide * units), F32)],
        grid_spec=pltpu.PrefetchScalarGridSpec(
            num_scalar_prefetch=1,
            grid=(1,),
            in_specs=[ANY] * len(pieces),
            out_specs=[vmem] * 3,
            scratch_shapes=[
                pltpu.VMEM((wide * narrow, 16, cols), BF),
                pltpu.SemaphoreType.DMA((wide * narrow,)),
            ],
        ),
        compiler_params=pltpu.CompilerParams(vmem_limit_bytes=8 * MB),
        cost_estimate=pl.CostEstimate(flops=FLOPS_PER_US // 100, bytes_accessed=1024, transcendentals=0),
    )(at, *[p.stack for p in pieces])


def pack_body(*refs):
    out = refs[-1]
    at = 0
    for ref in refs[:-1]:
        for k in range(0, ref.shape[1], D):
            out[at : at + 1, :] = ref[:, k : k + D]
            at += 1
    if at < out.shape[0]:
        out[at:, :] = jnp.zeros((out.shape[0] - at, D), F32)


def pack(*rows):
    count = -(-sum(r.shape[1] for r in rows) // (8 * D)) * 8
    vmem = pl.BlockSpec(memory_space=pltpu.VMEM)
    return pl.pallas_call(
        pack_body,
        out_shape=struct((count, D), F32),
        in_specs=[vmem] * len(rows),
        out_specs=vmem,
        compiler_params=pltpu.CompilerParams(vmem_limit_bytes=8 * MB),
        cost_estimate=pl.CostEstimate(flops=FLOPS_PER_US // 100, bytes_accessed=1024, transcendentals=0),
    )(*rows)


ANY = pl.BlockSpec(memory_space=pl.ANY)
IN_HBM = pl.BlockSpec(memory_space=pltpu.HBM)


def owner_sums_body(wide, narrow, cols, *refs):
    out = refs[-1]
    narrow_refs, qkv_ref, up_ref = refs[:6], refs[6], refs[7]
    part, units = D // wide, up_ref.shape[1] // wide
    for w in range(wide):
        for n in range(narrow):
            lines = [ref[:, n * cols : (n + 1) * cols] for ref in narrow_refs]
            lines.append(
                jnp.concatenate(
                    [qkv_ref[:, p * D + w * part : p * D + (w + 1) * part] for p in (0, 2)], axis=1
                )
            )
            lines += [
                up_ref[:, w * units + k : w * units + k + cols] for k in range(0, units, cols)
            ]
            lines.append(jnp.zeros((16 - len(lines), cols), F32))
            at = (w * narrow + n) * 16
            out[at : at + 16, :] = jnp.concatenate(lines, axis=0).astype(BF)


def owner_sums(wide, narrow, cols, *rows):
    vmem = pl.BlockSpec(memory_space=pltpu.VMEM)
    return pl.pallas_call(
        partial(owner_sums_body, wide, narrow, cols),
        out_shape=struct((wide * narrow * 16, cols), BF),
        in_specs=[vmem] * len(rows),
        out_specs=vmem,
        compiler_params=pltpu.CompilerParams(vmem_limit_bytes=8 * MB),
        cost_estimate=pl.CostEstimate(
            flops=FLOPS_PER_US // 100, bytes_accessed=1024, transcendentals=0
        ),
    )(*rows)


def build_body(plans, counts, inverse, parts_by, at_ref, tag_ref, *refs):
    refs, sem = refs[:-1], refs[-1]
    lists = len(counts)
    wholes, arrays = (refs[:-lists], refs[-lists:]) if inverse else (refs[lists:], refs[:lists])

    def each(act):
        first, slot = 0, 0
        for array, plan, count, by in zip(arrays, plans, counts, parts_by):
            moves = len(plan(0, 0, 0))

            def step(k, carry, array=array, plan=plan, by=by, first=first, slot=slot, moves=moves):
                w, n, q = (
                    at_ref[axis] ^ tag_ref[i, first + k] for i, axis in enumerate((0, 1, by))
                )
                for m, (which, (at_row, at_lane), (rows, lanes), (row, lane)) in enumerate(
                    plan(w, n, q)
                ):
                    piece = array.at[k, pl.ds(at_row, rows), pl.ds(at_lane, lanes)]
                    whole = wholes[which].at[
                        pl.ds(pl.multiple_of(row, 16), rows),
                        pl.ds(pl.multiple_of(lane, 128), lanes),
                    ]
                    ends = (whole, piece) if inverse else (piece, whole)
                    act(pltpu.make_async_copy(*ends, sem.at[slot + k * moves + m]))
                return carry

            lax.fori_loop(0, count, step, 0, unroll=4)
            first, slot = first + count, slot + count * moves

    each(lambda copy: copy.start())
    each(lambda copy: copy.wait())


def move_pieces(at, arrays, plans, tag_lists, inverse, parts_by, shapes, pinned=0):
    counts = [len(tags) for tags in tag_lists]
    moves = sum(count * len(plan(0, 0, 0)) for count, plan in zip(counts, plans))
    table = jnp.array([tag for tags in tag_lists for tag in tags], jnp.int32).T
    return pl.pallas_call(
        partial(build_body, plans, counts, inverse, parts_by),
        out_shape=[
            pltpu.HBM(shape, BF) if i < pinned else struct(shape, BF)
            for i, shape in enumerate(shapes)
        ],
        grid_spec=pltpu.PrefetchScalarGridSpec(
            num_scalar_prefetch=2,
            grid=(1,),
            in_specs=[ANY] * len(arrays),
            out_specs=[ANY] * len(shapes),
            scratch_shapes=[pltpu.SemaphoreType.DMA((moves,))],
        ),
        compiler_params=pltpu.CompilerParams(vmem_limit_bytes=4 * MB),
        cost_estimate=pl.CostEstimate(
            flops=FLOPS_PER_US // 100, bytes_accessed=1024, transcendentals=0
        ),
    )(at, table, *arrays)


CORE, DP_INDEX = 2, 3


def build_weights(at, shape, *groups):
    lists = [(p, plan, by) for pieces, plan, by in groups for p in pieces]
    arrays, tags = [p.stack for p, _, _ in lists], [p.tags for p, _, _ in lists]
    plans, parts_by = [plan for _, plan, _ in lists], [by for _, _, by in lists]
    return move_pieces(at, arrays, plans, tags, False, parts_by, [shape])[0]


def cut_grads(at, grads, plan, tags, shape, part_at=CORE):
    lists = [[(w, n, q ^ dc) for w, n, q in tags] for dc in range(2)]
    shapes = [(len(tags),) + shape] * 2
    return move_pieces(at, grads, [plan] * 2, lists, True, [part_at] * 2, shapes, 1)


def fence_body(x_ref, out_ref):
    out_ref[...] = x_ref[...]


def fence(token, us=200):
    vmem = pl.BlockSpec(memory_space=pltpu.VMEM)
    return pl.pallas_call(
        fence_body,
        out_shape=struct(token.shape, token.dtype),
        in_specs=[vmem],
        out_specs=vmem,
        compiler_params=pltpu.CompilerParams(vmem_limit_bytes=MB, has_side_effects=True),
        cost_estimate=pl.CostEstimate(
            flops=us * FLOPS_PER_US, bytes_accessed=1024, transcendentals=0
        ),
    )(token)


class Chain:
    def __init__(self, keep, send):
        self.keep, self.send = keep, send

    def go(self, axis, bit):
        if isinstance(self.send, (list, tuple)):
            self.got = [swap(part, axis, bit) for part in self.send]
        else:
            self.got = swap(self.send, axis, bit)

    def fold(self, *deps):
        self.keep, self.send = halves_summed(self.keep, hold(self.got, *deps))

    def spread(self, *deps):
        got = hold(self.got, *deps)
        order = (0, 2, 1, 3)
        total = [k.astype(F32) + g.astype(F32) for k, g in zip(self.keep, got)]
        self.keep = total[0]
        self.send = [total[order.index(bit)].astype(BF) for bit in range(1, len(total))]
        self.got = [swap(piece, WIDE, bit) for bit, piece in enumerate(self.send, 1)]

    def all_of(self, *deps):
        total = self.keep
        for got in hold(self.got, *deps):
            total = total + got.astype(F32)
        return total

    def total(self, *deps):
        return self.keep[0].astype(F32) + hold(self.got, *deps)[0].astype(F32)


def halves_summed(kept, got):
    def halves(stack):
        if isinstance(stack, (list, tuple)):
            return stack
        half = stack.shape[0] // 2
        return stack[:half], stack[half:]

    first, second = [a.astype(F32) + b.astype(F32) for a, b in zip(halves(kept), halves(got))]
    return first, second.astype(BF)


def quarter(at, shard):
    rows = shard.shape[0] // 4
    return lax.dynamic_slice_in_dim(shard, at[3] * rows, rows, axis=0)


def to_rows(blocks, narrow):
    got = lax.all_to_all(blocks, "narrow", 0, 0, tiled=True)
    return jnp.concatenate([got[n] for n in range(narrow)], axis=1)


def from_rows(rows, narrow):
    cols = rows.shape[1] // narrow
    blocks = jnp.stack([rows[:, n * cols : (n + 1) * cols] for n in range(narrow)])
    got = lax.all_to_all(blocks, "narrow", 0, 0, tiled=True)
    return got.reshape(-1, cols)


def gather_weight(shard, wide, narrow):
    got = lax.all_gather(shard.reshape(-1, 128), ("wide", "narrow"), axis=0, tiled=True)
    return got.reshape((wide, narrow) + shard.shape)


def scatter_grad(blocks):
    shape = blocks.shape[2:]
    got = lax.psum_scatter(
        blocks.reshape(-1, 128), ("wide", "narrow"), scatter_dimension=0, tiled=True
    )
    return lax.psum(got.astype(F32), "dp").reshape(shape)


def on_device(
    wide,
    narrow,
    patches,
    visible,
    w_qkv,
    b_qv,
    w_out,
    b_out,
    w_up,
    b_up,
    w_down,
    b_down,
    gain_one,
    shift_one,
    gain_two,
    shift_two,
    cotangent,
):
    images = visible.shape[0]
    pairs = images // 2
    cols = w_qkv.shape[0]
    heads_cols = w_qkv.shape[2]
    units = w_up.shape[1]
    swaps = cols % 128 == 0 and narrow == 2 and wide == 4 and lax.axis_size(DP) == 4
    swaps = swaps and pairs % 2 == 0

    at = jnp.stack(
        [
            lax.axis_index("wide"),
            lax.axis_index("narrow"),
            lax.axis_index("dp") % 2,
            lax.axis_index("dp"),
        ]
    ).astype(jnp.int32)

    index = (visible.reshape(pairs, 2, VISIBLE) + jnp.array([0, PATCHES])[None, :, None]).reshape(
        pairs, PAIR
    )
    index = jnp.pad(index, ((0, 0), (0, ROWS - PAIR)), constant_values=-1)[:, :, None]

    w_qkv_t = w_qkv.transpose(1, 2, 0)
    if swaps:
        pieces = prep(
            at,
            w_qkv_t,
            w_out,
            w_up,
            w_down,
            gain_one,
            shift_one,
            gain_two,
            shift_two,
            b_out,
            b_down,
            b_qv,
            b_up,
        )
        a_p, b_p, u_p, v_p, d_p = [first_piece(piece) for piece in pieces]

        def part_of(whole, side):
            return lax.dynamic_slice_in_dim(whole, side * cols, cols, axis=1)

        def join_cols(keep, got):
            return jnp.where(
                at[1] == 0,
                jnp.concatenate([keep, got], axis=1),
                jnp.concatenate([got, keep], axis=1),
            )

        mine, theirs = at[1], 1 - at[1]
        whole = (D, wide * units)

        b_z = [b_p.fetch(WIDE, bit) for bit in (1, 2, 3)]
        a_x, d_x = a_p.fetch(NARROW, 1), d_p.fetch(NARROW, 1)
        token = fence(hold(at, a_p.stack, b_p.stack, d_p.stack))
        a_p, d_p = a_p.join(a_x.after(token)), d_p.join(d_x.after(token))
        b_p = b_p.join(*[p.after(token) for p in b_z])

        b_x, a_z = b_p.fetch(NARROW, 1), a_p.fetch(WIDE, 2)
        rows_out = pick_rows(
            hold(at, a_p.stack, b_p.stack, d_p.stack), in_hbm(patches), index, cols
        )
        own = rows_out.shape[0] // 2
        rows_send = rows_out[:own]
        a_p, b_p = a_p.join(a_z.after(rows_send)), b_p.join(b_x.after(rows_send))

        b_y, a_z = b_p.fetch(DP, 2), a_p.fetch(WIDE, 1)
        v_z = v_p.fetch(WIDE, 2, rows_send)
        rows_got = swap(rows_send, NARROW, 1)
        cot_out = cot_rows(hold(at, rows_send, a_p.stack, b_p.stack), cotangent, pairs, cols)
        a_p, b_p = a_p.join(a_z.after(cot_out)), b_p.after(cot_out).join(b_y.after(cot_out))
        v_p = v_p.join(v_z.after(cot_out))
        rows = join_cols(rows_out[own:], hold(rows_got, cot_out))

        started = [a_p.stack, b_p.stack, v_p.stack, rows]
        a_c, b_c = a_p.fetch(DP, 1, *started), b_p.fetch(DP, 1, *started)
        u_z, v_z = u_p.fetch(WIDE, 2, *started), v_p.fetch(WIDE, 1, *started)
        cot_send = hold(cot_out[:own], *started)
        cot_got = swap(cot_send, NARROW, 1)
        half = heads_cols // 2
        vecs, bias_qkv, bias_up = vectors_of(at, [a_p], half, wide, narrow, cols, units)
        hidden_one = norm(hold(rows, *started, cot_send), vecs)
        u_p, v_p = u_p.join(u_z.after(hidden_one)), v_p.join(v_z.after(hidden_one))
        a_c, b_c = a_c.after(hidden_one), b_c.after(hidden_one)

        u_z, v_x = u_p.fetch(WIDE, 1), v_p.fetch(NARROW, 1)
        started = [u_p.stack, v_p.stack]
        d_z = d_p.fetch(WIDE, 2, *started)
        part = heads_cols // 4
        qkv_t = build_weights(
            at,
            (3 * D, D),
            ([a_p, a_c], qkv_plan(cols, heads_cols, 2, {0: (0, 0)}), CORE),
            (
                [b_p, b_c],
                qkv_plan(cols, heads_cols, 4, {1: (0, 0), 2: (part, 0)}),
                DP_INDEX,
            ),
        )
        out_w = build_weights(
            at, (D, D), ([a_p, a_c], out_plan(cols, heads_cols, 2, (half + 16, 0)), CORE)
        )
        triple = qkv(hold(hidden_one, *started), qkv_t, bias_qkv)
        u_p, v_p = u_p.join(u_z.after(triple)), v_p.join(v_x.after(triple))
        d_p = d_p.join(d_z.after(triple))
        cot = join_cols(cot_out[own:], hold(cot_got, triple))

        u_x, v_y, d_z = u_p.fetch(NARROW, 1), v_p.fetch(DP, 2), d_p.fetch(WIDE, 1)
        mixed, prob = attend(hold(triple, u_p.stack, v_p.stack, d_p.stack, cot))
        d_p = d_p.join(d_z.after(mixed))
        u_x, v_y = u_x.after(mixed), v_y.after(mixed)

        u_all, v_all = [u_p, u_x], [v_p, v_y]
        started = [d_p.stack, u_x.stack, v_y.stack]
        d_y = d_p.fetch(DP, 2)
        u_c = [p.fetch(DP, 1, *started) for p in u_all]
        v_c = [p.fetch(DP, 1, *started) for p in v_all]
        middle, hidden_two = mix(hold(mixed, *started), out_w, rows, vecs)
        half_flat = flat_plan(cols, units, cols // 2)
        part_flat = flat_plan(cols, units, cols // 4)
        up_w = build_weights(
            at,
            whole,
            (u_all + [p.after(hidden_two) for p in u_c], part_flat, CORE),
            (
                v_all + [p.after(hidden_two) for p in v_c],
                flat_plan(cols, units, cols // 8, cols // 2),
                DP_INDEX,
            ),
        )
        active, slope = up(hidden_two, up_w, bias_up)

        x_first = [(w, n, 0) for n in range(2) for w in (0, 2, 1, 3)]
        y_first = [(w, n, dy) for dy in (0, 2) for n in range(2) for w in (0, 2, 1, 3)]
        gd_keep, gd_send = outer_pieces(at, cot, in_hbm(active), cols, wide)
        gb_down = jnp.sum(cot, 0, dtype=F32)[None]
        d_y = d_y.after(*gd_send)
        d_c = [p.fetch(DP, 1, d_y.stack) for p in (d_p, d_y)]
        g_d = Chain(gd_keep, [hold(piece, d_y.stack) for piece in gd_send])
        g_d.go(DP, 1)
        d_c = [p.after(*g_d.send) for p in d_c]
        down_w = build_weights(at, whole, ([d_p, d_y] + d_c, part_flat, DP_INDEX))
        g_d.fold(down_w)
        g_d.go(NARROW, 1)
        grad_inner, gu_keep, gu_send, gb_up = inner_back_pieces(
            at, cot, hold(down_w, g_d.send), in_hbm(slope), hidden_two, cols, wide
        )

        result = down(hold(in_hbm(active), grad_inner), down_w, vecs, middle)
        g_u = Chain(gu_keep, [hold(piece, result) for piece in gu_send])
        g_u.go(DP, 1)
        g_d.fold(*g_u.send)
        g_d.go(WIDE, 1)
        g_u.fold(g_d.send)
        g_u.go(DP, 2)
        grad_middle, branch, gg_two, gs_two, gb_out = middle_back(
            hold(grad_inner, g_d.send, g_u.send), up_w, middle, cot, vecs
        )
        grad_mixed, gw_out = mixed_back(branch, out_w, mixed)

        g_d.fold(grad_mixed)
        g_d.go(WIDE, 2)
        result_send = hold(part_of(result, theirs), grad_mixed)
        result_got = swap(result_send, NARROW, 1)
        groups = rows.shape[0] // ROWS
        grad_triple = attend_back(
            triple, in_hbm(prob), hold(grad_mixed, g_d.send, result_send), 0, groups
        )
        grad_rows, gg_one, gs_one = first_back(grad_triple, qkv_t, rows, grad_middle, vecs)

        d_sum = g_d.total(grad_rows)
        d_got = swap(d_sum.astype(BF), DP, 2)
        g_u.fold(grad_rows)
        g_u.go(NARROW, 1)
        result_got = hold(result_got, grad_rows)
        gw_qkv, gb_qkv = qkv_grad(hold(grad_triple, d_sum, g_u.send, result_got), hidden_one)
        sums = owner_sums(
            wide,
            narrow,
            cols,
            gg_one,
            gs_one,
            gg_two,
            gs_two,
            gb_out,
            gb_down,
            gb_qkv,
            gb_up,
        )

        part = heads_cols // 4
        g_q = cut_grads(
            at,
            [gw_qkv],
            qkv_plan(cols, heads_cols, 4, {p: (p * part, 0) for p in range(3)}),
            y_first,
            (3 * part, cols),
            DP_INDEX,
        )
        g_q = Chain(*g_q)
        g_q.go(DP, 1)
        rest_plan = joined(
            out_plan(cols, heads_cols, 2, (0, 0), 0), sums_plan(cols, narrow, (half, 0), 1)
        )
        g_r = Chain(*cut_grads(at, [gw_out, sums], rest_plan, x_first, (half + 16, cols)))
        g_r.go(DP, 1)
        d_sum = d_sum + hold(d_got, g_r.send).astype(F32)
        d_got = swap(d_sum, DP, 1)
        g_u.fold(g_r.send)
        g_u.go(WIDE, 1)
        rows_send = hold(part_of(grad_rows, theirs), g_r.send).astype(BF)
        rows_back = swap(rows_send, NARROW, 1)
        token = fence(hold(vecs, g_q.send, d_sum, g_u.send, rows_send))

        g_q.fold(token)
        g_q.go(DP, 2)
        g_r.fold(token, g_q.send)
        g_r.go(NARROW, 1)
        g_u.fold(g_q.send, g_r.send)
        g_u.go(WIDE, 2)
        rows_back = hold(rows_back, g_u.send)
        grad_patches = put_rows(at, part_of(grad_rows, mine), rows_back, index, cols)

        def in_order(value, other, index):
            return jnp.where(index == 0, jnp.stack([value, other]), jnp.stack([other, value]))

        g_q.fold(grad_patches)
        g_q.go(NARROW, 1)
        g_r.spread(grad_patches, g_q.send)
        u_sum = g_u.total(g_q.send, *g_r.send)
        keep = hold(part_of(result, mine), g_q.send, u_sum, *g_r.send)
        block_output = flat_rows(at, keep, result_got, cols)
        g_q.spread(block_output)
        r_sum = g_r.all_of(block_output)
        r_got = swap(r_sum.astype(BF), DP, 2)
        u_got = swap(u_sum.astype(BF), DP, 2)
        token = fence(hold(token, r_sum, u_sum, *g_q.send))
        q_sum = g_q.all_of(token)
        q_got = [swap(q_sum.astype(BF), DP, bit) for bit in (1, 2, 3)]
        r_sum = r_sum + hold(r_got, q_sum).astype(F32)
        r_got = swap(r_sum[:half], DP, 1)
        u_sum = in_order(u_sum, hold(u_got, token).astype(F32), at[3] // 2)
        u_got = swap(u_sum, DP, 1)
        g_down = in_order(d_sum, d_got, at[2]).reshape(cols, units)
        g_up = in_order(u_sum, u_got, at[2]).transpose(1, 0, 2, 3).reshape(cols, units)
        q_got = [got.astype(F32) for got in q_got]
        pairs_of = [in_order(q_sum, q_got[0], at[2]), in_order(q_got[1], q_got[2], at[2])]
        q_sum = in_order(*pairs_of, at[3] // 2).reshape(4, 3, part, cols)
        g_out = in_order(r_sum[:half], r_got, at[2]).reshape(heads_cols, cols)
        g_qkv = q_sum.transpose(3, 1, 0, 2).reshape(cols, 3, heads_cols)
        grad_patches = grad_patches.reshape(1, -1)
        lines = r_sum[half:]
        vector_grads = [lines[i] for i in range(6)]
        g_bqv = lines[6].reshape(2, heads_cols)
        g_bup = lines[7:9].reshape(units)
    else:
        table = patches.reshape(images, PATCHES, cols)
        rows_mine = jnp.take_along_axis(table, visible[:, :, None], axis=1)
        rows_mine = jnp.pad(
            rows_mine.reshape(pairs, PAIR, cols), ((0, 0), (0, ROWS - PAIR), (0, 0))
        )
        cot_mine = jnp.pad(
            cotangent.reshape(pairs, PAIR, cols), ((0, 0), (0, ROWS - PAIR), (0, 0))
        )
        rows = to_rows(rows_mine.reshape(narrow, -1, cols), narrow)
        cot = to_rows(cot_mine.reshape(narrow, -1, cols), narrow)
        vec = jnp.concatenate(
            [gain_one, shift_one, gain_two, shift_two, b_out, b_down, b_qv.reshape(-1), b_up]
        )
        vec = lax.all_gather(vec, ("wide", "narrow"), axis=0, tiled=False).astype(F32)
        qkv_t = gather_weight(w_qkv_t, wide, narrow)
        qkv_t = qkv_t.transpose(2, 0, 3, 1, 4).reshape(3 * D, D)
        out_w = gather_weight(w_out, wide, narrow).transpose(0, 2, 1, 3).reshape(D, D)
        up_w = gather_weight(w_up, wide, narrow).transpose(1, 2, 0, 3).reshape(D, -1)
        down_w = gather_weight(w_down, wide, narrow).transpose(1, 2, 0, 3).reshape(D, -1)
        vec = vec.reshape(wide, narrow, -1)
        vecs = vec[0, :, : 6 * cols].reshape(narrow, 6, cols).transpose(1, 0, 2).reshape(6, D)
        vecs = jnp.pad(vecs, ((0, 2), (0, 0)))
        by_wide = vec[:, 0, 6 * cols :]
        bias_q = by_wide[:, :heads_cols].reshape(1, D)
        bias_v = by_wide[:, heads_cols : 2 * heads_cols].reshape(1, D)
        bias_qkv = jnp.concatenate([bias_q, jnp.zeros((1, D), F32), bias_v], axis=1)
        bias_up = by_wide[:, 2 * heads_cols :].reshape(1, -1)

        hidden_one = norm(rows, vecs)
        triple = qkv(hidden_one, qkv_t, bias_qkv)
        mixed, prob = attend(triple)
        middle, hidden_two = mix(mixed, out_w, rows, vecs)
        active, slope = up(hidden_two, up_w, bias_up)
        result = down(active, down_w, vecs, middle)
        gw_down = outer(cot, active)
        gb_down = jnp.sum(cot, 0, dtype=F32)[None]
        grad_inner, gw_up, gb_up = inner_back(cot, down_w, slope, hidden_two)
        grad_middle, branch, gg_two, gs_two, gb_out = middle_back(
            grad_inner, up_w, middle, cot, vecs
        )
        grad_mixed, gw_out = mixed_back(branch, out_w, mixed)
        grad_triple = attend_back(triple, prob, grad_mixed, 0, rows.shape[0] // ROWS)
        gw_qkv, gb_qkv = qkv_grad(grad_triple, hidden_one)
        grad_rows, gg_one, gs_one = first_back(grad_triple, qkv_t, rows, grad_middle, vecs)
        sums = pack(gg_one, gs_one, gg_two, gs_two, gb_out, gb_down, gb_qkv, gb_up)

        result = from_rows(result, narrow)
        grad_rows = from_rows(grad_rows, narrow)
        block_output = result.reshape(pairs, ROWS, cols)[:, :PAIR].reshape(1, -1)
        grad_rows = grad_rows.reshape(pairs, ROWS, cols)[:, :PAIR].reshape(images, VISIBLE, cols)
        grad_patches = (
            jnp.zeros((images, PATCHES, cols), F32)
            .at[jnp.arange(images)[:, None], visible]
            .set(grad_rows)
            .reshape(1, -1)
        )
        g_down = scatter_grad(gw_down.reshape(narrow, cols, wide, units).transpose(2, 0, 1, 3))
        g_up = scatter_grad(gw_up.reshape(narrow, cols, wide, units).transpose(2, 0, 1, 3))
        g_out = scatter_grad(gw_out.reshape(wide, heads_cols, narrow, cols).transpose(0, 2, 1, 3))
        g_qkv = scatter_grad(
            gw_qkv.reshape(3, wide, heads_cols, narrow, cols).transpose(1, 3, 0, 2, 4)
        )
        g_qkv = g_qkv.transpose(2, 0, 1)
        sums = lax.psum(sums, ("dp", "wide", "narrow"))
        sums = sums.reshape(-1)
        vector_grads = [
            lax.dynamic_slice_in_dim(sums, i * D + at[1] * cols, cols) for i in range(6)
        ]
        g_bqv = jnp.stack(
            [
                lax.dynamic_slice_in_dim(sums, (6 + i) * D + at[0] * heads_cols, heads_cols)
                for i in (0, 2)
            ]
        )
        g_bup = lax.dynamic_slice_in_dim(sums, 9 * D + at[0] * units, units)

    return (
        block_output,
        grad_patches,
        g_qkv,
        g_bqv,
        g_out,
        vector_grads[4],
        g_up,
        g_bup,
        g_down,
        vector_grads[5],
        vector_grads[0],
        vector_grads[1],
        vector_grads[2],
        vector_grads[3],
    )


def solution(mesh):
    in_specs = (
        P("narrow", ("dp", "wide")),
        P(("dp", "wide"), None),
        P("narrow", None, "wide"),
        P(None, "wide"),
        P("wide", "narrow"),
        P("narrow"),
        P("narrow", "wide"),
        P("wide"),
        P("narrow", "wide"),
        P("narrow"),
        P("narrow"),
        P("narrow"),
        P("narrow"),
        P("narrow"),
        P("narrow", ("dp", "wide")),
    )
    out_specs = (
        P("narrow", ("dp", "wide")),
        P("narrow", ("dp", "wide")),
        P("narrow", None, "wide"),
        P(None, "wide"),
        P("wide", "narrow"),
        P("narrow"),
        P("narrow", "wide"),
        P("wide"),
        P("narrow", "wide"),
        P("narrow"),
        P("narrow"),
        P("narrow"),
        P("narrow"),
        P("narrow"),
    )
    body = partial(on_device, mesh.shape["wide"], mesh.shape["narrow"])
    return jax.shard_map(body, mesh=mesh, in_specs=in_specs, out_specs=out_specs, check_vma=False)
```
